32 devices in a mesh: items: 16 (over z, y, core), seq: 2 (over x).
Axes of the slice: x: 2, y: 2, z: 4, core: 2. Of those that a mesh axis runs over, the one named last changes fastest.
Arguments:
- tokens: bfloat16 [16, 1280, 1024], P('items', 'seq'), may hold values from -6 to 6
- cotangent: bfloat16 [16, 1280, 1024], P('items', 'seq'), may hold values from -6 to 6
- prompt_len: int32 [16], P('items'), may hold values from 150 to 600
- section_ids: int32 [16], P('items'), may hold values from 0 to 7
- section_table: bfloat16 [8, 1024], replicated, may hold values from -6 to 6
- w_query: bfloat16 [1024, 1024], P('items'), may hold values from -0.1875 to 0.1875
- w_key: bfloat16 [1024, 1024], P('items'), may hold values from -0.1875 to 0.1875
- w_value: bfloat16 [1024, 1024], P('items'), may hold values from -0.1875 to 0.1875
- w_out: bfloat16 [1024, 1024], P('items'), may hold values from -4 to 4
- w_up: bfloat16 [1024, 4096], P('items'), may hold values from -0.1875 to 0.1875
- w_down: bfloat16 [4096, 1024], P('items'), may hold values from -0.09375 to 0.09375
- w_ada_one: bfloat16 [1024, 2048], P('items'), may hold values from -0.09375 to 0.09375
- w_ada_two: bfloat16 [1024, 2048], P('items'), may hold values from -0.09375 to 0.09375
Outputs:
- layer_out: bfloat16 [16, 1280, 1024], P('items', 'seq')
- input_grad: float32 [16, 1280, 1024], P('items', 'seq')
- grad_query: float32 [1024, 1024], P(('items', 'seq'))
- grad_key: float32 [1024, 1024], P(('items', 'seq'))
- grad_value: float32 [1024, 1024], P(('items', 'seq'))
- grad_out: float32 [1024, 1024], P(('items', 'seq'))
- grad_up: float32 [1024, 4096], P(('items', 'seq'))
- grad_down: float32 [4096, 1024], P(('items', 'seq'))
- grad_ada_one: float32 [1024, 2048], P(('items', 'seq'))
- grad_ada_two: float32 [1024, 2048], P(('items', 'seq'))
- grad_table: float32 [8, 1024], P(None, ('items', 'seq'))
The draws below stay inside these ranges and needn't reach their ends.
Inputs may be any that keep to these rules, and one draw needn't show every extreme that they name: `prompt_len`: prompt frames at and past an item's length are padding. `section_ids`: the number of items per section is uneven across sections.
All inputs are finite; a program needn't handle non-finite values.
Results may differ from the reference program's by a relative error of at most 0.019.
Values may be sent and summed in bfloat16 or wider, within the bound.
No kernel may reach another device: no remote copies, remote signals or barrier semaphores. Data moves between devices by JAX's collectives and lax.ppermute only.
A program may use at most 384 MiB of HBM per device.

```python
import math
import jax
import jax.numpy as jnp
import numpy as np
from jax import lax

D = 1024
HEADS = 16
HEAD_DIM = 64
FF = 4096
SECTIONS = 8
PROMPT = 640
LEN_LO = 150
LEN_HI = 600
ITEMS = 16
FRAMES = 1280


def set_ends(drawn, own_key, smallest, top_value):
    index_at = [jax.random.randint(jax.random.fold_in(own_key, axis), (), 0, length) for axis, length in enumerate(drawn.shape)]
    main_axis = drawn.shape.index(max(drawn.shape))
    beside = index_at[:main_axis] + [(index_at[main_axis] + 1) % drawn.shape[main_axis]] + index_at[main_axis + 1:]
    return drawn.at[tuple(index_at)].set(smallest).at[tuple(beside)].set(top_value)


def level_of(own_key, dims, split, low, high):
    def one(position, parts):
        heights = jax.random.uniform(jax.random.fold_in(jax.random.fold_in(own_key, 6), position), (parts,), jnp.float32, low / len(split), high / len(split))
        return jnp.repeat(jnp.exp(heights), dims[position] // parts).reshape((-1,) + (1,) * (len(dims) - position - 1))

    factor_of = one(*split[0])
    for cut in split[1:]:
        factor_of = factor_of * one(*cut)
    return factor_of


def rank_table(count, lean):
    portions = [(1 << 20) // math.isqrt(grade ** lean) + 1 for grade in range(1, count + 1)]
    scale = 1 + sum(portions) // (1 << 30)
    return np.cumsum(np.array([max(1, weight // scale) for weight in portions]))


def ranked_ids(rng, dims, amount, lean):
    listing = rank_table(amount, lean)
    ticket = jax.random.randint(jax.random.fold_in(rng, 1), dims, 0, int(listing[amount - 1]))
    rank = jnp.searchsorted(jnp.asarray(listing, jnp.int32), ticket, side="right")
    return jax.random.permutation(jax.random.fold_in(rng, 2), amount)[rank].astype(jnp.int32)


def gaussian(stream_key, shape, scale, limit, shards=(), kind=jnp.bfloat16):
    values = scale * jax.random.normal(stream_key, shape, jnp.float32)
    if shards:
        values = values * level_of(stream_key, shape, shards, -0.22, 0.18)
    return jnp.clip(values, -limit, limit).astype(kind)


def setup_inputs(seed: int = 0) -> dict:
    seeds = jax.random.split(jax.random.key(seed), 14)
    tokens = gaussian(seeds[0], (ITEMS, FRAMES, D), 1.0, 6.0, ((0, 16), (1, 2)))
    cotangent = gaussian(seeds[1], (ITEMS, FRAMES, D), 1.0, 6.0, ((0, 16), (1, 2)))
    prompt_len = set_ends(jax.random.randint(seeds[2], (ITEMS,), LEN_LO, LEN_HI + 1), jax.random.fold_in(seeds[2], 1), LEN_LO, LEN_HI).astype(jnp.int32)
    section_ids = set_ends(ranked_ids(seeds[3], (ITEMS,), SECTIONS, 2), jax.random.fold_in(seeds[3], 3), 0, SECTIONS - 1).astype(jnp.int32)
    section_table = gaussian(seeds[4], (SECTIONS, D), 1.0, 6.0)
    w_query = gaussian(seeds[5], (D, D), D ** -0.5, 0.1875, ((0, 16),))
    w_key = gaussian(seeds[6], (D, D), D ** -0.5, 0.1875, ((0, 16),))
    w_value = gaussian(seeds[7], (D, D), D ** -0.5, 0.1875, ((0, 16),))
    w_out = gaussian(seeds[8], (D, D), (max(D // 512, 1)) ** -0.5, 4.0, ((0, 16),))
    w_up = gaussian(seeds[9], (D, FF), D ** -0.5, 0.1875, ((0, 16),))
    w_down = gaussian(seeds[10], (FF, D), FF ** -0.5, 0.09375, ((0, 16),))
    w_ada_one = gaussian(seeds[11], (D, 2 * D), (4 * D) ** -0.5, 0.09375, ((0, 16),))
    w_ada_two = gaussian(seeds[12], (D, 2 * D), (4 * D) ** -0.5, 0.09375, ((0, 16),))
    return dict(tokens=tokens, cotangent=cotangent, prompt_len=prompt_len, section_ids=section_ids, section_table=section_table, w_query=w_query, w_key=w_key, w_value=w_value, w_out=w_out, w_up=w_up, w_down=w_down, w_ada_one=w_ada_one, w_ada_two=w_ada_two)


@jax.custom_vjp
def low(v):
    return lax.optimization_barrier(v.astype(jnp.bfloat16)).astype(jnp.float32)

@jax.custom_vjp
def low_back(v):
    return v

def low_keep(v):
    return (low(v), None)

def low_pass(kept, grad):
    return (grad,)

def back_keep(v):
    return (v, None)

def back_low(kept, grad):
    return (low(grad),)
low.defvjp(low_keep, low_pass)
low_back.defvjp(back_keep, back_low)
EPSILON = 1e-05
MASKED = -1e+30

def matmul(left, right):
    return jnp.dot(left, right, precision=lax.Precision.HIGHEST)

def ada_norm(values, ada):
    width = values.shape[-1]
    centred = values - lax.optimization_barrier(jnp.mean(values, axis=-1, keepdims=True))
    spread = lax.optimization_barrier(jnp.mean(centred * centred, axis=-1, keepdims=True))
    normed = centred * lax.rsqrt(spread + EPSILON)
    return (1.0 + ada[..., :width]) * normed + ada[..., width:]

def item_forward(frames, params, length, section):
    table, w_query, w_key, w_value, w_out, w_up, w_down, w_ada_one, w_ada_two = params
    count = frames.shape[0]
    scale = 1.0 / math.sqrt(HEAD_DIM)
    cond = table[section]
    ada_one = matmul(cond, w_ada_one)
    ada_two = matmul(cond, w_ada_two)
    normed = low(ada_norm(frames, ada_one))

    def project(weight):
        return low(low_back(matmul(normed, weight))).reshape(count, HEADS, HEAD_DIM)
    query = project(w_query)
    keys = project(w_key)
    values = project(w_value)
    place = jnp.arange(count)
    allowed = (place[None, :] < length) | (place[None, :] >= PROMPT) & (place[:, None] >= PROMPT)
    scores = low_back(jnp.einsum('qhd,khd->hqk', query, keys, precision=lax.Precision.HIGHEST) * scale)
    scores = jnp.where(allowed[None], scores, MASKED)
    probs = low(jax.nn.softmax(scores, axis=-1))
    mixed = jnp.einsum('hqk,khd->qhd', probs, values, precision=lax.Precision.HIGHEST).reshape(count, HEADS * HEAD_DIM)
    mixed = low(low_back(mixed))
    attended = frames + low_back(matmul(mixed, w_out))
    normed_two = low(ada_norm(attended, ada_two))
    upward = low_back(matmul(normed_two, w_up))
    active = low(jax.nn.gelu(upward, approximate=False))
    return attended + low_back(matmul(active, w_down))

def reference(tokens, cotangent, prompt_len, section_ids, section_table, w_query, w_key, w_value, w_out, w_up, w_down, w_ada_one, w_ada_two):
    params = tuple((arr.astype(jnp.float32) for arr in (section_table, w_query, w_key, w_value, w_out, w_up, w_down, w_ada_one, w_ada_two)))

    def step(totals, inputs):
        frames, grad_top, length, section = inputs
        result, pullback = jax.vjp(lambda held, weights: item_forward(held, weights, length, section), frames, params)
        grad_frames, grad_params = pullback(grad_top)
        return (tuple((tot + add for tot, add in zip(totals, grad_params))), (result, grad_frames))
    start = tuple((jnp.zeros_like(arr) for arr in params))
    totals, (results, grads_in) = lax.scan(step, start, (tokens.astype(jnp.float32), cotangent.astype(jnp.float32), prompt_len, section_ids))
    grad_table, grad_query, grad_key, grad_value, grad_out, grad_up, grad_down, grad_ada_one, grad_ada_two = totals
    return (results.astype(jnp.bfloat16), grads_in, grad_query, grad_key, grad_value, grad_out, grad_up, grad_down, grad_ada_one, grad_ada_two, grad_table)
```

```python
from functools import partial
import math

import jax
import jax.numpy as jnp
import numpy as np
from jax import lax
from jax.experimental import pallas as pl
from jax.experimental.pallas import tpu as pltpu
from jax.sharding import PartitionSpec as P

HEAD_DIM = 64
SCALE = 0.125
MASKED = -1e30
TILE = 128
LANES = 128

def row_ids(shape):
    return lax.broadcasted_iota(jnp.int32, shape, 0)
def lane_ids(shape):
    return lax.broadcasted_iota(jnp.int32, shape, 1)
def matmul(left, right):
    return jnp.dot(left, right, preferred_element_type=jnp.float32)
def twin_lanes(flipped):
    top = row_ids(flipped.shape) < HEAD_DIM
    return jnp.concatenate([jnp.where(top, flipped, 0.0), jnp.where(top, 0.0, flipped)], axis=1)
def twin_rows(block):
    first = lane_ids(block.shape) < HEAD_DIM
    return jnp.concatenate([jnp.where(first, block, 0.0), jnp.where(first, 0.0, block)], axis=0)
def untwin(wide):
    top = row_ids((LANES, LANES)) < HEAD_DIM
    return jnp.where(top, wide[:, :LANES], wide[:, LANES:]).T

def split3(value):
    high = value.astype(jnp.bfloat16).astype(jnp.float32)
    rest = value - high
    mid = rest.astype(jnp.bfloat16).astype(jnp.float32)
    return high, mid, rest - mid

def attend_kernel(place, q_ref, k_ref, v_ref, o_ref, lse_ref, keys_wide, values_t):
    half = q_ref.shape[0] // 2
    prompt = pl.multiple_of(place[0] * half, TILE)
    target = pl.multiple_of((1 - place[0]) * half, TILE)
    length = place[1]
    shape = (half, LANES)
    keys_wide[:half, :LANES] = k_ref[pl.ds(prompt, half), :]
    keys_wide[half:, :LANES] = k_ref[pl.ds(target, half), :]
    hidden = (lane_ids(shape) == 0) & (row_ids(shape) >= length)
    keys_wide[:half, LANES:] = jnp.where(hidden, MASKED, 0.0).astype(jnp.bfloat16)
    keys_wide[half:, LANES:] = jnp.zeros(shape, jnp.bfloat16)
    for piece in range(half // TILE):
        rows = slice(piece * TILE, (piece + 1) * TILE)
        values_t[:, rows] = v_ref[pl.ds(prompt + piece * TILE, TILE), :].astype(jnp.float32).T.astype(jnp.bfloat16)
        rows = slice(half + piece * TILE, half + (piece + 1) * TILE)
        values_t[:, rows] = v_ref[pl.ds(target + piece * TILE, TILE), :].astype(jnp.float32).T.astype(jnp.bfloat16)
    below = jnp.where(row_ids((LANES, 2 * TILE)) == 0, 1.0, 0.0)

    def score(start, seen):
        q_flip = (q_ref[pl.ds(start, TILE), :].astype(jnp.float32) * SCALE).T
        q_wide = jnp.concatenate([twin_lanes(q_flip), below], axis=0).astype(jnp.bfloat16)
        return matmul(keys_wide[:seen, :], q_wide)

    def tile(scores, start, seen, slot):
        peak = jnp.max(scores, axis=0, keepdims=True)
        expo = jnp.exp(scores - peak)
        total = jnp.sum(expo, axis=0, keepdims=True)
        out = matmul(values_t[:, :seen], expo.astype(jnp.bfloat16)) / total
        o_ref[pl.ds(start, TILE), :] = untwin(out).astype(jnp.bfloat16)
        lse_ref[0, pl.ds(slot, 1), :] = peak + jnp.log(total)

    tiles = half // TILE

    @pl.loop(0, tiles)
    def _(index):
        at_prompt = pl.multiple_of(prompt + index * TILE, TILE)
        at_target = pl.multiple_of(target + index * TILE, TILE)
        first = score(at_prompt, half)
        second = score(at_target, 2 * half)
        tile(first, at_prompt, half, index)
        tile(second, at_target, 2 * half, tiles + index)


def attend(qkv, place):
    rows = qkv.shape[0]
    width = qkv.shape[1] // 3
    pairs = width // LANES
    block = lambda shift: pl.BlockSpec((rows, LANES), lambda p, s, shift=shift: (0, shift * pairs + p))
    seen = rows * rows * 3 // 4
    return pl.pallas_call(
        attend_kernel,
        grid_spec=pltpu.PrefetchScalarGridSpec(
            num_scalar_prefetch=1, grid=(pairs,),
            in_specs=[block(0), block(1), block(2)],
            out_specs=[block(0), pl.BlockSpec((1, rows // TILE, 2 * TILE), lambda p, s: (p, 0, 0))],
            scratch_shapes=[pltpu.VMEM((rows, 2 * LANES), jnp.bfloat16), pltpu.VMEM((LANES, rows), jnp.bfloat16)],
        ),
        out_shape=[jax.ShapeDtypeStruct((rows, width), jnp.bfloat16),
                   jax.ShapeDtypeStruct((pairs, rows // TILE, 2 * TILE), jnp.float32)],
        compiler_params=pltpu.CompilerParams(vmem_limit_bytes=48 << 20),
        cost_estimate=pl.CostEstimate(flops=pairs * 2 * seen * 4 * HEAD_DIM * 4, transcendentals=pairs * 2 * seen, bytes_accessed=rows * width * 8),
        name="attend",
    )(place, qkv, qkv, qkv)


def attend_back_kernel(place, q_ref, k_ref, v_ref, o_ref, g_ref, lse_ref, out_ref, keys_wide, values_wide, keys_t, dq, dk, dv):
    half = q_ref.shape[0] // 2
    step = pl.program_id(1)
    prompt = pl.multiple_of(place[0] * half, TILE)
    target = pl.multiple_of((1 - place[0]) * half, TILE)
    length = place[1]

    @pl.when(step == 0)
    def _():
        shape = (half, LANES)
        lanes = lane_ids(shape)
        ones = jnp.where((lanes >= 1) & (lanes <= 3), 1.0, 0.0)
        hidden = (lanes == 0) & (row_ids(shape) >= length)
        keys_wide[:half, :LANES] = k_ref[pl.ds(prompt, half), :]
        keys_wide[half:, :LANES] = k_ref[pl.ds(target, half), :]
        keys_wide[:half, LANES:] = jnp.where(hidden, MASKED, ones).astype(jnp.bfloat16)
        keys_wide[half:, LANES:] = ones.astype(jnp.bfloat16)
        values_wide[:half, :LANES] = v_ref[pl.ds(prompt, half), :]
        values_wide[half:, :LANES] = v_ref[pl.ds(target, half), :]
        values_wide[:half, LANES:] = ones.astype(jnp.bfloat16)
        values_wide[half:, LANES:] = ones.astype(jnp.bfloat16)
        for piece in range(2 * half // TILE):
            rows = slice(piece * TILE, (piece + 1) * TILE)
            keys_t[:, rows] = keys_wide[rows, :LANES].astype(jnp.float32).T.astype(jnp.bfloat16)
        dk[...] = jnp.zeros_like(dk)
        dv[...] = jnp.zeros_like(dv)
        wide = (LANES, 2 * TILE)
        ids = row_ids(wide)

        def parts(value):
            high, mid, rest = split3(value)
            return jnp.where(ids == 1, -high, jnp.where(ids == 2, -mid, jnp.where(ids == 3, -rest, 0.0)))

        def tile(start, seen, slot):
            spot = pl.ds(start, TILE)
            q_here = q_ref[spot, :].astype(jnp.float32) * SCALE
            g_here = g_ref[spot, :].astype(jnp.float32)
            g_flip = g_here.T
            product = g_flip * o_ref[spot, :].astype(jnp.float32).T
            inner = jnp.concatenate(
                [jnp.sum(product[:HEAD_DIM], axis=0, keepdims=True), jnp.sum(product[HEAD_DIM:], axis=0, keepdims=True)], axis=1)
            lse = lse_ref[0, pl.ds(slot, 1), :]
            below = jnp.where(ids == 0, 1.0, parts(lse))
            q_wide = jnp.concatenate([twin_lanes(q_here.T), below], axis=0).astype(jnp.bfloat16)
            g_wide = jnp.concatenate([twin_lanes(g_flip), parts(inner)], axis=0).astype(jnp.bfloat16)
            probs = jnp.exp(matmul(keys_wide[:seen, :], q_wide))
            grads = matmul(values_wide[:seen, :], g_wide)
            scores = (probs * grads).astype(jnp.bfloat16)
            dk[:seen, :] += matmul(scores, twin_rows(q_here).astype(jnp.bfloat16))
            dv[:seen, :] += matmul(probs.astype(jnp.bfloat16), twin_rows(g_here).astype(jnp.bfloat16))
            dq[spot, :] = (untwin(matmul(keys_t[:, :seen], scores)) * SCALE).astype(jnp.bfloat16)

        tiles = half // TILE

        @pl.loop(0, tiles)
        def _(index):
            tile(pl.multiple_of(prompt + index * TILE, TILE), half, index)
            tile(pl.multiple_of(target + index * TILE, TILE), 2 * half, tiles + index)

        out_ref[...] = dq[...]

    for which, held in ((1, dk), (2, dv)):
        @pl.when(step == which)
        def _(held=held):
            out_ref[pl.ds(prompt, half), :] = held[:half, :].astype(jnp.bfloat16)
            out_ref[pl.ds(target, half), :] = held[half:, :].astype(jnp.bfloat16)


def attend_back(qkv, mixed, grad, lse, place):
    rows = qkv.shape[0]
    width = qkv.shape[1] // 3
    pairs = width // LANES
    block = lambda shift: pl.BlockSpec((rows, LANES), lambda p, j, s, shift=shift: (0, shift * pairs + p))
    seen = rows * rows * 3 // 4
    return pl.pallas_call(
        attend_back_kernel,
        grid_spec=pltpu.PrefetchScalarGridSpec(
            num_scalar_prefetch=1, grid=(pairs, 3),
            in_specs=[block(0), block(1), block(2), block(0), block(0), pl.BlockSpec((1, rows // TILE, 2 * TILE), lambda p, j, s: (p, 0, 0))],
            out_specs=pl.BlockSpec((rows, LANES), lambda p, j, s: (0, j * pairs + p)),
            scratch_shapes=[pltpu.VMEM((rows, 2 * LANES), jnp.bfloat16), pltpu.VMEM((rows, 2 * LANES), jnp.bfloat16), pltpu.VMEM((LANES, rows), jnp.bfloat16),
                pltpu.VMEM((rows, LANES), jnp.bfloat16), pltpu.VMEM((rows, LANES), jnp.float32), pltpu.VMEM((rows, LANES), jnp.float32)],
        ),
        out_shape=jax.ShapeDtypeStruct((rows, 3 * width), jnp.bfloat16),
        compiler_params=pltpu.CompilerParams(vmem_limit_bytes=48 << 20),
        cost_estimate=pl.CostEstimate(flops=pairs * 2 * seen * 10 * HEAD_DIM * 4, transcendentals=pairs * 2 * seen, bytes_accessed=rows * width * 20),
        name="attend_back",
    )(place, qkv, qkv, qkv, mixed, grad, lse)


HEADS = 16
EPSILON = 1e-05


def exact(left, right):
    return jnp.dot(left, right, precision=lax.Precision.HIGHEST)


def dot_rows(left, right):
    return lax.dot_general(
        left, right, (((0,), (0,)), ((), ())), preferred_element_type=jnp.float32
    )


def dot_last(left, right):
    return lax.dot_general(
        left, right, (((1,), (1,)), ((), ())), preferred_element_type=jnp.float32
    )


def standardise(values):
    centred = values - jnp.mean(values, axis=-1, keepdims=True)
    spread = jnp.mean(centred * centred, axis=-1, keepdims=True)
    inverse = lax.rsqrt(spread + EPSILON)
    return centred * inverse, inverse


def ada_norm(values, ada):
    width = values.shape[-1]
    normed, inverse = standardise(values)
    return (1.0 + ada[:width]) * normed + ada[width:], normed, inverse


def ada_norm_back(grad, normed, inverse, ada):
    width = normed.shape[-1]
    scaled = grad * (1.0 + ada[:width])
    inner = jnp.mean(scaled * normed, axis=-1, keepdims=True)
    values = inverse * (scaled - jnp.mean(scaled, axis=-1, keepdims=True) - normed * inner)
    return values, jnp.concatenate([jnp.sum(grad * normed, axis=0), jnp.sum(grad, axis=0)])


def ring_of(items_count):
    chips = items_count // 2
    outer = 4 if chips % 4 == 0 else chips
    inner = chips // outer
    order = [a * inner for a in range(outer)]
    for turn, a in enumerate(reversed(range(outer))):
        beside = list(range(1, inner))
        order += [a * inner + b for b in (beside if turn % 2 == 0 else beside[::-1])]
    return order


class Mover:
    def __init__(self, items_count, seq_count):
        self.items_count = items_count
        self.seq_count = seq_count
        self.chips = items_count // 2
        order = ring_of(items_count)
        self.forward = []
        self.backward = []
        table = np.zeros((items_count, self.chips), np.int32)
        for spot in range(self.chips):
            for core in range(2):
                here = 2 * order[spot] + core
                after = 2 * order[(spot + 1) % self.chips] + core
                self.forward.append((here, after))
                self.backward.append((after, here))
                for ahead in range(self.chips):
                    table[here, ahead] = order[(spot + ahead) % self.chips]
        self.item = lax.axis_index("items")
        self.core = self.item % 2
        self.seq = lax.axis_index("seq")
        row = lax.dynamic_index_in_dim(jnp.asarray(table), self.item, 0, keepdims=False)
        self.ahead = [row[j] for j in range(self.chips)]

    def flip(self, value, bit):
        pairs = [(i, i ^ bit) for i in range(self.items_count)]
        return lax.ppermute(value, "items", pairs)

    def across(self, value):
        return lax.ppermute(value, "seq", [(0, 1), (1, 0)])

    def sum_items(self, value):
        if self.items_count & (self.items_count - 1):
            return lax.psum(value, "items")
        bit = 1
        while bit < self.items_count:
            value = value + self.flip(value, bit)
            bit *= 2
        return value

    def sum_seq(self, value):
        if self.seq_count == 2:
            return value + self.across(value)
        return lax.psum(value, "seq")

    def frames(self, value):
        if self.seq_count == 2:
            return jnp.concatenate([value, self.across(value)], axis=0)
        return lax.all_gather(value, "seq", axis=0, tiled=True)

    def prompt_spot(self):
        return self.seq if self.seq_count == 2 else jnp.zeros((), jnp.int32)

    def to_rows(self, value):
        rows = value.shape[0] // self.seq_count
        if self.seq_count == 2:
            mine = value[:rows]
            other = self.across(value[rows:])
            return jnp.where(
                self.seq == 0,
                jnp.concatenate([mine, other], axis=1),
                jnp.concatenate([other, mine], axis=1),
            )
        return lax.all_to_all(value, "seq", split_axis=0, concat_axis=1, tiled=True)

    def to_heads(self, value):
        width = value.shape[1] // self.seq_count
        if self.seq_count == 2:
            sent = lax.dynamic_slice_in_dim(value, (1 - self.seq) * width, width, 1)
            held = lax.dynamic_slice_in_dim(value, self.seq * width, width, 1)
            return jnp.concatenate([held, self.across(sent)], axis=0)
        return lax.all_to_all(value, "seq", split_axis=1, concat_axis=0, tiled=True)

    def sum_frames(self, value):
        rows = value.shape[0] // self.seq_count
        if self.seq_count == 2:
            other = self.across(value[rows:].astype(jnp.bfloat16))
            return value[:rows] + other.astype(jnp.float32)
        return lax.psum_scatter(
            value.astype(jnp.bfloat16), "seq", scatter_dimension=0, tiled=True
        ).astype(jnp.float32)

    def reduce_items(self, total):
        chips = self.chips
        parts = total.astype(jnp.bfloat16).reshape(chips, 2, -1, total.shape[1])
        sent = lax.dynamic_index_in_dim(parts, 1 - self.core, 1, keepdims=False)
        kept = lax.dynamic_index_in_dim(parts, self.core, 1, keepdims=False)
        both = kept + self.flip(sent, 1)

        def block(ahead):
            return lax.dynamic_index_in_dim(both, self.ahead[ahead % chips], 0, keepdims=False)

        result = block(0).astype(jnp.float32)
        for pairs, sign, hops in (
            (self.forward, 1, chips // 2),
            (self.backward, -1, (chips - 1) // 2),
        ):
            moving = None
            for left in range(hops, 0, -1):
                piece = block(sign * left)
                moving = piece if moving is None else moving + piece
                moving = lax.ppermute(moving, "items", pairs)
            if moving is not None:
                result = result + moving.astype(jnp.float32)
        return result

    def reduce_seq(self, value):
        rows = value.shape[0] // self.seq_count
        if self.seq_count == 2:
            sent = lax.dynamic_slice_in_dim(value, (1 - self.seq) * rows, rows, 0)
            kept = lax.dynamic_slice_in_dim(value, self.seq * rows, rows, 0)
            return kept + self.across(sent.astype(jnp.bfloat16)).astype(jnp.float32)
        return lax.psum_scatter(
            value.astype(jnp.bfloat16), "seq", scatter_dimension=0, tiled=True
        ).astype(jnp.float32)

    def join_columns(self, value):
        rows = value.shape[0] // self.seq_count
        if self.seq_count == 2:
            sent = lax.dynamic_slice_in_dim(value, (1 - self.seq) * rows, rows, 0)
            kept = lax.dynamic_slice_in_dim(value, self.seq * rows, rows, 0)
            other = self.across(sent)
            return jnp.where(self.seq == 0, kept, other), jnp.where(self.seq == 0, other, kept)
        moved = lax.all_to_all(value, "seq", split_axis=0, concat_axis=0, tiled=True)
        return tuple(moved[j * rows : (j + 1) * rows] for j in range(self.seq_count))


def shards(
    tokens,
    cotangent,
    prompt_len,
    section_ids,
    section_table,
    w_query,
    w_key,
    w_value,
    w_out,
    w_up,
    w_down,
    w_ada_one,
    w_ada_two,
):
    items_count = lax.axis_size("items")
    seq_count = lax.axis_size("seq")
    mover = Mover(items_count, seq_count)
    batch, rows, width = tokens.shape
    hidden = w_up.shape[1]
    held = width // seq_count
    piece = w_query.shape[0]
    tokens = tokens.reshape(rows, width)
    grad_low = cotangent.reshape(rows, width)

    mine = [
        lax.dynamic_slice_in_dim(w, mover.seq * held, held, 1) for w in (w_query, w_key, w_value)
    ]
    qkv_w = lax.all_gather(jnp.concatenate(mine, axis=1), "items", axis=0, tiled=True)
    folds = hidden // width
    up_rows = jnp.concatenate([w_up[:, j * width : (j + 1) * width] for j in range(folds)], axis=0)
    rest = lax.all_gather(
        jnp.concatenate([w_out, up_rows, w_down], axis=0), "items", axis=0, tiled=False
    )
    out_w = rest[:, :piece].reshape(width, width)
    up_w = (
        rest[:, piece : piece + folds * piece]
        .reshape(items_count, folds, piece, width)
        .transpose(0, 2, 1, 3)
        .reshape(width, hidden)
    )
    down_w = rest[:, piece + folds * piece :].reshape(hidden, width)

    table = section_table.astype(jnp.float32)
    own_columns = lax.dynamic_slice_in_dim(section_table, mover.item * piece, piece, 1)
    ada_part = jnp.dot(
        own_columns,
        jnp.concatenate([w_ada_one, w_ada_two], axis=1),
        preferred_element_type=jnp.float32,
    )
    choose = (section_ids[0] == jnp.arange(section_table.shape[0])).astype(jnp.float32)
    ada_all = jnp.sum(choose[:, None] * mover.sum_items(ada_part), axis=0)
    ada_one = ada_all[: 2 * width]
    ada_two = ada_all[2 * width :]

    place = jnp.stack([mover.prompt_spot(), prompt_len[0]]).astype(jnp.int32)
    frames = mover.frames(tokens)
    normed_one, _, _ = ada_norm(frames.astype(jnp.float32), ada_one)
    low_one = normed_one.astype(jnp.bfloat16)
    qkv = jnp.dot(low_one, qkv_w, preferred_element_type=jnp.float32).astype(jnp.bfloat16)
    mixed_heads, lse = attend(qkv, place)
    mixed = mover.to_rows(mixed_heads)
    inputs = tokens.astype(jnp.float32)
    attended = inputs + jnp.dot(mixed, out_w, preferred_element_type=jnp.float32)
    normed_two, unit_two, inverse_two = ada_norm(attended, ada_two)
    low_two = normed_two.astype(jnp.bfloat16)
    upward = jnp.dot(low_two, up_w, preferred_element_type=jnp.float32)
    active, gelu_back = jax.vjp(partial(jax.nn.gelu, approximate=False), upward)
    active_low = active.astype(jnp.bfloat16)
    layer_out = (
        attended + jnp.dot(active_low, down_w, preferred_element_type=jnp.float32)
    ).astype(jnp.bfloat16)

    part_down = mover.reduce_items(dot_rows(active_low, grad_low))
    (grad_upward,) = gelu_back(dot_last(grad_low, down_w))
    upward_low = grad_upward.astype(jnp.bfloat16)
    part_up = mover.reduce_items(dot_rows(low_two, upward_low))
    grad_normed_two = dot_last(upward_low, up_w)
    back_mid, ada_two_rows = ada_norm_back(grad_normed_two, unit_two, inverse_two, ada_two)
    grad_attended = grad_low.astype(jnp.float32) + back_mid
    attended_low = grad_attended.astype(jnp.bfloat16)
    part_out = mover.reduce_items(dot_rows(mixed, attended_low))
    grad_mixed = dot_last(attended_low, out_w).astype(jnp.bfloat16)
    grad_heads = mover.to_heads(grad_mixed)
    grad_qkv = attend_back(qkv, mixed_heads, grad_heads, lse, place)
    part_qkv = mover.reduce_items(dot_rows(low_one, grad_qkv))
    grad_normed_one = mover.sum_frames(dot_last(grad_qkv, qkv_w))
    unit_one, inverse_one = standardise(inputs)
    back_in, ada_one_rows = ada_norm_back(grad_normed_one, unit_one, inverse_one, ada_one)
    input_grad = grad_attended + back_in

    ada_rows = jnp.concatenate([ada_one_rows, ada_two_rows])
    section_sums = mover.sum_items(mover.sum_seq(choose[:, None] * ada_rows[None, :]))
    out_piece = piece // seq_count
    first_row = mover.item * piece + mover.seq * out_piece
    table_rows = lax.dynamic_slice_in_dim(table, first_row, out_piece, 1)
    ada_grads = exact(table_rows.T, section_sums)
    grad_ada_one = ada_grads[:, : 2 * width]
    grad_ada_two = ada_grads[:, 2 * width :]
    own_ada = jnp.concatenate(
        [
            lax.dynamic_slice_in_dim(w, mover.seq * out_piece, out_piece, 0).astype(jnp.float32)
            for w in (w_ada_one, w_ada_two)
        ],
        axis=1,
    )
    grad_table = exact(section_sums, own_ada.T)

    grad_down = mover.reduce_seq(part_down)
    grad_up = mover.reduce_seq(part_up)
    grad_out = mover.reduce_seq(part_out)
    sides = mover.join_columns(part_qkv)
    grad_query, grad_key, grad_value = (
        jnp.concatenate([side[:, j * held : (j + 1) * held] for side in sides], axis=1)
        for j in range(3)
    )
    return (
        layer_out.reshape(batch, rows, width),
        input_grad.reshape(batch, rows, width),
        grad_query,
        grad_key,
        grad_value,
        grad_out,
        grad_up,
        grad_down,
        grad_ada_one,
        grad_ada_two,
        grad_table,
    )


def solution(mesh):
    return jax.shard_map(
        shards,
        mesh=mesh,
        in_specs=(
            P("items", "seq", None),
            P("items", "seq", None),
            P("items"),
            P("items"),
            P(),
            P("items", None),
            P("items", None),
            P("items", None),
            P("items", None),
            P("items", None),
            P("items", None),
            P("items", None),
            P("items", None),
        ),
        out_specs=(
            P("items", "seq", None),
            P("items", "seq", None),
            P(("items", "seq"), None),
            P(("items", "seq"), None),
            P(("items", "seq"), None),
            P(("items", "seq"), None),
            P(("items", "seq"), None),
            P(("items", "seq"), None),
            P(("items", "seq"), None),
            P(("items", "seq"), None),
            P(None, ("items", "seq")),
        ),
        check_vma=False,
    )
```

```python
from functools import partial
import math

import jax
import jax.numpy as jnp
import numpy as np
from jax import lax
from jax.experimental.layout import Layout, with_layout_constraint
from jax.experimental import pallas as pl
from jax.experimental.pallas import tpu as pltpu
from jax.sharding import PartitionSpec as P

HEAD_DIM = 64
SCALE = 0.125
MASKED = -1e30
COVER = 0.5
TILE = 128
LANES = 128

def row_ids(shape):
    return lax.broadcasted_iota(jnp.int32, shape, 0)
def lane_ids(shape):
    return lax.broadcasted_iota(jnp.int32, shape, 1)
def matmul(left, right):
    return jnp.dot(left, right, preferred_element_type=jnp.float32)
def twin_lanes(flipped):
    top = row_ids(flipped.shape) < HEAD_DIM
    return jnp.concatenate([jnp.where(top, flipped, 0.0), jnp.where(top, 0.0, flipped)], axis=1)
def twin_rows(block):
    first = lane_ids(block.shape) < HEAD_DIM
    return jnp.concatenate([jnp.where(first, block, 0.0), jnp.where(first, 0.0, block)], axis=0)
def untwin(wide):
    top = row_ids((LANES, LANES)) < HEAD_DIM
    return jnp.where(top, wide[:, :LANES], wide[:, LANES:]).T

def split3(value):
    high = value.astype(jnp.bfloat16).astype(jnp.float32)
    rest = value - high
    mid = rest.astype(jnp.bfloat16).astype(jnp.float32)
    return high, mid, rest - mid

def attend_kernel(place, q_ref, k_ref, v_ref, *refs):
    o_ref, lse_ref, keys_wide, values_t = refs[-4:]
    half = q_ref.shape[0] // 2
    prompt = pl.multiple_of(place[0] * half, TILE)
    target = pl.multiple_of((1 - place[0]) * half, TILE)
    length = place[1]
    shape = (half, LANES)
    keys_wide[:half, :LANES] = k_ref[pl.ds(prompt, half), :]
    keys_wide[half:, :LANES] = k_ref[pl.ds(target, half), :]
    hidden = (lane_ids(shape) == 0) & (row_ids(shape) >= length)
    keys_wide[:half, LANES:] = jnp.where(hidden, MASKED, 0.0).astype(jnp.bfloat16)
    keys_wide[half:, LANES:] = jnp.zeros(shape, jnp.bfloat16)
    for piece in range(half // TILE):
        rows = slice(piece * TILE, (piece + 1) * TILE)
        values_t[:, rows] = v_ref[pl.ds(prompt + piece * TILE, TILE), :].astype(jnp.float32).T.astype(jnp.bfloat16)
        rows = slice(half + piece * TILE, half + (piece + 1) * TILE)
        values_t[:, rows] = v_ref[pl.ds(target + piece * TILE, TILE), :].astype(jnp.float32).T.astype(jnp.bfloat16)
    below = jnp.where(row_ids((LANES, 2 * TILE)) == 0, 1.0, 0.0)

    def score(start, seen):
        q_flip = (q_ref[pl.ds(start, TILE), :].astype(jnp.float32) * SCALE).T
        q_wide = jnp.concatenate([twin_lanes(q_flip), below], axis=0).astype(jnp.bfloat16)
        return matmul(keys_wide[:seen, :], q_wide)

    def tile(scores, start, seen, slot):
        peak = jnp.max(scores, axis=0, keepdims=True)
        expo = jnp.exp(scores - peak)
        total = jnp.sum(expo, axis=0, keepdims=True)
        out = matmul(values_t[:, :seen], expo.astype(jnp.bfloat16)) / total
        o_ref[pl.ds(start, TILE), :] = untwin(out).astype(jnp.bfloat16)
        lse_ref[0, pl.ds(slot, 1), :] = peak + jnp.log(total)

    tiles = half // TILE

    @pl.loop(0, tiles)
    def _(index):
        at_prompt = pl.multiple_of(prompt + index * TILE, TILE)
        at_target = pl.multiple_of(target + index * TILE, TILE)
        first = score(at_prompt, half)
        second = score(at_target, 2 * half)
        tile(first, at_prompt, half, index)
        tile(second, at_target, 2 * half, tiles + index)


def attend(qkv, place, behind):
    rows = qkv.shape[0]
    width = qkv.shape[1] // 3
    pairs = width // LANES
    part = lambda shift: pl.BlockSpec((rows, LANES), lambda p, s, shift=shift: (0, 3 * p + shift))
    seen = rows * rows * 3 // 4
    return pl.pallas_call(
        attend_kernel,
        grid_spec=pltpu.PrefetchScalarGridSpec(
            num_scalar_prefetch=1, grid=(pairs,),
            in_specs=[part(0), part(1), part(2)] + [pl.BlockSpec(memory_space=pl.ANY)] * len(behind),
            out_specs=[pl.BlockSpec((rows, LANES), lambda p, s: (0, p)), pl.BlockSpec((1, rows // TILE, 2 * TILE), lambda p, s: (p, 0, 0))],
            scratch_shapes=[pltpu.VMEM((rows, 2 * LANES), jnp.bfloat16), pltpu.VMEM((LANES, rows), jnp.bfloat16)],
        ),
        out_shape=[jax.ShapeDtypeStruct((rows, width), jnp.bfloat16),
                   jax.ShapeDtypeStruct((pairs, rows // TILE, 2 * TILE), jnp.float32)],
        compiler_params=pltpu.CompilerParams(vmem_limit_bytes=48 << 20),
        cost_estimate=pl.CostEstimate(flops=int(COVER * pairs * 2 * seen * 4 * HEAD_DIM * 4), transcendentals=0, bytes_accessed=rows * width * 8),
        name="attend",
    )(place, qkv, qkv, qkv, *behind)


def attend_back_kernel(parts, place, q_ref, k_ref, v_ref, o_ref, lse_ref, *refs):
    g_refs = refs[:parts]
    out_ref, keys_wide, values_wide, keys_t, dq, dk, dv = refs[-7:]
    half = q_ref.shape[0] // 2
    step = pl.program_id(0)
    prompt = pl.multiple_of(place[0] * half, TILE)
    target = pl.multiple_of((1 - place[0]) * half, TILE)
    length = place[1]

    @pl.when(step == 0)
    def _():
        shape = (half, LANES)
        lanes = lane_ids(shape)
        ones = jnp.where((lanes >= 1) & (lanes <= 3), 1.0, 0.0)
        hidden = (lanes == 0) & (row_ids(shape) >= length)
        keys_wide[:half, :LANES] = k_ref[pl.ds(prompt, half), :]
        keys_wide[half:, :LANES] = k_ref[pl.ds(target, half), :]
        keys_wide[:half, LANES:] = jnp.where(hidden, MASKED, ones).astype(jnp.bfloat16)
        keys_wide[half:, LANES:] = ones.astype(jnp.bfloat16)
        values_wide[:half, :LANES] = v_ref[pl.ds(prompt, half), :]
        values_wide[half:, :LANES] = v_ref[pl.ds(target, half), :]
        values_wide[:half, LANES:] = ones.astype(jnp.bfloat16)
        values_wide[half:, LANES:] = ones.astype(jnp.bfloat16)
        for piece in range(2 * half // TILE):
            rows = slice(piece * TILE, (piece + 1) * TILE)
            keys_t[:, rows] = keys_wide[rows, :LANES].astype(jnp.float32).T.astype(jnp.bfloat16)
        dk[...] = jnp.zeros_like(dk)
        dv[...] = jnp.zeros_like(dv)
        wide = (LANES, 2 * TILE)
        ids = row_ids(wide)

        def lanes_of(value):
            high, mid, rest = split3(value)
            return jnp.where(ids == 1, -high, jnp.where(ids == 2, -mid, jnp.where(ids == 3, -rest, 0.0)))

        def g_tile(start):
            if parts == 1:
                return g_refs[0][pl.ds(start, TILE), :]
            inside = pl.multiple_of(jnp.where(start < half, start, start - half), TILE)
            first = g_refs[0][pl.ds(inside, TILE), :]
            return jnp.where(start < half, first, g_refs[1][pl.ds(inside, TILE), :])

        def tile(start, seen, slot):
            spot = pl.ds(start, TILE)
            q_here = q_ref[spot, :].astype(jnp.float32) * SCALE
            g_here = g_tile(start).astype(jnp.float32)
            g_flip = g_here.T
            product = g_flip * o_ref[spot, :].astype(jnp.float32).T
            inner = jnp.concatenate(
                [jnp.sum(product[:HEAD_DIM], axis=0, keepdims=True), jnp.sum(product[HEAD_DIM:], axis=0, keepdims=True)], axis=1)
            lse = lse_ref[0, pl.ds(slot, 1), :]
            below = jnp.where(ids == 0, 1.0, lanes_of(lse))
            q_wide = jnp.concatenate([twin_lanes(q_here.T), below], axis=0).astype(jnp.bfloat16)
            g_wide = jnp.concatenate([twin_lanes(g_flip), lanes_of(inner)], axis=0).astype(jnp.bfloat16)
            probs = jnp.exp(matmul(keys_wide[:seen, :], q_wide))
            grads = matmul(values_wide[:seen, :], g_wide)
            scores = (probs * grads).astype(jnp.bfloat16)
            dk[:seen, :] += matmul(scores, twin_rows(q_here).astype(jnp.bfloat16))
            dv[:seen, :] += matmul(probs.astype(jnp.bfloat16), twin_rows(g_here).astype(jnp.bfloat16))
            dq[spot, :] = (untwin(matmul(keys_t[:, :seen], scores)) * SCALE).astype(jnp.bfloat16)

        tiles = half // TILE

        @pl.loop(0, tiles)
        def _(index):
            tile(pl.multiple_of(prompt + index * TILE, TILE), half, index)
            tile(pl.multiple_of(target + index * TILE, TILE), 2 * half, tiles + index)

        out_ref[...] = dq[...]

    for which, held in ((1, dk), (2, dv)):
        @pl.when(step == which)
        def _(held=held):
            out_ref[pl.ds(prompt, half), :] = held[:half, :].astype(jnp.bfloat16)
            out_ref[pl.ds(target, half), :] = held[half:, :].astype(jnp.bfloat16)


def attend_back(place, qkv, mixed, grads, lse, held, behind):
    rows = qkv.shape[0]
    part = lambda shift: pl.BlockSpec((rows, LANES), lambda j, s, shift=shift: (0, 3 * s[2] + shift))
    block = pl.BlockSpec((rows, LANES), lambda j, s: (0, s[2]))
    lse_block = pl.BlockSpec((1, rows // TILE, 2 * TILE), lambda j, s: (s[2], 0, 0))
    seen = rows * rows * 3 // 4
    more = [] if held is None else [held]
    grad_blocks = [pl.BlockSpec((grad.shape[0], LANES), lambda j, s: (0, s[2])) for grad in grads]
    parts = len(grads)
    return pl.pallas_call(
        partial(attend_back_kernel, parts),
        grid_spec=pltpu.PrefetchScalarGridSpec(
            num_scalar_prefetch=1, grid=(3,),
            in_specs=[part(0), part(1), part(2), block, lse_block] + grad_blocks + [pl.BlockSpec(memory_space=pl.ANY)] * (len(more) + len(behind)),
            out_specs=pl.BlockSpec((rows, LANES), lambda j, s: (0, 3 * s[2] + j)),
            scratch_shapes=[pltpu.VMEM((rows, 2 * LANES), jnp.bfloat16), pltpu.VMEM((rows, 2 * LANES), jnp.bfloat16), pltpu.VMEM((LANES, rows), jnp.bfloat16),
                pltpu.VMEM((rows, LANES), jnp.bfloat16), pltpu.VMEM((rows, LANES), jnp.float32), pltpu.VMEM((rows, LANES), jnp.float32)],
        ),
        out_shape=jax.ShapeDtypeStruct(qkv.shape, jnp.bfloat16),
        input_output_aliases={6 + parts: 0} if more else {},
        compiler_params=pltpu.CompilerParams(vmem_limit_bytes=48 << 20),
        cost_estimate=pl.CostEstimate(flops=int(COVER * 2 * seen * 10 * HEAD_DIM * 4), transcendentals=0, bytes_accessed=rows * LANES * 20),
        name="attend_back",
    )(place, qkv, qkv, qkv, mixed, lse, *grads, *more, *behind)


EPSILON = 1e-05
ROOT_HALF = math.sqrt(0.5)
DENSITY = 1.0 / math.sqrt(2.0 * math.pi)
LATE_HOP = 2
BIG = pltpu.CompilerParams(vmem_limit_bytes=60 << 20)
ANYWHERE = pl.BlockSpec(memory_space=pl.ANY)


def cost(flops, moved, special=0):
    return pl.CostEstimate(
        flops=int(flops * COVER), bytes_accessed=int(moved * COVER), transcendentals=special
    )


def matmul_last(left, right):
    return lax.dot_general(
        left, right, (((1,), (1,)), ((), ())), preferred_element_type=jnp.float32
    )


def dot_rows(left, right):
    return lax.dot_general(
        left, right, (((0,), (0,)), ((), ())), preferred_element_type=jnp.float32
    )


def standardise(values):
    centred = values - jnp.mean(values, axis=-1, keepdims=True)
    spread = jnp.mean(centred * centred, axis=-1, keepdims=True)
    inverse = lax.rsqrt(spread + EPSILON)
    return centred * inverse, inverse


def add_rows(ref, scale, shift):
    step = pl.program_id(0)

    @pl.when(step == 0)
    def _():
        ref[0:1, :] = scale
        ref[1:2, :] = shift

    @pl.when(step > 0)
    def _():
        ref[0:1, :] += scale
        ref[1:2, :] += shift


def row_specs(parts, count):
    rows = sum(part.shape[0] for part in parts) // count
    specs = []
    first = 0
    for part in parts:
        steps = part.shape[0] // rows
        specs.append(
            pl.BlockSpec(
                (rows, part.shape[1]),
                lambda j, *s, first=first, steps=steps: (jnp.clip(j - first, 0, steps - 1), 0),
            )
        )
        first += steps
    return rows, specs


def current(refs, count):
    value = refs[0][...]
    for index, ref in enumerate(refs[1:], 1):
        value = jnp.where(pl.program_id(0) < index * count // len(refs), value, ref[...])
    return value


def first_kernel(parts, pieces, count, spots, *refs):
    frames = refs[:parts]
    ada = refs[parts]
    blocks = refs[parts + 1 : parts + 1 + pieces]
    low_ref, qkv_ref, weight_ref, sems = refs[-4:]
    rows = blocks[0].shape[0]

    @pl.when(pl.program_id(0) == 0)
    def _():
        copies = []
        for index, block in enumerate(blocks):
            start = pl.multiple_of(spots[index] * rows, rows)
            copy = pltpu.make_async_copy(
                block, weight_ref.at[pl.ds(start, rows), :], sems.at[index]
            )
            copy.start()
            copies.append(copy)
        for copy in copies:
            copy.wait()

    normed, _ = standardise(current(frames, count).astype(jnp.float32))
    low = ((1.0 + ada[0:1, :]) * normed + ada[1:2, :]).astype(jnp.bfloat16)
    low_ref[...] = low
    qkv_ref[...] = matmul(low, weight_ref[...]).astype(jnp.bfloat16)


def first_layer(frames, ada, blocks, spots):
    count = 4
    rows, specs = row_specs(frames, count)
    width = frames[0].shape[1]
    columns = blocks[0].shape[1]
    out = lambda size: pl.BlockSpec((rows, size), lambda j, s: (j, 0))
    shape = lambda *size: jax.ShapeDtypeStruct(size, jnp.bfloat16)
    return pl.pallas_call(
        partial(first_kernel, len(frames), len(blocks), count),
        grid_spec=pltpu.PrefetchScalarGridSpec(
            num_scalar_prefetch=1,
            grid=(count,),
            in_specs=specs
            + [pl.BlockSpec((2, width), lambda j, s: (0, 0))]
            + [ANYWHERE] * len(blocks),
            out_specs=[
                out(width),
                out(columns),
                pl.BlockSpec((width, columns), lambda j, s: (0, 0)),
            ],
            scratch_shapes=[pltpu.SemaphoreType.DMA((len(blocks),))],
        ),
        out_shape=[
            shape(rows * count, width),
            shape(rows * count, columns),
            shape(width, columns),
        ],
        compiler_params=BIG,
        cost_estimate=cost(
            2 * rows * count * width * columns, 4 * width * columns + 8 * rows * count * width
        ),
        name="first_layer",
    )(spots, *frames, ada, *blocks)


def second_kernel(pieces, spots, *refs):
    mixed = refs[:pieces]
    tokens, out_w, ada = refs[pieces : pieces + 3]
    attended_ref, low_ref = refs[-2:]
    weights = out_w.reshape(out_w.shape[0] * out_w.shape[2], out_w.shape[3])
    attended = tokens[...].astype(jnp.float32)
    for index, piece in enumerate(mixed):
        size = piece.shape[1]
        start = pl.multiple_of(spots[index] * size, size)
        attended = attended + matmul(piece[...], weights[pl.ds(start, size), :])
    attended_ref[...] = attended
    normed, _ = standardise(attended)
    low_ref[...] = ((1.0 + ada[0:1, :]) * normed + ada[1:2, :]).astype(jnp.bfloat16)


def second_layer(mixed, tokens, out_w, out_part, ada, spots):
    rows, width = tokens.shape
    count = 2
    block = lambda size: pl.BlockSpec((rows // count, size), lambda j, s: (j, 0))
    items, _, piece, _ = out_w.shape
    return pl.pallas_call(
        partial(second_kernel, len(mixed)),
        grid_spec=pltpu.PrefetchScalarGridSpec(
            num_scalar_prefetch=1,
            grid=(count,),
            in_specs=[block(part.shape[1]) for part in mixed]
            + [
                block(width),
                pl.BlockSpec((items, 1, piece, width), lambda j, s: (0, out_part, 0, 0)),
                pl.BlockSpec((2, width), lambda j, s: (0, 0)),
            ],
            out_specs=[block(width), block(width)],
        ),
        out_shape=[
            jax.ShapeDtypeStruct((rows, width), jnp.float32),
            jax.ShapeDtypeStruct((rows, width), jnp.bfloat16),
        ],
        compiler_params=BIG,
        cost_estimate=cost(2 * rows * width * width, 2 * width * width + 10 * rows * width),
        name="second_layer",
    )(spots, *mixed, tokens, out_w, ada)


class Weights:
    def __init__(self, up, up_first, down, down_parts, hidden, width):
        self.up = up
        self.down = down
        self.width = width
        self.hidden = hidden
        fold = up.shape[3]
        self.block = min(512, fold, hidden // 2)
        per_chip = down_parts * down.shape[3]
        per_fold = fold // self.block
        chips, _, _, piece, _ = down.shape
        self.steps = hidden // self.block
        per_core = self.steps // 2
        block = self.block
        self.up_spec = pl.BlockSpec(
            (up.shape[0], 1, up.shape[2], block),
            lambda j: (0, up_first + j // per_fold, 0, j % per_fold),
        )
        self.down_spec = pl.BlockSpec(
            (block // per_chip, 1, down_parts, piece, width),
            lambda j: (j % per_core, j // per_core, 0, 0, 0),
        )
        self.per_chip = per_chip
        self.bytes = 2 * hidden * width


def hidden_kernel(per_chip, x_ref, g_ref, up_ref, down_ref, *refs):
    active_ref, grad_ref = refs[-2:]
    columns = min(256, active_ref.shape[1])
    for start in range(0, active_ref.shape[1], columns):
        spot = slice(start, start + columns)
        upward = matmul(x_ref[...], up_ref[:, :, :, spot].reshape(-1, columns))
        chips = slice(start // per_chip, (start + columns) // per_chip)
        grad_active = matmul_last(g_ref[...], down_ref[chips].reshape(columns, -1))
        below = 0.5 * (1.0 + lax.erf(upward * ROOT_HALF))
        active_ref[:, spot] = (upward * below).astype(jnp.bfloat16)
        slope = below + upward * (DENSITY * jnp.exp(-0.5 * upward * upward))
        grad_ref[:, spot] = (grad_active * slope).astype(jnp.bfloat16)


def hidden_layer(x, grad, weights, total_rows, chunk, held=None):
    rows, width = x.shape
    whole = pl.BlockSpec((rows, width), lambda j: (0, 0))
    out = pl.BlockSpec((rows, weights.block), lambda j: (chunk, j))
    shape = jax.ShapeDtypeStruct((total_rows, weights.hidden), jnp.bfloat16)
    more = [] if held is None else list(held)
    return pl.pallas_call(
        partial(hidden_kernel, weights.per_chip),
        grid=(weights.steps,),
        in_specs=[whole, whole, weights.up_spec, weights.down_spec] + [ANYWHERE] * len(more),
        out_specs=[out, out],
        out_shape=[shape, shape],
        input_output_aliases={4: 0, 5: 1} if more else {},
        compiler_params=BIG,
        cost_estimate=cost(
            4 * rows * width * weights.hidden,
            2 * weights.bytes + 4 * rows * (width + weights.hidden),
        ),
        name="hidden_layer",
    )(x, grad, weights.up, weights.down, *more)


def accumulate(part, out_ref, total):
    step = pl.program_id(0)

    @pl.when(step == 0)
    def _():
        total[...] = part

    @pl.when(step > 0)
    def _():
        total[...] += part

    @pl.when(step == pl.num_programs(0) - 1)
    def _():
        out_ref[...] = total[...].astype(out_ref.dtype)


def down_kernel(a_ref, down_ref, *refs):
    out_ref, total = refs[-2:]
    accumulate(matmul(a_ref[...], down_ref[...].reshape(-1, out_ref.shape[1])), out_ref, total)


def up_back_kernel(g_ref, up_ref, *refs):
    out_ref, total = refs[-2:]
    weights = up_ref[...].reshape(out_ref.shape[1], -1)
    accumulate(matmul_last(g_ref[...], weights), out_ref, total)


def hidden_to_width(kernel, name, held, weights, spec, array, rows, chunk, dtype, behind):
    width = weights.width
    return pl.pallas_call(
        kernel,
        grid=(weights.steps,),
        in_specs=[pl.BlockSpec((rows, weights.block), lambda j: (chunk, j)), spec]
        + [ANYWHERE] * len(behind),
        out_specs=pl.BlockSpec((rows, width), lambda j: (0, 0)),
        out_shape=jax.ShapeDtypeStruct((rows, width), dtype),
        scratch_shapes=[pltpu.VMEM((rows, width), jnp.float32)],
        compiler_params=BIG,
        cost_estimate=cost(
            2 * rows * width * weights.hidden,
            weights.bytes + rows * (2 * weights.hidden + 4 * width),
        ),
        name=name,
    )(held, array, *behind)


def down_part(active, weights, rows, chunk, dtype, behind=()):
    return hidden_to_width(
        down_kernel,
        "down_part",
        active,
        weights,
        weights.down_spec,
        weights.down,
        rows,
        chunk,
        dtype,
        behind,
    )


def up_back(grad, weights, rows, chunk, dtype, behind=()):
    return hidden_to_width(
        up_back_kernel,
        "up_back",
        grad,
        weights,
        weights.up_spec,
        weights.up,
        rows,
        chunk,
        dtype,
        behind,
    )


def middle_back_kernel(pieces, spots, *refs):
    own_ref, other_ref, base_ref, top_ref, ada_ref, out_w = refs[:6]
    outs = refs[-3 - pieces :]
    grad_ref, low_ref, ada_grad_ref = outs[:3]
    grad = own_ref[...] + other_ref[...].astype(jnp.float32)
    normed, inverse = standardise(base_ref[...])
    scaled = grad * (1.0 + ada_ref[0:1, :])
    scale = jnp.sum(grad * normed, axis=0, keepdims=True)
    shift = jnp.sum(grad, axis=0, keepdims=True)
    inner = jnp.mean(scaled * normed, axis=-1, keepdims=True)
    shifted = scaled - jnp.mean(scaled, axis=-1, keepdims=True) - normed * inner
    out = top_ref[...].astype(jnp.float32) + inverse * shifted
    grad_ref[...] = out
    low = out.astype(jnp.bfloat16)
    low_ref[...] = low
    weights = out_w.reshape(out_w.shape[0] * out_w.shape[2], out_w.shape[3])
    for index, mixed_ref in enumerate(outs[3:]):
        size = mixed_ref.shape[1]
        start = pl.multiple_of(spots[index] * size, size)
        mixed_ref[...] = matmul_last(low, weights[pl.ds(start, size), :]).astype(jnp.bfloat16)
    add_rows(ada_grad_ref, scale, shift)


def middle_back(own, other, attended, cotangent, ada, out_w, out_part, spots, sizes, behind):
    rows, width = attended.shape
    count = 2
    block = lambda size: pl.BlockSpec((rows // count, size), lambda j, s: (j, 0))
    items, _, piece, _ = out_w.shape
    return pl.pallas_call(
        partial(middle_back_kernel, len(sizes)),
        grid_spec=pltpu.PrefetchScalarGridSpec(
            num_scalar_prefetch=1,
            grid=(count,),
            in_specs=[block(width)] * 4
            + [
                pl.BlockSpec((2, width), lambda j, s: (0, 0)),
                pl.BlockSpec((items, 1, piece, width), lambda j, s: (0, out_part, 0, 0)),
            ]
            + [ANYWHERE] * len(behind),
            out_specs=[block(width), block(width), pl.BlockSpec((2, width), lambda j, s: (0, 0))]
            + [block(size) for size in sizes],
        ),
        out_shape=[
            jax.ShapeDtypeStruct((rows, width), jnp.float32),
            jax.ShapeDtypeStruct((rows, width), jnp.bfloat16),
            jax.ShapeDtypeStruct((2, width), jnp.float32),
        ]
        + [jax.ShapeDtypeStruct((rows, size), jnp.bfloat16) for size in sizes],
        compiler_params=BIG,
        cost_estimate=cost(2 * rows * width * width, 2 * width * width + 20 * rows * width),
        name="middle_back",
    )(spots, own, other, attended, cotangent, ada, out_w, *behind)


def first_back_kernel(parts, count, grad_ref, weight_ref, *refs):
    frames = refs[:parts]
    out_ref, ada_grad_ref = refs[-2:]
    grad = matmul_last(grad_ref[...], weight_ref[...])
    normed, _ = standardise(current(frames, count).astype(jnp.float32))
    out_ref[...] = grad.astype(jnp.bfloat16)
    scale = jnp.sum(grad * normed, axis=0, keepdims=True)
    shift = jnp.sum(grad, axis=0, keepdims=True)
    add_rows(ada_grad_ref, scale, shift)


def first_back(grad, weights, frames, behind):
    width, columns = weights.shape
    count = 4
    rows, specs = row_specs(frames, count)
    block = pl.BlockSpec((rows, width), lambda j: (j, 0))
    return pl.pallas_call(
        partial(first_back_kernel, len(frames), count),
        grid=(count,),
        in_specs=[
            pl.BlockSpec((rows, columns), lambda j: (j, 0)),
            pl.BlockSpec((width, columns), lambda j: (0, 0)),
        ]
        + specs
        + [ANYWHERE] * len(behind),
        out_specs=[block, pl.BlockSpec((2, width), lambda j: (0, 0))],
        out_shape=[
            jax.ShapeDtypeStruct((rows * count, width), jnp.bfloat16),
            jax.ShapeDtypeStruct((2, width), jnp.float32),
        ],
        compiler_params=BIG,
        cost_estimate=cost(
            2 * rows * count * width * columns,
            2 * width * columns + 2 * rows * count * (2 * width + columns),
        ),
        name="first_back",
    )(grad, weights, *frames, *behind)


def stacked_dot(lefts, rights):
    total = None
    for left, right in zip(lefts, rights):
        part = dot_rows(left, right)
        total = part if total is None else total + part
    return total


def cut_rows(ref, count):
    rows = ref.shape[0] // count
    return [ref[j * rows : (j + 1) * rows, :] for j in range(count)]


def put_sum(out_ref, other_ref, value):
    if other_ref is not None:
        value = value + other_ref[...].astype(jnp.float32)
    out_ref[...] = value.astype(jnp.bfloat16)


def hidden_grads_kernel(count, more, core, *refs):
    active, upward = refs[:2]
    grads, lows = refs[2 : 2 + count], refs[2 + count : 2 + 2 * count]
    other = refs[2 + 2 * count] if more else None
    out_ref = refs[-1]
    step = pl.program_id(0)
    steps = pl.num_programs(0) // 2

    @pl.when(step < steps)
    def _():
        put_sum(
            out_ref, other, stacked_dot(cut_rows(active, count), [ref[...] for ref in grads])
        )

    @pl.when(step >= steps)
    def _():
        put_sum(out_ref, other, stacked_dot([ref[...] for ref in lows], cut_rows(upward, count)))


def hidden_grads(core, active, upward, grads, lows, other, behind):
    total, hidden = active.shape
    half = hidden // 2
    rows, width = lows[0].shape
    count = total // rows
    block = 512
    steps = half // block
    low = pl.BlockSpec((rows, width), lambda j, s: (0, 0))
    grad = pl.BlockSpec((rows, block), lambda j, s: (0, jnp.minimum(j, steps - 1)))
    out = pl.BlockSpec((width, block), lambda j, s: (0, j))
    more = [] if other is None else [other]
    return pl.pallas_call(
        partial(hidden_grads_kernel, count, bool(more)),
        grid_spec=pltpu.PrefetchScalarGridSpec(
            num_scalar_prefetch=1,
            grid=(2 * steps,),
            in_specs=[
                pl.BlockSpec((total, half), lambda j, s: (0, s[0])),
                pl.BlockSpec(
                    (total, block), lambda j, s: (0, s[0] * steps + jnp.maximum(j - steps, 0))
                ),
            ]
            + [grad] * count
            + [low] * count
            + [out] * len(more)
            + [ANYWHERE] * len(behind),
            out_specs=out,
        ),
        out_shape=jax.ShapeDtypeStruct((width, 2 * half), jnp.bfloat16),
        compiler_params=BIG,
        cost_estimate=cost(4 * total * half * width, 8 * total * half + 4 * width * half),
        name="hidden_grads",
    )(core, active, upward, *grads, *lows, *more, *behind)


def tail_grads_kernel(first, more, core, low, grad, mixed, attended, *refs):
    other = refs[0] if more else None
    out_ref = refs[-1]

    @pl.when(pl.program_id(0) < first)
    def _():
        put_sum(out_ref, other, dot_rows(low[...], grad[...]))

    @pl.when(pl.program_id(0) >= first)
    def _():
        put_sum(out_ref, other, dot_rows(mixed[...], attended[...]))


def tail_grads(core, low_one, grad_qkv, mixed, attended_low, other, behind):
    total, width = low_one.shape
    rows = mixed.shape[0]
    block = 256
    first = grad_qkv.shape[1] // 2 // block
    second = width // 2 // block
    out = pl.BlockSpec((width, block), lambda j, s: (0, j))
    more = [] if other is None else [other]
    return pl.pallas_call(
        partial(tail_grads_kernel, first, bool(more)),
        grid_spec=pltpu.PrefetchScalarGridSpec(
            num_scalar_prefetch=1,
            grid=(first + second,),
            in_specs=[
                pl.BlockSpec((total, width), lambda j, s: (0, 0)),
                pl.BlockSpec(
                    (total, block), lambda j, s: (0, s[0] * first + jnp.minimum(j, first - 1))
                ),
                pl.BlockSpec((rows, width), lambda j, s: (0, 0)),
                pl.BlockSpec(
                    (rows, block), lambda j, s: (0, s[0] * second + jnp.maximum(j - first, 0))
                ),
            ]
            + [out] * len(more)
            + [ANYWHERE] * len(behind),
            out_specs=out,
        ),
        out_shape=jax.ShapeDtypeStruct((width, (first + second) * block), jnp.bfloat16),
        compiler_params=BIG,
        cost_estimate=cost(
            2 * width * block * (total * first + rows * second), 8 * total * width
        ),
        name="tail_grads",
    )(core, low_one, grad_qkv, mixed, attended_low, *more, *behind)


def input_back_kernel(parts, tokens_ref, ada_ref, base_ref, *refs):
    out_ref = refs[-1]
    grad = refs[0][...].astype(jnp.float32)
    for ref in refs[1:parts]:
        grad = grad + ref[...].astype(jnp.float32)
    normed, inverse = standardise(tokens_ref[...].astype(jnp.float32))
    scaled = grad * (1.0 + ada_ref[0:1, :])
    inner = jnp.mean(scaled * normed, axis=-1, keepdims=True)
    shifted = scaled - jnp.mean(scaled, axis=-1, keepdims=True) - normed * inner
    out_ref[...] = base_ref[...] + inverse * shifted


def input_back(grads, tokens, ada, base):
    rows, width = tokens.shape
    count = 5 if rows % 80 == 0 else 1
    block = pl.BlockSpec((rows // count, width), lambda j: (j, 0))
    return pl.pallas_call(
        partial(input_back_kernel, len(grads)),
        grid=(count,),
        in_specs=[block, pl.BlockSpec((2, width), lambda j: (0, 0)), block] + [block] * len(grads),
        out_specs=block,
        out_shape=jax.ShapeDtypeStruct((rows, width), jnp.float32),
        compiler_params=BIG,
        cost_estimate=cost(20 * rows * width, 14 * rows * width),
        name="input_back",
    )(tokens, ada, base, *grads)


def exact(left, right):
    return jnp.dot(left, right, precision=lax.Precision.HIGHEST)


def rounded(total, other=None):
    if other is not None:
        total = total + other.astype(jnp.float32)
    return total.astype(jnp.bfloat16)


def tie(*values):
    return lax.optimization_barrier(values)


def cut(value, start, size, axis):
    return lax.dynamic_slice_in_dim(value, start, size, axis, allow_negative_indices=False)


def pick(value, index, axis):
    return lax.dynamic_index_in_dim(
        value, index, axis, keepdims=False, allow_negative_indices=False
    )


def ring_of(items_count):
    chips = items_count // 2
    outer = 4 if chips % 4 == 0 else chips
    inner = chips // outer
    order = [a * inner for a in range(outer)]
    for turn, a in enumerate(reversed(range(outer))):
        beside = list(range(1, inner))
        order += [a * inner + b for b in (beside if turn % 2 == 0 else beside[::-1])]
    return order


class Mover:
    def __init__(self, items_count, seq_count):
        self.items_count = items_count
        self.seq_count = seq_count
        self.pair = seq_count == 2
        self.chips = items_count // 2
        order = ring_of(items_count)
        self.forward = []
        self.backward = []
        table = np.zeros((items_count, self.chips + 2), np.int32)
        for spot in range(self.chips):
            for core in range(2):
                here = 2 * order[spot] + core
                next_one = 2 * order[(spot + 1) % self.chips] + core
                self.forward.append((here, next_one))
                self.backward.append((next_one, here))
                for ahead in range(self.chips):
                    table[here, ahead] = order[(spot + ahead) % self.chips]
                table[here, self.chips] = core
                table[here, self.chips + 1] = 1 - core
        self.item = lax.axis_index("items")
        row = pick(jnp.asarray(table), self.item, 0)
        self.ahead = [row[j] for j in range(self.chips)]
        self.core = row[self.chips]
        self.beside = row[self.chips + 1]
        self.core_spot = row[self.chips : self.chips + 1]
        self.beside_spot = row[self.chips + 1 :]
        self.spots = jnp.concatenate(
            [
                2 * row[: self.chips] + row[self.chips],
                2 * row[: self.chips] + row[self.chips + 1],
            ]
        )
        self.seq = lax.axis_index("seq")

    def flip(self, value, bit):
        pairs = [(i, i ^ bit) for i in range(self.items_count)]
        return lax.ppermute(value, "items", pairs)

    def across(self, value):
        return lax.ppermute(value, "seq", [(0, 1), (1, 0)])

    def gather_items(self, value, summed, late):
        bits = [1 << k for k in range(self.items_count.bit_length() - 1)]
        blocks = {0: value}
        moved = [value, value]
        for hop in range(1, self.chips // 2 + 1):
            ways = [self.forward, self.backward][: 2 if hop <= (self.chips - 1) // 2 else 1]
            moved = [lax.ppermute(v, "items", way) for v, way in zip(moved, ways)]
            if hop > 1 and bits:
                summed, moved = tie(summed, moved)
            if hop == LATE_HOP:
                late, moved = tie(late, moved)
            if bits:
                summed = summed + self.flip(summed, bits.pop(0))
            for v, sign in zip(moved, (-1, 1)):
                blocks[(sign * hop) % self.chips] = v
        while bits:
            summed = summed + self.flip(summed, bits.pop(0))
        mine = [blocks[ahead] for ahead in range(self.chips)]
        return mine + [self.flip(block, 1) for block in mine], summed, late

    def sum_seq(self, value):
        return value + self.across(value) if self.pair else lax.psum(value, "seq")

    def scatter_seq(self, value):
        rows = value.shape[0] // self.seq_count
        if self.pair:
            sent = cut(value, (1 - self.seq) * rows, rows, 0)
            kept = cut(value, self.seq * rows, rows, 0)
            return kept + self.across(sent.astype(jnp.bfloat16)).astype(jnp.float32)
        return lax.psum_scatter(
            value.astype(jnp.bfloat16), "seq", scatter_dimension=0, tiled=True
        ).astype(jnp.float32)

    def join_cores(self, value):
        parts = value.reshape(2, -1, value.shape[1])
        kept = pick(parts, self.core, 0)
        other = self.flip(pick(parts, self.beside, 0), 1)
        return jnp.where(self.core == 0, kept, other), jnp.where(self.core == 0, other, kept)

    def join_columns(self, value):
        rows = value.shape[0] // self.seq_count
        if self.pair:
            kept = cut(value, self.seq * rows, rows, 0)
            other = self.across(cut(value, (1 - self.seq) * rows, rows, 0))
            return jnp.where(self.seq == 0, kept, other), jnp.where(self.seq == 0, other, kept)
        moved = lax.all_to_all(value, "seq", split_axis=0, concat_axis=0, tiled=True)
        return tuple(moved[j * rows : (j + 1) * rows] for j in range(self.seq_count))


class RingSum:
    def __init__(self, mover, make, behind):
        self.mover = mover
        self.chips = mover.chips
        self.make = make
        self.flows = None
        self.sent = make(False, None, behind)
        self.arriving = [mover.flip(self.sent, 1)]

    def block(self, ahead):
        return pick(self.both, self.mover.ahead[ahead % self.chips], 0)

    def add_own(self, behind):
        self.both = self.make(True, self.arriving[0], behind)
        self.whole = self.both
        self.both = self.both.reshape(self.chips, -1, self.both.shape[1])
        self.result = self.block(0).astype(jnp.float32)
        flows = [
            (self.mover.forward, 1, self.chips // 2),
            (self.mover.backward, -1, (self.chips - 1) // 2),
        ]
        self.send([(flow, self.block(flow[1] * flow[2])) for flow in flows if flow[2]])

    def send(self, flows):
        self.arriving = [lax.ppermute(value, "items", flow[0]) for flow, value in flows]
        self.flows = [(pairs, sign, left - 1) for (pairs, sign, left), _ in flows]

    def advance(self):
        flows = []
        for flow, value in zip(self.flows, self.arriving):
            if flow[2]:
                flows.append((flow, self.block(flow[1] * flow[2]) + value))
            else:
                self.result = self.result + value.astype(jnp.float32)
        self.send(flows)

    def finish(self):
        while self.arriving:
            self.advance()
        return self.result


def in_rows(value):
    return with_layout_constraint(value, Layout((0, 1)))


def halves(value, core):
    half = value.shape[1] // 2
    return cut(value, core * half, half, 1)


def parted(value, at):
    return (None, None) if value is None else (value[:, :at], value[:, at:])


def shards(
    tokens,
    cotangent,
    prompt_len,
    section_ids,
    section_table,
    w_query,
    w_key,
    w_value,
    w_out,
    w_up,
    w_down,
    w_ada_one,
    w_ada_two,
):
    items_count = lax.axis_size("items")
    seq_count = lax.axis_size("seq")
    mover = Mover(items_count, seq_count)
    chips = mover.chips
    batch, rows, width = tokens.shape
    total_rows = rows * seq_count
    hidden = w_up.shape[1] // seq_count
    held = width // seq_count
    pairs = held // LANES
    piece = w_query.shape[0]
    units = w_down.shape[0] // seq_count
    tokens = tokens.reshape(rows, width)
    grad_low = cotangent.reshape(rows, width)

    def quarters(one, two):
        return jnp.stack([one[:, :width], one[:, width:], two[:, :width], two[:, width:]])

    up_shard = w_up.reshape(piece, chips, 2, seq_count, units).transpose(3, 0, 2, 1, 4)
    up_shard = pick(up_shard, mover.seq, 0).reshape(piece, hidden)
    down_shard = cut(w_down, mover.seq * units, units, 0)
    merged = hidden % width == 0 and units % piece == 0
    late = down_shard
    if merged:
        folds = hidden // width
        down_parts = units // piece
        up_rows = [up_shard[:, j * width : (j + 1) * width] for j in range(folds)]
        late = jnp.concatenate([down_shard] + up_rows + [w_out], axis=0)

    table_part = cut(section_table, mover.item * piece, piece, 1)
    ada_part = jnp.dot(
        table_part,
        jnp.concatenate([w_ada_one, w_ada_two], axis=1),
        preferred_element_type=jnp.float32,
    )
    ada_part = quarters(ada_part[:, : 2 * width], ada_part[:, 2 * width :])
    mine = [cut(w, mover.seq * held, held, 1) for w in (w_query, w_key, w_value)]
    mine = [w[:, p * LANES : (p + 1) * LANES] for p in range(pairs) for w in mine]
    blocks, ada_sum, late = mover.gather_items(jnp.concatenate(mine, axis=1), ada_part, late)

    def gathered(value):
        return lax.all_gather(value, "items", axis=0, tiled=False)

    if merged:
        rest = gathered(late)
        rest = rest.reshape(items_count, down_parts + folds + 1, piece, width)
        by_core = rest.reshape((chips, 2) + rest.shape[1:])
        weights = Weights(rest, down_parts, by_core, down_parts, hidden, width)
        out_w, out_part = rest, down_parts + folds
    else:
        by_core = gathered(late).reshape(chips, 2, 1, units, width)
        weights = Weights(gathered(up_shard)[:, None], 0, by_core, 1, hidden, width)
        out_w, out_part = gathered(w_out)[:, None], 0

    choose = (section_ids[0] == jnp.arange(section_table.shape[0])).astype(jnp.float32)
    ada = jnp.sum(choose[None, :, None] * ada_sum, axis=1)
    ada_one = ada[:2]
    ada_two = ada[2:]

    if mover.pair:
        prompt_at = mover.seq
        tokens_other = mover.across(tokens)
        grad_other = mover.across(grad_low)
        frames = [tokens, tokens_other]
        grads = [grad_low, grad_other]
        spots = jnp.stack([mover.seq, 1 - mover.seq])
        other_spots = jnp.stack([1 - mover.seq, mover.seq])
    else:
        prompt_at = jnp.zeros((), jnp.int32)
        frames = [lax.all_gather(tokens, "seq", axis=0, tiled=True)]
        grads = [lax.all_gather(grad_low, "seq", axis=0, tiled=True)]
        spots = other_spots = jnp.zeros((1,), jnp.int32)
    low_one, qkv, qkv_w = first_layer(frames, ada_one, blocks, mover.spots)
    length = prompt_len[0]
    mixed_heads, lse = attend(
        qkv, jnp.stack([prompt_at, length]).astype(jnp.int32), grads[1:]
    )
    if mover.pair:
        mixed_parts = [mixed_heads[:rows], mover.across(mixed_heads[rows:])]
        mixed = jnp.where(
            mover.seq == 0,
            jnp.concatenate(mixed_parts, axis=1),
            jnp.concatenate(mixed_parts[::-1], axis=1),
        )
    else:
        mixed = lax.all_to_all(mixed_heads, "seq", split_axis=0, concat_axis=1, tiled=True)
        mixed_parts = [mixed]
    attended, low_two = second_layer(mixed_parts, tokens, out_w, out_part, ada_two, spots)

    if mover.pair:
        low_other = mover.across(low_two)
        both = hidden_layer(low_two, grad_low, weights, total_rows, 0)
        active, upward = hidden_layer(low_other, grad_other, weights, total_rows, 1, both)
        lows = [low_two, low_other]
        for_other = up_back(upward, weights, rows, 1, jnp.bfloat16)
        from_other = mover.across(for_other)
        start = [for_other]
    else:
        lows = [lax.all_gather(low_two, "seq", axis=0, tiled=True)]
        active, upward = hidden_layer(lows[0], grads[0], weights, total_rows, 0)
        start = []

    down_columns = hidden // 2

    def hidden_parts(own, other, behind):
        spot = mover.core_spot if own else mover.beside_spot
        if down_columns == width:
            return hidden_grads(spot, active, upward, grads, lows, other, behind)
        core = mover.core if own else mover.beside
        first, second = parted(other, down_columns)
        down = dot_rows(halves(active, core), grads[0]).reshape(width, down_columns)
        up = dot_rows(lows[0], halves(upward, core))
        return in_rows(jnp.concatenate([rounded(down, first), rounded(up, second)], axis=1))

    ring = RingSum(mover, hidden_parts, start)
    if mover.pair:
        own = up_back(upward, weights, rows, 0, jnp.float32, [ring.sent])
        sizes = [held, held]
    else:
        own = lax.psum_scatter(
            up_back(upward, weights, total_rows, 0, jnp.bfloat16),
            "seq",
            scatter_dimension=0,
            tiled=True,
        ).astype(jnp.float32)
        from_other = jnp.zeros((rows, width), jnp.bfloat16)
        sizes = [width]
    ring.add_own([own])
    grad_attended, attended_low, ada_two_rows, *grad_mixed = middle_back(
        own,
        from_other,
        attended,
        grad_low,
        ada_two,
        out_w,
        out_part,
        other_spots,
        sizes,
        [ring.whole],
    )
    if mover.pair:
        out_other = down_part(active, weights, rows, 1, jnp.bfloat16, grad_mixed[:1])
        grad_heads = [grad_mixed[1], mover.across(grad_mixed[0])]
        filler = [out_other]
        out_other = mover.across(out_other)
    else:
        grad_heads = [
            lax.all_to_all(grad_mixed[0], "seq", split_axis=1, concat_axis=0, tiled=True)
        ]
        filler = []

    split = pairs // 2 if pairs % 2 == 0 else 0

    def tail_parts(own, other, behind):
        spot = mover.core_spot if own else mover.beside_spot
        if pairs % 4 == 0:
            return tail_grads(spot, low_one, grad_qkv, mixed, attended_low, other, behind)
        core = mover.core if own else mover.beside
        first, second = parted(other, grad_qkv.shape[1] // 2)
        qkv_part = rounded(dot_rows(low_one, halves(grad_qkv, core)), first)
        out_part = rounded(dot_rows(mixed, halves(attended_low, core)), second)
        return in_rows(jnp.concatenate([qkv_part, out_part], axis=1))

    tail = None
    grad_qkv = None
    for turn in range(pairs):
        behind = filler
        filler = []
        if turn != 1:
            behind = behind + ring.arriving
        pair = (mover.beside * split + turn) & (pairs - 1)
        place = jnp.stack([prompt_at, length, pair]).astype(jnp.int32)
        grad_qkv = attend_back(place, qkv, mixed_heads, grad_heads, lse, grad_qkv, behind)
        if turn != 1:
            ring.advance()
        if turn + 1 == split:
            tail = RingSum(mover, tail_parts, [])
            filler = [tail.sent]
    if tail is None:
        tail = RingSum(mover, tail_parts, [])
    tail.add_own([])
    grad_first, ada_one_rows = first_back(grad_qkv, qkv_w, frames, [tail.whole])
    ada_rows = jnp.concatenate([ada_one_rows, ada_two_rows])
    if mover.pair:
        grad_parts = [grad_first[:rows], mover.across(grad_first[rows:])]
        layer_sum = down_part(active, weights, rows, 0, jnp.float32, [ada_one_rows])
        layer_sum = layer_sum + out_other.astype(jnp.float32)
    else:
        grad_parts = [lax.psum_scatter(grad_first, "seq", scatter_dimension=0, tiled=True)]
        layer_sum = lax.psum_scatter(
            down_part(active, weights, total_rows, 0, jnp.bfloat16),
            "seq",
            scatter_dimension=0,
            tiled=True,
        ).astype(jnp.float32)
    layer_out = (attended + layer_sum).astype(jnp.bfloat16)
    input_grad = input_back(grad_parts, tokens, ada_one, grad_attended)

    sums = mover.sum_seq(choose[None, :, None] * ada_rows[:, None, :])
    bit = 1
    while bit < items_count:
        sums = sums + mover.flip(sums, bit)
        bit *= 2
    out_piece = piece // seq_count
    first_row = mover.item * piece + mover.seq * out_piece
    table_rows = cut(section_table, first_row, out_piece, 1).astype(jnp.float32)
    ada_grads = jnp.einsum("sr,ksd->krd", table_rows, sums, precision=lax.Precision.HIGHEST)
    grad_ada_one = jnp.concatenate([ada_grads[0], ada_grads[1]], axis=1)
    grad_ada_two = jnp.concatenate([ada_grads[2], ada_grads[3]], axis=1)
    own_ada = quarters(
        *(cut(w, mover.seq * out_piece, out_piece, 0) for w in (w_ada_one, w_ada_two))
    ).astype(jnp.float32)
    grad_table = jnp.einsum("ksd,krd->sr", sums, own_ada, precision=lax.Precision.HIGHEST)

    ring_total = ring.finish()
    grad_down = ring_total[:, :down_columns].reshape(units, width)
    up_sides = mover.join_columns(
        jnp.concatenate(mover.join_cores(ring_total[:, down_columns:]), axis=1)
    )
    grad_up = jnp.stack(
        [side.reshape(out_piece, 2, chips, units) for side in up_sides], axis=1
    )
    grad_up = grad_up.transpose(0, 3, 2, 1, 4).reshape(out_piece, hidden * seq_count)
    tail_total = tail.finish()
    cores = jnp.concatenate(mover.join_cores(tail_total), axis=1)
    half_qkv = 3 * held // 2
    half_all = cores.shape[1] // 2
    qkv_total = jnp.concatenate(
        [cores[:, :half_qkv], cores[:, half_all : half_all + half_qkv]], axis=1
    )
    out_total = jnp.concatenate([cores[:, half_qkv:half_all], cores[:, half_all + half_qkv :]], axis=1)
    sides = mover.join_columns(qkv_total)
    grad_out = mover.scatter_seq(out_total)
    grad_query, grad_key, grad_value = (
        jnp.concatenate(
            [
                side[:, (3 * p + j) * LANES : (3 * p + j + 1) * LANES]
                for side in sides
                for p in range(pairs)
            ],
            axis=1,
        )
        for j in range(3)
    )
    return (
        layer_out.reshape(batch, rows, width),
        input_grad.reshape(batch, rows, width),
        grad_query,
        grad_key,
        grad_value,
        grad_out,
        grad_up,
        grad_down,
        grad_ada_one,
        grad_ada_two,
        grad_table,
    )


def solution(mesh):
    return jax.shard_map(
        shards,
        mesh=mesh,
        in_specs=(
            P("items", "seq", None),
            P("items", "seq", None),
            P("items"),
            P("items"),
            P(),
            P("items", None),
            P("items", None),
            P("items", None),
            P("items", None),
            P("items", None),
            P("items", None),
            P("items", None),
            P("items", None),
        ),
        out_specs=(
            P("items", "seq", None),
            P("items", "seq", None),
            P(("items", "seq"), None),
            P(("items", "seq"), None),
            P(("items", "seq"), None),
            P(("items", "seq"), None),
            P(("items", "seq"), None),
            P(("items", "seq"), None),
            P(("items", "seq"), None),
            P(("items", "seq"), None),
            P(None, ("items", "seq")),
        ),
        check_vma=False,
    )
```

```python
from functools import partial
import math

import jax
import jax.numpy as jnp
import numpy as np
from jax import lax
from jax.experimental.layout import Layout, with_layout_constraint
from jax.experimental import pallas as pl
from jax.experimental.pallas import tpu as pltpu
from jax.sharding import PartitionSpec as P

HEAD_DIM = 64
SCALE = 0.125
MASKED = -1e30
COVER = 0.5
TILE = 128
LANES = 128

def row_ids(shape):
    return lax.broadcasted_iota(jnp.int32, shape, 0)
def lane_ids(shape):
    return lax.broadcasted_iota(jnp.int32, shape, 1)
def matmul(left, right):
    return jnp.dot(left, right, preferred_element_type=jnp.float32)
def twin_lanes(flipped):
    top = row_ids(flipped.shape) < HEAD_DIM
    return jnp.concatenate([jnp.where(top, flipped, 0.0), jnp.where(top, 0.0, flipped)], axis=1)
def twin_rows(block):
    first = lane_ids(block.shape) < HEAD_DIM
    return jnp.concatenate([jnp.where(first, block, 0.0), jnp.where(first, 0.0, block)], axis=0)
def untwin(wide):
    top = row_ids((LANES, LANES)) < HEAD_DIM
    return jnp.where(top, wide[:, :LANES], wide[:, LANES:]).T

def split3(value):
    high = value.astype(jnp.bfloat16).astype(jnp.float32)
    rest = value - high
    mid = rest.astype(jnp.bfloat16).astype(jnp.float32)
    return high, mid, rest - mid

def attend_kernel(place, q_ref, k_ref, v_ref, *refs):
    o_ref, lse_ref, keys_wide, values_t = refs[-4:]
    half = q_ref.shape[0] // 2
    prompt = pl.multiple_of(place[0] * half, TILE)
    target = pl.multiple_of((1 - place[0]) * half, TILE)
    length = place[1]
    shape = (half, LANES)
    keys_wide[:half, :LANES] = k_ref[pl.ds(prompt, half), :]
    keys_wide[half:, :LANES] = k_ref[pl.ds(target, half), :]
    hidden = (lane_ids(shape) == 0) & (row_ids(shape) >= length)
    keys_wide[:half, LANES:] = jnp.where(hidden, MASKED, 0.0).astype(jnp.bfloat16)
    keys_wide[half:, LANES:] = jnp.zeros(shape, jnp.bfloat16)
    for piece in range(half // TILE):
        rows = slice(piece * TILE, (piece + 1) * TILE)
        values_t[:, rows] = v_ref[pl.ds(prompt + piece * TILE, TILE), :].astype(jnp.float32).T.astype(jnp.bfloat16)
        rows = slice(half + piece * TILE, half + (piece + 1) * TILE)
        values_t[:, rows] = v_ref[pl.ds(target + piece * TILE, TILE), :].astype(jnp.float32).T.astype(jnp.bfloat16)
    below = jnp.where(row_ids((LANES, 2 * TILE)) == 0, 1.0, 0.0)

    def score(start, seen):
        q_flip = (q_ref[pl.ds(start, TILE), :].astype(jnp.float32) * SCALE).T
        q_wide = jnp.concatenate([twin_lanes(q_flip), below], axis=0).astype(jnp.bfloat16)
        return matmul(keys_wide[:seen, :], q_wide)

    def tile(scores, start, seen, slot):
        peak = jnp.max(scores, axis=0, keepdims=True)
        expo = jnp.exp(scores - peak)
        total = jnp.sum(expo, axis=0, keepdims=True)
        out = matmul(values_t[:, :seen], expo.astype(jnp.bfloat16)) / total
        o_ref[pl.ds(start, TILE), :] = untwin(out).astype(jnp.bfloat16)
        lse_ref[0, pl.ds(slot, 1), :] = peak + jnp.log(total)

    tiles = half // TILE

    @pl.loop(0, tiles)
    def _(index):
        at_prompt = pl.multiple_of(prompt + index * TILE, TILE)
        at_target = pl.multiple_of(target + index * TILE, TILE)
        first = score(at_prompt, half)
        second = score(at_target, 2 * half)
        tile(first, at_prompt, half, index)
        tile(second, at_target, 2 * half, tiles + index)


def attend(qkv, place, first, pairs, behind):
    rows = qkv.shape[0]
    width = pairs * LANES
    part = lambda shift: pl.BlockSpec((rows, LANES), lambda p, s, shift=shift: (0, 3 * (first + p) + shift))
    seen = rows * rows * 3 // 4
    return pl.pallas_call(
        attend_kernel,
        grid_spec=pltpu.PrefetchScalarGridSpec(
            num_scalar_prefetch=1, grid=(pairs,),
            in_specs=[part(0), part(1), part(2)] + [pl.BlockSpec(memory_space=pl.ANY)] * len(behind),
            out_specs=[pl.BlockSpec((rows, LANES), lambda p, s: (0, p)), pl.BlockSpec((1, rows // TILE, 2 * TILE), lambda p, s: (p, 0, 0))],
            scratch_shapes=[pltpu.VMEM((rows, 2 * LANES), jnp.bfloat16), pltpu.VMEM((LANES, rows), jnp.bfloat16)],
        ),
        out_shape=[jax.ShapeDtypeStruct((rows, width), jnp.bfloat16),
                   jax.ShapeDtypeStruct((pairs, rows // TILE, 2 * TILE), jnp.float32)],
        compiler_params=pltpu.CompilerParams(vmem_limit_bytes=60 << 20),
        cost_estimate=pl.CostEstimate(flops=int(COVER * pairs * 2 * seen * 4 * HEAD_DIM * 4), transcendentals=0, bytes_accessed=rows * width * 8),
        name="attend",
    )(place, qkv, qkv, qkv, *behind)


def attend_back_kernel(parts, calls, place, q_ref, k_ref, v_ref, *refs):
    o_refs, lse_refs, g_refs = refs[:calls], refs[calls:2 * calls], refs[2 * calls:2 * calls + parts]
    per = place[3]
    out_ref, keys_wide, values_wide, keys_t, dq, dk, dv = refs[-7:]
    half = q_ref.shape[0] // 2
    step = pl.program_id(0)
    prompt = pl.multiple_of(place[0] * half, TILE)
    target = pl.multiple_of((1 - place[0]) * half, TILE)
    length = place[1]

    @pl.when(step == 0)
    def _():
        shape = (half, LANES)
        lanes = lane_ids(shape)
        ones = jnp.where((lanes >= 1) & (lanes <= 3), 1.0, 0.0)
        hidden = (lanes == 0) & (row_ids(shape) >= length)
        keys_wide[:half, :LANES] = k_ref[pl.ds(prompt, half), :]
        keys_wide[half:, :LANES] = k_ref[pl.ds(target, half), :]
        keys_wide[:half, LANES:] = jnp.where(hidden, MASKED, ones).astype(jnp.bfloat16)
        keys_wide[half:, LANES:] = ones.astype(jnp.bfloat16)
        values_wide[:half, :LANES] = v_ref[pl.ds(prompt, half), :]
        values_wide[half:, :LANES] = v_ref[pl.ds(target, half), :]
        values_wide[:half, LANES:] = ones.astype(jnp.bfloat16)
        values_wide[half:, LANES:] = ones.astype(jnp.bfloat16)
        for piece in range(2 * half // TILE):
            rows = slice(piece * TILE, (piece + 1) * TILE)
            keys_t[:, rows] = keys_wide[rows, :LANES].astype(jnp.float32).T.astype(jnp.bfloat16)
        dk[...] = jnp.zeros_like(dk)
        dv[...] = jnp.zeros_like(dv)
        wide = (LANES, 2 * TILE)
        ids = row_ids(wide)

        def lanes_of(value):
            high, mid, rest = split3(value)
            return jnp.where(ids == 1, -high, jnp.where(ids == 2, -mid, jnp.where(ids == 3, -rest, 0.0)))

        def g_tile(start):
            if parts == 1:
                return g_refs[0][pl.ds(start, TILE), :]
            inside = pl.multiple_of(jnp.where(start < half, start, start - half), TILE)
            first = g_refs[0][pl.ds(inside, TILE), :]
            return jnp.where(start < half, first, g_refs[1][pl.ds(inside, TILE), :])

        def of_call(values):
            value = values[0]
            for call, later in enumerate(values[1:], 1):
                value = jnp.where(place[2] < call * per, value, later)
            return value

        def tile(start, seen, slot):
            spot = pl.ds(start, TILE)
            q_here = q_ref[spot, :].astype(jnp.float32) * SCALE
            g_here = g_tile(start).astype(jnp.float32)
            g_flip = g_here.T
            o_here = of_call([ref[spot, :].astype(jnp.float32) for ref in o_refs])
            product = g_flip * o_here.T
            inner = jnp.concatenate(
                [jnp.sum(product[:HEAD_DIM], axis=0, keepdims=True), jnp.sum(product[HEAD_DIM:], axis=0, keepdims=True)], axis=1)
            lse = of_call([ref[0, pl.ds(slot, 1), :] for ref in lse_refs])
            below = jnp.where(ids == 0, 1.0, lanes_of(lse))
            q_wide = jnp.concatenate([twin_lanes(q_here.T), below], axis=0).astype(jnp.bfloat16)
            g_wide = jnp.concatenate([twin_lanes(g_flip), lanes_of(inner)], axis=0).astype(jnp.bfloat16)
            probs = jnp.exp(matmul(keys_wide[:seen, :], q_wide))
            grads = matmul(values_wide[:seen, :], g_wide)
            scores = (probs * grads).astype(jnp.bfloat16)
            dk[:seen, :] += matmul(scores, twin_rows(q_here).astype(jnp.bfloat16))
            dv[:seen, :] += matmul(probs.astype(jnp.bfloat16), twin_rows(g_here).astype(jnp.bfloat16))
            dq[spot, :] = (untwin(matmul(keys_t[:, :seen], scores)) * SCALE).astype(jnp.bfloat16)

        tiles = half // TILE

        @pl.loop(0, tiles)
        def _(index):
            tile(pl.multiple_of(prompt + index * TILE, TILE), half, index)
            tile(pl.multiple_of(target + index * TILE, TILE), 2 * half, tiles + index)

        out_ref[...] = dq[...]

    for which, held in ((1, dk), (2, dv)):
        @pl.when(step == which)
        def _(held=held):
            out_ref[pl.ds(prompt, half), :] = held[:half, :].astype(jnp.bfloat16)
            out_ref[pl.ds(target, half), :] = held[half:, :].astype(jnp.bfloat16)


def attend_back(place, qkv, mixed, grads, lse, held, behind):
    rows = qkv.shape[0]
    part = lambda shift: pl.BlockSpec((rows, LANES), lambda j, s, shift=shift: (0, 3 * s[2] + shift))
    calls = len(mixed)
    parts = len(grads)
    block = pl.BlockSpec((rows, LANES), lambda j, s: (0, s[2] & (s[3] - 1)))
    lse_block = pl.BlockSpec((1, rows // TILE, 2 * TILE), lambda j, s: (s[2] & (s[3] - 1), 0, 0))
    grad_blocks = [pl.BlockSpec((grad.shape[0], LANES), lambda j, s: (0, s[2])) for grad in grads]
    seen = rows * rows * 3 // 4
    more = [] if held is None else [held]
    return pl.pallas_call(
        partial(attend_back_kernel, parts, calls),
        grid_spec=pltpu.PrefetchScalarGridSpec(
            num_scalar_prefetch=1, grid=(3,),
            in_specs=[part(0), part(1), part(2)] + [block] * calls + [lse_block] * calls + grad_blocks + [pl.BlockSpec(memory_space=pl.ANY)] * (len(more) + len(behind)),
            out_specs=pl.BlockSpec((rows, LANES), lambda j, s: (0, 3 * s[2] + j)),
            scratch_shapes=[pltpu.VMEM((rows, 2 * LANES), jnp.bfloat16), pltpu.VMEM((rows, 2 * LANES), jnp.bfloat16), pltpu.VMEM((LANES, rows), jnp.bfloat16),
                pltpu.VMEM((rows, LANES), jnp.bfloat16), pltpu.VMEM((rows, LANES), jnp.float32), pltpu.VMEM((rows, LANES), jnp.float32)],
        ),
        out_shape=jax.ShapeDtypeStruct(qkv.shape, jnp.bfloat16),
        input_output_aliases={4 + 2 * calls + parts: 0} if more else {},
        compiler_params=pltpu.CompilerParams(vmem_limit_bytes=60 << 20),
        cost_estimate=pl.CostEstimate(flops=int(COVER * 2 * seen * 10 * HEAD_DIM * 4), transcendentals=0, bytes_accessed=rows * LANES * 20),
        name="attend_back",
    )(place, qkv, qkv, qkv, *mixed, *lse, *grads, *more, *behind)


EPSILON = 1e-05
ROOT_HALF = math.sqrt(0.5)
DENSITY = 1.0 / math.sqrt(2.0 * math.pi)
LATE_HOP = 2
BIG = pltpu.CompilerParams(vmem_limit_bytes=60 << 20)
ANYWHERE = pl.BlockSpec(memory_space=pl.ANY)


def cost(flops, moved, special=0):
    return pl.CostEstimate(
        flops=int(flops * COVER), bytes_accessed=int(moved * COVER), transcendentals=special
    )


def matmul_last(left, right):
    return lax.dot_general(
        left, right, (((1,), (1,)), ((), ())), preferred_element_type=jnp.float32
    )


def dot_rows(left, right):
    return lax.dot_general(
        left, right, (((0,), (0,)), ((), ())), preferred_element_type=jnp.float32
    )


def standardise(values):
    centred = values - jnp.mean(values, axis=-1, keepdims=True)
    spread = jnp.mean(centred * centred, axis=-1, keepdims=True)
    inverse = lax.rsqrt(spread + EPSILON)
    return centred * inverse, inverse


def add_rows(ref, scale, shift):
    step = pl.program_id(0)

    @pl.when(step == 0)
    def _():
        ref[0:1, :] = scale
        ref[1:2, :] = shift

    @pl.when(step > 0)
    def _():
        ref[0:1, :] += scale
        ref[1:2, :] += shift


def row_specs(parts, count):
    rows = sum(part.shape[0] for part in parts) // count
    specs = []
    first = 0
    for part in parts:
        steps = part.shape[0] // rows
        specs.append(
            pl.BlockSpec(
                (rows, part.shape[1]),
                lambda j, *s, first=first, steps=steps: (jnp.clip(j - first, 0, steps - 1), 0),
            )
        )
        first += steps
    return rows, specs


def current(refs, count):
    value = refs[0][...]
    for index, ref in enumerate(refs[1:], 1):
        value = jnp.where(pl.program_id(0) < index * count // len(refs), value, ref[...])
    return value


def pack_kernel(place, query_ref, key_ref, value_ref, out_ref):
    for pair in range(query_ref.shape[1] // LANES):
        for which, ref in enumerate((query_ref, key_ref, value_ref)):
            start = (3 * pair + which) * LANES
            out_ref[:, start : start + LANES] = ref[:, pair * LANES : (pair + 1) * LANES]


def pack_columns(query, key, value, held, place):
    rows = query.shape[0]
    return pl.pallas_call(
        pack_kernel,
        grid_spec=pltpu.PrefetchScalarGridSpec(
            num_scalar_prefetch=1,
            grid=(1,),
            in_specs=[pl.BlockSpec((rows, held), lambda j, s: (0, s[0]))] * 3,
            out_specs=pl.BlockSpec((rows, 3 * held), lambda j, s: (0, 0)),
        ),
        out_shape=jax.ShapeDtypeStruct((rows, 3 * held), query.dtype),
        cost_estimate=cost(0, 12 * rows * held),
        name="pack_columns",
    )(place, query, key, value)


def first_kernel(parts, pieces, count, spots, *refs):
    frames = refs[:parts]
    ada = refs[parts]
    blocks = refs[parts + 1 : parts + 1 + pieces]
    low_ref, qkv_ref, weight_ref, sems = refs[-4:]
    rows = blocks[0].shape[0]

    @pl.when(pl.program_id(0) == 0)
    def _():
        copies = []
        for index, block in enumerate(blocks):
            start = pl.multiple_of(spots[index] * rows, rows)
            copy = pltpu.make_async_copy(
                block, weight_ref.at[pl.ds(start, rows), :], sems.at[index]
            )
            copy.start()
            copies.append(copy)
        for copy in copies:
            copy.wait()

    normed, _ = standardise(current(frames, count).astype(jnp.float32))
    low = ((1.0 + ada[0:1, :]) * normed + ada[1:2, :]).astype(jnp.bfloat16)
    low_ref[...] = low
    qkv_ref[...] = matmul(low, weight_ref[...]).astype(jnp.bfloat16)


def first_layer(frames, ada, blocks, spots):
    count = 4
    rows, specs = row_specs(frames, count)
    width = frames[0].shape[1]
    columns = blocks[0].shape[1]
    out = lambda size: pl.BlockSpec((rows, size), lambda j, s: (j, 0))
    shape = lambda *size: jax.ShapeDtypeStruct(size, jnp.bfloat16)
    return pl.pallas_call(
        partial(first_kernel, len(frames), len(blocks), count),
        grid_spec=pltpu.PrefetchScalarGridSpec(
            num_scalar_prefetch=1,
            grid=(count,),
            in_specs=specs
            + [pl.BlockSpec((2, width), lambda j, s: (0, 0))]
            + [ANYWHERE] * len(blocks),
            out_specs=[
                out(width),
                out(columns),
                pl.BlockSpec((width, columns), lambda j, s: (0, 0)),
            ],
            scratch_shapes=[pltpu.SemaphoreType.DMA((len(blocks),))],
        ),
        out_shape=[
            shape(rows * count, width),
            shape(rows * count, columns),
            shape(width, columns),
        ],
        compiler_params=BIG,
        cost_estimate=cost(
            2 * rows * count * width * columns, 4 * width * columns + 8 * rows * count * width
        ),
        name="first_layer",
    )(spots, *frames, ada, *blocks)


def second_kernel(pieces, parts, count, spots, *refs):
    mixed = refs[:pieces]
    tokens = refs[pieces : pieces + parts]
    out_w, ada = refs[pieces + parts : pieces + parts + 2]
    attended_ref, low_ref = refs[-2:]
    weights = out_w.reshape(out_w.shape[0] * out_w.shape[2], out_w.shape[3])
    attended = current(tokens, count).astype(jnp.float32)
    for index, piece in enumerate(mixed):
        size = piece.shape[1]
        start = pl.multiple_of(spots[index] * size, size)
        attended = attended + matmul(piece[...], weights[pl.ds(start, size), :])
    attended_ref[...] = attended
    normed, _ = standardise(attended)
    low_ref[...] = ((1.0 + ada[0:1, :]) * normed + ada[1:2, :]).astype(jnp.bfloat16)


def second_layer(mixed, swapped, tokens, out_w, out_part, ada, spots):
    rows, width = tokens[-1].shape
    parts = len(tokens)
    count = 2 * parts
    size, token_specs = row_specs(tokens, count)
    later = count - 2
    block = lambda columns, order: pl.BlockSpec((size, columns), lambda j, s: (order(j), 0))
    first = lambda j: (j + later) % count
    items, _, piece, _ = out_w.shape
    return pl.pallas_call(
        partial(second_kernel, len(mixed) + len(swapped), parts, count),
        grid_spec=pltpu.PrefetchScalarGridSpec(
            num_scalar_prefetch=1,
            grid=(count,),
            in_specs=[block(part.shape[1], first) for part in mixed]
            + [block(part.shape[1], lambda j: j) for part in swapped]
            + token_specs
            + [
                pl.BlockSpec((items, 1, piece, width), lambda j, s: (0, out_part, 0, 0)),
                pl.BlockSpec((2, width), lambda j, s: (0, 0)),
            ],
            out_specs=[block(width, lambda j: jnp.maximum(j - later, 0)), block(width, first)],
        ),
        out_shape=[
            jax.ShapeDtypeStruct((rows, width), jnp.float32),
            jax.ShapeDtypeStruct((rows * parts, width), jnp.bfloat16),
        ],
        compiler_params=BIG,
        cost_estimate=cost(
            2 * rows * parts * width * width, 2 * width * width + 10 * rows * parts * width
        ),
        name="second_layer",
    )(spots, *mixed, *swapped, *tokens, out_w, ada)


class Weights:
    def __init__(self, up, up_first, down, down_parts, hidden, width):
        self.up = up
        self.down = down
        self.width = width
        self.hidden = hidden
        fold = up.shape[3]
        self.block = min(512, fold, hidden // 2)
        per_chip = down_parts * down.shape[3]
        per_fold = fold // self.block
        chips, _, _, piece, _ = down.shape
        self.steps = hidden // self.block
        per_core = self.steps // 2
        block = self.block
        self.up_spec = pl.BlockSpec(
            (up.shape[0], 1, up.shape[2], block),
            lambda j: (0, up_first + j // per_fold, 0, j % per_fold),
        )
        self.down_spec = pl.BlockSpec(
            (block // per_chip, 1, down_parts, piece, width),
            lambda j: (j % per_core, j // per_core, 0, 0, 0),
        )
        self.per_chip = per_chip
        self.bytes = 2 * hidden * width


def hidden_kernel(per_chip, parts, x_ref, up_ref, down_ref, *refs):
    g_refs = refs[:parts]
    active_ref, grad_ref = refs[-2:]
    columns = min(256, active_ref.shape[1])
    size = x_ref.shape[0] // parts
    for start in range(0, active_ref.shape[1], columns):
        spot = slice(start, start + columns)
        up = up_ref[:, :, :, spot].reshape(-1, columns)
        chips = slice(start // per_chip, (start + columns) // per_chip)
        down = down_ref[chips].reshape(columns, -1)
        for index, g_ref in enumerate(g_refs):
            rows = slice(index * size, (index + 1) * size)
            upward = matmul(x_ref[rows, :], up)
            grad_active = matmul_last(g_ref[...], down)
            below = 0.5 * (1.0 + lax.erf(upward * ROOT_HALF))
            active_ref[rows, spot] = (upward * below).astype(jnp.bfloat16)
            slope = below + upward * (DENSITY * jnp.exp(-0.5 * upward * upward))
            grad_ref[rows, spot] = (grad_active * slope).astype(jnp.bfloat16)


def hidden_layer(x, grads, weights):
    rows, width = x.shape
    out = pl.BlockSpec((rows, weights.block), lambda j: (0, j))
    shape = jax.ShapeDtypeStruct((rows, weights.hidden), jnp.bfloat16)
    return pl.pallas_call(
        partial(hidden_kernel, weights.per_chip, len(grads)),
        grid=(weights.steps,),
        in_specs=[
            pl.BlockSpec((rows, width), lambda j: (0, 0)),
            weights.up_spec,
            weights.down_spec,
        ]
        + [pl.BlockSpec(grad.shape, lambda j: (0, 0)) for grad in grads],
        out_specs=[out, out],
        out_shape=[shape, shape],
        compiler_params=BIG,
        cost_estimate=cost(
            4 * rows * width * weights.hidden,
            2 * weights.bytes + 4 * rows * (width + weights.hidden),
        ),
        name="hidden_layer",
    )(x, weights.up, weights.down, *grads)


def accumulate(part, out_ref, total):
    step = pl.program_id(0)

    @pl.when(step == 0)
    def _():
        total[...] = part

    @pl.when(step > 0)
    def _():
        total[...] += part

    @pl.when(step == pl.num_programs(0) - 1)
    def _():
        out_ref[...] = total[...].astype(out_ref.dtype)


def down_kernel(a_ref, down_ref, *refs):
    out_ref, total = refs[-2:]
    accumulate(matmul(a_ref[...], down_ref[...].reshape(-1, out_ref.shape[1])), out_ref, total)


def up_back_kernel(g_ref, up_ref, *refs):
    out_ref, total = refs[-2:]
    weights = up_ref[...].reshape(out_ref.shape[1], -1)
    accumulate(matmul_last(g_ref[...], weights), out_ref, total)


def hidden_to_width(kernel, name, held, weights, spec, array, rows, chunk, dtype, behind):
    width = weights.width
    return pl.pallas_call(
        kernel,
        grid=(weights.steps,),
        in_specs=[pl.BlockSpec((rows, weights.block), lambda j: (chunk, j)), spec]
        + [ANYWHERE] * len(behind),
        out_specs=pl.BlockSpec((rows, width), lambda j: (0, 0)),
        out_shape=jax.ShapeDtypeStruct((rows, width), dtype),
        scratch_shapes=[pltpu.VMEM((rows, width), jnp.float32)],
        compiler_params=BIG,
        cost_estimate=cost(
            2 * rows * width * weights.hidden,
            weights.bytes + rows * (2 * weights.hidden + 4 * width),
        ),
        name=name,
    )(held, array, *behind)


def down_part(active, weights, rows, chunk, dtype, behind=()):
    return hidden_to_width(
        down_kernel,
        "down_part",
        active,
        weights,
        weights.down_spec,
        weights.down,
        rows,
        chunk,
        dtype,
        behind,
    )


def up_back(grad, weights, rows, chunk, dtype, behind=()):
    return hidden_to_width(
        up_back_kernel,
        "up_back",
        grad,
        weights,
        weights.up_spec,
        weights.up,
        rows,
        chunk,
        dtype,
        behind,
    )


def middle_back_kernel(pieces, parts, spots, *refs):
    own_ref, base_ref, top_ref, ada_ref, out_w = refs[:5]
    others = refs[5 : 5 + parts]
    outs = refs[-3 - pieces :]
    grad_ref, low_ref, ada_grad_ref = outs[:3]
    grad = own_ref[...] + current(others, 2).astype(jnp.float32)
    normed, inverse = standardise(base_ref[...])
    scaled = grad * (1.0 + ada_ref[0:1, :])
    scale = jnp.sum(grad * normed, axis=0, keepdims=True)
    shift = jnp.sum(grad, axis=0, keepdims=True)
    inner = jnp.mean(scaled * normed, axis=-1, keepdims=True)
    shifted = scaled - jnp.mean(scaled, axis=-1, keepdims=True) - normed * inner
    out = top_ref[...].astype(jnp.float32) + inverse * shifted
    grad_ref[...] = out
    low = out.astype(jnp.bfloat16)
    low_ref[...] = low
    weights = out_w.reshape(out_w.shape[0] * out_w.shape[2], out_w.shape[3])
    for index, mixed_ref in enumerate(outs[3:]):
        size = mixed_ref.shape[1]
        start = pl.multiple_of(spots[index] * size, size)
        mixed_ref[...] = matmul_last(low, weights[pl.ds(start, size), :]).astype(jnp.bfloat16)
    add_rows(ada_grad_ref, scale, shift)


def middle_back(own, other, attended, cotangent, ada, out_w, out_part, spots, sizes, behind):
    rows, width = attended.shape
    count = 2
    block = lambda size: pl.BlockSpec((rows // count, size), lambda j, s: (j, 0))
    items, _, piece, _ = out_w.shape
    _, other_specs = row_specs(other, count)
    return pl.pallas_call(
        partial(middle_back_kernel, len(sizes), len(other)),
        grid_spec=pltpu.PrefetchScalarGridSpec(
            num_scalar_prefetch=1,
            grid=(count,),
            in_specs=[block(width)] * 3
            + [
                pl.BlockSpec((2, width), lambda j, s: (0, 0)),
                pl.BlockSpec((items, 1, piece, width), lambda j, s: (0, out_part, 0, 0)),
            ]
            + other_specs
            + [ANYWHERE] * len(behind),
            out_specs=[block(width), block(width), pl.BlockSpec((2, width), lambda j, s: (0, 0))]
            + [block(size) for size in sizes],
        ),
        out_shape=[
            jax.ShapeDtypeStruct((rows, width), jnp.float32),
            jax.ShapeDtypeStruct((rows, width), jnp.bfloat16),
            jax.ShapeDtypeStruct((2, width), jnp.float32),
        ]
        + [jax.ShapeDtypeStruct((rows, size), jnp.bfloat16) for size in sizes],
        compiler_params=BIG,
        cost_estimate=cost(2 * rows * width * width, 2 * width * width + 20 * rows * width),
        name="middle_back",
    )(spots, own, attended, cotangent, ada, out_w, *other, *behind)


def first_back_kernel(grad_ref, weight_ref, frames, *refs):
    out_ref, ada_grad_ref = refs[-2:]
    grad = matmul_last(grad_ref[...], weight_ref[...])
    normed, _ = standardise(frames[...].astype(jnp.float32))
    out_ref[...] = grad.astype(jnp.bfloat16)
    scale = jnp.sum(grad * normed, axis=0, keepdims=True)
    shift = jnp.sum(grad, axis=0, keepdims=True)
    add_rows(ada_grad_ref, scale, shift)


def first_back(grad, weights, frames, part, behind):
    width, columns = weights.shape
    count = 2
    rows = frames.shape[0] // count
    block = pl.BlockSpec((rows, width), lambda j: (j, 0))
    return pl.pallas_call(
        first_back_kernel,
        grid=(count,),
        in_specs=[
            pl.BlockSpec((rows, columns), lambda j: (part * count + j, 0)),
            pl.BlockSpec((width, columns), lambda j: (0, 0)),
            block,
        ]
        + [ANYWHERE] * len(behind),
        out_specs=[block, pl.BlockSpec((2, width), lambda j: (0, 0))],
        out_shape=[
            jax.ShapeDtypeStruct((rows * count, width), jnp.bfloat16),
            jax.ShapeDtypeStruct((2, width), jnp.float32),
        ],
        compiler_params=BIG,
        cost_estimate=cost(
            2 * rows * count * width * columns,
            2 * width * columns + 2 * rows * count * (2 * width + columns),
        ),
        name="first_back",
    )(grad, weights, frames, *behind)


def stacked_dot(lefts, rights):
    total = None
    for left, right in zip(lefts, rights):
        part = dot_rows(left, right)
        total = part if total is None else total + part
    return total


def cut_rows(ref, count):
    rows = ref.shape[0] // count
    return [ref[j * rows : (j + 1) * rows, :] for j in range(count)]


def put_sum(out_ref, other_ref, value):
    if other_ref is not None:
        value = value + other_ref[...].astype(jnp.float32)
    out_ref[...] = value.astype(jnp.bfloat16)


def hidden_grads_kernel(count, more, core, *refs):
    active, upward = refs[:2]
    grads, low = refs[2 : 2 + count], refs[2 + count]
    other = refs[3 + count] if more else None
    out_ref = refs[-1]
    step = pl.program_id(0)
    steps = pl.num_programs(0) // 2

    @pl.when(step < steps)
    def _():
        put_sum(
            out_ref, other, stacked_dot(cut_rows(active, count), [ref[...] for ref in grads])
        )

    @pl.when(step >= steps)
    def _():
        put_sum(out_ref, other, dot_rows(low[...], upward[...]))


def hidden_grads(core, active, upward, grads, low, other, behind):
    total, hidden = active.shape
    half = hidden // 2
    rows, width = grads[0].shape
    count = len(grads)
    block = 512
    steps = half // block
    whole = pl.BlockSpec((total, width), lambda j, s: (0, 0))
    grad = pl.BlockSpec((rows, block), lambda j, s: (0, jnp.minimum(j, steps - 1)))
    out = pl.BlockSpec((width, block), lambda j, s: (0, j))
    more = [] if other is None else [other]
    return pl.pallas_call(
        partial(hidden_grads_kernel, count, bool(more)),
        grid_spec=pltpu.PrefetchScalarGridSpec(
            num_scalar_prefetch=1,
            grid=(2 * steps,),
            in_specs=[
                pl.BlockSpec((total, half), lambda j, s: (0, s[0])),
                pl.BlockSpec(
                    (total, block), lambda j, s: (0, s[0] * steps + jnp.maximum(j - steps, 0))
                ),
            ]
            + [grad] * count
            + [whole]
            + [out] * len(more)
            + [ANYWHERE] * len(behind),
            out_specs=out,
        ),
        out_shape=jax.ShapeDtypeStruct((width, 2 * half), jnp.bfloat16),
        compiler_params=BIG,
        cost_estimate=cost(4 * total * half * width, 8 * total * half + 4 * width * half),
        name="hidden_grads",
    )(core, active, upward, *grads, low, *more, *behind)


def tail_grads_kernel(first, more, pieces, place, low, grad, attended, *refs):
    mixed = refs[:pieces]
    other = refs[pieces] if more else None
    out_ref = refs[-1]

    @pl.when(pl.program_id(0) < first)
    def _():
        put_sum(out_ref, other, dot_rows(low[...], grad[...]))

    @pl.when(pl.program_id(0) >= first)
    def _():
        for index, piece in enumerate(mixed):
            size = piece.shape[1]
            rows = pl.ds(pl.multiple_of(place[1 + index] * size, size), size)
            value = dot_rows(piece[...], attended[...])
            if more:
                value = value + other[rows, :].astype(jnp.float32)
            out_ref[rows, :] = value.astype(jnp.bfloat16)


def tail_grads(place, low_one, grad_qkv, mixed, swapped, attended_low, other, behind):
    total, width = low_one.shape
    rows = attended_low.shape[0]
    block = 256
    first = grad_qkv.shape[1] // 2 // block
    second = width // 2 // block
    out = pl.BlockSpec((width, block), lambda j, s: (0, j))
    more = [] if other is None else [other]
    return pl.pallas_call(
        partial(tail_grads_kernel, first, bool(more), len(mixed) + len(swapped)),
        grid_spec=pltpu.PrefetchScalarGridSpec(
            num_scalar_prefetch=1,
            grid=(first + second,),
            in_specs=[
                pl.BlockSpec((total, width), lambda j, s: (0, 0)),
                pl.BlockSpec(
                    (total, block), lambda j, s: (0, s[0] * first + jnp.minimum(j, first - 1))
                ),
                pl.BlockSpec(
                    (rows, block), lambda j, s: (0, s[0] * second + jnp.maximum(j - first, 0))
                ),
            ]
            + [pl.BlockSpec((rows, part.shape[1]), lambda j, s: (0, 0)) for part in mixed]
            + [pl.BlockSpec((rows, part.shape[1]), lambda j, s: (1, 0)) for part in swapped]
            + [out] * len(more)
            + [ANYWHERE] * len(behind),
            out_specs=out,
        ),
        out_shape=jax.ShapeDtypeStruct((width, (first + second) * block), jnp.bfloat16),
        compiler_params=BIG,
        cost_estimate=cost(
            2 * width * block * (total * first + rows * second), 8 * total * width
        ),
        name="tail_grads",
    )(place, low_one, grad_qkv, attended_low, *mixed, *swapped, *more, *behind)


def input_back_kernel(parts, count, own_ref, tokens_ref, ada_ref, base_ref, *refs):
    out_ref = refs[-1]
    grad = own_ref[...].astype(jnp.float32) + current(refs[:parts], count).astype(jnp.float32)
    normed, inverse = standardise(tokens_ref[...].astype(jnp.float32))
    scaled = grad * (1.0 + ada_ref[0:1, :])
    inner = jnp.mean(scaled * normed, axis=-1, keepdims=True)
    shifted = scaled - jnp.mean(scaled, axis=-1, keepdims=True) - normed * inner
    out_ref[...] = base_ref[...] + inverse * shifted


def input_back(own, others, tokens, ada, base):
    rows, width = tokens.shape
    count = 4
    block = pl.BlockSpec((rows // count, width), lambda j: (j, 0))
    _, specs = row_specs(others, count)
    return pl.pallas_call(
        partial(input_back_kernel, len(others), count),
        grid=(count,),
        in_specs=[block, block, pl.BlockSpec((2, width), lambda j: (0, 0)), block] + specs,
        out_specs=block,
        out_shape=jax.ShapeDtypeStruct((rows, width), jnp.float32),
        compiler_params=BIG,
        cost_estimate=cost(20 * rows * width, 14 * rows * width),
        name="input_back",
    )(own, tokens, ada, base, *others)


def exact(left, right):
    return jnp.dot(left, right, precision=lax.Precision.HIGHEST)


def rounded(total, other=None):
    if other is not None:
        total = total + other.astype(jnp.float32)
    return total.astype(jnp.bfloat16)


def tie(*values):
    return lax.optimization_barrier(values)


def cut(value, start, size, axis):
    return lax.dynamic_slice_in_dim(value, start, size, axis, allow_negative_indices=False)


def pick(value, index, axis):
    return lax.dynamic_index_in_dim(
        value, index, axis, keepdims=False, allow_negative_indices=False
    )


def ring_of(items_count):
    chips = items_count // 2
    outer = 4 if chips % 4 == 0 else chips
    inner = chips // outer
    order = [a * inner for a in range(outer)]
    for turn, a in enumerate(reversed(range(outer))):
        beside = list(range(1, inner))
        order += [a * inner + b for b in (beside if turn % 2 == 0 else beside[::-1])]
    return order


class Mover:
    def __init__(self, items_count, seq_count):
        self.items_count = items_count
        self.seq_count = seq_count
        self.pair = seq_count == 2
        self.chips = items_count // 2
        order = ring_of(items_count)
        self.forward = []
        self.backward = []
        chips = self.chips
        table = np.zeros((items_count, 2 * chips + 2), np.int32)
        hops = list(range(chips // 2 + 1)) + [-hop for hop in range(1, (chips + 1) // 2)]
        for spot in range(self.chips):
            for core in range(2):
                here = 2 * order[spot] + core
                next_one = 2 * order[(spot + 1) % self.chips] + core
                self.forward.append((here, next_one))
                self.backward.append((next_one, here))
                for ahead in range(self.chips):
                    table[here, ahead] = order[(spot + ahead) % self.chips]
                table[here, chips] = core
                table[here, chips + 1] = 1 - core
                for spot_of, hop in enumerate(hops):
                    ahead = hop if core == 1 else -hop
                    table[here, chips + 2 + spot_of] = order[(spot + ahead) % chips]
        self.both_ways = [p for p in self.forward if p[0] % 2 == 0]
        self.both_ways += [p for p in self.backward if p[0] % 2 == 1]
        self.item = lax.axis_index("items")
        row = pick(jnp.asarray(table), self.item, 0)
        self.ahead = [row[j] for j in range(self.chips)]
        self.core = row[self.chips]
        self.beside = row[self.chips + 1]
        self.core_spot = row[self.chips : self.chips + 1]
        self.beside_spot = row[self.chips + 1 : self.chips + 2]
        self.spots = row[self.chips + 2 :]
        self.seq = lax.axis_index("seq")

    def flip(self, value, bit):
        pairs = [(i, i ^ bit) for i in range(self.items_count)]
        return lax.ppermute(value, "items", pairs)

    def across(self, value):
        return lax.ppermute(value, "seq", [(0, 1), (1, 0)])

    def gather_items(self, value, summed, early, late):
        for bit in [1 << k for k in range(self.items_count.bit_length() - 1)]:
            summed = summed + self.flip(summed, bit)
        beside = self.flip(value, 1)
        block = jnp.where(
            self.core == 0,
            jnp.concatenate([value, beside], axis=0),
            jnp.concatenate([beside, value], axis=0),
        )
        direct = [block]
        for hop in range(1, self.chips // 2 + 1):
            moved = lax.ppermute(direct[-1], "items", self.both_ways)
            if hop == min(LATE_HOP, self.chips // 2):
                late, summed, moved, early = tie(late, summed, moved, early)
            direct.append(moved)
        beside = [self.flip(moved, 1) for moved in direct[1 : (self.chips + 1) // 2]]
        return direct + beside, summed, early, late

    def sum_seq(self, value):
        return value + self.across(value) if self.pair else lax.psum(value, "seq")

    def scatter_seq(self, value):
        rows = value.shape[0] // self.seq_count
        if self.pair:
            sent = cut(value, (1 - self.seq) * rows, rows, 0)
            kept = cut(value, self.seq * rows, rows, 0)
            return kept + self.across(sent.astype(jnp.bfloat16)).astype(jnp.float32)
        return lax.psum_scatter(
            value.astype(jnp.bfloat16), "seq", scatter_dimension=0, tiled=True
        ).astype(jnp.float32)

    def join_cores(self, value):
        parts = value.reshape(2, -1, value.shape[1])
        kept = pick(parts, self.core, 0)
        other = self.flip(pick(parts, self.beside, 0), 1)
        return jnp.where(self.core == 0, kept, other), jnp.where(self.core == 0, other, kept)

    def join_columns(self, value):
        rows = value.shape[0] // self.seq_count
        if self.pair:
            kept = cut(value, self.seq * rows, rows, 0)
            other = self.across(cut(value, (1 - self.seq) * rows, rows, 0))
            return jnp.where(self.seq == 0, kept, other), jnp.where(self.seq == 0, other, kept)
        moved = lax.all_to_all(value, "seq", split_axis=0, concat_axis=0, tiled=True)
        return tuple(moved[j * rows : (j + 1) * rows] for j in range(self.seq_count))


class RingSum:
    def __init__(self, mover, make, behind, ready=()):
        self.mover = mover
        self.chips = mover.chips
        self.make = make
        self.flows = None
        sent, self.ready = tie(make(False, None, behind), list(ready))
        self.sent = sent
        self.arriving = [mover.flip(sent, 1)]

    def block(self, ahead):
        return pick(self.both, self.mover.ahead[ahead % self.chips], 0)

    def add_own(self, behind):
        self.both = self.make(True, self.arriving[0], behind)
        self.whole = self.both
        self.both = self.both.reshape(self.chips, -1, self.both.shape[1])
        self.result = self.block(0).astype(jnp.float32)
        flows = [
            (self.mover.forward, 1, self.chips // 2),
            (self.mover.backward, -1, (self.chips - 1) // 2),
        ]
        self.send([(flow, self.block(flow[1] * flow[2])) for flow in flows if flow[2]])

    def send(self, flows):
        self.arriving = [lax.ppermute(value, "items", flow[0]) for flow, value in flows]
        self.flows = [(pairs, sign, left - 1) for (pairs, sign, left), _ in flows]

    def advance(self, anchor=None):
        flows = []
        if anchor is not None:
            self.arriving, anchor = tie(self.arriving, anchor)
        for flow, value in zip(self.flows, self.arriving):
            if flow[2]:
                flows.append((flow, self.block(flow[1] * flow[2]) + value))
            else:
                self.result = self.result + value.astype(jnp.float32)
        self.send(flows)
        return anchor

    def finish(self):
        while self.arriving:
            self.advance()
        return self.result


def in_rows(value):
    return with_layout_constraint(value, Layout((0, 1)))


def halves(value, core):
    half = value.shape[1] // 2
    return cut(value, core * half, half, 1)


def parted(value, at):
    return (None, None) if value is None else (value[:, :at], value[:, at:])


def shards(
    tokens,
    cotangent,
    prompt_len,
    section_ids,
    section_table,
    w_query,
    w_key,
    w_value,
    w_out,
    w_up,
    w_down,
    w_ada_one,
    w_ada_two,
):
    items_count = lax.axis_size("items")
    seq_count = lax.axis_size("seq")
    mover = Mover(items_count, seq_count)
    chips = mover.chips
    batch, rows, width = tokens.shape
    total_rows = rows * seq_count
    hidden = w_up.shape[1] // seq_count
    held = width // seq_count
    pairs = held // LANES
    piece = w_query.shape[0]
    units = w_down.shape[0] // seq_count
    tokens = tokens.reshape(rows, width)
    grad_low = cotangent.reshape(rows, width)

    def quarters(one, two):
        return jnp.stack([one[:, :width], one[:, width:], two[:, :width], two[:, width:]])

    up_shard = w_up.reshape(piece, chips, 2, seq_count, units).transpose(3, 0, 2, 1, 4)
    up_shard = pick(up_shard, mover.seq, 0).reshape(piece, hidden)
    down_shard = cut(w_down, mover.seq * units, units, 0)
    merged = hidden % width == 0 and units % piece == 0
    late = down_shard
    if merged:
        folds = hidden // width
        down_parts = units // piece
        up_rows = [up_shard[:, j * width : (j + 1) * width] for j in range(folds)]
        late = jnp.concatenate([down_shard] + up_rows + [w_out], axis=0)

    table_part = cut(section_table, mover.item * piece, piece, 1)
    ada_part = jnp.dot(
        table_part,
        jnp.concatenate([w_ada_one, w_ada_two], axis=1),
        preferred_element_type=jnp.float32,
    )
    ada_part = quarters(ada_part[:, : 2 * width], ada_part[:, 2 * width :])
    seq_place = jnp.reshape(mover.seq, (1,)).astype(jnp.int32)
    mine = pack_columns(w_query, w_key, w_value, held, seq_place)
    early = [mover.across(tokens)] if mover.pair else []
    blocks, ada_sum, early, late = mover.gather_items(
        mine, ada_part, early, late
    )

    def gathered(value):
        return lax.all_gather(value, "items", axis=0, tiled=False)

    if merged:
        rest = gathered(late)
        rest = rest.reshape(items_count, down_parts + folds + 1, piece, width)
        by_core = rest.reshape((chips, 2) + rest.shape[1:])
        weights = Weights(rest, down_parts, by_core, down_parts, hidden, width)
        out_w, out_part = rest, down_parts + folds
    else:
        by_core = gathered(late).reshape(chips, 2, 1, units, width)
        weights = Weights(gathered(up_shard)[:, None], 0, by_core, 1, hidden, width)
        out_w, out_part = gathered(w_out)[:, None], 0

    choose = (section_ids[0] == jnp.arange(section_table.shape[0])).astype(jnp.float32)
    ada = jnp.sum(choose[None, :, None] * ada_sum, axis=1)
    ada_one = ada[:2]
    ada_two = ada[2:]

    if mover.pair:
        prompt_at = mover.seq
        tokens_other, grad_sent = tie(early[0], grad_low)
        grad_other = mover.across(grad_sent)
        frames = [tokens, tokens_other]
        grads = [grad_low, grad_other]
        calls = 2 if pairs % 2 == 0 else 1
        own_spots = [mover.seq * calls + call for call in range(calls)]
        far_spots = [(1 - mover.seq) * calls + call for call in range(calls)]
        spots = jnp.stack(own_spots + far_spots)
        other_spots = jnp.stack([1 - mover.seq, mover.seq])
    else:
        prompt_at = jnp.zeros((), jnp.int32)
        frames = [lax.all_gather(tokens, "seq", axis=0, tiled=True)]
        grads = [lax.all_gather(grad_low, "seq", axis=0, tiled=True)]
        calls = 1
        spots = other_spots = jnp.zeros((1,), jnp.int32)
    low_one, qkv, qkv_w = first_layer(frames, ada_one, blocks, mover.spots)
    length = prompt_len[0]
    per_call = pairs // calls
    mixed_heads = []
    lse = []
    for call in range(calls):
        place = jnp.stack([prompt_at, length]).astype(jnp.int32)
        behind = grads[1:] + mixed_heads
        out = attend(qkv, place, call * per_call, per_call, behind)
        mixed_heads.append(out[0])
        lse.append(out[1])
    if mover.pair:
        mixed_far = []
        for call in range(calls):
            sent = mixed_heads[call]
            if mixed_far:
                sent, mixed_far[-1] = tie(sent, mixed_far[-1])
            mixed_far.append(mover.across(sent))
        attended, low_two = second_layer(
            mixed_heads, mixed_far, frames[::-1], out_w, out_part, ada_two, spots
        )
        lows = low_two
        active, upward = hidden_layer(lows, grads, weights)
        for_other = up_back(upward, weights, rows, 1, jnp.bfloat16)
        half = rows // 2
        first_half, last_half = for_other[:half], for_other[half:]
        start = [for_other]
        ready = [mover.across(first_half), last_half]
    else:
        mixed = lax.all_to_all(mixed_heads[0], "seq", split_axis=0, concat_axis=1, tiled=True)
        attended, low_two = second_layer(
            [mixed], [], [tokens], out_w, out_part, ada_two, spots
        )
        lows = lax.all_gather(low_two, "seq", axis=0, tiled=True)
        active, upward = hidden_layer(lows, grads, weights)
        start = []
        ready = []

    down_columns = hidden // 2

    def hidden_parts(own, other, behind):
        spot = mover.core_spot if own else mover.beside_spot
        if down_columns == width:
            return hidden_grads(spot, active, upward, grads, lows, other, behind)
        core = mover.core if own else mover.beside
        first, second = parted(other, down_columns)
        down = dot_rows(halves(active, core), grads[0]).reshape(width, down_columns)
        up = dot_rows(lows, halves(upward, core))
        return in_rows(jnp.concatenate([rounded(down, first), rounded(up, second)], axis=1))

    ring = RingSum(mover, hidden_parts, start, ready)
    if mover.pair:
        own = up_back(upward, weights, rows, 0, jnp.float32, [ring.sent])
        from_other = [ring.ready[0], mover.across(ring.ready[1])]
        sizes = [held, held]
    else:
        own = lax.psum_scatter(
            up_back(upward, weights, total_rows, 0, jnp.bfloat16),
            "seq",
            scatter_dimension=0,
            tiled=True,
        ).astype(jnp.float32)
        from_other = [jnp.zeros((rows, width), jnp.bfloat16)]
        sizes = [width]
    ring.add_own([own])
    grad_attended, attended_low, ada_two_rows, *grad_mixed = middle_back(
        own,
        from_other,
        attended,
        grad_low,
        ada_two,
        out_w,
        out_part,
        other_spots,
        sizes,
        [ring.whole],
    )
    if mover.pair:
        out_other = down_part(active, weights, rows, 1, jnp.bfloat16, grad_mixed[:1])
        grad_heads = [grad_mixed[1], mover.across(grad_mixed[0])]
        out_other = ring.advance(out_other)
        out_own = down_part(active, weights, rows, 0, jnp.float32, [out_other])
        filler = [out_own]
        out_other = mover.across(out_other)
    else:
        grad_heads = [
            lax.all_to_all(grad_mixed[0], "seq", split_axis=1, concat_axis=0, tiled=True)
        ]
        filler = []

    split = pairs // 2 if pairs % 2 == 0 else 0

    def tail_parts(own, other, behind):
        spot = mover.core_spot if own else mover.beside_spot
        if mover.pair:
            return tail_grads(
                jnp.concatenate([spot, spots.astype(jnp.int32)]),
                low_one,
                grad_qkv,
                mixed_heads,
                mixed_far,
                attended_low,
                other,
                behind,
            )
        core = mover.core if own else mover.beside
        first, second = parted(other, grad_qkv.shape[1] // 2)
        qkv_part = rounded(dot_rows(low_one, halves(grad_qkv, core)), first)
        out_part = rounded(dot_rows(mixed, halves(attended_low, core)), second)
        return in_rows(jnp.concatenate([qkv_part, out_part], axis=1))

    tail = None
    grad_qkv = None
    for turn in range(pairs):
        behind = filler
        filler = []
        pair = (mover.beside * split + turn) & (pairs - 1)
        place = jnp.stack([prompt_at, length, pair, per_call]).astype(jnp.int32)
        grad_qkv = attend_back(place, qkv, mixed_heads, grad_heads, lse, grad_qkv, behind)
        grad_qkv = ring.advance(grad_qkv)
        if turn + 1 == split:
            tail = RingSum(mover, tail_parts, [])
            filler = [tail.sent]
    if tail is None:
        tail = RingSum(mover, tail_parts, [])
    tail.add_own([])
    if mover.pair:
        far_first, far_rows = first_back(grad_qkv, qkv_w, frames[1], 1, [tail.whole])
        far_first = tail.advance(far_first)
        half = rows // 2
        near_half, last_half = far_first[:half], far_first[half:]
        near_half = mover.across(near_half)
        own_first, own_rows = first_back(grad_qkv, qkv_w, frames[0], 0, [far_first])
        ada_rows = jnp.concatenate([own_rows + far_rows, ada_two_rows])
        ada_other = mover.across(ada_rows)
        near_half, last_half, ada_other, out_other = tail.advance(
            [near_half, last_half, ada_other, out_other]
        )
        ada_rows = ada_rows + ada_other
        far_parts = [near_half, mover.across(last_half)]
        layer_sum = out_own + out_other.astype(jnp.float32)
    else:
        grad_first, ada_one_rows = first_back(grad_qkv, qkv_w, frames[0], 0, [tail.whole])
        ada_rows = lax.psum(jnp.concatenate([ada_one_rows, ada_two_rows]), "seq")
        own_first = lax.psum_scatter(grad_first, "seq", scatter_dimension=0, tiled=True)
        far_parts = [jnp.zeros((rows, width), jnp.bfloat16)]
        layer_sum = lax.psum_scatter(
            down_part(active, weights, total_rows, 0, jnp.bfloat16),
            "seq",
            scatter_dimension=0,
            tiled=True,
        ).astype(jnp.float32)
    layer_out = (attended + layer_sum).astype(jnp.bfloat16)
    sums = choose[None, :, None] * ada_rows[:, None, :]
    for bit in [1 << k for k in range(items_count.bit_length() - 1)]:
        sums = sums + mover.flip(sums, bit)
        if bit == 2:
            sums = tail.advance(sums)
    input_grad = input_back(own_first, far_parts, tokens, ada_one, grad_attended)
    out_piece = piece // seq_count
    first_row = mover.item * piece + mover.seq * out_piece
    table_rows = cut(section_table, first_row, out_piece, 1).astype(jnp.float32)
    ada_grads = jnp.einsum("sr,ksd->krd", table_rows, sums, precision=lax.Precision.HIGHEST)
    grad_ada_one = jnp.concatenate([ada_grads[0], ada_grads[1]], axis=1)
    grad_ada_two = jnp.concatenate([ada_grads[2], ada_grads[3]], axis=1)
    own_ada = quarters(
        *(cut(w, mover.seq * out_piece, out_piece, 0) for w in (w_ada_one, w_ada_two))
    ).astype(jnp.float32)
    grad_table = jnp.einsum("ksd,krd->sr", sums, own_ada, precision=lax.Precision.HIGHEST)

    ring_total = ring.finish()
    grad_down = ring_total[:, :down_columns].reshape(units, width)
    up_sides = mover.join_columns(
        jnp.concatenate(mover.join_cores(ring_total[:, down_columns:]), axis=1)
    )
    grad_up = jnp.stack(
        [side.reshape(out_piece, 2, chips, units) for side in up_sides], axis=1
    )
    grad_up = grad_up.transpose(0, 3, 2, 1, 4).reshape(out_piece, hidden * seq_count)
    tail_total = tail.finish()
    cores = jnp.concatenate(mover.join_cores(tail_total), axis=1)
    half_qkv = 3 * held // 2
    half_all = cores.shape[1] // 2
    qkv_total = jnp.concatenate(
        [cores[:, :half_qkv], cores[:, half_all : half_all + half_qkv]], axis=1
    )
    out_total = jnp.concatenate([cores[:, half_qkv:half_all], cores[:, half_all + half_qkv :]], axis=1)
    sides = mover.join_columns(qkv_total)
    grad_out = mover.scatter_seq(out_total)
    grad_query, grad_key, grad_value = (
        jnp.concatenate(
            [
                side[:, (3 * p + j) * LANES : (3 * p + j + 1) * LANES]
                for side in sides
                for p in range(pairs)
            ],
            axis=1,
        )
        for j in range(3)
    )
    return (
        layer_out.reshape(batch, rows, width),
        input_grad.reshape(batch, rows, width),
        grad_query,
        grad_key,
        grad_value,
        grad_out,
        grad_up,
        grad_down,
        grad_ada_one,
        grad_ada_two,
        grad_table,
    )


def solution(mesh):
    return jax.shard_map(
        shards,
        mesh=mesh,
        in_specs=(
            P("items", "seq", None),
            P("items", "seq", None),
            P("items"),
            P("items"),
            P(),
            P("items", None),
            P("items", None),
            P("items", None),
            P("items", None),
            P("items", None),
            P("items", None),
            P("items", None),
            P("items", None),
        ),
        out_specs=(
            P("items", "seq", None),
            P("items", "seq", None),
            P(("items", "seq"), None),
            P(("items", "seq"), None),
            P(("items", "seq"), None),
            P(("items", "seq"), None),
            P(("items", "seq"), None),
            P(("items", "seq"), None),
            P(("items", "seq"), None),
            P(("items", "seq"), None),
            P(None, ("items", "seq")),
        ),
        check_vma=False,
    )
```

```python
from functools import partial
import math

import jax
import jax.numpy as jnp
import numpy as np
from jax import lax
from jax.experimental.layout import Layout, with_layout_constraint
from jax.experimental import pallas as pl
from jax.experimental.pallas import tpu as pltpu
from jax.sharding import PartitionSpec as P

HEAD_DIM = 64
SCALE = 0.125
MASKED = -1e30
COVER = 0.5
TILE = 128
LANES = 128

def row_ids(shape):
    return lax.broadcasted_iota(jnp.int32, shape, 0)
def lane_ids(shape):
    return lax.broadcasted_iota(jnp.int32, shape, 1)
def matmul(left, right):
    return jnp.dot(left, right, preferred_element_type=jnp.float32)
def twin_lanes(flipped):
    top = row_ids(flipped.shape) < HEAD_DIM
    return jnp.concatenate([jnp.where(top, flipped, 0.0), jnp.where(top, 0.0, flipped)], axis=1)
def twin_rows(block):
    first = lane_ids(block.shape) < HEAD_DIM
    return jnp.concatenate([jnp.where(first, block, 0.0), jnp.where(first, 0.0, block)], axis=0)
def untwin(wide):
    top = row_ids((LANES, LANES)) < HEAD_DIM
    return jnp.where(top, wide[:, :LANES], wide[:, LANES:]).T

def split3(value):
    high = value.astype(jnp.bfloat16).astype(jnp.float32)
    rest = value - high
    mid = rest.astype(jnp.bfloat16).astype(jnp.float32)
    return high, mid, rest - mid

def attend_kernel(place, q_ref, k_ref, v_ref, *refs):
    o_ref, lse_ref, keys_wide, values_t = refs[-4:]
    half = q_ref.shape[0] // 2
    prompt = pl.multiple_of(place[0] * half, TILE)
    target = pl.multiple_of((1 - place[0]) * half, TILE)
    length = place[1]
    shape = (half, LANES)
    keys_wide[:half, :LANES] = k_ref[pl.ds(prompt, half), :]
    keys_wide[half:, :LANES] = k_ref[pl.ds(target, half), :]
    hidden = (lane_ids(shape) == 0) & (row_ids(shape) >= length)
    keys_wide[:half, LANES:] = jnp.where(hidden, MASKED, 0.0).astype(jnp.bfloat16)
    keys_wide[half:, LANES:] = jnp.zeros(shape, jnp.bfloat16)
    for piece in range(half // TILE):
        rows = slice(piece * TILE, (piece + 1) * TILE)
        values_t[:, rows] = v_ref[pl.ds(prompt + piece * TILE, TILE), :].astype(jnp.float32).T.astype(jnp.bfloat16)
        rows = slice(half + piece * TILE, half + (piece + 1) * TILE)
        values_t[:, rows] = v_ref[pl.ds(target + piece * TILE, TILE), :].astype(jnp.float32).T.astype(jnp.bfloat16)
    below = jnp.where(row_ids((LANES, 2 * TILE)) == 0, 1.0, 0.0)

    def score(start, seen):
        q_flip = (q_ref[pl.ds(start, TILE), :].astype(jnp.float32) * SCALE).T
        q_wide = jnp.concatenate([twin_lanes(q_flip), below], axis=0).astype(jnp.bfloat16)
        return matmul(keys_wide[:seen, :], q_wide)

    def tile(scores, start, seen, slot):
        peak = jnp.max(scores, axis=0, keepdims=True)
        expo = jnp.exp(scores - peak)
        total = jnp.sum(expo, axis=0, keepdims=True)
        out = matmul(values_t[:, :seen], expo.astype(jnp.bfloat16)) / total
        o_ref[pl.ds(start, TILE), :] = untwin(out).astype(jnp.bfloat16)
        lse_ref[0, pl.ds(slot, 1), :] = peak + jnp.log(total)

    tiles = half // TILE

    @pl.loop(0, tiles)
    def _(index):
        at_prompt = pl.multiple_of(prompt + index * TILE, TILE)
        at_target = pl.multiple_of(target + index * TILE, TILE)
        first = score(at_prompt, half)
        second = score(at_target, 2 * half)
        tile(first, at_prompt, half, index)
        tile(second, at_target, 2 * half, tiles + index)


def attend(qkv, place, first, pairs, behind):
    rows = qkv.shape[0]
    width = pairs * LANES
    part = lambda shift: pl.BlockSpec((rows, LANES), lambda p, s, shift=shift: (0, 3 * (first + p) + shift))
    seen = rows * rows * 3 // 4
    return pl.pallas_call(
        attend_kernel,
        grid_spec=pltpu.PrefetchScalarGridSpec(
            num_scalar_prefetch=1, grid=(pairs,),
            in_specs=[part(0), part(1), part(2)] + [pl.BlockSpec(memory_space=pl.ANY)] * len(behind),
            out_specs=[pl.BlockSpec((rows, LANES), lambda p, s: (0, p)), pl.BlockSpec((1, rows // TILE, 2 * TILE), lambda p, s: (p, 0, 0))],
            scratch_shapes=[pltpu.VMEM((rows, 2 * LANES), jnp.bfloat16), pltpu.VMEM((LANES, rows), jnp.bfloat16)],
        ),
        out_shape=[jax.ShapeDtypeStruct((rows, width), jnp.bfloat16),
                   jax.ShapeDtypeStruct((pairs, rows // TILE, 2 * TILE), jnp.float32)],
        compiler_params=pltpu.CompilerParams(vmem_limit_bytes=60 << 20),
        cost_estimate=pl.CostEstimate(flops=int(COVER * pairs * 2 * seen * 4 * HEAD_DIM * 4), transcendentals=0, bytes_accessed=rows * width * 8),
        name="attend",
    )(place, qkv, qkv, qkv, *behind)


def attend_back_kernel(parts, calls, per, at, place, q_ref, k_ref, v_ref, *refs):
    o_refs, lse_refs, g_refs = refs[:calls], refs[calls:2 * calls], refs[2 * calls:2 * calls + parts]
    out_ref, keys_wide, values_wide, keys_t, dq, dk, dv = refs[-7:]
    half = q_ref.shape[0] // 2
    step = pl.program_id(0)
    prompt = pl.multiple_of(place[0] * half, TILE)
    target = pl.multiple_of((1 - place[0]) * half, TILE)
    length = place[1]

    @pl.when(step == 0)
    def _():
        shape = (half, LANES)
        lanes = lane_ids(shape)
        ones = jnp.where((lanes >= 1) & (lanes <= 3), 1.0, 0.0)
        hidden = (lanes == 0) & (row_ids(shape) >= length)
        keys_wide[:half, :LANES] = k_ref[pl.ds(prompt, half), :]
        keys_wide[half:, :LANES] = k_ref[pl.ds(target, half), :]
        keys_wide[:half, LANES:] = jnp.where(hidden, MASKED, ones).astype(jnp.bfloat16)
        keys_wide[half:, LANES:] = ones.astype(jnp.bfloat16)
        values_wide[:half, :LANES] = v_ref[pl.ds(prompt, half), :]
        values_wide[half:, :LANES] = v_ref[pl.ds(target, half), :]
        values_wide[:half, LANES:] = ones.astype(jnp.bfloat16)
        values_wide[half:, LANES:] = ones.astype(jnp.bfloat16)
        for piece in range(2 * half // TILE):
            rows = slice(piece * TILE, (piece + 1) * TILE)
            keys_t[:, rows] = keys_wide[rows, :LANES].astype(jnp.float32).T.astype(jnp.bfloat16)
        dk[...] = jnp.zeros_like(dk)
        dv[...] = jnp.zeros_like(dv)
        wide = (LANES, 2 * TILE)
        ids = row_ids(wide)

        def lanes_of(value):
            high, mid, rest = split3(value)
            return jnp.where(ids == 1, -high, jnp.where(ids == 2, -mid, jnp.where(ids == 3, -rest, 0.0)))

        def g_tile(start):
            if parts == 1:
                return g_refs[0][pl.ds(start, TILE), :]
            inside = pl.multiple_of(jnp.where(start < half, start, start - half), TILE)
            first = g_refs[0][pl.ds(inside, TILE), :]
            return jnp.where(start < half, first, g_refs[1][pl.ds(inside, TILE), :])

        def of_call(values):
            value = values[0]
            for call, later in enumerate(values[1:], 1):
                value = jnp.where(at(place) < call * per, value, later)
            return value

        def tile(start, seen, slot):
            spot = pl.ds(start, TILE)
            q_here = q_ref[spot, :].astype(jnp.float32) * SCALE
            g_here = g_tile(start).astype(jnp.float32)
            g_flip = g_here.T
            o_here = of_call([ref[spot, :].astype(jnp.float32) for ref in o_refs])
            product = g_flip * o_here.T
            inner = jnp.concatenate(
                [jnp.sum(product[:HEAD_DIM], axis=0, keepdims=True), jnp.sum(product[HEAD_DIM:], axis=0, keepdims=True)], axis=1)
            lse = of_call([ref[0, pl.ds(slot, 1), :] for ref in lse_refs])
            below = jnp.where(ids == 0, 1.0, lanes_of(lse))
            q_wide = jnp.concatenate([twin_lanes(q_here.T), below], axis=0).astype(jnp.bfloat16)
            g_wide = jnp.concatenate([twin_lanes(g_flip), lanes_of(inner)], axis=0).astype(jnp.bfloat16)
            probs = jnp.exp(matmul(keys_wide[:seen, :], q_wide))
            grads = matmul(values_wide[:seen, :], g_wide)
            scores = (probs * grads).astype(jnp.bfloat16)
            dk[:seen, :] += matmul(scores, twin_rows(q_here).astype(jnp.bfloat16))
            dv[:seen, :] += matmul(probs.astype(jnp.bfloat16), twin_rows(g_here).astype(jnp.bfloat16))
            dq[spot, :] = (untwin(matmul(keys_t[:, :seen], scores)) * SCALE).astype(jnp.bfloat16)

        tiles = half // TILE

        @pl.loop(0, tiles)
        def _(index):
            tile(pl.multiple_of(prompt + index * TILE, TILE), half, index)
            tile(pl.multiple_of(target + index * TILE, TILE), 2 * half, tiles + index)

        out_ref[...] = dq[...]

    for which, held in ((1, dk), (2, dv)):
        @pl.when(step == which)
        def _(held=held):
            out_ref[pl.ds(prompt, half), :] = held[:half, :].astype(jnp.bfloat16)
            out_ref[pl.ds(target, half), :] = held[half:, :].astype(jnp.bfloat16)


def attend_back(place, turn, pairs, qkv, mixed, grads, lse, held, behind):
    rows = qkv.shape[0]
    part = lambda shift: pl.BlockSpec((rows, LANES), lambda j, s, shift=shift: (0, 3 * at(s) + shift))
    calls = len(mixed)
    per = pairs // calls
    split = pairs // 2 if pairs % 2 == 0 else 0
    at = lambda s: (s[3] * split + turn) & (pairs - 1)
    parts = len(grads)
    block = pl.BlockSpec((rows, LANES), lambda j, s: (0, at(s) & (per - 1)))
    lse_block = pl.BlockSpec((1, rows // TILE, 2 * TILE), lambda j, s: (at(s) & (per - 1), 0, 0))
    grad_blocks = [pl.BlockSpec((grad.shape[0], LANES), lambda j, s: (0, at(s))) for grad in grads]
    seen = rows * rows * 3 // 4
    more = [] if held is None else [held]
    return pl.pallas_call(
        partial(attend_back_kernel, parts, calls, per, at),
        grid_spec=pltpu.PrefetchScalarGridSpec(
            num_scalar_prefetch=1, grid=(3,),
            in_specs=[part(0), part(1), part(2)] + [block] * calls + [lse_block] * calls + grad_blocks + [pl.BlockSpec(memory_space=pl.ANY)] * (len(more) + len(behind)),
            out_specs=pl.BlockSpec((rows, LANES), lambda j, s: (0, 3 * at(s) + j)),
            scratch_shapes=[pltpu.VMEM((rows, 2 * LANES), jnp.bfloat16), pltpu.VMEM((rows, 2 * LANES), jnp.bfloat16), pltpu.VMEM((LANES, rows), jnp.bfloat16),
                pltpu.VMEM((rows, LANES), jnp.bfloat16), pltpu.VMEM((rows, LANES), jnp.float32), pltpu.VMEM((rows, LANES), jnp.float32)],
        ),
        out_shape=jax.ShapeDtypeStruct(qkv.shape, jnp.bfloat16),
        input_output_aliases={4 + 2 * calls + parts: 0} if more else {},
        compiler_params=pltpu.CompilerParams(vmem_limit_bytes=60 << 20),
        cost_estimate=pl.CostEstimate(flops=int(COVER * 2 * seen * 10 * HEAD_DIM * 4), transcendentals=0, bytes_accessed=rows * LANES * 20),
        name="attend_back",
    )(place, qkv, qkv, qkv, *mixed, *lse, *grads, *more, *behind)


EPSILON = 1e-05
ROOT_HALF = math.sqrt(0.5)
DENSITY = 1.0 / math.sqrt(2.0 * math.pi)
LATE_HOP = 2
BIG = pltpu.CompilerParams(vmem_limit_bytes=60 << 20)
ANYWHERE = pl.BlockSpec(memory_space=pl.ANY)


def cost(flops, moved, special=0):
    return pl.CostEstimate(
        flops=int(flops * COVER), bytes_accessed=int(moved * COVER), transcendentals=special
    )


def matmul_last(left, right):
    return lax.dot_general(
        left, right, (((1,), (1,)), ((), ())), preferred_element_type=jnp.float32
    )


def dot_rows(left, right):
    return lax.dot_general(
        left, right, (((0,), (0,)), ((), ())), preferred_element_type=jnp.float32
    )


def standardise(values):
    centred = values - jnp.mean(values, axis=-1, keepdims=True)
    spread = jnp.mean(centred * centred, axis=-1, keepdims=True)
    inverse = lax.rsqrt(spread + EPSILON)
    return centred * inverse, inverse


def add_rows(ref, scale, shift):
    step = pl.program_id(0)

    @pl.when(step == 0)
    def _():
        ref[0:1, :] = scale
        ref[1:2, :] = shift

    @pl.when(step > 0)
    def _():
        ref[0:1, :] += scale
        ref[1:2, :] += shift


def row_specs(parts, count):
    rows = sum(part.shape[0] for part in parts) // count
    specs = []
    first = 0
    for part in parts:
        steps = part.shape[0] // rows
        specs.append(
            pl.BlockSpec(
                (rows, part.shape[1]),
                lambda j, *s, first=first, steps=steps: (jnp.clip(j - first, 0, steps - 1), 0),
            )
        )
        first += steps
    return rows, specs


def current(refs, count):
    value = refs[0][...]
    for index, ref in enumerate(refs[1:], 1):
        value = jnp.where(pl.program_id(0) < index * count // len(refs), value, ref[...])
    return value


def pack_kernel(place, query_ref, key_ref, value_ref, out_ref):
    for pair in range(query_ref.shape[1] // LANES):
        for which, ref in enumerate((query_ref, key_ref, value_ref)):
            start = (3 * pair + which) * LANES
            out_ref[:, start : start + LANES] = ref[:, pair * LANES : (pair + 1) * LANES]


def pack_columns(query, key, value, held, place):
    rows = query.shape[0]
    return pl.pallas_call(
        pack_kernel,
        grid_spec=pltpu.PrefetchScalarGridSpec(
            num_scalar_prefetch=1,
            grid=(1,),
            in_specs=[pl.BlockSpec((rows, held), lambda j, s: (0, s[4]))] * 3,
            out_specs=pl.BlockSpec((rows, 3 * held), lambda j, s: (0, 0)),
        ),
        out_shape=jax.ShapeDtypeStruct((rows, 3 * held), query.dtype),
        cost_estimate=cost(0, 12 * rows * held),
        name="pack_columns",
    )(place, query, key, value)


def first_kernel(parts, pieces, count, spots, *refs):
    frames = refs[:parts]
    ada = refs[parts]
    blocks = refs[parts + 1 : parts + 1 + pieces]
    low_ref, qkv_ref, weight_ref, sems = refs[-4:]
    rows = blocks[0].shape[0]

    @pl.when(pl.program_id(0) == 0)
    def _():
        copies = []
        for index, block in enumerate(blocks):
            start = pl.multiple_of(spots[index] * rows, rows)
            copy = pltpu.make_async_copy(
                block, weight_ref.at[pl.ds(start, rows), :], sems.at[index]
            )
            copy.start()
            copies.append(copy)
        for copy in copies:
            copy.wait()

    normed, _ = standardise(current(frames, count).astype(jnp.float32))
    low = ((1.0 + ada[0:1, :]) * normed + ada[1:2, :]).astype(jnp.bfloat16)
    low_ref[...] = low
    qkv_ref[...] = matmul(low, weight_ref[...]).astype(jnp.bfloat16)


def first_layer(frames, ada, blocks, spots):
    count = 4
    rows, specs = row_specs(frames, count)
    width = frames[0].shape[1]
    columns = blocks[0].shape[1]
    out = lambda size: pl.BlockSpec((rows, size), lambda j, s: (j, 0))
    shape = lambda *size: jax.ShapeDtypeStruct(size, jnp.bfloat16)
    return pl.pallas_call(
        partial(first_kernel, len(frames), len(blocks), count),
        grid_spec=pltpu.PrefetchScalarGridSpec(
            num_scalar_prefetch=1,
            grid=(count,),
            in_specs=specs
            + [pl.BlockSpec((2, width), lambda j, s: (0, 0))]
            + [ANYWHERE] * len(blocks),
            out_specs=[
                out(width),
                out(columns),
                pl.BlockSpec((width, columns), lambda j, s: (0, 0)),
            ],
            scratch_shapes=[pltpu.SemaphoreType.DMA((len(blocks),))],
        ),
        out_shape=[
            shape(rows * count, width),
            shape(rows * count, columns),
            shape(width, columns),
        ],
        compiler_params=BIG,
        cost_estimate=cost(
            2 * rows * count * width * columns, 4 * width * columns + 8 * rows * count * width
        ),
        name="first_layer",
    )(spots, *frames, ada, *blocks)


def second_kernel(pieces, calls, parts, count, place, *refs):
    mixed = refs[:pieces]
    tokens = refs[pieces : pieces + parts]
    out_w, ada = refs[pieces + parts : pieces + parts + 2]
    attended_ref, low_ref = refs[-2:]
    weights = out_w.reshape(out_w.shape[0] * out_w.shape[2], out_w.shape[3])
    spots = head_spots(place[4], calls, pieces)
    attended = current(tokens, count).astype(jnp.float32)
    for index, piece in enumerate(mixed):
        size = piece.shape[1]
        start = pl.multiple_of(spots[index] * size, size)
        attended = attended + matmul(piece[...], weights[pl.ds(start, size), :])
    attended_ref[...] = attended
    normed, _ = standardise(attended)
    low_ref[...] = ((1.0 + ada[0:1, :]) * normed + ada[1:2, :]).astype(jnp.bfloat16)


def second_layer(mixed, swapped, tokens, out_w, out_part, ada, spots):
    rows, width = tokens[-1].shape
    parts = len(tokens)
    count = 2 * parts
    size, token_specs = row_specs(tokens, count)
    later = count - 2
    block = lambda columns, order: pl.BlockSpec((size, columns), lambda j, s: (order(j), 0))
    first = lambda j: (j + later) % count
    items, _, piece, _ = out_w.shape
    return pl.pallas_call(
        partial(second_kernel, len(mixed) + len(swapped), len(mixed), parts, count),
        grid_spec=pltpu.PrefetchScalarGridSpec(
            num_scalar_prefetch=1,
            grid=(count,),
            in_specs=[block(part.shape[1], first) for part in mixed]
            + [block(part.shape[1], lambda j: j) for part in swapped]
            + token_specs
            + [
                pl.BlockSpec((items, 1, piece, width), lambda j, s: (0, out_part, 0, 0)),
                pl.BlockSpec((2, width), lambda j, s: (0, 0)),
            ],
            out_specs=[block(width, lambda j: jnp.maximum(j - later, 0)), block(width, first)],
        ),
        out_shape=[
            jax.ShapeDtypeStruct((rows, width), jnp.float32),
            jax.ShapeDtypeStruct((rows * parts, width), jnp.bfloat16),
        ],
        compiler_params=BIG,
        cost_estimate=cost(
            2 * rows * parts * width * width, 2 * width * width + 10 * rows * parts * width
        ),
        name="second_layer",
    )(spots, *mixed, *swapped, *tokens, out_w, ada)


def head_spots(seq, calls, pieces):
    if pieces == 1:
        return [0]
    own = [seq * calls + call for call in range(calls)]
    return own + [(1 - seq) * calls + call for call in range(pieces - calls)]


class Weights:
    def __init__(self, up, up_first, down, down_parts, hidden, width):
        self.up = up
        self.down = down
        self.width = width
        self.hidden = hidden
        fold = up.shape[3]
        self.block = min(512, fold, hidden // 2)
        per_chip = down_parts * down.shape[3]
        per_fold = fold // self.block
        chips, _, _, piece, _ = down.shape
        self.steps = hidden // self.block
        per_core = self.steps // 2
        block = self.block
        self.up_spec = pl.BlockSpec(
            (up.shape[0], 1, up.shape[2], block),
            lambda j: (0, up_first + j // per_fold, 0, j % per_fold),
        )
        self.down_spec = pl.BlockSpec(
            (block // per_chip, 1, down_parts, piece, width),
            lambda j: (j % per_core, j // per_core, 0, 0, 0),
        )
        self.per_chip = per_chip
        self.bytes = 2 * hidden * width


def hidden_kernel(per_chip, parts, x_ref, up_ref, down_ref, *refs):
    g_refs = refs[:parts]
    active_ref, grad_ref = refs[-2:]
    columns = min(256, active_ref.shape[1])
    size = x_ref.shape[0] // parts
    for start in range(0, active_ref.shape[1], columns):
        spot = slice(start, start + columns)
        up = up_ref[:, :, :, spot].reshape(-1, columns)
        chips = slice(start // per_chip, (start + columns) // per_chip)
        down = down_ref[chips].reshape(columns, -1)
        for index, g_ref in enumerate(g_refs):
            rows = slice(index * size, (index + 1) * size)
            upward = matmul(x_ref[rows, :], up)
            grad_active = matmul_last(g_ref[...], down)
            below = 0.5 * (1.0 + lax.erf(upward * ROOT_HALF))
            active_ref[rows, spot] = (upward * below).astype(jnp.bfloat16)
            slope = below + upward * (DENSITY * jnp.exp(-0.5 * upward * upward))
            grad_ref[rows, spot] = (grad_active * slope).astype(jnp.bfloat16)


def hidden_layer(x, grads, weights):
    rows, width = x.shape
    out = pl.BlockSpec((rows, weights.block), lambda j: (0, j))
    shape = jax.ShapeDtypeStruct((rows, weights.hidden), jnp.bfloat16)
    return pl.pallas_call(
        partial(hidden_kernel, weights.per_chip, len(grads)),
        grid=(weights.steps,),
        in_specs=[
            pl.BlockSpec((rows, width), lambda j: (0, 0)),
            weights.up_spec,
            weights.down_spec,
        ]
        + [pl.BlockSpec(grad.shape, lambda j: (0, 0)) for grad in grads],
        out_specs=[out, out],
        out_shape=[shape, shape],
        compiler_params=BIG,
        cost_estimate=cost(
            4 * rows * width * weights.hidden,
            2 * weights.bytes + 4 * rows * (width + weights.hidden),
        ),
        name="hidden_layer",
    )(x, weights.up, weights.down, *grads)


def accumulate(part, out_ref, total):
    step = pl.program_id(0)

    @pl.when(step == 0)
    def _():
        total[...] = part

    @pl.when(step > 0)
    def _():
        total[...] += part

    @pl.when(step == pl.num_programs(0) - 1)
    def _():
        out_ref[...] = total[...].astype(out_ref.dtype)


def down_kernel(a_ref, down_ref, *refs):
    out_ref, total = refs[-2:]
    accumulate(matmul(a_ref[...], down_ref[...].reshape(-1, out_ref.shape[1])), out_ref, total)


def up_back_kernel(g_ref, up_ref, *refs):
    out_ref, total = refs[-2:]
    weights = up_ref[...].reshape(out_ref.shape[1], -1)
    accumulate(matmul_last(g_ref[...], weights), out_ref, total)


def hidden_to_width(kernel, name, held, weights, spec, array, rows, chunk, dtype, behind):
    width = weights.width
    return pl.pallas_call(
        kernel,
        grid=(weights.steps,),
        in_specs=[pl.BlockSpec((rows, weights.block), lambda j: (chunk, j)), spec]
        + [ANYWHERE] * len(behind),
        out_specs=pl.BlockSpec((rows, width), lambda j: (0, 0)),
        out_shape=jax.ShapeDtypeStruct((rows, width), dtype),
        scratch_shapes=[pltpu.VMEM((rows, width), jnp.float32)],
        compiler_params=BIG,
        cost_estimate=cost(
            2 * rows * width * weights.hidden,
            weights.bytes + rows * (2 * weights.hidden + 4 * width),
        ),
        name=name,
    )(held, array, *behind)


def down_part(active, weights, rows, chunk, dtype, behind=()):
    return hidden_to_width(
        down_kernel,
        "down_part",
        active,
        weights,
        weights.down_spec,
        weights.down,
        rows,
        chunk,
        dtype,
        behind,
    )


def up_back(grad, weights, rows, chunk, dtype, behind=()):
    return hidden_to_width(
        up_back_kernel,
        "up_back",
        grad,
        weights,
        weights.up_spec,
        weights.up,
        rows,
        chunk,
        dtype,
        behind,
    )


def middle_back_kernel(pieces, parts, place, *refs):
    own_ref, base_ref, top_ref, ada_ref, out_w = refs[:5]
    others = refs[5 : 5 + parts]
    outs = refs[-3 - pieces :]
    grad_ref, low_ref, ada_grad_ref = outs[:3]
    grad = own_ref[...] + current(others, 2).astype(jnp.float32)
    normed, inverse = standardise(base_ref[...])
    scaled = grad * (1.0 + ada_ref[0:1, :])
    scale = jnp.sum(grad * normed, axis=0, keepdims=True)
    shift = jnp.sum(grad, axis=0, keepdims=True)
    inner = jnp.mean(scaled * normed, axis=-1, keepdims=True)
    shifted = scaled - jnp.mean(scaled, axis=-1, keepdims=True) - normed * inner
    out = top_ref[...].astype(jnp.float32) + inverse * shifted
    grad_ref[...] = out
    low = out.astype(jnp.bfloat16)
    low_ref[...] = low
    weights = out_w.reshape(out_w.shape[0] * out_w.shape[2], out_w.shape[3])
    spots = head_spots(1 - place[4], 1, pieces)
    for index, mixed_ref in enumerate(outs[3:]):
        size = mixed_ref.shape[1]
        start = pl.multiple_of(spots[index] * size, size)
        mixed_ref[...] = matmul_last(low, weights[pl.ds(start, size), :]).astype(jnp.bfloat16)
    add_rows(ada_grad_ref, scale, shift)


def middle_back(own, other, attended, cotangent, ada, out_w, out_part, spots, sizes, behind):
    rows, width = attended.shape
    count = 2
    block = lambda size: pl.BlockSpec((rows // count, size), lambda j, s: (j, 0))
    items, _, piece, _ = out_w.shape
    _, other_specs = row_specs(other, count)
    return pl.pallas_call(
        partial(middle_back_kernel, len(sizes), len(other)),
        grid_spec=pltpu.PrefetchScalarGridSpec(
            num_scalar_prefetch=1,
            grid=(count,),
            in_specs=[block(width)] * 3
            + [
                pl.BlockSpec((2, width), lambda j, s: (0, 0)),
                pl.BlockSpec((items, 1, piece, width), lambda j, s: (0, out_part, 0, 0)),
            ]
            + other_specs
            + [ANYWHERE] * len(behind),
            out_specs=[block(width), block(width), pl.BlockSpec((2, width), lambda j, s: (0, 0))]
            + [block(size) for size in sizes],
        ),
        out_shape=[
            jax.ShapeDtypeStruct((rows, width), jnp.float32),
            jax.ShapeDtypeStruct((rows, width), jnp.bfloat16),
            jax.ShapeDtypeStruct((2, width), jnp.float32),
        ]
        + [jax.ShapeDtypeStruct((rows, size), jnp.bfloat16) for size in sizes],
        compiler_params=BIG,
        cost_estimate=cost(2 * rows * width * width, 2 * width * width + 20 * rows * width),
        name="middle_back",
    )(spots, own, attended, cotangent, ada, out_w, *other, *behind)


def first_back_kernel(grad_ref, weight_ref, frames, *refs):
    out_ref, ada_grad_ref = refs[-2:]
    grad = matmul_last(grad_ref[...], weight_ref[...])
    normed, _ = standardise(frames[...].astype(jnp.float32))
    out_ref[...] = grad.astype(jnp.bfloat16)
    scale = jnp.sum(grad * normed, axis=0, keepdims=True)
    shift = jnp.sum(grad, axis=0, keepdims=True)
    add_rows(ada_grad_ref, scale, shift)


def first_back(grad, weights, frames, part, behind):
    width, columns = weights.shape
    count = 2
    rows = frames.shape[0] // count
    block = pl.BlockSpec((rows, width), lambda j: (j, 0))
    return pl.pallas_call(
        first_back_kernel,
        grid=(count,),
        in_specs=[
            pl.BlockSpec((rows, columns), lambda j: (part * count + j, 0)),
            pl.BlockSpec((width, columns), lambda j: (0, 0)),
            block,
        ]
        + [ANYWHERE] * len(behind),
        out_specs=[block, pl.BlockSpec((2, width), lambda j: (0, 0))],
        out_shape=[
            jax.ShapeDtypeStruct((rows * count, width), jnp.bfloat16),
            jax.ShapeDtypeStruct((2, width), jnp.float32),
        ],
        compiler_params=BIG,
        cost_estimate=cost(
            2 * rows * count * width * columns,
            2 * width * columns + 2 * rows * count * (2 * width + columns),
        ),
        name="first_back",
    )(grad, weights, frames, *behind)


def stacked_dot(lefts, rights):
    total = None
    for left, right in zip(lefts, rights):
        part = dot_rows(left, right)
        total = part if total is None else total + part
    return total


def cut_rows(ref, count):
    rows = ref.shape[0] // count
    return [ref[j * rows : (j + 1) * rows, :] for j in range(count)]


def put_sum(out_ref, other_ref, value):
    if other_ref is not None:
        value = value + other_ref[...].astype(jnp.float32)
    out_ref[...] = value.astype(jnp.bfloat16)


def hidden_grads_kernel(count, more, place, *refs):
    active, upward = refs[:2]
    grads, low = refs[2 : 2 + count], refs[2 + count]
    other = refs[3 + count] if more else None
    out_ref = refs[-1]
    step = pl.program_id(0)
    steps = pl.num_programs(0) // 2

    @pl.when(step < steps)
    def _():
        put_sum(
            out_ref, other, stacked_dot(cut_rows(active, count), [ref[...] for ref in grads])
        )

    @pl.when(step >= steps)
    def _():
        put_sum(out_ref, other, dot_rows(low[...], upward[...]))


def hidden_grads(place, who, active, upward, grads, low, other, behind):
    total, hidden = active.shape
    half = hidden // 2
    rows, width = grads[0].shape
    count = len(grads)
    block = 512
    steps = half // block
    whole = pl.BlockSpec((total, width), lambda j, s: (0, 0))
    grad = pl.BlockSpec((rows, block), lambda j, s: (0, jnp.minimum(j, steps - 1)))
    out = pl.BlockSpec((width, block), lambda j, s: (0, j))
    more = [] if other is None else [other]
    return pl.pallas_call(
        partial(hidden_grads_kernel, count, bool(more)),
        grid_spec=pltpu.PrefetchScalarGridSpec(
            num_scalar_prefetch=1,
            grid=(2 * steps,),
            in_specs=[
                pl.BlockSpec((total, half), lambda j, s: (0, s[who])),
                pl.BlockSpec(
                    (total, block), lambda j, s: (0, s[who] * steps + jnp.maximum(j - steps, 0))
                ),
            ]
            + [grad] * count
            + [whole]
            + [out] * len(more)
            + [ANYWHERE] * len(behind),
            out_specs=out,
        ),
        out_shape=jax.ShapeDtypeStruct((width, 2 * half), jnp.bfloat16),
        compiler_params=BIG,
        cost_estimate=cost(4 * total * half * width, 8 * total * half + 4 * width * half),
        name="hidden_grads",
    )(place, active, upward, *grads, low, *more, *behind)


def tail_grads_kernel(first, more, pieces, calls, place, low, grad, attended, *refs):
    mixed = refs[:pieces]
    other = refs[pieces] if more else None
    out_ref = refs[-1]

    @pl.when(pl.program_id(0) < first)
    def _():
        put_sum(out_ref, other, dot_rows(low[...], grad[...]))

    @pl.when(pl.program_id(0) >= first)
    def _():
        spots = head_spots(place[4], calls, pieces)
        for index, piece in enumerate(mixed):
            size = piece.shape[1]
            rows = pl.ds(pl.multiple_of(spots[index] * size, size), size)
            value = dot_rows(piece[...], attended[...])
            if more:
                value = value + other[rows, :].astype(jnp.float32)
            out_ref[rows, :] = value.astype(jnp.bfloat16)


def tail_grads(place, who, low_one, grad_qkv, mixed, swapped, attended_low, other, behind):
    total, width = low_one.shape
    rows = attended_low.shape[0]
    block = 256
    first = grad_qkv.shape[1] // 2 // block
    second = width // 2 // block
    out = pl.BlockSpec((width, block), lambda j, s: (0, j))
    more = [] if other is None else [other]
    return pl.pallas_call(
        partial(
            tail_grads_kernel, first, bool(more), len(mixed) + len(swapped), len(mixed)
        ),
        grid_spec=pltpu.PrefetchScalarGridSpec(
            num_scalar_prefetch=1,
            grid=(first + second,),
            in_specs=[
                pl.BlockSpec((total, width), lambda j, s: (0, 0)),
                pl.BlockSpec(
                    (total, block), lambda j, s: (0, s[who] * first + jnp.minimum(j, first - 1))
                ),
                pl.BlockSpec(
                    (rows, block), lambda j, s: (0, s[who] * second + jnp.maximum(j - first, 0))
                ),
            ]
            + [pl.BlockSpec((rows, part.shape[1]), lambda j, s: (0, 0)) for part in mixed]
            + [pl.BlockSpec((rows, part.shape[1]), lambda j, s: (1, 0)) for part in swapped]
            + [out] * len(more)
            + [ANYWHERE] * len(behind),
            out_specs=out,
        ),
        out_shape=jax.ShapeDtypeStruct((width, (first + second) * block), jnp.bfloat16),
        compiler_params=BIG,
        cost_estimate=cost(
            2 * width * block * (total * first + rows * second), 8 * total * width
        ),
        name="tail_grads",
    )(place, low_one, grad_qkv, attended_low, *mixed, *swapped, *more, *behind)


def input_back_kernel(parts, count, own_ref, tokens_ref, ada_ref, base_ref, *refs):
    out_ref = refs[-1]
    grad = own_ref[...].astype(jnp.float32) + current(refs[:parts], count).astype(jnp.float32)
    normed, inverse = standardise(tokens_ref[...].astype(jnp.float32))
    scaled = grad * (1.0 + ada_ref[0:1, :])
    inner = jnp.mean(scaled * normed, axis=-1, keepdims=True)
    shifted = scaled - jnp.mean(scaled, axis=-1, keepdims=True) - normed * inner
    out_ref[...] = base_ref[...] + inverse * shifted


def input_back(own, others, tokens, ada, base):
    rows, width = tokens.shape
    count = 4
    block = pl.BlockSpec((rows // count, width), lambda j: (j, 0))
    _, specs = row_specs(others, count)
    return pl.pallas_call(
        partial(input_back_kernel, len(others), count),
        grid=(count,),
        in_specs=[block, block, pl.BlockSpec((2, width), lambda j: (0, 0)), block] + specs,
        out_specs=block,
        out_shape=jax.ShapeDtypeStruct((rows, width), jnp.float32),
        compiler_params=BIG,
        cost_estimate=cost(20 * rows * width, 14 * rows * width),
        name="input_back",
    )(own, tokens, ada, base, *others)


def exact(left, right):
    return jnp.dot(left, right, precision=lax.Precision.HIGHEST)


def rounded(total, other=None):
    if other is not None:
        total = total + other.astype(jnp.float32)
    return total.astype(jnp.bfloat16)


def tie(*values):
    return lax.optimization_barrier(values)


def cut(value, start, size, axis):
    return lax.dynamic_slice_in_dim(value, start, size, axis, allow_negative_indices=False)


def pick(value, index, axis):
    return lax.dynamic_index_in_dim(
        value, index, axis, keepdims=False, allow_negative_indices=False
    )


def ring_of(items_count):
    chips = items_count // 2
    outer = 4 if chips % 4 == 0 else chips
    inner = chips // outer
    order = [a * inner for a in range(outer)]
    for turn, a in enumerate(reversed(range(outer))):
        beside = list(range(1, inner))
        order += [a * inner + b for b in (beside if turn % 2 == 0 else beside[::-1])]
    return order


class Mover:
    def __init__(self, items_count, seq_count):
        self.items_count = items_count
        self.seq_count = seq_count
        self.pair = seq_count == 2
        self.chips = items_count // 2
        order = ring_of(items_count)
        self.forward = []
        self.backward = []
        chips = self.chips
        table = np.zeros((items_count, 2 * chips + 2), np.int32)
        hops = list(range(chips // 2 + 1)) + [-hop for hop in range(1, (chips + 1) // 2)]
        for spot in range(self.chips):
            for core in range(2):
                here = 2 * order[spot] + core
                next_one = 2 * order[(spot + 1) % self.chips] + core
                self.forward.append((here, next_one))
                self.backward.append((next_one, here))
                for ahead in range(self.chips):
                    table[here, ahead] = order[(spot + ahead) % self.chips]
                table[here, chips] = core
                table[here, chips + 1] = 1 - core
                for spot_of, hop in enumerate(hops):
                    ahead = hop if core == 1 else -hop
                    table[here, chips + 2 + spot_of] = order[(spot + ahead) % chips]
        self.both_ways = [p for p in self.forward if p[0] % 2 == 0]
        self.both_ways += [p for p in self.backward if p[0] % 2 == 1]
        self.item = lax.axis_index("items")
        row = pick(jnp.asarray(table), self.item, 0)
        self.ahead = [row[j] for j in range(self.chips)]
        self.core = row[self.chips]
        self.beside = row[self.chips + 1]
        self.spots = row[self.chips + 2 :]
        self.seq = lax.axis_index("seq")

    def flip(self, value, bit):
        pairs = [(i, i ^ bit) for i in range(self.items_count)]
        return lax.ppermute(value, "items", pairs)

    def across(self, value):
        return lax.ppermute(value, "seq", [(0, 1), (1, 0)])

    def gather_items(self, value, summed, early, late):
        for bit in [1 << k for k in range(self.items_count.bit_length() - 1)]:
            summed = summed + self.flip(summed, bit)
        beside = self.flip(value, 1)
        block = jnp.where(
            self.core == 0,
            jnp.concatenate([value, beside], axis=0),
            jnp.concatenate([beside, value], axis=0),
        )
        direct = [block]
        for hop in range(1, self.chips // 2 + 1):
            moved = lax.ppermute(direct[-1], "items", self.both_ways)
            if hop == min(LATE_HOP, self.chips // 2):
                late, summed, moved, early = tie(late, summed, moved, early)
            direct.append(moved)
        beside = [self.flip(moved, 1) for moved in direct[1 : (self.chips + 1) // 2]]
        return direct + beside, summed, early, late

    def sum_seq(self, value):
        return value + self.across(value) if self.pair else lax.psum(value, "seq")

    def scatter_seq(self, value):
        rows = value.shape[0] // self.seq_count
        if self.pair:
            sent = cut(value, (1 - self.seq) * rows, rows, 0)
            kept = cut(value, self.seq * rows, rows, 0)
            return kept + self.across(sent.astype(jnp.bfloat16)).astype(jnp.float32)
        return lax.psum_scatter(
            value.astype(jnp.bfloat16), "seq", scatter_dimension=0, tiled=True
        ).astype(jnp.float32)

    def join_cores(self, value):
        parts = value.reshape(2, -1, value.shape[1])
        kept = pick(parts, self.core, 0)
        other = self.flip(pick(parts, self.beside, 0), 1)
        return jnp.where(self.core == 0, kept, other), jnp.where(self.core == 0, other, kept)

    def join_columns(self, value):
        rows = value.shape[0] // self.seq_count
        if self.pair:
            kept = cut(value, self.seq * rows, rows, 0)
            other = self.across(cut(value, (1 - self.seq) * rows, rows, 0))
            return jnp.where(self.seq == 0, kept, other), jnp.where(self.seq == 0, other, kept)
        moved = lax.all_to_all(value, "seq", split_axis=0, concat_axis=0, tiled=True)
        return tuple(moved[j * rows : (j + 1) * rows] for j in range(self.seq_count))


class RingSum:
    def __init__(self, mover, make, behind, ready=()):
        self.mover = mover
        self.chips = mover.chips
        self.make = make
        self.flows = None
        sent, self.ready = tie(make(False, None, behind), list(ready))
        self.sent = sent
        self.arriving = [mover.flip(sent, 1)]

    def block(self, ahead):
        return pick(self.both, self.mover.ahead[ahead % self.chips], 0)

    def add_own(self, behind):
        self.both = self.make(True, self.arriving[0], behind)
        self.whole = self.both
        self.both = self.both.reshape(self.chips, -1, self.both.shape[1])
        self.result = self.block(0).astype(jnp.float32)
        flows = [
            (self.mover.forward, 1, self.chips // 2),
            (self.mover.backward, -1, (self.chips - 1) // 2),
        ]
        self.send([(flow, self.block(flow[1] * flow[2])) for flow in flows if flow[2]])

    def send(self, flows):
        self.arriving = [lax.ppermute(value, "items", flow[0]) for flow, value in flows]
        self.flows = [(pairs, sign, left - 1) for (pairs, sign, left), _ in flows]

    def advance(self, anchor=None):
        flows = []
        if anchor is not None:
            self.arriving, anchor = tie(self.arriving, anchor)
        for flow, value in zip(self.flows, self.arriving):
            if flow[2]:
                flows.append((flow, self.block(flow[1] * flow[2]) + value))
            else:
                self.result = self.result + value.astype(jnp.float32)
        self.send(flows)
        return anchor

    def finish(self):
        while self.arriving:
            self.advance()
        return self.result


def in_rows(value):
    return with_layout_constraint(value, Layout((0, 1)))


def halves(value, core):
    half = value.shape[1] // 2
    return cut(value, core * half, half, 1)


def parted(value, at):
    return (None, None) if value is None else (value[:, :at], value[:, at:])


def shards(
    tokens,
    cotangent,
    prompt_len,
    section_ids,
    section_table,
    w_query,
    w_key,
    w_value,
    w_out,
    w_up,
    w_down,
    w_ada_one,
    w_ada_two,
):
    items_count = lax.axis_size("items")
    seq_count = lax.axis_size("seq")
    mover = Mover(items_count, seq_count)
    chips = mover.chips
    batch, rows, width = tokens.shape
    total_rows = rows * seq_count
    hidden = w_up.shape[1] // seq_count
    held = width // seq_count
    pairs = held // LANES
    piece = w_query.shape[0]
    units = w_down.shape[0] // seq_count
    tokens = tokens.reshape(rows, width)
    grad_low = cotangent.reshape(rows, width)

    def quarters(one, two):
        return jnp.stack([one[:, :width], one[:, width:], two[:, :width], two[:, width:]])

    up_shard = w_up.reshape(piece, chips, 2, seq_count, units).transpose(3, 0, 2, 1, 4)
    up_shard = pick(up_shard, mover.seq, 0).reshape(piece, hidden)
    down_shard = cut(w_down, mover.seq * units, units, 0)
    merged = hidden % width == 0 and units % piece == 0
    late = down_shard
    if merged:
        folds = hidden // width
        down_parts = units // piece
        up_rows = [up_shard[:, j * width : (j + 1) * width] for j in range(folds)]
        late = jnp.concatenate([down_shard] + up_rows + [w_out], axis=0)

    table_part = cut(section_table, mover.item * piece, piece, 1)
    ada_part = jnp.dot(
        table_part,
        jnp.concatenate([w_ada_one, w_ada_two], axis=1),
        preferred_element_type=jnp.float32,
    )
    ada_part = quarters(ada_part[:, : 2 * width], ada_part[:, 2 * width :])
    prompt_at = mover.seq if mover.pair else jnp.zeros((), jnp.int32)
    place = jnp.stack([prompt_at, prompt_len[0], mover.core, mover.beside, mover.seq])
    mine = pack_columns(w_query, w_key, w_value, held, place)
    early = [mover.across(tokens)] if mover.pair else []
    blocks, ada_sum, early, late = mover.gather_items(
        mine, ada_part, early, late
    )

    def gathered(value):
        return lax.all_gather(value, "items", axis=0, tiled=False)

    if merged:
        rest = gathered(late)
        rest = rest.reshape(items_count, down_parts + folds + 1, piece, width)
        by_core = rest.reshape((chips, 2) + rest.shape[1:])
        weights = Weights(rest, down_parts, by_core, down_parts, hidden, width)
        out_w, out_part = rest, down_parts + folds
    else:
        by_core = gathered(late).reshape(chips, 2, 1, units, width)
        weights = Weights(gathered(up_shard)[:, None], 0, by_core, 1, hidden, width)
        out_w, out_part = gathered(w_out)[:, None], 0

    choose = (section_ids[0] == jnp.arange(section_table.shape[0])).astype(jnp.float32)
    ada = jnp.sum(choose[None, :, None] * ada_sum, axis=1)
    ada_one = ada[:2]
    ada_two = ada[2:]

    if mover.pair:
        tokens_other, grad_sent = tie(early[0], grad_low)
        grad_other = mover.across(grad_sent)
        frames = [tokens, tokens_other]
        grads = [grad_low, grad_other]
        calls = 2 if pairs % 2 == 0 else 1
    else:
        frames = [lax.all_gather(tokens, "seq", axis=0, tiled=True)]
        grads = [lax.all_gather(grad_low, "seq", axis=0, tiled=True)]
        calls = 1
    low_one, qkv, qkv_w = first_layer(frames, ada_one, blocks, mover.spots)
    per_call = pairs // calls
    mixed_heads = []
    lse = []
    for call in range(calls):
        behind = grads[1:] + mixed_heads
        out = attend(qkv, place, call * per_call, per_call, behind)
        mixed_heads.append(out[0])
        lse.append(out[1])
    if mover.pair:
        mixed_far = []
        for call in range(calls):
            sent = mixed_heads[call]
            if mixed_far:
                sent, mixed_far[-1] = tie(sent, mixed_far[-1])
            mixed_far.append(mover.across(sent))
        attended, low_two = second_layer(
            mixed_heads, mixed_far, frames[::-1], out_w, out_part, ada_two, place
        )
        lows = low_two
        active, upward = hidden_layer(lows, grads, weights)
        for_other = up_back(upward, weights, rows, 1, jnp.bfloat16)
        half = rows // 2
        first_half, last_half = for_other[:half], for_other[half:]
        start = [for_other]
        ready = [mover.across(first_half), last_half]
    else:
        mixed = lax.all_to_all(mixed_heads[0], "seq", split_axis=0, concat_axis=1, tiled=True)
        attended, low_two = second_layer(
            [mixed], [], [tokens], out_w, out_part, ada_two, place
        )
        lows = lax.all_gather(low_two, "seq", axis=0, tiled=True)
        active, upward = hidden_layer(lows, grads, weights)
        start = []
        ready = []

    down_columns = hidden // 2

    def hidden_parts(own, other, behind):
        who = 2 if own else 3
        if down_columns == width:
            return hidden_grads(place, who, active, upward, grads, lows, other, behind)
        core = mover.core if own else mover.beside
        first, second = parted(other, down_columns)
        down = dot_rows(halves(active, core), grads[0]).reshape(width, down_columns)
        up = dot_rows(lows, halves(upward, core))
        return in_rows(jnp.concatenate([rounded(down, first), rounded(up, second)], axis=1))

    ring = RingSum(mover, hidden_parts, start, ready)
    if mover.pair:
        own = up_back(upward, weights, rows, 0, jnp.float32, [ring.sent])
        from_other = [ring.ready[0], mover.across(ring.ready[1])]
        sizes = [held, held]
    else:
        own = lax.psum_scatter(
            up_back(upward, weights, total_rows, 0, jnp.bfloat16),
            "seq",
            scatter_dimension=0,
            tiled=True,
        ).astype(jnp.float32)
        from_other = [jnp.zeros((rows, width), jnp.bfloat16)]
        sizes = [width]
    ring.add_own([own])
    grad_attended, attended_low, ada_two_rows, *grad_mixed = middle_back(
        own,
        from_other,
        attended,
        grad_low,
        ada_two,
        out_w,
        out_part,
        place,
        sizes,
        [ring.whole],
    )
    if mover.pair:
        out_other = down_part(active, weights, rows, 1, jnp.bfloat16, grad_mixed[:1])
        grad_heads = [grad_mixed[1], mover.across(grad_mixed[0])]
        out_other = ring.advance(out_other)
        out_own = down_part(active, weights, rows, 0, jnp.float32, [out_other])
        filler = [out_own]
        out_other = mover.across(out_other)
    else:
        grad_heads = [
            lax.all_to_all(grad_mixed[0], "seq", split_axis=1, concat_axis=0, tiled=True)
        ]
        filler = []

    split = pairs // 2 if pairs % 2 == 0 else 0

    def tail_parts(own, other, behind):
        if mover.pair:
            return tail_grads(
                place,
                2 if own else 3,
                low_one,
                grad_qkv,
                mixed_heads,
                mixed_far,
                attended_low,
                other,
                behind,
            )
        core = mover.core if own else mover.beside
        first, second = parted(other, grad_qkv.shape[1] // 2)
        qkv_part = rounded(dot_rows(low_one, halves(grad_qkv, core)), first)
        out_part = rounded(dot_rows(mixed, halves(attended_low, core)), second)
        return in_rows(jnp.concatenate([qkv_part, out_part], axis=1))

    tail = None
    grad_qkv = None
    for turn in range(pairs):
        behind = filler
        filler = []
        grad_qkv = attend_back(
            place, turn, pairs, qkv, mixed_heads, grad_heads, lse, grad_qkv, behind
        )
        grad_qkv = ring.advance(grad_qkv)
        if turn + 1 == split:
            tail = RingSum(mover, tail_parts, [])
            filler = [tail.sent]
    if tail is None:
        tail = RingSum(mover, tail_parts, [])
    tail.add_own([])
    if mover.pair:
        far_first, far_rows = first_back(grad_qkv, qkv_w, frames[1], 1, [tail.whole])
        far_first = tail.advance(far_first)
        half = rows // 2
        near_half, last_half = far_first[:half], far_first[half:]
        near_half = mover.across(near_half)
        own_first, own_rows = first_back(grad_qkv, qkv_w, frames[0], 0, [far_first])
        ada_rows = jnp.concatenate([own_rows + far_rows, ada_two_rows])
        ada_other = mover.across(ada_rows)
        near_half, last_half, ada_other, out_other = tail.advance(
            [near_half, last_half, ada_other, out_other]
        )
        ada_rows = ada_rows + ada_other
        far_parts = [near_half, mover.across(last_half)]
        layer_sum = out_own + out_other.astype(jnp.float32)
    else:
        grad_first, ada_one_rows = first_back(grad_qkv, qkv_w, frames[0], 0, [tail.whole])
        ada_rows = lax.psum(jnp.concatenate([ada_one_rows, ada_two_rows]), "seq")
        own_first = lax.psum_scatter(grad_first, "seq", scatter_dimension=0, tiled=True)
        far_parts = [jnp.zeros((rows, width), jnp.bfloat16)]
        layer_sum = lax.psum_scatter(
            down_part(active, weights, total_rows, 0, jnp.bfloat16),
            "seq",
            scatter_dimension=0,
            tiled=True,
        ).astype(jnp.float32)
    layer_out = (attended + layer_sum).astype(jnp.bfloat16)
    sums = choose[None, :, None] * ada_rows[:, None, :]
    for bit in [1 << k for k in range(items_count.bit_length() - 1)]:
        sums = sums + mover.flip(sums, bit)
        if bit == 2:
            sums = tail.advance(sums)
    input_grad = input_back(own_first, far_parts, tokens, ada_one, grad_attended)
    out_piece = piece // seq_count
    first_row = mover.item * piece + mover.seq * out_piece
    table_rows = cut(section_table, first_row, out_piece, 1).astype(jnp.float32)
    ada_grads = jnp.einsum("sr,ksd->krd", table_rows, sums, precision=lax.Precision.HIGHEST)
    grad_ada_one = jnp.concatenate([ada_grads[0], ada_grads[1]], axis=1)
    grad_ada_two = jnp.concatenate([ada_grads[2], ada_grads[3]], axis=1)
    own_ada = quarters(
        *(cut(w, mover.seq * out_piece, out_piece, 0) for w in (w_ada_one, w_ada_two))
    ).astype(jnp.float32)
    grad_table = jnp.einsum("ksd,krd->sr", sums, own_ada, precision=lax.Precision.HIGHEST)

    ring_total = ring.finish()
    grad_down = ring_total[:, :down_columns].reshape(units, width)
    up_sides = mover.join_columns(
        jnp.concatenate(mover.join_cores(ring_total[:, down_columns:]), axis=1)
    )
    grad_up = jnp.stack(
        [side.reshape(out_piece, 2, chips, units) for side in up_sides], axis=1
    )
    grad_up = grad_up.transpose(0, 3, 2, 1, 4).reshape(out_piece, hidden * seq_count)
    tail_total = tail.finish()
    cores = jnp.concatenate(mover.join_cores(tail_total), axis=1)
    half_qkv = 3 * held // 2
    half_all = cores.shape[1] // 2
    qkv_total = jnp.concatenate(
        [cores[:, :half_qkv], cores[:, half_all : half_all + half_qkv]], axis=1
    )
    out_total = jnp.concatenate([cores[:, half_qkv:half_all], cores[:, half_all + half_qkv :]], axis=1)
    sides = mover.join_columns(qkv_total)
    grad_out = mover.scatter_seq(out_total)
    grad_query, grad_key, grad_value = (
        jnp.concatenate(
            [
                side[:, (3 * p + j) * LANES : (3 * p + j + 1) * LANES]
                for side in sides
                for p in range(pairs)
            ],
            axis=1,
        )
        for j in range(3)
    )
    return (
        layer_out.reshape(batch, rows, width),
        input_grad.reshape(batch, rows, width),
        grad_query,
        grad_key,
        grad_value,
        grad_out,
        grad_up,
        grad_down,
        grad_ada_one,
        grad_ada_two,
        grad_table,
    )


def solution(mesh):
    return jax.shard_map(
        shards,
        mesh=mesh,
        in_specs=(
            P("items", "seq", None),
            P("items", "seq", None),
            P("items"),
            P("items"),
            P(),
            P("items", None),
            P("items", None),
            P("items", None),
            P("items", None),
            P("items", None),
            P("items", None),
            P("items", None),
            P("items", None),
        ),
        out_specs=(
            P("items", "seq", None),
            P("items", "seq", None),
            P(("items", "seq"), None),
            P(("items", "seq"), None),
            P(("items", "seq"), None),
            P(("items", "seq"), None),
            P(("items", "seq"), None),
            P(("items", "seq"), None),
            P(("items", "seq"), None),
            P(("items", "seq"), None),
            P(None, ("items", "seq")),
        ),
        check_vma=False,
    )
```

```python
from functools import partial
import math

import jax
import jax.numpy as jnp
import numpy as np
from jax import lax
from jax.experimental.layout import Layout, with_layout_constraint
from jax.experimental import pallas as pl
from jax.experimental.pallas import tpu as pltpu
from jax.sharding import PartitionSpec as P

HEAD_DIM = 64
SCALE = 0.125
MASKED = -1e30
COVER = 0.5
TILE = 128
LANES = 128

def row_ids(shape):
    return lax.broadcasted_iota(jnp.int32, shape, 0)
def lane_ids(shape):
    return lax.broadcasted_iota(jnp.int32, shape, 1)
def matmul(left, right):
    return jnp.dot(left, right, preferred_element_type=jnp.float32)
def twin_lanes(flipped):
    top = row_ids(flipped.shape) < HEAD_DIM
    return jnp.concatenate([jnp.where(top, flipped, 0.0), jnp.where(top, 0.0, flipped)], axis=1)
def twin_rows(block):
    first = lane_ids(block.shape) < HEAD_DIM
    return jnp.concatenate([jnp.where(first, block, 0.0), jnp.where(first, 0.0, block)], axis=0)
def untwin(wide):
    top = row_ids((LANES, LANES)) < HEAD_DIM
    return jnp.where(top, wide[:, :LANES], wide[:, LANES:]).T

def split3(value):
    high = value.astype(jnp.bfloat16).astype(jnp.float32)
    rest = value - high
    mid = rest.astype(jnp.bfloat16).astype(jnp.float32)
    return high, mid, rest - mid

def attend_kernel(place, q_ref, k_ref, v_ref, *refs):
    o_ref, lse_ref, keys_wide, values_t = refs[-4:]
    half = q_ref.shape[0] // 2
    prompt = pl.multiple_of(place[0] * half, TILE)
    target = pl.multiple_of((1 - place[0]) * half, TILE)
    length = place[1]
    shape = (half, LANES)
    keys_wide[:half, :LANES] = k_ref[pl.ds(prompt, half), :]
    keys_wide[half:, :LANES] = k_ref[pl.ds(target, half), :]
    hidden = (lane_ids(shape) == 0) & (row_ids(shape) >= length)
    keys_wide[:half, LANES:] = jnp.where(hidden, MASKED, 0.0).astype(jnp.bfloat16)
    keys_wide[half:, LANES:] = jnp.zeros(shape, jnp.bfloat16)
    for piece in range(half // TILE):
        rows = slice(piece * TILE, (piece + 1) * TILE)
        values_t[:, rows] = v_ref[pl.ds(prompt + piece * TILE, TILE), :].astype(jnp.float32).T.astype(jnp.bfloat16)
        rows = slice(half + piece * TILE, half + (piece + 1) * TILE)
        values_t[:, rows] = v_ref[pl.ds(target + piece * TILE, TILE), :].astype(jnp.float32).T.astype(jnp.bfloat16)
    below = jnp.where(row_ids((LANES, 2 * TILE)) == 0, 1.0, 0.0)

    def score(start, seen):
        q_flip = (q_ref[pl.ds(start, TILE), :].astype(jnp.float32) * SCALE).T
        q_wide = jnp.concatenate([twin_lanes(q_flip), below], axis=0).astype(jnp.bfloat16)
        return matmul(keys_wide[:seen, :], q_wide)

    def tile(scores, start, seen, slot):
        peak = jnp.max(scores, axis=0, keepdims=True)
        expo = jnp.exp(scores - peak)
        total = jnp.sum(expo, axis=0, keepdims=True)
        out = matmul(values_t[:, :seen], expo.astype(jnp.bfloat16)) / total
        o_ref[pl.ds(start, TILE), :] = untwin(out).astype(jnp.bfloat16)
        lse_ref[0, pl.ds(slot, 1), :] = peak + jnp.log(total)

    tiles = half // TILE

    @pl.loop(0, tiles)
    def _(index):
        at_prompt = pl.multiple_of(prompt + index * TILE, TILE)
        at_target = pl.multiple_of(target + index * TILE, TILE)
        first = score(at_prompt, half)
        second = score(at_target, 2 * half)
        tile(first, at_prompt, half, index)
        tile(second, at_target, 2 * half, tiles + index)


def attend(qkv, place, first, pairs, behind):
    rows = qkv.shape[0]
    width = pairs * LANES
    part = lambda shift: pl.BlockSpec((rows, LANES), lambda p, s, shift=shift: (0, 3 * (first + p) + shift))
    seen = rows * rows * 3 // 4
    return pl.pallas_call(
        attend_kernel,
        grid_spec=pltpu.PrefetchScalarGridSpec(
            num_scalar_prefetch=1, grid=(pairs,),
            in_specs=[part(0), part(1), part(2)] + [pl.BlockSpec(memory_space=pl.ANY)] * len(behind),
            out_specs=[pl.BlockSpec((rows, LANES), lambda p, s: (0, p)), pl.BlockSpec((1, rows // TILE, 2 * TILE), lambda p, s: (p, 0, 0))],
            scratch_shapes=[pltpu.VMEM((rows, 2 * LANES), jnp.bfloat16), pltpu.VMEM((LANES, rows), jnp.bfloat16)],
        ),
        out_shape=[jax.ShapeDtypeStruct((rows, width), jnp.bfloat16),
                   jax.ShapeDtypeStruct((pairs, rows // TILE, 2 * TILE), jnp.float32)],
        compiler_params=pltpu.CompilerParams(vmem_limit_bytes=60 << 20),
        cost_estimate=pl.CostEstimate(flops=int(COVER * pairs * 2 * seen * 4 * HEAD_DIM * 4), transcendentals=0, bytes_accessed=rows * width * 8),
        name="attend",
    )(place, qkv, qkv, qkv, *behind)


def attend_back_kernel(parts, calls, per, at, place, q_ref, k_ref, v_ref, *refs):
    o_refs, lse_refs, g_refs = refs[:calls], refs[calls:2 * calls], refs[2 * calls:2 * calls + parts]
    out_ref, keys_wide, values_wide, keys_t, dq, dk, dv = refs[-7:]
    half = q_ref.shape[0] // 2
    step = pl.program_id(0)
    prompt = pl.multiple_of(place[0] * half, TILE)
    target = pl.multiple_of((1 - place[0]) * half, TILE)
    length = place[1]

    @pl.when(step == 0)
    def _():
        shape = (half, LANES)
        lanes = lane_ids(shape)
        ones = jnp.where((lanes >= 1) & (lanes <= 3), 1.0, 0.0)
        hidden = (lanes == 0) & (row_ids(shape) >= length)
        keys_wide[:half, :LANES] = k_ref[pl.ds(prompt, half), :]
        keys_wide[half:, :LANES] = k_ref[pl.ds(target, half), :]
        keys_wide[:half, LANES:] = jnp.where(hidden, MASKED, ones).astype(jnp.bfloat16)
        keys_wide[half:, LANES:] = ones.astype(jnp.bfloat16)
        values_wide[:half, :LANES] = v_ref[pl.ds(prompt, half), :]
        values_wide[half:, :LANES] = v_ref[pl.ds(target, half), :]
        values_wide[:half, LANES:] = ones.astype(jnp.bfloat16)
        values_wide[half:, LANES:] = ones.astype(jnp.bfloat16)
        for piece in range(2 * half // TILE):
            rows = slice(piece * TILE, (piece + 1) * TILE)
            keys_t[:, rows] = keys_wide[rows, :LANES].astype(jnp.float32).T.astype(jnp.bfloat16)
        dk[...] = jnp.zeros_like(dk)
        dv[...] = jnp.zeros_like(dv)
        wide = (LANES, 2 * TILE)
        ids = row_ids(wide)

        def lanes_of(value):
            high, mid, rest = split3(value)
            return jnp.where(ids == 1, -high, jnp.where(ids == 2, -mid, jnp.where(ids == 3, -rest, 0.0)))

        def g_tile(start):
            if parts == 1:
                return g_refs[0][pl.ds(start, TILE), :]
            inside = pl.multiple_of(jnp.where(start < half, start, start - half), TILE)
            first = g_refs[0][pl.ds(inside, TILE), :]
            return jnp.where(start < half, first, g_refs[1][pl.ds(inside, TILE), :])

        def of_call(values):
            value = values[0]
            for call, later in enumerate(values[1:], 1):
                value = jnp.where(at(place) < call * per, value, later)
            return value

        def tile(start, seen, slot):
            spot = pl.ds(start, TILE)
            q_here = q_ref[spot, :].astype(jnp.float32) * SCALE
            g_here = g_tile(start).astype(jnp.float32)
            g_flip = g_here.T
            o_here = of_call([ref[spot, :].astype(jnp.float32) for ref in o_refs])
            product = g_flip * o_here.T
            inner = jnp.concatenate(
                [jnp.sum(product[:HEAD_DIM], axis=0, keepdims=True), jnp.sum(product[HEAD_DIM:], axis=0, keepdims=True)], axis=1)
            lse = of_call([ref[0, pl.ds(slot, 1), :] for ref in lse_refs])
            below = jnp.where(ids == 0, 1.0, lanes_of(lse))
            q_wide = jnp.concatenate([twin_lanes(q_here.T), below], axis=0).astype(jnp.bfloat16)
            g_wide = jnp.concatenate([twin_lanes(g_flip), lanes_of(inner)], axis=0).astype(jnp.bfloat16)
            probs = jnp.exp(matmul(keys_wide[:seen, :], q_wide))
            grads = matmul(values_wide[:seen, :], g_wide)
            scores = (probs * grads).astype(jnp.bfloat16)
            dk[:seen, :] += matmul(scores, twin_rows(q_here).astype(jnp.bfloat16))
            dv[:seen, :] += matmul(probs.astype(jnp.bfloat16), twin_rows(g_here).astype(jnp.bfloat16))
            dq[spot, :] = (untwin(matmul(keys_t[:, :seen], scores)) * SCALE).astype(jnp.bfloat16)

        tiles = half // TILE

        @pl.loop(0, tiles)
        def _(index):
            tile(pl.multiple_of(prompt + index * TILE, TILE), half, index)
            tile(pl.multiple_of(target + index * TILE, TILE), 2 * half, tiles + index)

        out_ref[...] = dq[...]

    for which, held in ((1, dk), (2, dv)):
        @pl.when(step == which)
        def _(held=held):
            out_ref[pl.ds(prompt, half), :] = held[:half, :].astype(jnp.bfloat16)
            out_ref[pl.ds(target, half), :] = held[half:, :].astype(jnp.bfloat16)


def attend_back(place, turn, pairs, qkv, mixed, grads, lse, held, behind):
    rows = qkv.shape[0]
    part = lambda shift: pl.BlockSpec((rows, LANES), lambda j, s, shift=shift: (0, 3 * at(s) + shift))
    calls = len(mixed)
    per = pairs // calls
    split = pairs // 2 if pairs % 2 == 0 else 0
    at = lambda s: (s[3] * split + turn) & (pairs - 1)
    parts = len(grads)
    block = pl.BlockSpec((rows, LANES), lambda j, s: (0, at(s) & (per - 1)))
    lse_block = pl.BlockSpec((1, rows // TILE, 2 * TILE), lambda j, s: (at(s) & (per - 1), 0, 0))
    grad_blocks = [pl.BlockSpec((grad.shape[0], LANES), lambda j, s: (0, at(s))) for grad in grads]
    seen = rows * rows * 3 // 4
    more = [] if held is None else [held]
    return pl.pallas_call(
        partial(attend_back_kernel, parts, calls, per, at),
        grid_spec=pltpu.PrefetchScalarGridSpec(
            num_scalar_prefetch=1, grid=(3,),
            in_specs=[part(0), part(1), part(2)] + [block] * calls + [lse_block] * calls + grad_blocks + [pl.BlockSpec(memory_space=pl.ANY)] * (len(more) + len(behind)),
            out_specs=pl.BlockSpec((rows, LANES), lambda j, s: (0, 3 * at(s) + j)),
            scratch_shapes=[pltpu.VMEM((rows, 2 * LANES), jnp.bfloat16), pltpu.VMEM((rows, 2 * LANES), jnp.bfloat16), pltpu.VMEM((LANES, rows), jnp.bfloat16),
                pltpu.VMEM((rows, LANES), jnp.bfloat16), pltpu.VMEM((rows, LANES), jnp.float32), pltpu.VMEM((rows, LANES), jnp.float32)],
        ),
        out_shape=jax.ShapeDtypeStruct(qkv.shape, jnp.bfloat16),
        input_output_aliases={4 + 2 * calls + parts: 0} if more else {},
        compiler_params=pltpu.CompilerParams(vmem_limit_bytes=60 << 20),
        cost_estimate=pl.CostEstimate(flops=int(COVER * 2 * seen * 10 * HEAD_DIM * 4), transcendentals=0, bytes_accessed=rows * LANES * 20),
        name="attend_back",
    )(place, qkv, qkv, qkv, *mixed, *lse, *grads, *more, *behind)


EPSILON = 1e-05
ROOT_HALF = math.sqrt(0.5)
DENSITY = 1.0 / math.sqrt(2.0 * math.pi)
LATE_HOP = 2
BIG = pltpu.CompilerParams(vmem_limit_bytes=60 << 20)
ANYWHERE = pl.BlockSpec(memory_space=pl.ANY)


def cost(flops, moved, special=0):
    return pl.CostEstimate(
        flops=int(flops * COVER), bytes_accessed=int(moved * COVER), transcendentals=special
    )


def matmul_last(left, right):
    return lax.dot_general(
        left, right, (((1,), (1,)), ((), ())), preferred_element_type=jnp.float32
    )


def dot_rows(left, right):
    return lax.dot_general(
        left, right, (((0,), (0,)), ((), ())), preferred_element_type=jnp.float32
    )


def standardise(values):
    centred = values - jnp.mean(values, axis=-1, keepdims=True)
    spread = jnp.mean(centred * centred, axis=-1, keepdims=True)
    inverse = lax.rsqrt(spread + EPSILON)
    return centred * inverse, inverse


def add_rows(ref, scale, shift):
    step = pl.program_id(0)

    @pl.when(step == 0)
    def _():
        ref[0:1, :] = scale
        ref[1:2, :] = shift

    @pl.when(step > 0)
    def _():
        ref[0:1, :] += scale
        ref[1:2, :] += shift


def row_specs(parts, count):
    rows = sum(part.shape[0] for part in parts) // count
    specs = []
    first = 0
    for part in parts:
        steps = part.shape[0] // rows
        specs.append(
            pl.BlockSpec(
                (rows, part.shape[1]),
                lambda j, *s, first=first, steps=steps: (jnp.clip(j - first, 0, steps - 1), 0),
            )
        )
        first += steps
    return rows, specs


def current(refs, count):
    value = refs[0][...]
    for index, ref in enumerate(refs[1:], 1):
        value = jnp.where(pl.program_id(0) < index * count // len(refs), value, ref[...])
    return value


def pack_kernel(place, query_ref, key_ref, value_ref, out_ref):
    for pair in range(query_ref.shape[1] // LANES):
        for which, ref in enumerate((query_ref, key_ref, value_ref)):
            start = (3 * pair + which) * LANES
            out_ref[:, start : start + LANES] = ref[:, pair * LANES : (pair + 1) * LANES]


def pack_columns(query, key, value, held, place):
    rows = query.shape[0]
    return pl.pallas_call(
        pack_kernel,
        grid_spec=pltpu.PrefetchScalarGridSpec(
            num_scalar_prefetch=1,
            grid=(1,),
            in_specs=[pl.BlockSpec((rows, held), lambda j, s: (0, s[0]))] * 3,
            out_specs=pl.BlockSpec((rows, 3 * held), lambda j, s: (0, 0)),
        ),
        out_shape=jax.ShapeDtypeStruct((rows, 3 * held), query.dtype),
        cost_estimate=cost(0, 12 * rows * held),
        name="pack_columns",
    )(place, query, key, value)


def first_kernel(parts, pieces, count, spots, *refs):
    frames = refs[:parts]
    ada = refs[parts]
    blocks = refs[parts + 1 : parts + 1 + pieces]
    low_ref, qkv_ref, weight_ref, sems = refs[-4:]
    rows = blocks[0].shape[0]

    @pl.when(pl.program_id(0) == 0)
    def _():
        copies = []
        for index, block in enumerate(blocks):
            start = pl.multiple_of(spots[index] * rows, rows)
            copy = pltpu.make_async_copy(
                block, weight_ref.at[pl.ds(start, rows), :], sems.at[index]
            )
            copy.start()
            copies.append(copy)
        for copy in copies:
            copy.wait()

    normed, _ = standardise(current(frames, count).astype(jnp.float32))
    low = ((1.0 + ada[0:1, :]) * normed + ada[1:2, :]).astype(jnp.bfloat16)
    low_ref[...] = low
    qkv_ref[...] = matmul(low, weight_ref[...]).astype(jnp.bfloat16)


def first_layer(frames, ada, blocks, spots):
    count = 4
    rows, specs = row_specs(frames, count)
    width = frames[0].shape[1]
    columns = blocks[0].shape[1]
    out = lambda size: pl.BlockSpec((rows, size), lambda j, s: (j, 0))
    shape = lambda *size: jax.ShapeDtypeStruct(size, jnp.bfloat16)
    return pl.pallas_call(
        partial(first_kernel, len(frames), len(blocks), count),
        grid_spec=pltpu.PrefetchScalarGridSpec(
            num_scalar_prefetch=1,
            grid=(count,),
            in_specs=specs
            + [pl.BlockSpec((2, width), lambda j, s: (0, 0))]
            + [ANYWHERE] * len(blocks),
            out_specs=[
                out(width),
                out(columns),
                pl.BlockSpec((width, columns), lambda j, s: (0, 0)),
            ],
            scratch_shapes=[pltpu.SemaphoreType.DMA((len(blocks),))],
        ),
        out_shape=[
            shape(rows * count, width),
            shape(rows * count, columns),
            shape(width, columns),
        ],
        compiler_params=BIG,
        cost_estimate=cost(
            2 * rows * count * width * columns, 4 * width * columns + 8 * rows * count * width
        ),
        name="first_layer",
    )(spots, *frames, ada, *blocks)


def second_kernel(pieces, calls, parts, count, place, *refs):
    mixed = refs[:pieces]
    tokens = refs[pieces : pieces + parts]
    out_w, ada = refs[pieces + parts : pieces + parts + 2]
    attended_ref, low_ref = refs[-2:]
    weights = out_w.reshape(out_w.shape[0] * out_w.shape[2], out_w.shape[3])
    spots = head_spots(place[4], calls, pieces)
    attended = current(tokens, count).astype(jnp.float32)
    for index, piece in enumerate(mixed):
        size = piece.shape[1]
        start = pl.multiple_of(spots[index] * size, size)
        attended = attended + matmul(piece[...], weights[pl.ds(start, size), :])
    attended_ref[...] = attended
    normed, _ = standardise(attended)
    low_ref[...] = ((1.0 + ada[0:1, :]) * normed + ada[1:2, :]).astype(jnp.bfloat16)


def second_layer(mixed, swapped, tokens, out_w, out_part, ada, spots):
    rows, width = tokens[-1].shape
    parts = len(tokens)
    count = 2 * parts
    size, token_specs = row_specs(tokens, count)
    later = count - 2
    block = lambda columns, order: pl.BlockSpec((size, columns), lambda j, s: (order(j), 0))
    first = lambda j: (j + later) % count
    items, _, piece, _ = out_w.shape
    return pl.pallas_call(
        partial(second_kernel, len(mixed) + len(swapped), len(mixed), parts, count),
        grid_spec=pltpu.PrefetchScalarGridSpec(
            num_scalar_prefetch=1,
            grid=(count,),
            in_specs=[block(part.shape[1], first) for part in mixed]
            + [block(part.shape[1], lambda j: j) for part in swapped]
            + token_specs
            + [
                pl.BlockSpec((items, 1, piece, width), lambda j, s: (0, out_part, 0, 0)),
                pl.BlockSpec((2, width), lambda j, s: (0, 0)),
            ],
            out_specs=[block(width, lambda j: jnp.maximum(j - later, 0)), block(width, first)],
        ),
        out_shape=[
            jax.ShapeDtypeStruct((rows, width), jnp.float32),
            jax.ShapeDtypeStruct((rows * parts, width), jnp.bfloat16),
        ],
        compiler_params=BIG,
        cost_estimate=cost(
            2 * rows * parts * width * width, 2 * width * width + 10 * rows * parts * width
        ),
        name="second_layer",
    )(spots, *mixed, *swapped, *tokens, out_w, ada)


def head_spots(seq, calls, pieces):
    if pieces == 1:
        return [0]
    own = [seq * calls + call for call in range(calls)]
    return own + [(1 - seq) * calls + call for call in range(pieces - calls)]


class Weights:
    def __init__(self, up, up_first, down, down_parts, hidden, width):
        self.up = up
        self.down = down
        self.width = width
        self.hidden = hidden
        fold = up.shape[3]
        self.block = min(512, fold, hidden // 2)
        per_chip = down_parts * down.shape[3]
        per_fold = fold // self.block
        chips, _, _, piece, _ = down.shape
        self.steps = hidden // self.block
        per_core = self.steps // 2
        block = self.block
        self.up_spec = pl.BlockSpec(
            (up.shape[0], 1, up.shape[2], block),
            lambda j: (0, up_first + j // per_fold, 0, j % per_fold),
        )
        self.down_spec = pl.BlockSpec(
            (block // per_chip, 1, down_parts, piece, width),
            lambda j: (j % per_core, j // per_core, 0, 0, 0),
        )
        self.per_chip = per_chip
        self.bytes = 2 * hidden * width


def hidden_kernel(per_chip, parts, x_ref, up_ref, down_ref, *refs):
    g_refs = refs[:parts]
    active_ref, grad_ref = refs[-2:]
    columns = min(256, active_ref.shape[1])
    size = x_ref.shape[0] // parts
    for start in range(0, active_ref.shape[1], columns):
        spot = slice(start, start + columns)
        up = up_ref[:, :, :, spot].reshape(-1, columns)
        chips = slice(start // per_chip, (start + columns) // per_chip)
        down = down_ref[chips].reshape(columns, -1)
        for index, g_ref in enumerate(g_refs):
            rows = slice(index * size, (index + 1) * size)
            upward = matmul(x_ref[rows, :], up)
            grad_active = matmul_last(g_ref[...], down)
            below = 0.5 * (1.0 + lax.erf(upward * ROOT_HALF))
            active_ref[rows, spot] = (upward * below).astype(jnp.bfloat16)
            slope = below + upward * (DENSITY * jnp.exp(-0.5 * upward * upward))
            grad_ref[rows, spot] = (grad_active * slope).astype(jnp.bfloat16)


def hidden_layer(x, grads, weights):
    rows, width = x.shape
    out = pl.BlockSpec((rows, weights.block), lambda j: (0, j))
    shape = jax.ShapeDtypeStruct((rows, weights.hidden), jnp.bfloat16)
    return pl.pallas_call(
        partial(hidden_kernel, weights.per_chip, len(grads)),
        grid=(weights.steps,),
        in_specs=[
            pl.BlockSpec((rows, width), lambda j: (0, 0)),
            weights.up_spec,
            weights.down_spec,
        ]
        + [pl.BlockSpec(grad.shape, lambda j: (0, 0)) for grad in grads],
        out_specs=[out, out],
        out_shape=[shape, shape],
        compiler_params=BIG,
        cost_estimate=cost(
            4 * rows * width * weights.hidden,
            2 * weights.bytes + 4 * rows * (width + weights.hidden),
        ),
        name="hidden_layer",
    )(x, weights.up, weights.down, *grads)


def accumulate(part, outs, total):
    step = pl.program_id(0)

    @pl.when(step == 0)
    def _():
        total[...] = part

    @pl.when(step > 0)
    def _():
        total[...] += part

    @pl.when(step == pl.num_programs(0) - 1)
    def _():
        rows = total.shape[0] // len(outs)
        for index, out_ref in enumerate(outs):
            value = total[index * rows : (index + 1) * rows, :]
            out_ref[...] = value.astype(out_ref.dtype)


def down_kernel(splits, a_ref, down_ref, *refs):
    total = refs[-1]
    part = matmul(a_ref[...], down_ref[...].reshape(-1, total.shape[1]))
    accumulate(part, refs[-1 - splits : -1], total)


def up_back_kernel(splits, g_ref, up_ref, *refs):
    total = refs[-1]
    weights = up_ref[...].reshape(total.shape[1], -1)
    accumulate(matmul_last(g_ref[...], weights), refs[-1 - splits : -1], total)


def hidden_to_width(kernel, name, held, weights, spec, array, rows, chunk, dtype, behind, splits=1):
    width = weights.width
    outs = pl.pallas_call(
        partial(kernel, splits),
        grid=(weights.steps,),
        in_specs=[pl.BlockSpec((rows, weights.block), lambda j: (chunk, j)), spec]
        + [ANYWHERE] * len(behind),
        out_specs=[pl.BlockSpec((rows // splits, width), lambda j: (0, 0))] * splits,
        out_shape=[jax.ShapeDtypeStruct((rows // splits, width), dtype)] * splits,
        scratch_shapes=[pltpu.VMEM((rows, width), jnp.float32)],
        compiler_params=BIG,
        cost_estimate=cost(
            2 * rows * width * weights.hidden,
            weights.bytes + rows * (2 * weights.hidden + 4 * width),
        ),
        name=name,
    )(held, array, *behind)
    return outs[0] if splits == 1 else outs


def down_part(active, weights, rows, chunk, dtype, behind=()):
    return hidden_to_width(
        down_kernel,
        "down_part",
        active,
        weights,
        weights.down_spec,
        weights.down,
        rows,
        chunk,
        dtype,
        behind,
    )


def up_back(grad, weights, rows, chunk, dtype, behind=(), splits=1):
    return hidden_to_width(
        up_back_kernel,
        "up_back",
        grad,
        weights,
        weights.up_spec,
        weights.up,
        rows,
        chunk,
        dtype,
        behind,
        splits,
    )


def middle_back_kernel(pieces, parts, place, *refs):
    own_ref, base_ref, top_ref, ada_ref, out_w = refs[:5]
    others = refs[5 : 5 + parts]
    outs = refs[-3 - pieces :]
    grad_ref, low_ref, ada_grad_ref = outs[:3]
    grad = own_ref[...] + current(others, 2).astype(jnp.float32)
    normed, inverse = standardise(base_ref[...])
    scaled = grad * (1.0 + ada_ref[0:1, :])
    scale = jnp.sum(grad * normed, axis=0, keepdims=True)
    shift = jnp.sum(grad, axis=0, keepdims=True)
    inner = jnp.mean(scaled * normed, axis=-1, keepdims=True)
    shifted = scaled - jnp.mean(scaled, axis=-1, keepdims=True) - normed * inner
    out = top_ref[...].astype(jnp.float32) + inverse * shifted
    grad_ref[...] = out
    low = out.astype(jnp.bfloat16)
    low_ref[...] = low
    weights = out_w.reshape(out_w.shape[0] * out_w.shape[2], out_w.shape[3])
    spots = head_spots(1 - place[4], 1, pieces)
    for index, mixed_ref in enumerate(outs[3:]):
        size = mixed_ref.shape[1]
        start = pl.multiple_of(spots[index] * size, size)
        mixed_ref[...] = matmul_last(low, weights[pl.ds(start, size), :]).astype(jnp.bfloat16)
    add_rows(ada_grad_ref, scale, shift)


def middle_back(own, other, attended, cotangent, ada, out_w, out_part, spots, sizes, behind):
    rows, width = attended.shape
    count = 2
    block = lambda size: pl.BlockSpec((rows // count, size), lambda j, s: (j, 0))
    items, _, piece, _ = out_w.shape
    _, other_specs = row_specs(other, count)
    return pl.pallas_call(
        partial(middle_back_kernel, len(sizes), len(other)),
        grid_spec=pltpu.PrefetchScalarGridSpec(
            num_scalar_prefetch=1,
            grid=(count,),
            in_specs=[block(width)] * 3
            + [
                pl.BlockSpec((2, width), lambda j, s: (0, 0)),
                pl.BlockSpec((items, 1, piece, width), lambda j, s: (0, out_part, 0, 0)),
            ]
            + other_specs
            + [ANYWHERE] * len(behind),
            out_specs=[block(width), block(width), pl.BlockSpec((2, width), lambda j, s: (0, 0))]
            + [block(size) for size in sizes],
        ),
        out_shape=[
            jax.ShapeDtypeStruct((rows, width), jnp.float32),
            jax.ShapeDtypeStruct((rows, width), jnp.bfloat16),
            jax.ShapeDtypeStruct((2, width), jnp.float32),
        ]
        + [jax.ShapeDtypeStruct((rows, size), jnp.bfloat16) for size in sizes],
        compiler_params=BIG,
        cost_estimate=cost(2 * rows * width * width, 2 * width * width + 20 * rows * width),
        name="middle_back",
    )(spots, own, attended, cotangent, ada, out_w, *other, *behind)


def first_back_kernel(splits, grad_ref, weight_ref, frames, *refs):
    outs, ada_grad_ref = refs[-1 - splits : -1], refs[-1]
    grad = matmul_last(grad_ref[...], weight_ref[...])
    normed, _ = standardise(frames[...].astype(jnp.float32))
    for index, out_ref in enumerate(outs):

        @pl.when((pl.program_id(0) == index) | (splits == 1))
        def _(out_ref=out_ref):
            out_ref[...] = grad.astype(jnp.bfloat16)

    scale = jnp.sum(grad * normed, axis=0, keepdims=True)
    shift = jnp.sum(grad, axis=0, keepdims=True)
    add_rows(ada_grad_ref, scale, shift)


def first_back(grad, weights, frames, part, behind, splits=1):
    width, columns = weights.shape
    count = 2
    rows = frames.shape[0] // count
    block = pl.BlockSpec((rows, width), lambda j: (j, 0))
    out = block if splits == 1 else pl.BlockSpec((rows, width), lambda j: (0, 0))
    return pl.pallas_call(
        partial(first_back_kernel, splits),
        grid=(count,),
        in_specs=[
            pl.BlockSpec((rows, columns), lambda j: (part * count + j, 0)),
            pl.BlockSpec((width, columns), lambda j: (0, 0)),
            block,
        ]
        + [ANYWHERE] * len(behind),
        out_specs=[out] * splits + [pl.BlockSpec((2, width), lambda j: (0, 0))],
        out_shape=[jax.ShapeDtypeStruct((rows * count // splits, width), jnp.bfloat16)] * splits
        + [jax.ShapeDtypeStruct((2, width), jnp.float32)],
        compiler_params=BIG,
        cost_estimate=cost(
            2 * rows * count * width * columns,
            2 * width * columns + 2 * rows * count * (2 * width + columns),
        ),
        name="first_back",
    )(grad, weights, frames, *behind)


def stacked_dot(lefts, rights):
    total = None
    for left, right in zip(lefts, rights):
        part = dot_rows(left, right)
        total = part if total is None else total + part
    return total


def cut_rows(ref, count):
    rows = ref.shape[0] // count
    return [ref[j * rows : (j + 1) * rows, :] for j in range(count)]


def put_sum(out_ref, other_ref, value):
    if other_ref is not None:
        value = value + other_ref[...].astype(jnp.float32)
    out_ref[...] = value.astype(jnp.bfloat16)


def hidden_grads_kernel(count, more, place, *refs):
    active, upward = refs[:2]
    grads, low = refs[2 : 2 + count], refs[2 + count]
    other = refs[3 + count] if more else None
    out_ref = refs[-1]
    step = pl.program_id(0)
    steps = pl.num_programs(0) // 2

    @pl.when(step < steps)
    def _():
        put_sum(
            out_ref, other, stacked_dot(cut_rows(active, count), [ref[...] for ref in grads])
        )

    @pl.when(step >= steps)
    def _():
        put_sum(out_ref, other, dot_rows(low[...], upward[...]))


def hidden_grads(place, who, active, upward, grads, low, other, behind):
    total, hidden = active.shape
    half = hidden // 2
    rows, width = grads[0].shape
    count = len(grads)
    block = 512
    steps = half // block
    whole = pl.BlockSpec((total, width), lambda j, s: (0, 0))
    grad = pl.BlockSpec((rows, block), lambda j, s: (0, jnp.minimum(j, steps - 1)))
    out = pl.BlockSpec((width, block), lambda j, s: (0, j))
    more = [] if other is None else [other]
    return pl.pallas_call(
        partial(hidden_grads_kernel, count, bool(more)),
        grid_spec=pltpu.PrefetchScalarGridSpec(
            num_scalar_prefetch=1,
            grid=(2 * steps,),
            in_specs=[
                pl.BlockSpec((total, half), lambda j, s: (0, s[who])),
                pl.BlockSpec(
                    (total, block), lambda j, s: (0, s[who] * steps + jnp.maximum(j - steps, 0))
                ),
            ]
            + [grad] * count
            + [whole]
            + [out] * len(more)
            + [ANYWHERE] * len(behind),
            out_specs=out,
        ),
        out_shape=jax.ShapeDtypeStruct((width, 2 * half), jnp.bfloat16),
        compiler_params=BIG,
        cost_estimate=cost(4 * total * half * width, 8 * total * half + 4 * width * half),
        name="hidden_grads",
    )(place, active, upward, *grads, low, *more, *behind)


def tail_grads_kernel(first, more, pieces, calls, place, low, grad, attended, *refs):
    mixed = refs[:pieces]
    other = refs[pieces] if more else None
    out_ref = refs[-1]

    @pl.when(pl.program_id(0) < first)
    def _():
        put_sum(out_ref, other, dot_rows(low[...], grad[...]))

    @pl.when(pl.program_id(0) >= first)
    def _():
        spots = head_spots(place[4], calls, pieces)
        for index, piece in enumerate(mixed):
            size = piece.shape[1]
            rows = pl.ds(pl.multiple_of(spots[index] * size, size), size)
            value = dot_rows(piece[...], attended[...])
            if more:
                value = value + other[rows, :].astype(jnp.float32)
            out_ref[rows, :] = value.astype(jnp.bfloat16)


def tail_grads(place, who, low_one, grad_qkv, mixed, swapped, attended_low, other, behind):
    total, width = low_one.shape
    rows = attended_low.shape[0]
    block = 256
    first = grad_qkv.shape[1] // 2 // block
    second = width // 2 // block
    out = pl.BlockSpec((width, block), lambda j, s: (0, j))
    more = [] if other is None else [other]
    return pl.pallas_call(
        partial(
            tail_grads_kernel, first, bool(more), len(mixed) + len(swapped), len(mixed)
        ),
        grid_spec=pltpu.PrefetchScalarGridSpec(
            num_scalar_prefetch=1,
            grid=(first + second,),
            in_specs=[
                pl.BlockSpec((total, width), lambda j, s: (0, 0)),
                pl.BlockSpec(
                    (total, block), lambda j, s: (0, s[who] * first + jnp.minimum(j, first - 1))
                ),
                pl.BlockSpec(
                    (rows, block), lambda j, s: (0, s[who] * second + jnp.maximum(j - first, 0))
                ),
            ]
            + [pl.BlockSpec((rows, part.shape[1]), lambda j, s: (0, 0)) for part in mixed]
            + [pl.BlockSpec((rows, part.shape[1]), lambda j, s: (1, 0)) for part in swapped]
            + [out] * len(more)
            + [ANYWHERE] * len(behind),
            out_specs=out,
        ),
        out_shape=jax.ShapeDtypeStruct((width, (first + second) * block), jnp.bfloat16),
        compiler_params=BIG,
        cost_estimate=cost(
            2 * width * block * (total * first + rows * second), 8 * total * width
        ),
        name="tail_grads",
    )(place, low_one, grad_qkv, attended_low, *mixed, *swapped, *more, *behind)


def input_back_kernel(parts, count, own_ref, tokens_ref, ada_ref, base_ref, *refs):
    out_ref = refs[-1]
    grad = own_ref[...].astype(jnp.float32) + current(refs[:parts], count).astype(jnp.float32)
    normed, inverse = standardise(tokens_ref[...].astype(jnp.float32))
    scaled = grad * (1.0 + ada_ref[0:1, :])
    inner = jnp.mean(scaled * normed, axis=-1, keepdims=True)
    shifted = scaled - jnp.mean(scaled, axis=-1, keepdims=True) - normed * inner
    out_ref[...] = base_ref[...] + inverse * shifted


def input_back(own, others, tokens, ada, base):
    rows, width = tokens.shape
    count = 4
    block = pl.BlockSpec((rows // count, width), lambda j: (j, 0))
    _, specs = row_specs(others, count)
    return pl.pallas_call(
        partial(input_back_kernel, len(others), count),
        grid=(count,),
        in_specs=[block, block, pl.BlockSpec((2, width), lambda j: (0, 0)), block] + specs,
        out_specs=block,
        out_shape=jax.ShapeDtypeStruct((rows, width), jnp.float32),
        compiler_params=BIG,
        cost_estimate=cost(20 * rows * width, 14 * rows * width),
        name="input_back",
    )(own, tokens, ada, base, *others)


def exact(left, right):
    return jnp.dot(left, right, precision=lax.Precision.HIGHEST)


def rounded(total, other=None):
    if other is not None:
        total = total + other.astype(jnp.float32)
    return total.astype(jnp.bfloat16)


def tie(*values):
    return lax.optimization_barrier(values)


def cut(value, start, size, axis):
    return lax.dynamic_slice_in_dim(value, start, size, axis, allow_negative_indices=False)


def pick(value, index, axis):
    return lax.dynamic_index_in_dim(
        value, index, axis, keepdims=False, allow_negative_indices=False
    )


def ring_of(items_count):
    chips = items_count // 2
    outer = 4 if chips % 4 == 0 else chips
    inner = chips // outer
    order = [a * inner for a in range(outer)]
    for turn, a in enumerate(reversed(range(outer))):
        beside = list(range(1, inner))
        order += [a * inner + b for b in (beside if turn % 2 == 0 else beside[::-1])]
    return order


class Mover:
    def __init__(self, items_count, seq_count):
        self.items_count = items_count
        self.seq_count = seq_count
        self.pair = seq_count == 2
        self.chips = items_count // 2
        order = ring_of(items_count)
        self.forward = []
        self.backward = []
        chips = self.chips
        table = np.zeros((items_count, 2 * chips + 2), np.int32)
        hops = list(range(chips // 2 + 1)) + [-hop for hop in range(1, (chips + 1) // 2)]
        for spot in range(self.chips):
            for core in range(2):
                here = 2 * order[spot] + core
                next_one = 2 * order[(spot + 1) % self.chips] + core
                self.forward.append((here, next_one))
                self.backward.append((next_one, here))
                for ahead in range(self.chips):
                    table[here, ahead] = order[(spot + ahead) % self.chips]
                table[here, chips] = core
                table[here, chips + 1] = 1 - core
                for spot_of, hop in enumerate(hops):
                    ahead = hop if core == 1 else -hop
                    table[here, chips + 2 + spot_of] = order[(spot + ahead) % chips]
        self.both_ways = [p for p in self.forward if p[0] % 2 == 0]
        self.both_ways += [p for p in self.backward if p[0] % 2 == 1]
        self.item = lax.axis_index("items")
        row = pick(jnp.asarray(table), self.item, 0)
        self.ahead = [row[j] for j in range(self.chips)]
        self.core = row[self.chips]
        self.beside = row[self.chips + 1]
        self.spots = row[self.chips + 2 :]
        self.seq = lax.axis_index("seq")

    def flip(self, value, bit):
        pairs = [(i, i ^ bit) for i in range(self.items_count)]
        return lax.ppermute(value, "items", pairs)

    def across(self, value):
        return lax.ppermute(value, "seq", [(0, 1), (1, 0)])

    def gather_items(self, value, summed, early, late):
        for bit in [1 << k for k in range(self.items_count.bit_length() - 1)]:
            summed = summed + self.flip(summed, bit)
        beside = self.flip(value, 1)
        block = jnp.where(
            self.core == 0,
            jnp.concatenate([value, beside], axis=0),
            jnp.concatenate([beside, value], axis=0),
        )
        direct = [block]
        for hop in range(1, self.chips // 2 + 1):
            moved = lax.ppermute(direct[-1], "items", self.both_ways)
            if hop == min(LATE_HOP, self.chips // 2):
                late, summed, moved, early = tie(late, summed, moved, early)
            direct.append(moved)
        beside = [self.flip(moved, 1) for moved in direct[1 : (self.chips + 1) // 2]]
        return direct + beside, summed, early, late

    def sum_seq(self, value):
        return value + self.across(value) if self.pair else lax.psum(value, "seq")

    def scatter_seq(self, value):
        rows = value.shape[0] // self.seq_count
        if self.pair:
            sent = cut(value, (1 - self.seq) * rows, rows, 0)
            kept = cut(value, self.seq * rows, rows, 0)
            return kept + self.across(sent.astype(jnp.bfloat16)).astype(jnp.float32)
        return lax.psum_scatter(
            value.astype(jnp.bfloat16), "seq", scatter_dimension=0, tiled=True
        ).astype(jnp.float32)

    def join_cores(self, value):
        parts = value.reshape(2, -1, value.shape[1])
        kept = pick(parts, self.core, 0)
        other = self.flip(pick(parts, self.beside, 0), 1)
        return jnp.where(self.core == 0, kept, other), jnp.where(self.core == 0, other, kept)

    def join_columns(self, value):
        rows = value.shape[0] // self.seq_count
        if self.pair:
            kept = cut(value, self.seq * rows, rows, 0)
            other = self.across(cut(value, (1 - self.seq) * rows, rows, 0))
            return jnp.where(self.seq == 0, kept, other), jnp.where(self.seq == 0, other, kept)
        moved = lax.all_to_all(value, "seq", split_axis=0, concat_axis=0, tiled=True)
        return tuple(moved[j * rows : (j + 1) * rows] for j in range(self.seq_count))


class RingSum:
    def __init__(self, mover, make, behind, ready=()):
        self.mover = mover
        self.chips = mover.chips
        self.make = make
        self.flows = None
        sent, self.ready = tie(make(False, None, behind), list(ready))
        self.sent = sent
        self.arriving = [mover.flip(sent, 1)]

    def block(self, ahead):
        return pick(self.both, self.mover.ahead[ahead % self.chips], 0)

    def add_own(self, behind):
        self.both = self.make(True, self.arriving[0], behind)
        self.whole = self.both
        self.both = self.both.reshape(self.chips, -1, self.both.shape[1])
        self.arrived = []
        flows = [
            (self.mover.forward, 1, self.chips // 2),
            (self.mover.backward, -1, (self.chips - 1) // 2),
        ]
        self.send([(flow, self.block(flow[1] * flow[2])) for flow in flows if flow[2]])

    def send(self, flows):
        self.arriving = [lax.ppermute(value, "items", flow[0]) for flow, value in flows]
        self.flows = [(pairs, sign, left - 1) for (pairs, sign, left), _ in flows]

    def advance(self, anchor=None):
        flows = []
        if anchor is not None:
            self.arriving, anchor = tie(self.arriving, anchor)
        for flow, value in zip(self.flows, self.arriving):
            if flow[2]:
                flows.append((flow, self.block(flow[1] * flow[2]) + value))
            else:
                self.arrived.append(value)
        self.send(flows)
        return anchor

    def finish(self, anchor=None):
        while self.arriving:
            self.advance()
        if anchor is not None:
            self.arrived, anchor = tie(self.arrived, anchor)
        result = self.block(0).astype(jnp.float32)
        for value in self.arrived:
            result = result + value.astype(jnp.float32)
        return result if anchor is None else (result, anchor)


def in_rows(value):
    return with_layout_constraint(value, Layout((0, 1)))


def halves(value, core):
    half = value.shape[1] // 2
    return cut(value, core * half, half, 1)


def parted(value, at):
    return (None, None) if value is None else (value[:, :at], value[:, at:])


def shards(
    tokens,
    cotangent,
    prompt_len,
    section_ids,
    section_table,
    w_query,
    w_key,
    w_value,
    w_out,
    w_up,
    w_down,
    w_ada_one,
    w_ada_two,
):
    items_count = lax.axis_size("items")
    seq_count = lax.axis_size("seq")
    mover = Mover(items_count, seq_count)
    chips = mover.chips
    batch, rows, width = tokens.shape
    total_rows = rows * seq_count
    hidden = w_up.shape[1] // seq_count
    held = width // seq_count
    pairs = held // LANES
    piece = w_query.shape[0]
    units = w_down.shape[0] // seq_count
    tokens = tokens.reshape(rows, width)
    grad_low = cotangent.reshape(rows, width)

    def quarters(one, two):
        return jnp.stack([one[:, :width], one[:, width:], two[:, :width], two[:, width:]])

    up_shard = w_up.reshape(piece, chips, 2, seq_count, units).transpose(3, 0, 2, 1, 4)
    up_shard = pick(up_shard, mover.seq, 0).reshape(piece, hidden)
    down_shard = cut(w_down, mover.seq * units, units, 0)
    merged = hidden % width == 0 and units % piece == 0
    late = down_shard
    if merged:
        folds = hidden // width
        down_parts = units // piece
        up_rows = [up_shard[:, j * width : (j + 1) * width] for j in range(folds)]
        late = jnp.concatenate([down_shard] + up_rows + [w_out], axis=0)

    table_part = cut(section_table, mover.item * piece, piece, 1)
    ada_part = jnp.dot(
        table_part,
        jnp.concatenate([w_ada_one, w_ada_two], axis=1),
        preferred_element_type=jnp.float32,
    )
    ada_part = quarters(ada_part[:, : 2 * width], ada_part[:, 2 * width :])
    prompt_at = mover.seq if mover.pair else jnp.zeros((), jnp.int32)
    place = jnp.stack([prompt_at, prompt_len[0], mover.core, mover.beside, mover.seq])
    seq_place = jnp.reshape(mover.seq, (1,)).astype(jnp.int32)
    mine = pack_columns(w_query, w_key, w_value, held, seq_place)
    early = [mover.across(tokens)] if mover.pair else []
    blocks, ada_sum, early, late = mover.gather_items(
        mine, ada_part, early, late
    )

    def gathered(value):
        return lax.all_gather(value, "items", axis=0, tiled=False)

    if merged:
        rest = gathered(late)
        rest = rest.reshape(items_count, down_parts + folds + 1, piece, width)
        by_core = rest.reshape((chips, 2) + rest.shape[1:])
        weights = Weights(rest, down_parts, by_core, down_parts, hidden, width)
        out_w, out_part = rest, down_parts + folds
    else:
        by_core = gathered(late).reshape(chips, 2, 1, units, width)
        weights = Weights(gathered(up_shard)[:, None], 0, by_core, 1, hidden, width)
        out_w, out_part = gathered(w_out)[:, None], 0

    choose = (section_ids[0] == jnp.arange(section_table.shape[0])).astype(jnp.float32)
    ada = jnp.sum(choose[None, :, None] * ada_sum, axis=1)
    ada_one = ada[:2]
    ada_two = ada[2:]

    if mover.pair:
        tokens_other, grad_sent = tie(early[0], grad_low)
        grad_other = mover.across(grad_sent)
        frames = [tokens, tokens_other]
        grads = [grad_low, grad_other]
        calls = 2 if pairs % 2 == 0 else 1
    else:
        frames = [lax.all_gather(tokens, "seq", axis=0, tiled=True)]
        grads = [lax.all_gather(grad_low, "seq", axis=0, tiled=True)]
        calls = 1
    low_one, qkv, qkv_w = first_layer(frames, ada_one, blocks, mover.spots)
    per_call = pairs // calls
    mixed_heads = []
    lse = []
    for call in range(calls):
        behind = grads[1:] + mixed_heads
        out = attend(qkv, place, call * per_call, per_call, behind)
        mixed_heads.append(out[0])
        lse.append(out[1])
    if mover.pair:
        mixed_far = []
        for call in range(calls):
            sent = mixed_heads[call]
            if mixed_far:
                sent, mixed_far[-1] = tie(sent, mixed_far[-1])
            mixed_far.append(mover.across(sent))
        attended, low_two = second_layer(
            mixed_heads, mixed_far, frames[::-1], out_w, out_part, ada_two, place
        )
        lows = low_two
        active, upward = hidden_layer(lows, grads, weights)
        first_half, last_half = up_back(upward, weights, rows, 1, jnp.bfloat16, (), 2)
        start = [first_half]
        ready = [mover.across(first_half), last_half]
    else:
        mixed = lax.all_to_all(mixed_heads[0], "seq", split_axis=0, concat_axis=1, tiled=True)
        attended, low_two = second_layer(
            [mixed], [], [tokens], out_w, out_part, ada_two, place
        )
        lows = lax.all_gather(low_two, "seq", axis=0, tiled=True)
        active, upward = hidden_layer(lows, grads, weights)
        start = []
        ready = []

    down_columns = hidden // 2

    def hidden_parts(own, other, behind):
        who = 2 if own else 3
        if down_columns == width:
            return hidden_grads(place, who, active, upward, grads, lows, other, behind)
        core = mover.core if own else mover.beside
        first, second = parted(other, down_columns)
        down = dot_rows(halves(active, core), grads[0]).reshape(width, down_columns)
        up = dot_rows(lows, halves(upward, core))
        return in_rows(jnp.concatenate([rounded(down, first), rounded(up, second)], axis=1))

    ring = RingSum(mover, hidden_parts, start, ready)
    if mover.pair:
        own = up_back(upward, weights, rows, 0, jnp.float32, [ring.sent])
        from_other = [ring.ready[0], mover.across(ring.ready[1])]
        sizes = [held, held]
    else:
        own = lax.psum_scatter(
            up_back(upward, weights, total_rows, 0, jnp.bfloat16),
            "seq",
            scatter_dimension=0,
            tiled=True,
        ).astype(jnp.float32)
        from_other = [jnp.zeros((rows, width), jnp.bfloat16)]
        sizes = [width]
    ring.add_own([own])
    grad_attended, attended_low, ada_two_rows, *grad_mixed = middle_back(
        own,
        from_other,
        attended,
        grad_low,
        ada_two,
        out_w,
        out_part,
        place,
        sizes,
        [ring.whole],
    )
    if mover.pair:
        out_other = down_part(active, weights, rows, 1, jnp.bfloat16, grad_mixed[:1])
        grad_heads = [grad_mixed[1], mover.across(grad_mixed[0])]
        out_other = ring.advance(out_other)
        out_own = down_part(active, weights, rows, 0, jnp.float32, [out_other])
        filler = [out_own]
        out_other = mover.across(out_other)
    else:
        grad_heads = [
            lax.all_to_all(grad_mixed[0], "seq", split_axis=1, concat_axis=0, tiled=True)
        ]
        filler = []

    split = pairs // 2 if pairs % 2 == 0 else 0

    def tail_parts(own, other, behind):
        if mover.pair:
            return tail_grads(
                place,
                2 if own else 3,
                low_one,
                grad_qkv,
                mixed_heads,
                mixed_far,
                attended_low,
                other,
                behind,
            )
        core = mover.core if own else mover.beside
        first, second = parted(other, grad_qkv.shape[1] // 2)
        qkv_part = rounded(dot_rows(low_one, halves(grad_qkv, core)), first)
        out_part = rounded(dot_rows(mixed, halves(attended_low, core)), second)
        return in_rows(jnp.concatenate([qkv_part, out_part], axis=1))

    tail = None
    grad_qkv = None
    for turn in range(pairs):
        behind = filler
        filler = []
        grad_qkv = attend_back(
            place, turn, pairs, qkv, mixed_heads, grad_heads, lse, grad_qkv, behind
        )
        grad_qkv = ring.advance(grad_qkv)
        if turn + 1 == split:
            tail = RingSum(mover, tail_parts, [])
            filler = [tail.sent]
    if tail is None:
        tail = RingSum(mover, tail_parts, [])
    tail.add_own([])
    if mover.pair:
        near_half, last_half, far_rows = first_back(
            grad_qkv, qkv_w, frames[1], 1, [tail.whole, out_other], 2
        )
        near_half = mover.across(near_half)
        last_half = tail.advance(last_half)
        hidden_total, last_half = ring.finish(last_half)
        own_first, own_rows = first_back(grad_qkv, qkv_w, frames[0], 0, [last_half])
        own_rows, near_half, last_half = tail.advance([own_rows, near_half, last_half])
        far_parts = [near_half, mover.across(last_half)]
        ada_rows = jnp.concatenate([own_rows + far_rows, ada_two_rows])
        ada_rows = ada_rows + mover.across(ada_rows)
        layer_sum = out_own + out_other.astype(jnp.float32)
    else:
        grad_first, ada_one_rows = first_back(grad_qkv, qkv_w, frames[0], 0, [tail.whole])
        ada_rows = lax.psum(jnp.concatenate([ada_one_rows, ada_two_rows]), "seq")
        own_first = lax.psum_scatter(grad_first, "seq", scatter_dimension=0, tiled=True)
        far_parts = [jnp.zeros((rows, width), jnp.bfloat16)]
        hidden_total = ring.finish()
        layer_sum = lax.psum_scatter(
            down_part(active, weights, total_rows, 0, jnp.bfloat16),
            "seq",
            scatter_dimension=0,
            tiled=True,
        ).astype(jnp.float32)
    layer_out = (attended + layer_sum).astype(jnp.bfloat16)
    sums = choose[None, :, None] * ada_rows[:, None, :]
    for bit in [1 << k for k in range(items_count.bit_length() - 1)]:
        sums = sums + mover.flip(sums, bit)
        if bit == 2:
            sums, far_parts = tail.advance([sums, far_parts])
    input_grad = input_back(own_first, far_parts, tokens, ada_one, grad_attended)
    out_piece = piece // seq_count
    first_row = mover.item * piece + mover.seq * out_piece
    table_rows = cut(section_table, first_row, out_piece, 1).astype(jnp.float32)
    ada_grads = jnp.einsum("sr,ksd->krd", table_rows, sums, precision=lax.Precision.HIGHEST)
    grad_ada_one = jnp.concatenate([ada_grads[0], ada_grads[1]], axis=1)
    grad_ada_two = jnp.concatenate([ada_grads[2], ada_grads[3]], axis=1)
    own_ada = quarters(
        *(cut(w, mover.seq * out_piece, out_piece, 0) for w in (w_ada_one, w_ada_two))
    ).astype(jnp.float32)
    grad_table = jnp.einsum("ksd,krd->sr", sums, own_ada, precision=lax.Precision.HIGHEST)

    grad_down = hidden_total[:, :down_columns].reshape(units, width)
    up_sides = mover.join_columns(
        jnp.concatenate(mover.join_cores(hidden_total[:, down_columns:]), axis=1)
    )
    grad_up = jnp.stack(
        [side.reshape(out_piece, 2, chips, units) for side in up_sides], axis=1
    )
    grad_up = grad_up.transpose(0, 3, 2, 1, 4).reshape(out_piece, hidden * seq_count)
    tail_total = tail.finish()
    cores = jnp.concatenate(mover.join_cores(tail_total), axis=1)
    half_qkv = 3 * held // 2
    half_all = cores.shape[1] // 2
    qkv_total = jnp.concatenate(
        [cores[:, :half_qkv], cores[:, half_all : half_all + half_qkv]], axis=1
    )
    out_total = jnp.concatenate([cores[:, half_qkv:half_all], cores[:, half_all + half_qkv :]], axis=1)
    sides = mover.join_columns(qkv_total)
    grad_out = mover.scatter_seq(out_total)
    grad_query, grad_key, grad_value = (
        jnp.concatenate(
            [
                side[:, (3 * p + j) * LANES : (3 * p + j + 1) * LANES]
                for side in sides
                for p in range(pairs)
            ],
            axis=1,
        )
        for j in range(3)
    )
    return (
        layer_out.reshape(batch, rows, width),
        input_grad.reshape(batch, rows, width),
        grad_query,
        grad_key,
        grad_value,
        grad_out,
        grad_up,
        grad_down,
        grad_ada_one,
        grad_ada_two,
        grad_table,
    )


def solution(mesh):
    return jax.shard_map(
        shards,
        mesh=mesh,
        in_specs=(
            P("items", "seq", None),
            P("items", "seq", None),
            P("items"),
            P("items"),
            P(),
            P("items", None),
            P("items", None),
            P("items", None),
            P("items", None),
            P("items", None),
            P("items", None),
            P("items", None),
            P("items", None),
        ),
        out_specs=(
            P("items", "seq", None),
            P("items", "seq", None),
            P(("items", "seq"), None),
            P(("items", "seq"), None),
            P(("items", "seq"), None),
            P(("items", "seq"), None),
            P(("items", "seq"), None),
            P(("items", "seq"), None),
            P(("items", "seq"), None),
            P(("items", "seq"), None),
            P(None, ("items", "seq")),
        ),
        check_vma=False,
    )
```

```python
from functools import partial
import math

import jax
import jax.numpy as jnp
import numpy as np
from jax import lax
from jax.experimental.layout import Layout, with_layout_constraint
from jax.experimental import pallas as pl
from jax.experimental.pallas import tpu as pltpu
from jax.sharding import PartitionSpec as P

HEAD_DIM = 64
SCALE = 0.125
MASKED = -1e30
COVER = 0.5
TILE = 128
LANES = 128

def row_ids(shape):
    return lax.broadcasted_iota(jnp.int32, shape, 0)
def lane_ids(shape):
    return lax.broadcasted_iota(jnp.int32, shape, 1)
def matmul(left, right):
    return jnp.dot(left, right, preferred_element_type=jnp.float32)
def twin_lanes(flipped):
    top = row_ids(flipped.shape) < HEAD_DIM
    return jnp.concatenate([jnp.where(top, flipped, 0.0), jnp.where(top, 0.0, flipped)], axis=1)
def twin_rows(block):
    first = lane_ids(block.shape) < HEAD_DIM
    return jnp.concatenate([jnp.where(first, block, 0.0), jnp.where(first, 0.0, block)], axis=0)
def untwin(wide):
    top = row_ids((LANES, LANES)) < HEAD_DIM
    return jnp.where(top, wide[:, :LANES], wide[:, LANES:]).T

def split3(value):
    high = value.astype(jnp.bfloat16).astype(jnp.float32)
    rest = value - high
    mid = rest.astype(jnp.bfloat16).astype(jnp.float32)
    return high, mid, rest - mid

def attend_kernel(place, q_ref, k_ref, v_ref, *refs):
    o_ref, lse_ref, keys_wide, values_t = refs[-4:]
    half = q_ref.shape[0] // 2
    prompt = pl.multiple_of(place[0] * half, TILE)
    target = pl.multiple_of((1 - place[0]) * half, TILE)
    length = place[1]
    shape = (half, LANES)
    keys_wide[:half, :LANES] = k_ref[pl.ds(prompt, half), :]
    keys_wide[half:, :LANES] = k_ref[pl.ds(target, half), :]
    hidden = (lane_ids(shape) == 0) & (row_ids(shape) >= length)
    keys_wide[:half, LANES:] = jnp.where(hidden, MASKED, 0.0).astype(jnp.bfloat16)
    keys_wide[half:, LANES:] = jnp.zeros(shape, jnp.bfloat16)
    for piece in range(half // TILE):
        rows = slice(piece * TILE, (piece + 1) * TILE)
        values_t[:, rows] = v_ref[pl.ds(prompt + piece * TILE, TILE), :].astype(jnp.float32).T.astype(jnp.bfloat16)
        rows = slice(half + piece * TILE, half + (piece + 1) * TILE)
        values_t[:, rows] = v_ref[pl.ds(target + piece * TILE, TILE), :].astype(jnp.float32).T.astype(jnp.bfloat16)
    below = jnp.where(row_ids((LANES, 2 * TILE)) == 0, 1.0, 0.0)

    def score(start, seen):
        q_flip = (q_ref[pl.ds(start, TILE), :].astype(jnp.float32) * SCALE).T
        q_wide = jnp.concatenate([twin_lanes(q_flip), below], axis=0).astype(jnp.bfloat16)
        return matmul(keys_wide[:seen, :], q_wide)

    def tile(scores, start, seen, slot):
        peak = jnp.max(scores, axis=0, keepdims=True)
        expo = jnp.exp(scores - peak)
        total = jnp.sum(expo, axis=0, keepdims=True)
        out = matmul(values_t[:, :seen], expo.astype(jnp.bfloat16)) / total
        o_ref[pl.ds(start, TILE), :] = untwin(out).astype(jnp.bfloat16)
        lse_ref[0, pl.ds(slot, 1), :] = peak + jnp.log(total)

    tiles = half // TILE

    @pl.loop(0, tiles)
    def _(index):
        at_prompt = pl.multiple_of(prompt + index * TILE, TILE)
        at_target = pl.multiple_of(target + index * TILE, TILE)
        first = score(at_prompt, half)
        second = score(at_target, 2 * half)
        tile(first, at_prompt, half, index)
        tile(second, at_target, 2 * half, tiles + index)


def attend(qkv, place, first, pairs, behind):
    rows = qkv.shape[0]
    width = pairs * LANES
    part = lambda shift: pl.BlockSpec((rows, LANES), lambda p, s, shift=shift: (0, 3 * (first + p) + shift))
    seen = rows * rows * 3 // 4
    return pl.pallas_call(
        attend_kernel,
        grid_spec=pltpu.PrefetchScalarGridSpec(
            num_scalar_prefetch=1, grid=(pairs,),
            in_specs=[part(0), part(1), part(2)] + [pl.BlockSpec(memory_space=pl.ANY)] * len(behind),
            out_specs=[pl.BlockSpec((rows, LANES), lambda p, s: (0, p)), pl.BlockSpec((1, rows // TILE, 2 * TILE), lambda p, s: (p, 0, 0))],
            scratch_shapes=[pltpu.VMEM((rows, 2 * LANES), jnp.bfloat16), pltpu.VMEM((LANES, rows), jnp.bfloat16)],
        ),
        out_shape=[jax.ShapeDtypeStruct((rows, width), jnp.bfloat16),
                   jax.ShapeDtypeStruct((pairs, rows // TILE, 2 * TILE), jnp.float32)],
        compiler_params=pltpu.CompilerParams(vmem_limit_bytes=60 << 20),
        cost_estimate=pl.CostEstimate(flops=int(COVER * pairs * 2 * seen * 4 * HEAD_DIM * 4), transcendentals=0, bytes_accessed=rows * width * 8),
        name="attend",
    )(place, qkv, qkv, qkv, *behind)


def attend_back_kernel(parts, calls, per, at, place, q_ref, k_ref, v_ref, *refs):
    o_refs, lse_refs, g_refs = refs[:calls], refs[calls:2 * calls], refs[2 * calls:2 * calls + parts]
    out_ref, keys_wide, values_wide, keys_t, dq, dk, dv = refs[-7:]
    half = q_ref.shape[0] // 2
    step = pl.program_id(0)
    prompt = pl.multiple_of(place[0] * half, TILE)
    target = pl.multiple_of((1 - place[0]) * half, TILE)
    length = place[1]

    @pl.when(step == 0)
    def _():
        shape = (half, LANES)
        lanes = lane_ids(shape)
        ones = jnp.where((lanes >= 1) & (lanes <= 3), 1.0, 0.0)
        hidden = (lanes == 0) & (row_ids(shape) >= length)
        keys_wide[:half, :LANES] = k_ref[pl.ds(prompt, half), :]
        keys_wide[half:, :LANES] = k_ref[pl.ds(target, half), :]
        keys_wide[:half, LANES:] = jnp.where(hidden, MASKED, ones).astype(jnp.bfloat16)
        keys_wide[half:, LANES:] = ones.astype(jnp.bfloat16)
        values_wide[:half, :LANES] = v_ref[pl.ds(prompt, half), :]
        values_wide[half:, :LANES] = v_ref[pl.ds(target, half), :]
        values_wide[:half, LANES:] = ones.astype(jnp.bfloat16)
        values_wide[half:, LANES:] = ones.astype(jnp.bfloat16)
        for piece in range(2 * half // TILE):
            rows = slice(piece * TILE, (piece + 1) * TILE)
            keys_t[:, rows] = keys_wide[rows, :LANES].astype(jnp.float32).T.astype(jnp.bfloat16)
        dk[...] = jnp.zeros_like(dk)
        dv[...] = jnp.zeros_like(dv)
        wide = (LANES, 2 * TILE)
        ids = row_ids(wide)

        def lanes_of(value):
            high, mid, rest = split3(value)
            return jnp.where(ids == 1, -high, jnp.where(ids == 2, -mid, jnp.where(ids == 3, -rest, 0.0)))

        def g_tile(start):
            if parts == 1:
                return g_refs[0][pl.ds(start, TILE), :]
            inside = pl.multiple_of(jnp.where(start < half, start, start - half), TILE)
            first = g_refs[0][pl.ds(inside, TILE), :]
            return jnp.where(start < half, first, g_refs[1][pl.ds(inside, TILE), :])

        def of_call(values):
            value = values[0]
            for call, later in enumerate(values[1:], 1):
                value = jnp.where(at(place) < call * per, value, later)
            return value

        def tile(start, seen, slot):
            spot = pl.ds(start, TILE)
            q_here = q_ref[spot, :].astype(jnp.float32) * SCALE
            g_here = g_tile(start).astype(jnp.float32)
            g_flip = g_here.T
            o_here = of_call([ref[spot, :].astype(jnp.float32) for ref in o_refs])
            product = g_flip * o_here.T
            inner = jnp.concatenate(
                [jnp.sum(product[:HEAD_DIM], axis=0, keepdims=True), jnp.sum(product[HEAD_DIM:], axis=0, keepdims=True)], axis=1)
            lse = of_call([ref[0, pl.ds(slot, 1), :] for ref in lse_refs])
            below = jnp.where(ids == 0, 1.0, lanes_of(lse))
            q_wide = jnp.concatenate([twin_lanes(q_here.T), below], axis=0).astype(jnp.bfloat16)
            g_wide = jnp.concatenate([twin_lanes(g_flip), lanes_of(inner)], axis=0).astype(jnp.bfloat16)
            probs = jnp.exp(matmul(keys_wide[:seen, :], q_wide))
            grads = matmul(values_wide[:seen, :], g_wide)
            scores = (probs * grads).astype(jnp.bfloat16)
            dk[:seen, :] += matmul(scores, twin_rows(q_here).astype(jnp.bfloat16))
            dv[:seen, :] += matmul(probs.astype(jnp.bfloat16), twin_rows(g_here).astype(jnp.bfloat16))
            dq[spot, :] = (untwin(matmul(keys_t[:, :seen], scores)) * SCALE).astype(jnp.bfloat16)

        tiles = half // TILE

        @pl.loop(0, tiles)
        def _(index):
            tile(pl.multiple_of(prompt + index * TILE, TILE), half, index)
            tile(pl.multiple_of(target + index * TILE, TILE), 2 * half, tiles + index)

        out_ref[...] = dq[...]

    for which, held in ((1, dk), (2, dv)):
        @pl.when(step == which)
        def _(held=held):
            out_ref[pl.ds(prompt, half), :] = held[:half, :].astype(jnp.bfloat16)
            out_ref[pl.ds(target, half), :] = held[half:, :].astype(jnp.bfloat16)


def attend_back(place, turn, pairs, qkv, mixed, grads, lse, held, behind):
    rows = qkv.shape[0]
    part = lambda shift: pl.BlockSpec((rows, LANES), lambda j, s, shift=shift: (0, 3 * at(s) + shift))
    calls = len(mixed)
    per = pairs // calls
    split = pairs // 2 if pairs % 2 == 0 else 0
    at = lambda s: (s[3] * split + turn) & (pairs - 1)
    parts = len(grads)
    block = pl.BlockSpec((rows, LANES), lambda j, s: (0, at(s) & (per - 1)))
    lse_block = pl.BlockSpec((1, rows // TILE, 2 * TILE), lambda j, s: (at(s) & (per - 1), 0, 0))
    grad_blocks = [pl.BlockSpec((grad.shape[0], LANES), lambda j, s: (0, at(s))) for grad in grads]
    seen = rows * rows * 3 // 4
    more = [] if held is None else [held]
    return pl.pallas_call(
        partial(attend_back_kernel, parts, calls, per, at),
        grid_spec=pltpu.PrefetchScalarGridSpec(
            num_scalar_prefetch=1, grid=(3,),
            in_specs=[part(0), part(1), part(2)] + [block] * calls + [lse_block] * calls + grad_blocks + [pl.BlockSpec(memory_space=pl.ANY)] * (len(more) + len(behind)),
            out_specs=pl.BlockSpec((rows, LANES), lambda j, s: (0, 3 * at(s) + j)),
            scratch_shapes=[pltpu.VMEM((rows, 2 * LANES), jnp.bfloat16), pltpu.VMEM((rows, 2 * LANES), jnp.bfloat16), pltpu.VMEM((LANES, rows), jnp.bfloat16),
                pltpu.VMEM((rows, LANES), jnp.bfloat16), pltpu.VMEM((rows, LANES), jnp.float32), pltpu.VMEM((rows, LANES), jnp.float32)],
        ),
        out_shape=jax.ShapeDtypeStruct(qkv.shape, jnp.bfloat16),
        input_output_aliases={4 + 2 * calls + parts: 0} if more else {},
        compiler_params=pltpu.CompilerParams(vmem_limit_bytes=60 << 20),
        cost_estimate=pl.CostEstimate(flops=int(COVER * 2 * seen * 10 * HEAD_DIM * 4), transcendentals=0, bytes_accessed=rows * LANES * 20),
        name="attend_back",
    )(place, qkv, qkv, qkv, *mixed, *lse, *grads, *more, *behind)


EPSILON = 1e-05
ROOT_HALF = math.sqrt(0.5)
DENSITY = 1.0 / math.sqrt(2.0 * math.pi)
LATE_HOP = 2
BIG = pltpu.CompilerParams(vmem_limit_bytes=60 << 20)
ANYWHERE = pl.BlockSpec(memory_space=pl.ANY)


def cost(flops, moved, special=0):
    return pl.CostEstimate(
        flops=int(flops * COVER), bytes_accessed=int(moved * COVER), transcendentals=special
    )


def matmul_last(left, right):
    return lax.dot_general(
        left, right, (((1,), (1,)), ((), ())), preferred_element_type=jnp.float32
    )


def dot_rows(left, right):
    return lax.dot_general(
        left, right, (((0,), (0,)), ((), ())), preferred_element_type=jnp.float32
    )


def standardise(values):
    centred = values - jnp.mean(values, axis=-1, keepdims=True)
    spread = jnp.mean(centred * centred, axis=-1, keepdims=True)
    inverse = lax.rsqrt(spread + EPSILON)
    return centred * inverse, inverse


def add_rows(ref, scale, shift):
    step = pl.program_id(0)

    @pl.when(step == 0)
    def _():
        ref[0:1, :] = scale
        ref[1:2, :] = shift

    @pl.when(step > 0)
    def _():
        ref[0:1, :] += scale
        ref[1:2, :] += shift


def row_specs(parts, count):
    rows = sum(part.shape[0] for part in parts) // count
    specs = []
    first = 0
    for part in parts:
        steps = part.shape[0] // rows
        specs.append(
            pl.BlockSpec(
                (rows, part.shape[1]),
                lambda j, *s, first=first, steps=steps: (jnp.clip(j - first, 0, steps - 1), 0),
            )
        )
        first += steps
    return rows, specs


def current(refs, count):
    value = refs[0][...]
    for index, ref in enumerate(refs[1:], 1):
        value = jnp.where(pl.program_id(0) < index * count // len(refs), value, ref[...])
    return value


def pack_kernel(place, query_ref, key_ref, value_ref, out_ref):
    for pair in range(query_ref.shape[1] // LANES):
        for which, ref in enumerate((query_ref, key_ref, value_ref)):
            start = (3 * pair + which) * LANES
            out_ref[:, start : start + LANES] = ref[:, pair * LANES : (pair + 1) * LANES]


def pack_columns(query, key, value, held, place):
    rows = query.shape[0]
    return pl.pallas_call(
        pack_kernel,
        grid_spec=pltpu.PrefetchScalarGridSpec(
            num_scalar_prefetch=1,
            grid=(1,),
            in_specs=[pl.BlockSpec((rows, held), lambda j, s: (0, s[0]))] * 3,
            out_specs=pl.BlockSpec((rows, 3 * held), lambda j, s: (0, 0)),
        ),
        out_shape=jax.ShapeDtypeStruct((rows, 3 * held), query.dtype),
        cost_estimate=cost(0, 12 * rows * held),
        name="pack_columns",
    )(place, query, key, value)


def first_kernel(parts, pieces, count, spots, *refs):
    frames = refs[:parts]
    ada = refs[parts]
    blocks = refs[parts + 1 : parts + 1 + pieces]
    low_ref, qkv_ref, weight_ref, sems = refs[-4:]
    rows = blocks[0].shape[0]

    @pl.when(pl.program_id(0) == 0)
    def _():
        copies = []
        for index, block in enumerate(blocks):
            start = pl.multiple_of(spots[index] * rows, rows)
            copy = pltpu.make_async_copy(
                block, weight_ref.at[pl.ds(start, rows), :], sems.at[index]
            )
            copy.start()
            copies.append(copy)
        for copy in copies:
            copy.wait()

    normed, _ = standardise(current(frames, count).astype(jnp.float32))
    low = ((1.0 + ada[0:1, :]) * normed + ada[1:2, :]).astype(jnp.bfloat16)
    low_ref[...] = low
    qkv_ref[...] = matmul(low, weight_ref[...]).astype(jnp.bfloat16)


def first_layer(frames, ada, blocks, spots):
    count = 4
    rows, specs = row_specs(frames, count)
    width = frames[0].shape[1]
    columns = blocks[0].shape[1]
    out = lambda size: pl.BlockSpec((rows, size), lambda j, s: (j, 0))
    shape = lambda *size: jax.ShapeDtypeStruct(size, jnp.bfloat16)
    return pl.pallas_call(
        partial(first_kernel, len(frames), len(blocks), count),
        grid_spec=pltpu.PrefetchScalarGridSpec(
            num_scalar_prefetch=1,
            grid=(count,),
            in_specs=specs
            + [pl.BlockSpec((2, width), lambda j, s: (0, 0))]
            + [ANYWHERE] * len(blocks),
            out_specs=[
                out(width),
                out(columns),
                pl.BlockSpec((width, columns), lambda j, s: (0, 0)),
            ],
            scratch_shapes=[pltpu.SemaphoreType.DMA((len(blocks),))],
        ),
        out_shape=[
            shape(rows * count, width),
            shape(rows * count, columns),
            shape(width, columns),
        ],
        compiler_params=BIG,
        cost_estimate=cost(
            2 * rows * count * width * columns, 4 * width * columns + 8 * rows * count * width
        ),
        name="first_layer",
    )(spots, *frames, ada, *blocks)


def second_kernel(pieces, calls, parts, count, place, *refs):
    mixed = refs[:pieces]
    tokens = refs[pieces : pieces + parts]
    out_w, ada = refs[pieces + parts : pieces + parts + 2]
    attended_ref, low_ref = refs[-2:]
    weights = out_w.reshape(out_w.shape[0] * out_w.shape[2], out_w.shape[3])
    spots = head_spots(place[4], calls, pieces)
    attended = current(tokens, count).astype(jnp.float32)
    for index, piece in enumerate(mixed):
        size = piece.shape[1]
        start = pl.multiple_of(spots[index] * size, size)
        attended = attended + matmul(piece[...], weights[pl.ds(start, size), :])
    attended_ref[...] = attended
    normed, _ = standardise(attended)
    low_ref[...] = ((1.0 + ada[0:1, :]) * normed + ada[1:2, :]).astype(jnp.bfloat16)


def second_layer(mixed, swapped, tokens, out_w, out_part, ada, spots):
    rows, width = tokens[-1].shape
    parts = len(tokens)
    count = 2 * parts
    size, token_specs = row_specs(tokens, count)
    later = count - 2
    block = lambda columns, order: pl.BlockSpec((size, columns), lambda j, s: (order(j), 0))
    first = lambda j: (j + later) % count
    items, _, piece, _ = out_w.shape
    return pl.pallas_call(
        partial(second_kernel, len(mixed) + len(swapped), len(mixed), parts, count),
        grid_spec=pltpu.PrefetchScalarGridSpec(
            num_scalar_prefetch=1,
            grid=(count,),
            in_specs=[block(part.shape[1], first) for part in mixed]
            + [block(part.shape[1], lambda j: j) for part in swapped]
            + token_specs
            + [
                pl.BlockSpec((items, 1, piece, width), lambda j, s: (0, out_part, 0, 0)),
                pl.BlockSpec((2, width), lambda j, s: (0, 0)),
            ],
            out_specs=[block(width, lambda j: jnp.maximum(j - later, 0)), block(width, first)],
        ),
        out_shape=[
            jax.ShapeDtypeStruct((rows, width), jnp.float32),
            jax.ShapeDtypeStruct((rows * parts, width), jnp.bfloat16),
        ],
        compiler_params=BIG,
        cost_estimate=cost(
            2 * rows * parts * width * width, 2 * width * width + 10 * rows * parts * width
        ),
        name="second_layer",
    )(spots, *mixed, *swapped, *tokens, out_w, ada)


def head_spots(seq, calls, pieces):
    if pieces == 1:
        return [0]
    own = [seq * calls + call for call in range(calls)]
    return own + [(1 - seq) * calls + call for call in range(pieces - calls)]


class Weights:
    def __init__(self, up, up_first, down, down_parts, hidden, width):
        self.up = up
        self.down = down
        self.width = width
        self.hidden = hidden
        fold = up.shape[3]
        self.block = min(512, fold, hidden // 2)
        per_chip = down_parts * down.shape[3]
        per_fold = fold // self.block
        chips, _, _, piece, _ = down.shape
        self.steps = hidden // self.block
        per_core = self.steps // 2
        block = self.block
        self.up_spec = pl.BlockSpec(
            (up.shape[0], 1, up.shape[2], block),
            lambda j: (0, up_first + j // per_fold, 0, j % per_fold),
        )
        self.down_spec = pl.BlockSpec(
            (block // per_chip, 1, down_parts, piece, width),
            lambda j: (j % per_core, j // per_core, 0, 0, 0),
        )
        self.per_chip = per_chip
        self.bytes = 2 * hidden * width


def hidden_kernel(per_chip, parts, x_ref, up_ref, down_ref, *refs):
    g_refs = refs[:parts]
    active_ref, grad_ref = refs[-2:]
    columns = min(256, active_ref.shape[1])
    size = x_ref.shape[0] // parts
    for start in range(0, active_ref.shape[1], columns):
        spot = slice(start, start + columns)
        up = up_ref[:, :, :, spot].reshape(-1, columns)
        chips = slice(start // per_chip, (start + columns) // per_chip)
        down = down_ref[chips].reshape(columns, -1)
        for index, g_ref in enumerate(g_refs):
            rows = slice(index * size, (index + 1) * size)
            upward = matmul(x_ref[rows, :], up)
            grad_active = matmul_last(g_ref[...], down)
            below = 0.5 * (1.0 + lax.erf(upward * ROOT_HALF))
            active_ref[rows, spot] = (upward * below).astype(jnp.bfloat16)
            slope = below + upward * (DENSITY * jnp.exp(-0.5 * upward * upward))
            grad_ref[rows, spot] = (grad_active * slope).astype(jnp.bfloat16)


def hidden_layer(x, grads, weights):
    rows, width = x.shape
    out = pl.BlockSpec((rows, weights.block), lambda j: (0, j))
    shape = jax.ShapeDtypeStruct((rows, weights.hidden), jnp.bfloat16)
    return pl.pallas_call(
        partial(hidden_kernel, weights.per_chip, len(grads)),
        grid=(weights.steps,),
        in_specs=[
            pl.BlockSpec((rows, width), lambda j: (0, 0)),
            weights.up_spec,
            weights.down_spec,
        ]
        + [pl.BlockSpec(grad.shape, lambda j: (0, 0)) for grad in grads],
        out_specs=[out, out],
        out_shape=[shape, shape],
        compiler_params=BIG,
        cost_estimate=cost(
            4 * rows * width * weights.hidden,
            2 * weights.bytes + 4 * rows * (width + weights.hidden),
        ),
        name="hidden_layer",
    )(x, weights.up, weights.down, *grads)


def accumulate(part, outs, total):
    step = pl.program_id(0)

    @pl.when(step == 0)
    def _():
        total[...] = part

    @pl.when(step > 0)
    def _():
        total[...] += part

    @pl.when(step == pl.num_programs(0) - 1)
    def _():
        rows = total.shape[0] // len(outs)
        for index, out_ref in enumerate(outs):
            value = total[index * rows : (index + 1) * rows, :]
            out_ref[...] = value.astype(out_ref.dtype)


def down_kernel(splits, a_ref, down_ref, *refs):
    total = refs[-1]
    part = matmul(a_ref[...], down_ref[...].reshape(-1, total.shape[1]))
    accumulate(part, refs[-1 - splits : -1], total)


def up_back_kernel(splits, g_ref, up_ref, *refs):
    total = refs[-1]
    weights = up_ref[...].reshape(total.shape[1], -1)
    accumulate(matmul_last(g_ref[...], weights), refs[-1 - splits : -1], total)


def hidden_to_width(kernel, name, held, weights, spec, array, rows, chunk, dtype, behind, splits=1):
    width = weights.width
    outs = pl.pallas_call(
        partial(kernel, splits),
        grid=(weights.steps,),
        in_specs=[pl.BlockSpec((rows, weights.block), lambda j: (chunk, j)), spec]
        + [ANYWHERE] * len(behind),
        out_specs=[pl.BlockSpec((rows // splits, width), lambda j: (0, 0))] * splits,
        out_shape=[jax.ShapeDtypeStruct((rows // splits, width), dtype)] * splits,
        scratch_shapes=[pltpu.VMEM((rows, width), jnp.float32)],
        compiler_params=BIG,
        cost_estimate=cost(
            2 * rows * width * weights.hidden,
            weights.bytes + rows * (2 * weights.hidden + 4 * width),
        ),
        name=name,
    )(held, array, *behind)
    return outs[0] if splits == 1 else outs


def down_part(active, weights, rows, chunk, dtype, behind=()):
    return hidden_to_width(
        down_kernel,
        "down_part",
        active,
        weights,
        weights.down_spec,
        weights.down,
        rows,
        chunk,
        dtype,
        behind,
    )


def up_back(grad, weights, rows, chunk, dtype, behind=(), splits=1):
    return hidden_to_width(
        up_back_kernel,
        "up_back",
        grad,
        weights,
        weights.up_spec,
        weights.up,
        rows,
        chunk,
        dtype,
        behind,
        splits,
    )


def middle_back_kernel(pieces, parts, place, *refs):
    own_ref, base_ref, top_ref, ada_ref, out_w = refs[:5]
    others = refs[5 : 5 + parts]
    outs = refs[-3 - pieces :]
    grad_ref, low_ref, ada_grad_ref = outs[:3]
    grad = own_ref[...] + current(others, 2).astype(jnp.float32)
    normed, inverse = standardise(base_ref[...])
    scaled = grad * (1.0 + ada_ref[0:1, :])
    scale = jnp.sum(grad * normed, axis=0, keepdims=True)
    shift = jnp.sum(grad, axis=0, keepdims=True)
    inner = jnp.mean(scaled * normed, axis=-1, keepdims=True)
    shifted = scaled - jnp.mean(scaled, axis=-1, keepdims=True) - normed * inner
    out = top_ref[...].astype(jnp.float32) + inverse * shifted
    grad_ref[...] = out
    low = out.astype(jnp.bfloat16)
    low_ref[...] = low
    weights = out_w.reshape(out_w.shape[0] * out_w.shape[2], out_w.shape[3])
    spots = head_spots(1 - place[4], 1, pieces)
    for index, mixed_ref in enumerate(outs[3:]):
        size = mixed_ref.shape[1]
        start = pl.multiple_of(spots[index] * size, size)
        mixed_ref[...] = matmul_last(low, weights[pl.ds(start, size), :]).astype(jnp.bfloat16)
    add_rows(ada_grad_ref, scale, shift)


def middle_back(own, other, attended, cotangent, ada, out_w, out_part, spots, sizes, behind):
    rows, width = attended.shape
    count = 2
    block = lambda size: pl.BlockSpec((rows // count, size), lambda j, s: (j, 0))
    items, _, piece, _ = out_w.shape
    _, other_specs = row_specs(other, count)
    return pl.pallas_call(
        partial(middle_back_kernel, len(sizes), len(other)),
        grid_spec=pltpu.PrefetchScalarGridSpec(
            num_scalar_prefetch=1,
            grid=(count,),
            in_specs=[block(width)] * 3
            + [
                pl.BlockSpec((2, width), lambda j, s: (0, 0)),
                pl.BlockSpec((items, 1, piece, width), lambda j, s: (0, out_part, 0, 0)),
            ]
            + other_specs
            + [ANYWHERE] * len(behind),
            out_specs=[block(width), block(width), pl.BlockSpec((2, width), lambda j, s: (0, 0))]
            + [block(size) for size in sizes],
        ),
        out_shape=[
            jax.ShapeDtypeStruct((rows, width), jnp.float32),
            jax.ShapeDtypeStruct((rows, width), jnp.bfloat16),
            jax.ShapeDtypeStruct((2, width), jnp.float32),
        ]
        + [jax.ShapeDtypeStruct((rows, size), jnp.bfloat16) for size in sizes],
        compiler_params=BIG,
        cost_estimate=cost(2 * rows * width * width, 2 * width * width + 20 * rows * width),
        name="middle_back",
    )(spots, own, attended, cotangent, ada, out_w, *other, *behind)


def first_back_kernel(splits, grad_ref, weight_ref, frames, *refs):
    outs, ada_grad_ref = refs[-1 - splits : -1], refs[-1]
    grad = matmul_last(grad_ref[...], weight_ref[...])
    normed, _ = standardise(frames[...].astype(jnp.float32))
    for index, out_ref in enumerate(outs):

        @pl.when((pl.program_id(0) == index) | (splits == 1))
        def _(out_ref=out_ref):
            out_ref[...] = grad.astype(jnp.bfloat16)

    scale = jnp.sum(grad * normed, axis=0, keepdims=True)
    shift = jnp.sum(grad, axis=0, keepdims=True)
    add_rows(ada_grad_ref, scale, shift)


def first_back(grad, weights, frames, part, behind, splits=1):
    width, columns = weights.shape
    count = 2
    rows = frames.shape[0] // count
    block = pl.BlockSpec((rows, width), lambda j: (j, 0))
    out = block if splits == 1 else pl.BlockSpec((rows, width), lambda j: (0, 0))
    return pl.pallas_call(
        partial(first_back_kernel, splits),
        grid=(count,),
        in_specs=[
            pl.BlockSpec((rows, columns), lambda j: (part * count + j, 0)),
            pl.BlockSpec((width, columns), lambda j: (0, 0)),
            block,
        ]
        + [ANYWHERE] * len(behind),
        out_specs=[out] * splits + [pl.BlockSpec((2, width), lambda j: (0, 0))],
        out_shape=[jax.ShapeDtypeStruct((rows * count // splits, width), jnp.bfloat16)] * splits
        + [jax.ShapeDtypeStruct((2, width), jnp.float32)],
        compiler_params=BIG,
        cost_estimate=cost(
            2 * rows * count * width * columns,
            2 * width * columns + 2 * rows * count * (2 * width + columns),
        ),
        name="first_back",
    )(grad, weights, frames, *behind)


def stacked_dot(lefts, rights):
    total = None
    for left, right in zip(lefts, rights):
        part = dot_rows(left, right)
        total = part if total is None else total + part
    return total


def cut_rows(ref, count):
    rows = ref.shape[0] // count
    return [ref[j * rows : (j + 1) * rows, :] for j in range(count)]


def put_sum(out_ref, other_ref, value):
    if other_ref is not None:
        value = value + other_ref[...].astype(jnp.float32)
    out_ref[...] = value.astype(jnp.bfloat16)


def hidden_grads_kernel(count, more, place, *refs):
    active, upward = refs[:2]
    grads, low = refs[2 : 2 + count], refs[2 + count]
    other = refs[3 + count] if more else None
    out_ref = refs[-1]
    step = pl.program_id(0)
    steps = pl.num_programs(0) // 2

    @pl.when(step < steps)
    def _():
        put_sum(
            out_ref, other, stacked_dot(cut_rows(active, count), [ref[...] for ref in grads])
        )

    @pl.when(step >= steps)
    def _():
        put_sum(out_ref, other, dot_rows(low[...], upward[...]))


def hidden_grads(place, who, active, upward, grads, low, other, behind):
    total, hidden = active.shape
    half = hidden // 2
    rows, width = grads[0].shape
    count = len(grads)
    block = 512
    steps = half // block
    whole = pl.BlockSpec((total, width), lambda j, s: (0, 0))
    grad = pl.BlockSpec((rows, block), lambda j, s: (0, jnp.minimum(j, steps - 1)))
    out = pl.BlockSpec((width, block), lambda j, s: (0, j))
    more = [] if other is None else [other]
    return pl.pallas_call(
        partial(hidden_grads_kernel, count, bool(more)),
        grid_spec=pltpu.PrefetchScalarGridSpec(
            num_scalar_prefetch=1,
            grid=(2 * steps,),
            in_specs=[
                pl.BlockSpec((total, half), lambda j, s: (0, s[who])),
                pl.BlockSpec(
                    (total, block), lambda j, s: (0, s[who] * steps + jnp.maximum(j - steps, 0))
                ),
            ]
            + [grad] * count
            + [whole]
            + [out] * len(more)
            + [ANYWHERE] * len(behind),
            out_specs=out,
        ),
        out_shape=jax.ShapeDtypeStruct((width, 2 * half), jnp.bfloat16),
        compiler_params=BIG,
        cost_estimate=cost(4 * total * half * width, 8 * total * half + 4 * width * half),
        name="hidden_grads",
    )(place, active, upward, *grads, low, *more, *behind)


def tail_grads_kernel(first, more, pieces, calls, place, low, grad, attended, *refs):
    mixed = refs[:pieces]
    other = refs[pieces] if more else None
    out_ref = refs[-1]

    @pl.when(pl.program_id(0) < first)
    def _():
        put_sum(out_ref, other, dot_rows(low[...], grad[...]))

    @pl.when(pl.program_id(0) >= first)
    def _():
        spots = head_spots(place[4], calls, pieces)
        for index, piece in enumerate(mixed):
            size = piece.shape[1]
            rows = pl.ds(pl.multiple_of(spots[index] * size, size), size)
            value = dot_rows(piece[...], attended[...])
            if more:
                value = value + other[rows, :].astype(jnp.float32)
            out_ref[rows, :] = value.astype(jnp.bfloat16)


def tail_grads(place, who, low_one, grad_qkv, mixed, swapped, attended_low, other, behind):
    total, width = low_one.shape
    rows = attended_low.shape[0]
    block = 256
    first = grad_qkv.shape[1] // 2 // block
    second = width // 2 // block
    out = pl.BlockSpec((width, block), lambda j, s: (0, j))
    more = [] if other is None else [other]
    return pl.pallas_call(
        partial(
            tail_grads_kernel, first, bool(more), len(mixed) + len(swapped), len(mixed)
        ),
        grid_spec=pltpu.PrefetchScalarGridSpec(
            num_scalar_prefetch=1,
            grid=(first + second,),
            in_specs=[
                pl.BlockSpec((total, width), lambda j, s: (0, 0)),
                pl.BlockSpec(
                    (total, block), lambda j, s: (0, s[who] * first + jnp.minimum(j, first - 1))
                ),
                pl.BlockSpec(
                    (rows, block), lambda j, s: (0, s[who] * second + jnp.maximum(j - first, 0))
                ),
            ]
            + [pl.BlockSpec((rows, part.shape[1]), lambda j, s: (0, 0)) for part in mixed]
            + [pl.BlockSpec((rows, part.shape[1]), lambda j, s: (1, 0)) for part in swapped]
            + [out] * len(more)
            + [ANYWHERE] * len(behind),
            out_specs=out,
        ),
        out_shape=jax.ShapeDtypeStruct((width, (first + second) * block), jnp.bfloat16),
        compiler_params=BIG,
        cost_estimate=cost(
            2 * width * block * (total * first + rows * second), 8 * total * width
        ),
        name="tail_grads",
    )(place, low_one, grad_qkv, attended_low, *mixed, *swapped, *more, *behind)


def input_back_kernel(parts, count, own_ref, tokens_ref, ada_ref, base_ref, *refs):
    out_ref = refs[-1]
    grad = own_ref[...].astype(jnp.float32) + current(refs[:parts], count).astype(jnp.float32)
    normed, inverse = standardise(tokens_ref[...].astype(jnp.float32))
    scaled = grad * (1.0 + ada_ref[0:1, :])
    inner = jnp.mean(scaled * normed, axis=-1, keepdims=True)
    shifted = scaled - jnp.mean(scaled, axis=-1, keepdims=True) - normed * inner
    out_ref[...] = base_ref[...] + inverse * shifted


def input_back(own, others, tokens, ada, base):
    rows, width = tokens.shape
    count = 4
    block = pl.BlockSpec((rows // count, width), lambda j: (j, 0))
    _, specs = row_specs(others, count)
    return pl.pallas_call(
        partial(input_back_kernel, len(others), count),
        grid=(count,),
        in_specs=[block, block, pl.BlockSpec((2, width), lambda j: (0, 0)), block] + specs,
        out_specs=block,
        out_shape=jax.ShapeDtypeStruct((rows, width), jnp.float32),
        compiler_params=BIG,
        cost_estimate=cost(20 * rows * width, 14 * rows * width),
        name="input_back",
    )(own, tokens, ada, base, *others)


def join_tail_kernel(held, place, mine, seq_ref, core_ref, both_ref, *outs):
    core, seq = place[2], place[4]
    half = 3 * held // 2
    width = held // 2

    def chosen(side, core_half, spot):
        near = jnp.where(core == core_half, mine[:, spot], core_ref[:, spot])
        far = jnp.where(core == core_half, seq_ref[:, spot], both_ref[:, spot])
        return jnp.where(seq == side, near, far)

    for side in range(2):
        for core_half in range(2):
            for pair in range(width // LANES):
                for which in range(3):
                    start = (3 * pair + which) * LANES
                    to = side * held + core_half * width + pair * LANES
                    value = chosen(side, core_half, slice(start, start + LANES))
                    outs[which][:, to : to + LANES] = value
    for core_half in range(2):
        spot = slice(half, None)
        near = jnp.where(core == core_half, mine[:, spot], core_ref[:, spot])
        far = jnp.where(core == core_half, seq_ref[:, spot], both_ref[:, spot])
        outs[3][:, core_half * held : (core_half + 1) * held] = near + far


def join_tail(place, parts, held):
    rows, columns = parts[0].shape
    whole = lambda size: pl.BlockSpec((rows, size), lambda j, s: (0, 0))
    return pl.pallas_call(
        partial(join_tail_kernel, held),
        grid_spec=pltpu.PrefetchScalarGridSpec(
            num_scalar_prefetch=1,
            grid=(1,),
            in_specs=[whole(columns)] * 4,
            out_specs=[whole(2 * held)] * 4,
        ),
        out_shape=[jax.ShapeDtypeStruct((rows, 2 * held), jnp.float32)] * 4,
        cost_estimate=cost(0, 16 * rows * columns),
        name="join_tail",
    )(place, *parts)


def exact(left, right):
    return jnp.dot(left, right, precision=lax.Precision.HIGHEST)


def rounded(total, other=None):
    if other is not None:
        total = total + other.astype(jnp.float32)
    return total.astype(jnp.bfloat16)


def tie(*values):
    return lax.optimization_barrier(values)


def cut(value, start, size, axis):
    return lax.dynamic_slice_in_dim(value, start, size, axis, allow_negative_indices=False)


def pick(value, index, axis):
    return lax.dynamic_index_in_dim(
        value, index, axis, keepdims=False, allow_negative_indices=False
    )


def ring_of(items_count):
    chips = items_count // 2
    outer = 4 if chips % 4 == 0 else chips
    inner = chips // outer
    order = [a * inner for a in range(outer)]
    for turn, a in enumerate(reversed(range(outer))):
        beside = list(range(1, inner))
        order += [a * inner + b for b in (beside if turn % 2 == 0 else beside[::-1])]
    return order


class Mover:
    def __init__(self, items_count, seq_count):
        self.items_count = items_count
        self.seq_count = seq_count
        self.pair = seq_count == 2
        self.chips = items_count // 2
        order = ring_of(items_count)
        self.forward = []
        self.backward = []
        chips = self.chips
        table = np.zeros((items_count, 2 * chips + 2), np.int32)
        hops = list(range(chips // 2 + 1)) + [-hop for hop in range(1, (chips + 1) // 2)]
        for spot in range(self.chips):
            for core in range(2):
                here = 2 * order[spot] + core
                next_one = 2 * order[(spot + 1) % self.chips] + core
                self.forward.append((here, next_one))
                self.backward.append((next_one, here))
                for ahead in range(self.chips):
                    table[here, ahead] = order[(spot + ahead) % self.chips]
                table[here, chips] = core
                table[here, chips + 1] = 1 - core
                for spot_of, hop in enumerate(hops):
                    ahead = hop if core == 1 else -hop
                    table[here, chips + 2 + spot_of] = order[(spot + ahead) % chips]
        self.both_ways = [p for p in self.forward if p[0] % 2 == 0]
        self.both_ways += [p for p in self.backward if p[0] % 2 == 1]
        self.item = lax.axis_index("items")
        row = pick(jnp.asarray(table), self.item, 0)
        self.ahead = [row[j] for j in range(self.chips)]
        self.core = row[self.chips]
        self.beside = row[self.chips + 1]
        self.spots = row[self.chips + 2 :]
        self.seq = lax.axis_index("seq")
        self.quarter = 2 * self.core + self.seq

    def flip(self, value, bit):
        pairs = [(i, i ^ bit) for i in range(self.items_count)]
        return lax.ppermute(value, "items", pairs)

    def opposite(self, value):
        pairs = [(2 * i + x, 2 * (i ^ 1) + 1 - x) for i in range(self.items_count) for x in (0, 1)]
        return lax.ppermute(value, ("items", "seq"), pairs)

    def across(self, value):
        return lax.ppermute(value, "seq", [(0, 1), (1, 0)])

    def gather_items(self, value, summed, early, late):
        for bit in [1 << k for k in range(self.items_count.bit_length() - 1)]:
            summed = summed + self.flip(summed, bit)
        beside = self.flip(value, 1)
        block = jnp.where(
            self.core == 0,
            jnp.concatenate([value, beside], axis=0),
            jnp.concatenate([beside, value], axis=0),
        )
        direct = [block]
        for hop in range(1, self.chips // 2 + 1):
            moved = lax.ppermute(direct[-1], "items", self.both_ways)
            if hop == min(LATE_HOP, self.chips // 2):
                late, summed, moved, early = tie(late, summed, moved, early)
            direct.append(moved)
        beside = [self.flip(moved, 1) for moved in direct[1 : (self.chips + 1) // 2]]
        return direct + beside, summed, early, late

    def sum_seq(self, value):
        return value + self.across(value) if self.pair else lax.psum(value, "seq")

    def scatter_seq(self, value):
        rows = value.shape[0] // self.seq_count
        if self.pair:
            sent = cut(value, (1 - self.seq) * rows, rows, 0)
            kept = cut(value, self.seq * rows, rows, 0)
            return kept + self.across(sent.astype(jnp.bfloat16)).astype(jnp.float32)
        return lax.psum_scatter(
            value.astype(jnp.bfloat16), "seq", scatter_dimension=0, tiled=True
        ).astype(jnp.float32)

    def join_cores(self, value):
        parts = value.reshape(2, -1, value.shape[1])
        kept = pick(parts, self.core, 0)
        other = self.flip(pick(parts, self.beside, 0), 1)
        return jnp.where(self.core == 0, kept, other), jnp.where(self.core == 0, other, kept)

    def join_columns(self, value):
        rows = value.shape[0] // self.seq_count
        if self.pair:
            kept = cut(value, self.seq * rows, rows, 0)
            other = self.across(cut(value, (1 - self.seq) * rows, rows, 0))
            return jnp.where(self.seq == 0, kept, other), jnp.where(self.seq == 0, other, kept)
        moved = lax.all_to_all(value, "seq", split_axis=0, concat_axis=0, tiled=True)
        return tuple(moved[j * rows : (j + 1) * rows] for j in range(self.seq_count))


class RingSum:
    def __init__(self, mover, make, behind, ready=()):
        self.mover = mover
        self.chips = mover.chips
        self.make = make
        self.flows = None
        sent, self.ready = tie(make(False, None, behind), list(ready))
        self.sent = sent
        self.arriving = [mover.flip(sent, 1)]

    def block(self, ahead):
        return pick(self.both, self.mover.ahead[ahead % self.chips], 0)

    def add_own(self, behind):
        self.both = self.make(True, self.arriving[0], behind)
        self.whole = self.both
        self.both = self.both.reshape(self.chips, -1, self.both.shape[1])
        self.arrived = []
        flows = [
            (self.mover.forward, 1, self.chips // 2),
            (self.mover.backward, -1, (self.chips - 1) // 2),
        ]
        self.send([(flow, self.block(flow[1] * flow[2])) for flow in flows if flow[2]])

    def send(self, flows):
        self.arriving = [lax.ppermute(value, "items", flow[0]) for flow, value in flows]
        self.flows = [(pairs, sign, left - 1) for (pairs, sign, left), _ in flows]

    def advance(self, anchor=None):
        flows = []
        if anchor is not None:
            self.arriving, anchor = tie(self.arriving, anchor)
        for flow, value in zip(self.flows, self.arriving):
            if flow[2]:
                flows.append((flow, self.block(flow[1] * flow[2]) + value))
            else:
                self.arrived.append(value)
        self.send(flows)
        return anchor

    def finish(self, anchor=None):
        while self.arriving:
            self.advance()
        if anchor is not None:
            self.arrived, anchor = tie(self.arrived, anchor)
        result = self.block(0).astype(jnp.float32)
        for value in self.arrived:
            result = result + value.astype(jnp.float32)
        return result if anchor is None else (result, anchor)


def in_rows(value):
    return with_layout_constraint(value, Layout((0, 1)))


def halves(value, core):
    half = value.shape[1] // 2
    return cut(value, core * half, half, 1)


def parted(value, at):
    return (None, None) if value is None else (value[:, :at], value[:, at:])


def shards(
    tokens,
    cotangent,
    prompt_len,
    section_ids,
    section_table,
    w_query,
    w_key,
    w_value,
    w_out,
    w_up,
    w_down,
    w_ada_one,
    w_ada_two,
):
    items_count = lax.axis_size("items")
    seq_count = lax.axis_size("seq")
    mover = Mover(items_count, seq_count)
    chips = mover.chips
    batch, rows, width = tokens.shape
    total_rows = rows * seq_count
    hidden = w_up.shape[1] // seq_count
    held = width // seq_count
    pairs = held // LANES
    piece = w_query.shape[0]
    units = w_down.shape[0] // seq_count
    tokens = tokens.reshape(rows, width)
    grad_low = cotangent.reshape(rows, width)

    def quarters(one, two):
        return jnp.stack([one[:, :width], one[:, width:], two[:, :width], two[:, width:]])

    up_shard = w_up.reshape(piece, chips, 2, seq_count, units).transpose(3, 0, 2, 1, 4)
    up_shard = pick(up_shard, mover.seq, 0).reshape(piece, hidden)
    down_shard = cut(w_down, mover.seq * units, units, 0)
    merged = hidden % width == 0 and units % piece == 0
    late = down_shard
    if merged:
        folds = hidden // width
        down_parts = units // piece
        up_rows = [up_shard[:, j * width : (j + 1) * width] for j in range(folds)]
        late = jnp.concatenate([down_shard] + up_rows + [w_out], axis=0)

    table_part = cut(section_table, mover.item * piece, piece, 1)
    ada_part = jnp.dot(
        table_part,
        jnp.concatenate([w_ada_one, w_ada_two], axis=1),
        preferred_element_type=jnp.float32,
    )
    ada_part = quarters(ada_part[:, : 2 * width], ada_part[:, 2 * width :])
    prompt_at = mover.seq if mover.pair else jnp.zeros((), jnp.int32)
    place = jnp.stack([prompt_at, prompt_len[0], mover.core, mover.beside, mover.seq])
    seq_place = jnp.reshape(mover.seq, (1,)).astype(jnp.int32)
    mine = pack_columns(w_query, w_key, w_value, held, seq_place)
    early = [mover.across(tokens)] if mover.pair else []
    blocks, ada_sum, early, late = mover.gather_items(
        mine, ada_part, early, late
    )

    def gathered(value):
        return lax.all_gather(value, "items", axis=0, tiled=False)

    if merged:
        rest = gathered(late)
        rest = rest.reshape(items_count, down_parts + folds + 1, piece, width)
        by_core = rest.reshape((chips, 2) + rest.shape[1:])
        weights = Weights(rest, down_parts, by_core, down_parts, hidden, width)
        out_w, out_part = rest, down_parts + folds
    else:
        by_core = gathered(late).reshape(chips, 2, 1, units, width)
        weights = Weights(gathered(up_shard)[:, None], 0, by_core, 1, hidden, width)
        out_w, out_part = gathered(w_out)[:, None], 0

    choose = (section_ids[0] == jnp.arange(section_table.shape[0])).astype(jnp.float32)
    ada = jnp.sum(choose[None, :, None] * ada_sum, axis=1)
    ada_one = ada[:2]
    ada_two = ada[2:]

    if mover.pair:
        tokens_other, grad_sent = tie(early[0], grad_low)
        grad_other = mover.across(grad_sent)
        frames = [tokens, tokens_other]
        grads = [grad_low, grad_other]
        calls = 2 if pairs % 2 == 0 else 1
    else:
        frames = [lax.all_gather(tokens, "seq", axis=0, tiled=True)]
        grads = [lax.all_gather(grad_low, "seq", axis=0, tiled=True)]
        calls = 1
    low_one, qkv, qkv_w = first_layer(frames, ada_one, blocks, mover.spots)
    per_call = pairs // calls
    mixed_heads = []
    lse = []
    for call in range(calls):
        behind = grads[1:] + mixed_heads
        out = attend(qkv, place, call * per_call, per_call, behind)
        mixed_heads.append(out[0])
        lse.append(out[1])
    if mover.pair:
        mixed_far = []
        for call in range(calls):
            sent = mixed_heads[call]
            if mixed_far:
                sent, mixed_far[-1] = tie(sent, mixed_far[-1])
            mixed_far.append(mover.across(sent))
        attended, low_two = second_layer(
            mixed_heads, mixed_far, frames[::-1], out_w, out_part, ada_two, place
        )
        lows = low_two
        active, upward = hidden_layer(lows, grads, weights)
        first_half, last_half = up_back(upward, weights, rows, 1, jnp.bfloat16, (), 2)
        start = [first_half]
        ready = [mover.across(first_half), last_half]
    else:
        mixed = lax.all_to_all(mixed_heads[0], "seq", split_axis=0, concat_axis=1, tiled=True)
        attended, low_two = second_layer(
            [mixed], [], [tokens], out_w, out_part, ada_two, place
        )
        lows = lax.all_gather(low_two, "seq", axis=0, tiled=True)
        active, upward = hidden_layer(lows, grads, weights)
        start = []
        ready = []

    down_columns = hidden // 2

    def hidden_parts(own, other, behind):
        who = 2 if own else 3
        if down_columns == width:
            return hidden_grads(place, who, active, upward, grads, lows, other, behind)
        core = mover.core if own else mover.beside
        first, second = parted(other, down_columns)
        down = dot_rows(halves(active, core), grads[0]).reshape(width, down_columns)
        up = dot_rows(lows, halves(upward, core))
        return in_rows(jnp.concatenate([rounded(down, first), rounded(up, second)], axis=1))

    ring = RingSum(mover, hidden_parts, start, ready)
    if mover.pair:
        own = up_back(upward, weights, rows, 0, jnp.float32, [ring.sent])
        from_other = [ring.ready[0], mover.across(ring.ready[1])]
        sizes = [held, held]
    else:
        own = lax.psum_scatter(
            up_back(upward, weights, total_rows, 0, jnp.bfloat16),
            "seq",
            scatter_dimension=0,
            tiled=True,
        ).astype(jnp.float32)
        from_other = [jnp.zeros((rows, width), jnp.bfloat16)]
        sizes = [width]
    ring.add_own([own])
    grad_attended, attended_low, ada_two_rows, *grad_mixed = middle_back(
        own,
        from_other,
        attended,
        grad_low,
        ada_two,
        out_w,
        out_part,
        place,
        sizes,
        [ring.whole],
    )
    if mover.pair:
        out_other = down_part(active, weights, rows, 1, jnp.bfloat16, grad_mixed[:1])
        grad_heads = [grad_mixed[1], mover.across(grad_mixed[0])]
        out_other = ring.advance(out_other)
        out_own = down_part(active, weights, rows, 0, jnp.float32, [out_other])
        filler = [out_own]
        out_other = mover.across(out_other)
    else:
        grad_heads = [
            lax.all_to_all(grad_mixed[0], "seq", split_axis=1, concat_axis=0, tiled=True)
        ]
        filler = []

    split = pairs // 2 if pairs % 2 == 0 else 0

    def tail_parts(own, other, behind):
        if mover.pair:
            return tail_grads(
                place,
                2 if own else 3,
                low_one,
                grad_qkv,
                mixed_heads,
                mixed_far,
                attended_low,
                other,
                behind,
            )
        core = mover.core if own else mover.beside
        first, second = parted(other, grad_qkv.shape[1] // 2)
        qkv_part = rounded(dot_rows(low_one, halves(grad_qkv, core)), first)
        out_part = rounded(dot_rows(mixed, halves(attended_low, core)), second)
        return in_rows(jnp.concatenate([qkv_part, out_part], axis=1))

    tail = None
    grad_qkv = None
    for turn in range(pairs):
        behind = filler
        filler = []
        grad_qkv = attend_back(
            place, turn, pairs, qkv, mixed_heads, grad_heads, lse, grad_qkv, behind
        )
        grad_qkv = ring.advance(grad_qkv)
        if turn + 1 == split:
            tail = RingSum(mover, tail_parts, [])
            filler = [tail.sent]
    if tail is None:
        tail = RingSum(mover, tail_parts, [])
    tail.add_own([])
    if mover.pair:
        near_half, last_half, far_rows = first_back(
            grad_qkv, qkv_w, frames[1], 1, [tail.whole, out_other], 2
        )
        near_half = mover.across(near_half)
        last_half = tail.advance(last_half)
        hidden_total, last_half = ring.finish(last_half)
        own_first, own_rows = first_back(grad_qkv, qkv_w, frames[0], 0, [last_half])
        own_rows, near_half, last_half, out_other = tail.advance(
            [own_rows, near_half, last_half, out_other]
        )
        far_parts = [near_half, mover.across(last_half)]
        ada_rows = jnp.concatenate([own_rows + far_rows, ada_two_rows])
        ada_rows = ada_rows + mover.across(ada_rows)
        layer_sum = out_own + out_other.astype(jnp.float32)
    else:
        grad_first, ada_one_rows = first_back(grad_qkv, qkv_w, frames[0], 0, [tail.whole])
        ada_rows = lax.psum(jnp.concatenate([ada_one_rows, ada_two_rows]), "seq")
        own_first = lax.psum_scatter(grad_first, "seq", scatter_dimension=0, tiled=True)
        far_parts = [jnp.zeros((rows, width), jnp.bfloat16)]
        hidden_total = ring.finish()
        layer_sum = lax.psum_scatter(
            down_part(active, weights, total_rows, 0, jnp.bfloat16),
            "seq",
            scatter_dimension=0,
            tiled=True,
        ).astype(jnp.float32)
    layer_out = (attended + layer_sum).astype(jnp.bfloat16)
    sums = choose[None, :, None] * ada_rows[:, None, :]
    for bit in [1 << k for k in range(items_count.bit_length() - 1)]:
        sums = sums + mover.flip(sums, bit)
        if bit == 1:
            sums = tail.advance(sums)
        if bit == 4:
            sums, far_parts = tie(sums, far_parts)
    input_grad = input_back(own_first, far_parts, tokens, ada_one, grad_attended)
    out_piece = piece // seq_count
    first_row = mover.item * piece + mover.seq * out_piece
    table_rows = cut(section_table, first_row, out_piece, 1).astype(jnp.float32)
    ada_grads = jnp.einsum("sr,ksd->krd", table_rows, sums, precision=lax.Precision.HIGHEST)
    grad_ada_one = jnp.concatenate([ada_grads[0], ada_grads[1]], axis=1)
    grad_ada_two = jnp.concatenate([ada_grads[2], ada_grads[3]], axis=1)
    own_ada = quarters(
        *(cut(w, mover.seq * out_piece, out_piece, 0) for w in (w_ada_one, w_ada_two))
    ).astype(jnp.float32)
    grad_table = jnp.einsum("ksd,krd->sr", sums, own_ada, precision=lax.Precision.HIGHEST)

    grad_down = hidden_total[:, :down_columns].reshape(units, width)
    up_sides = mover.join_columns(
        jnp.concatenate(mover.join_cores(hidden_total[:, down_columns:]), axis=1)
    )
    grad_up = jnp.stack(
        [side.reshape(out_piece, 2, chips, units) for side in up_sides], axis=1
    )
    grad_up = grad_up.transpose(0, 3, 2, 1, 4).reshape(out_piece, hidden * seq_count)
    if mover.pair:
        quarters_of = tail.finish().reshape(4, piece // 2, -1)
        mine, to_seq, to_core, to_both = (
            pick(quarters_of, mover.quarter ^ flipped, 0) for flipped in (0, 1, 2, 3)
        )
        grad_query, grad_key, grad_value, grad_out = join_tail(
            place,
            [mine, mover.across(to_seq), mover.flip(to_core, 1), mover.opposite(to_both)],
            held,
        )
    else:
        tail_total = tail.finish()
        cores = jnp.concatenate(mover.join_cores(tail_total), axis=1)
        half_qkv = 3 * held // 2
        half_all = cores.shape[1] // 2
        qkv_total = jnp.concatenate(
            [cores[:, :half_qkv], cores[:, half_all : half_all + half_qkv]], axis=1
        )
        out_total = jnp.concatenate([cores[:, half_qkv:half_all], cores[:, half_all + half_qkv :]], axis=1)
        sides = mover.join_columns(qkv_total)
        grad_out = mover.scatter_seq(out_total)
        grad_query, grad_key, grad_value = (
            jnp.concatenate(
                [
                    side[:, (3 * p + j) * LANES : (3 * p + j + 1) * LANES]
                    for side in sides
                    for p in range(pairs)
                ],
                axis=1,
            )
            for j in range(3)
        )
    return (
        layer_out.reshape(batch, rows, width),
        input_grad.reshape(batch, rows, width),
        grad_query,
        grad_key,
        grad_value,
        grad_out,
        grad_up,
        grad_down,
        grad_ada_one,
        grad_ada_two,
        grad_table,
    )


def solution(mesh):
    return jax.shard_map(
        shards,
        mesh=mesh,
        in_specs=(
            P("items", "seq", None),
            P("items", "seq", None),
            P("items"),
            P("items"),
            P(),
            P("items", None),
            P("items", None),
            P("items", None),
            P("items", None),
            P("items", None),
            P("items", None),
            P("items", None),
            P("items", None),
        ),
        out_specs=(
            P("items", "seq", None),
            P("items", "seq", None),
            P(("items", "seq"), None),
            P(("items", "seq"), None),
            P(("items", "seq"), None),
            P(("items", "seq"), None),
            P(("items", "seq"), None),
            P(("items", "seq"), None),
            P(("items", "seq"), None),
            P(("items", "seq"), None),
            P(None, ("items", "seq")),
        ),
        check_vma=False,
    )
```

```python
from functools import partial
import math

import jax
import jax.numpy as jnp
import numpy as np
from jax import lax
from jax.experimental.layout import Layout, with_layout_constraint
from jax.experimental import pallas as pl
from jax.experimental.pallas import tpu as pltpu
from jax.sharding import PartitionSpec as P

HEAD_DIM = 64
SCALE = 0.125
MASKED = -1e30
COVER = 0.5
TILE = 128
LANES = 128

def row_ids(shape):
    return lax.broadcasted_iota(jnp.int32, shape, 0)
def lane_ids(shape):
    return lax.broadcasted_iota(jnp.int32, shape, 1)
def matmul(left, right):
    return jnp.dot(left, right, preferred_element_type=jnp.float32)
def twin_lanes(flipped):
    top = row_ids(flipped.shape) < HEAD_DIM
    return jnp.concatenate([jnp.where(top, flipped, 0.0), jnp.where(top, 0.0, flipped)], axis=1)
def twin_rows(block):
    first = lane_ids(block.shape) < HEAD_DIM
    return jnp.concatenate([jnp.where(first, block, 0.0), jnp.where(first, 0.0, block)], axis=0)
def untwin(wide):
    top = row_ids((LANES, LANES)) < HEAD_DIM
    return jnp.where(top, wide[:, :LANES], wide[:, LANES:]).T

def split3(value):
    high = value.astype(jnp.bfloat16).astype(jnp.float32)
    rest = value - high
    mid = rest.astype(jnp.bfloat16).astype(jnp.float32)
    return high, mid, rest - mid

def attend_kernel(place, q_ref, k_ref, v_ref, *refs):
    o_ref, lse_ref, keys_wide, values_t = refs[-4:]
    half = q_ref.shape[0] // 2
    prompt = pl.multiple_of(place[0] * half, TILE)
    target = pl.multiple_of((1 - place[0]) * half, TILE)
    length = place[1]
    shape = (half, LANES)
    keys_wide[:half, :LANES] = k_ref[pl.ds(prompt, half), :]
    keys_wide[half:, :LANES] = k_ref[pl.ds(target, half), :]
    hidden = (lane_ids(shape) == 0) & (row_ids(shape) >= length)
    keys_wide[:half, LANES:] = jnp.where(hidden, MASKED, 0.0).astype(jnp.bfloat16)
    keys_wide[half:, LANES:] = jnp.zeros(shape, jnp.bfloat16)
    for piece in range(half // TILE):
        rows = slice(piece * TILE, (piece + 1) * TILE)
        values_t[:, rows] = v_ref[pl.ds(prompt + piece * TILE, TILE), :].astype(jnp.float32).T.astype(jnp.bfloat16)
        rows = slice(half + piece * TILE, half + (piece + 1) * TILE)
        values_t[:, rows] = v_ref[pl.ds(target + piece * TILE, TILE), :].astype(jnp.float32).T.astype(jnp.bfloat16)
    below = jnp.where(row_ids((LANES, 2 * TILE)) == 0, 1.0, 0.0)

    def score(start, seen):
        q_flip = (q_ref[pl.ds(start, TILE), :].astype(jnp.float32) * SCALE).T
        q_wide = jnp.concatenate([twin_lanes(q_flip), below], axis=0).astype(jnp.bfloat16)
        return matmul(keys_wide[:seen, :], q_wide)

    def tile(scores, start, seen, slot):
        peak = jnp.max(scores, axis=0, keepdims=True)
        expo = jnp.exp(scores - peak)
        total = jnp.sum(expo, axis=0, keepdims=True)
        out = matmul(values_t[:, :seen], expo.astype(jnp.bfloat16)) / total
        o_ref[pl.ds(start, TILE), :] = untwin(out).astype(jnp.bfloat16)
        lse_ref[0, pl.ds(slot, 1), :] = peak + jnp.log(total)

    tiles = half // TILE

    @pl.loop(0, tiles)
    def _(index):
        at_prompt = pl.multiple_of(prompt + index * TILE, TILE)
        at_target = pl.multiple_of(target + index * TILE, TILE)
        first = score(at_prompt, half)
        second = score(at_target, 2 * half)
        tile(first, at_prompt, half, index)
        tile(second, at_target, 2 * half, tiles + index)


def attend(qkv, place, first, pairs, behind):
    rows = qkv.shape[0]
    width = pairs * LANES
    part = lambda shift: pl.BlockSpec((rows, LANES), lambda p, s, shift=shift: (0, 3 * (first + p) + shift))
    seen = rows * rows * 3 // 4
    return pl.pallas_call(
        attend_kernel,
        grid_spec=pltpu.PrefetchScalarGridSpec(
            num_scalar_prefetch=1, grid=(pairs,),
            in_specs=[part(0), part(1), part(2)] + [pl.BlockSpec(memory_space=pl.ANY)] * len(behind),
            out_specs=[pl.BlockSpec((rows, LANES), lambda p, s: (0, p)), pl.BlockSpec((1, rows // TILE, 2 * TILE), lambda p, s: (p, 0, 0))],
            scratch_shapes=[pltpu.VMEM((rows, 2 * LANES), jnp.bfloat16), pltpu.VMEM((LANES, rows), jnp.bfloat16)],
        ),
        out_shape=[jax.ShapeDtypeStruct((rows, width), jnp.bfloat16),
                   jax.ShapeDtypeStruct((pairs, rows // TILE, 2 * TILE), jnp.float32)],
        compiler_params=pltpu.CompilerParams(vmem_limit_bytes=60 << 20),
        cost_estimate=pl.CostEstimate(flops=int(COVER * pairs * 2 * seen * 4 * HEAD_DIM * 4), transcendentals=0, bytes_accessed=rows * width * 8),
        name="attend",
    )(place, qkv, qkv, qkv, *behind)


def attend_back_kernel(parts, calls, per, at, place, q_ref, k_ref, v_ref, *refs):
    o_refs, lse_refs, g_refs = refs[:calls], refs[calls:2 * calls], refs[2 * calls:2 * calls + parts]
    out_ref, keys_wide, values_wide, keys_t, dq, dk, dv = refs[-7:]
    half = q_ref.shape[0] // 2
    step = pl.program_id(0)
    prompt = pl.multiple_of(place[0] * half, TILE)
    target = pl.multiple_of((1 - place[0]) * half, TILE)
    length = place[1]

    @pl.when(step == 0)
    def _():
        shape = (half, LANES)
        lanes = lane_ids(shape)
        ones = jnp.where((lanes >= 1) & (lanes <= 3), 1.0, 0.0)
        hidden = (lanes == 0) & (row_ids(shape) >= length)
        keys_wide[:half, :LANES] = k_ref[pl.ds(prompt, half), :]
        keys_wide[half:, :LANES] = k_ref[pl.ds(target, half), :]
        keys_wide[:half, LANES:] = jnp.where(hidden, MASKED, ones).astype(jnp.bfloat16)
        keys_wide[half:, LANES:] = ones.astype(jnp.bfloat16)
        values_wide[:half, :LANES] = v_ref[pl.ds(prompt, half), :]
        values_wide[half:, :LANES] = v_ref[pl.ds(target, half), :]
        values_wide[:half, LANES:] = ones.astype(jnp.bfloat16)
        values_wide[half:, LANES:] = ones.astype(jnp.bfloat16)
        for piece in range(2 * half // TILE):
            rows = slice(piece * TILE, (piece + 1) * TILE)
            keys_t[:, rows] = keys_wide[rows, :LANES].astype(jnp.float32).T.astype(jnp.bfloat16)
        dk[...] = jnp.zeros_like(dk)
        dv[...] = jnp.zeros_like(dv)
        wide = (LANES, 2 * TILE)
        ids = row_ids(wide)

        def lanes_of(value):
            high, mid, rest = split3(value)
            return jnp.where(ids == 1, -high, jnp.where(ids == 2, -mid, jnp.where(ids == 3, -rest, 0.0)))

        def g_tile(start):
            if parts == 1:
                return g_refs[0][pl.ds(start, TILE), :]
            inside = pl.multiple_of(jnp.where(start < half, start, start - half), TILE)
            first = g_refs[0][pl.ds(inside, TILE), :]
            return jnp.where(start < half, first, g_refs[1][pl.ds(inside, TILE), :])

        def of_call(values):
            value = values[0]
            for call, later in enumerate(values[1:], 1):
                value = jnp.where(at(place) < call * per, value, later)
            return value

        def tile(start, seen, slot):
            spot = pl.ds(start, TILE)
            q_here = q_ref[spot, :].astype(jnp.float32) * SCALE
            g_here = g_tile(start).astype(jnp.float32)
            g_flip = g_here.T
            o_here = of_call([ref[spot, :].astype(jnp.float32) for ref in o_refs])
            product = g_flip * o_here.T
            inner = jnp.concatenate(
                [jnp.sum(product[:HEAD_DIM], axis=0, keepdims=True), jnp.sum(product[HEAD_DIM:], axis=0, keepdims=True)], axis=1)
            lse = of_call([ref[0, pl.ds(slot, 1), :] for ref in lse_refs])
            below = jnp.where(ids == 0, 1.0, lanes_of(lse))
            q_wide = jnp.concatenate([twin_lanes(q_here.T), below], axis=0).astype(jnp.bfloat16)
            g_wide = jnp.concatenate([twin_lanes(g_flip), lanes_of(inner)], axis=0).astype(jnp.bfloat16)
            probs = jnp.exp(matmul(keys_wide[:seen, :], q_wide))
            grads = matmul(values_wide[:seen, :], g_wide)
            scores = (probs * grads).astype(jnp.bfloat16)
            dk[:seen, :] += matmul(scores, twin_rows(q_here).astype(jnp.bfloat16))
            dv[:seen, :] += matmul(probs.astype(jnp.bfloat16), twin_rows(g_here).astype(jnp.bfloat16))
            dq[spot, :] = (untwin(matmul(keys_t[:, :seen], scores)) * SCALE).astype(jnp.bfloat16)

        tiles = half // TILE

        @pl.loop(0, tiles)
        def _(index):
            tile(pl.multiple_of(prompt + index * TILE, TILE), half, index)
            tile(pl.multiple_of(target + index * TILE, TILE), 2 * half, tiles + index)

        out_ref[...] = dq[...]

    for which, held in ((1, dk), (2, dv)):
        @pl.when(step == which)
        def _(held=held):
            out_ref[pl.ds(prompt, half), :] = held[:half, :].astype(jnp.bfloat16)
            out_ref[pl.ds(target, half), :] = held[half:, :].astype(jnp.bfloat16)


def attend_back(place, turn, pairs, qkv, mixed, grads, lse, held, behind):
    rows = qkv.shape[0]
    part = lambda shift: pl.BlockSpec((rows, LANES), lambda j, s, shift=shift: (0, 3 * at(s) + shift))
    calls = len(mixed)
    per = pairs // calls
    split = pairs // 2 if pairs % 2 == 0 else 0
    at = lambda s: (s[3] * split + turn) & (pairs - 1)
    parts = len(grads)
    block = pl.BlockSpec((rows, LANES), lambda j, s: (0, at(s) & (per - 1)))
    lse_block = pl.BlockSpec((1, rows // TILE, 2 * TILE), lambda j, s: (at(s) & (per - 1), 0, 0))
    grad_blocks = [pl.BlockSpec((grad.shape[0], LANES), lambda j, s: (0, at(s))) for grad in grads]
    seen = rows * rows * 3 // 4
    more = [] if held is None else [held]
    return pl.pallas_call(
        partial(attend_back_kernel, parts, calls, per, at),
        grid_spec=pltpu.PrefetchScalarGridSpec(
            num_scalar_prefetch=1, grid=(3,),
            in_specs=[part(0), part(1), part(2)] + [block] * calls + [lse_block] * calls + grad_blocks + [pl.BlockSpec(memory_space=pl.ANY)] * (len(more) + len(behind)),
            out_specs=pl.BlockSpec((rows, LANES), lambda j, s: (0, 3 * at(s) + j)),
            scratch_shapes=[pltpu.VMEM((rows, 2 * LANES), jnp.bfloat16), pltpu.VMEM((rows, 2 * LANES), jnp.bfloat16), pltpu.VMEM((LANES, rows), jnp.bfloat16),
                pltpu.VMEM((rows, LANES), jnp.bfloat16), pltpu.VMEM((rows, LANES), jnp.float32), pltpu.VMEM((rows, LANES), jnp.float32)],
        ),
        out_shape=jax.ShapeDtypeStruct(qkv.shape, jnp.bfloat16),
        input_output_aliases={4 + 2 * calls + parts: 0} if more else {},
        compiler_params=pltpu.CompilerParams(vmem_limit_bytes=60 << 20),
        cost_estimate=pl.CostEstimate(flops=int(COVER * 2 * seen * 10 * HEAD_DIM * 4), transcendentals=0, bytes_accessed=rows * LANES * 20),
        name="attend_back",
    )(place, qkv, qkv, qkv, *mixed, *lse, *grads, *more, *behind)


EPSILON = 1e-05
ROOT_HALF = math.sqrt(0.5)
DENSITY = 1.0 / math.sqrt(2.0 * math.pi)
LATE_HOP = 2
BIG = pltpu.CompilerParams(vmem_limit_bytes=60 << 20)
ANYWHERE = pl.BlockSpec(memory_space=pl.ANY)


def cost(flops, moved, special=0):
    return pl.CostEstimate(
        flops=int(flops * COVER), bytes_accessed=int(moved * COVER), transcendentals=special
    )


def matmul_last(left, right):
    return lax.dot_general(
        left, right, (((1,), (1,)), ((), ())), preferred_element_type=jnp.float32
    )


def dot_rows(left, right):
    return lax.dot_general(
        left, right, (((0,), (0,)), ((), ())), preferred_element_type=jnp.float32
    )


def standardise(values):
    centred = values - jnp.mean(values, axis=-1, keepdims=True)
    spread = jnp.mean(centred * centred, axis=-1, keepdims=True)
    inverse = lax.rsqrt(spread + EPSILON)
    return centred * inverse, inverse


def add_rows(ref, scale, shift):
    step = pl.program_id(0)

    @pl.when(step == 0)
    def _():
        ref[0:1, :] = scale
        ref[1:2, :] = shift

    @pl.when(step > 0)
    def _():
        ref[0:1, :] += scale
        ref[1:2, :] += shift


def row_specs(parts, count):
    rows = sum(part.shape[0] for part in parts) // count
    specs = []
    first = 0
    for part in parts:
        steps = part.shape[0] // rows
        specs.append(
            pl.BlockSpec(
                (rows, part.shape[1]),
                lambda j, *s, first=first, steps=steps: (jnp.clip(j - first, 0, steps - 1), 0),
            )
        )
        first += steps
    return rows, specs


def current(refs, count):
    value = refs[0][...]
    for index, ref in enumerate(refs[1:], 1):
        value = jnp.where(pl.program_id(0) < index * count // len(refs), value, ref[...])
    return value


def pack_kernel(place, query_ref, key_ref, value_ref, out_ref):
    for pair in range(query_ref.shape[1] // LANES):
        for which, ref in enumerate((query_ref, key_ref, value_ref)):
            start = (3 * pair + which) * LANES
            out_ref[:, start : start + LANES] = ref[:, pair * LANES : (pair + 1) * LANES]


def pack_columns(query, key, value, held, place):
    rows = query.shape[0]
    return pl.pallas_call(
        pack_kernel,
        grid_spec=pltpu.PrefetchScalarGridSpec(
            num_scalar_prefetch=1,
            grid=(1,),
            in_specs=[pl.BlockSpec((rows, held), lambda j, s: (0, s[0]))] * 3,
            out_specs=pl.BlockSpec((rows, 3 * held), lambda j, s: (0, 0)),
        ),
        out_shape=jax.ShapeDtypeStruct((rows, 3 * held), query.dtype),
        cost_estimate=cost(0, 12 * rows * held),
        name="pack_columns",
    )(place, query, key, value)


def first_kernel(parts, pieces, count, spots, *refs):
    frames = refs[:parts]
    ada = refs[parts]
    blocks = refs[parts + 1 : parts + 1 + pieces]
    low_ref, qkv_ref, weight_ref, sems = refs[-4:]
    rows = blocks[0].shape[0]

    @pl.when(pl.program_id(0) == 0)
    def _():
        copies = []
        for index, block in enumerate(blocks):
            start = pl.multiple_of(spots[index] * rows, rows)
            copy = pltpu.make_async_copy(
                block, weight_ref.at[pl.ds(start, rows), :], sems.at[index]
            )
            copy.start()
            copies.append(copy)
        for copy in copies:
            copy.wait()

    normed, _ = standardise(current(frames, count).astype(jnp.float32))
    low = ((1.0 + ada[0:1, :]) * normed + ada[1:2, :]).astype(jnp.bfloat16)
    low_ref[...] = low
    qkv_ref[...] = matmul(low, weight_ref[...]).astype(jnp.bfloat16)


def first_layer(frames, ada, blocks, spots):
    count = 4
    rows, specs = row_specs(frames, count)
    width = frames[0].shape[1]
    columns = blocks[0].shape[1]
    out = lambda size: pl.BlockSpec((rows, size), lambda j, s: (j, 0))
    shape = lambda *size: jax.ShapeDtypeStruct(size, jnp.bfloat16)
    return pl.pallas_call(
        partial(first_kernel, len(frames), len(blocks), count),
        grid_spec=pltpu.PrefetchScalarGridSpec(
            num_scalar_prefetch=1,
            grid=(count,),
            in_specs=specs
            + [pl.BlockSpec((2, width), lambda j, s: (0, 0))]
            + [ANYWHERE] * len(blocks),
            out_specs=[
                out(width),
                out(columns),
                pl.BlockSpec((width, columns), lambda j, s: (0, 0)),
            ],
            scratch_shapes=[pltpu.SemaphoreType.DMA((len(blocks),))],
        ),
        out_shape=[
            shape(rows * count, width),
            shape(rows * count, columns),
            shape(width, columns),
        ],
        compiler_params=BIG,
        cost_estimate=cost(
            2 * rows * count * width * columns, 4 * width * columns + 8 * rows * count * width
        ),
        name="first_layer",
    )(spots, *frames, ada, *blocks)


def second_kernel(pieces, calls, parts, count, place, *refs):
    mixed = refs[:pieces]
    tokens = refs[pieces : pieces + parts]
    out_w, ada = refs[pieces + parts : pieces + parts + 2]
    attended_ref, low_ref = refs[-2:]
    weights = out_w.reshape(out_w.shape[0] * out_w.shape[2], out_w.shape[3])
    spots = head_spots(place[4], calls, pieces)
    attended = current(tokens, count).astype(jnp.float32)
    for index, piece in enumerate(mixed):
        size = piece.shape[1]
        start = pl.multiple_of(spots[index] * size, size)
        attended = attended + matmul(piece[...], weights[pl.ds(start, size), :])
    attended_ref[...] = attended
    normed, _ = standardise(attended)
    low_ref[...] = ((1.0 + ada[0:1, :]) * normed + ada[1:2, :]).astype(jnp.bfloat16)


def second_layer(mixed, swapped, tokens, out_w, out_part, ada, spots):
    rows, width = tokens[-1].shape
    parts = len(tokens)
    count = 2 * parts
    size, token_specs = row_specs(tokens, count)
    later = count - 2
    block = lambda columns, order: pl.BlockSpec((size, columns), lambda j, s: (order(j), 0))
    first = lambda j: (j + later) % count
    items, _, piece, _ = out_w.shape
    return pl.pallas_call(
        partial(second_kernel, len(mixed) + len(swapped), len(mixed), parts, count),
        grid_spec=pltpu.PrefetchScalarGridSpec(
            num_scalar_prefetch=1,
            grid=(count,),
            in_specs=[block(part.shape[1], first) for part in mixed]
            + [block(part.shape[1], lambda j: j) for part in swapped]
            + token_specs
            + [
                pl.BlockSpec((items, 1, piece, width), lambda j, s: (0, out_part, 0, 0)),
                pl.BlockSpec((2, width), lambda j, s: (0, 0)),
            ],
            out_specs=[block(width, lambda j: jnp.maximum(j - later, 0)), block(width, first)],
        ),
        out_shape=[
            jax.ShapeDtypeStruct((rows, width), jnp.float32),
            jax.ShapeDtypeStruct((rows * parts, width), jnp.bfloat16),
        ],
        compiler_params=BIG,
        cost_estimate=cost(
            2 * rows * parts * width * width, 2 * width * width + 10 * rows * parts * width
        ),
        name="second_layer",
    )(spots, *mixed, *swapped, *tokens, out_w, ada)


def head_spots(seq, calls, pieces):
    if pieces == 1:
        return [0]
    own = [seq * calls + call for call in range(calls)]
    return own + [(1 - seq) * calls + call for call in range(pieces - calls)]


class Weights:
    def __init__(self, up, up_first, down, down_parts, hidden, width):
        self.up = up
        self.down = down
        self.width = width
        self.hidden = hidden
        fold = up.shape[3]
        self.block = min(512, fold, hidden // 2)
        per_chip = down_parts * down.shape[3]
        per_fold = fold // self.block
        chips, _, _, piece, _ = down.shape
        self.steps = hidden // self.block
        per_core = self.steps // 2
        block = self.block
        self.up_spec = pl.BlockSpec(
            (up.shape[0], 1, up.shape[2], block),
            lambda j: (0, up_first + j // per_fold, 0, j % per_fold),
        )
        self.down_spec = pl.BlockSpec(
            (block // per_chip, 1, down_parts, piece, width),
            lambda j: (j % per_core, j // per_core, 0, 0, 0),
        )
        self.per_chip = per_chip
        self.bytes = 2 * hidden * width


def hidden_kernel(per_chip, parts, x_ref, up_ref, down_ref, *refs):
    g_refs = refs[:parts]
    active_ref, grad_ref = refs[-2:]
    columns = min(256, active_ref.shape[1])
    size = x_ref.shape[0] // parts
    for start in range(0, active_ref.shape[1], columns):
        spot = slice(start, start + columns)
        up = up_ref[:, :, :, spot].reshape(-1, columns)
        chips = slice(start // per_chip, (start + columns) // per_chip)
        down = down_ref[chips].reshape(columns, -1)
        for index, g_ref in enumerate(g_refs):
            rows = slice(index * size, (index + 1) * size)
            upward = matmul(x_ref[rows, :], up)
            grad_active = matmul_last(g_ref[...], down)
            below = 0.5 * (1.0 + lax.erf(upward * ROOT_HALF))
            active_ref[rows, spot] = (upward * below).astype(jnp.bfloat16)
            slope = below + upward * (DENSITY * jnp.exp(-0.5 * upward * upward))
            grad_ref[rows, spot] = (grad_active * slope).astype(jnp.bfloat16)


def hidden_layer(x, grads, weights):
    rows, width = x.shape
    out = pl.BlockSpec((rows, weights.block), lambda j: (0, j))
    shape = jax.ShapeDtypeStruct((rows, weights.hidden), jnp.bfloat16)
    return pl.pallas_call(
        partial(hidden_kernel, weights.per_chip, len(grads)),
        grid=(weights.steps,),
        in_specs=[
            pl.BlockSpec((rows, width), lambda j: (0, 0)),
            weights.up_spec,
            weights.down_spec,
        ]
        + [pl.BlockSpec(grad.shape, lambda j: (0, 0)) for grad in grads],
        out_specs=[out, out],
        out_shape=[shape, shape],
        compiler_params=BIG,
        cost_estimate=cost(
            4 * rows * width * weights.hidden,
            2 * weights.bytes + 4 * rows * (width + weights.hidden),
        ),
        name="hidden_layer",
    )(x, weights.up, weights.down, *grads)


def accumulate(part, outs, total):
    step = pl.program_id(0)

    @pl.when(step == 0)
    def _():
        total[...] = part

    @pl.when(step > 0)
    def _():
        total[...] += part

    @pl.when(step == pl.num_programs(0) - 1)
    def _():
        rows = total.shape[0] // len(outs)
        for index, out_ref in enumerate(outs):
            value = total[index * rows : (index + 1) * rows, :]
            out_ref[...] = value.astype(out_ref.dtype)


def down_kernel(splits, a_ref, down_ref, *refs):
    total = refs[-1]
    part = matmul(a_ref[...], down_ref[...].reshape(-1, total.shape[1]))
    accumulate(part, refs[-1 - splits : -1], total)


def up_back_kernel(splits, g_ref, up_ref, *refs):
    total = refs[-1]
    weights = up_ref[...].reshape(total.shape[1], -1)
    accumulate(matmul_last(g_ref[...], weights), refs[-1 - splits : -1], total)


def hidden_to_width(kernel, name, held, weights, spec, array, rows, chunk, dtype, behind, splits=1):
    width = weights.width
    outs = pl.pallas_call(
        partial(kernel, splits),
        grid=(weights.steps,),
        in_specs=[pl.BlockSpec((rows, weights.block), lambda j: (chunk, j)), spec]
        + [ANYWHERE] * len(behind),
        out_specs=[pl.BlockSpec((rows // splits, width), lambda j: (0, 0))] * splits,
        out_shape=[jax.ShapeDtypeStruct((rows // splits, width), dtype)] * splits,
        scratch_shapes=[pltpu.VMEM((rows, width), jnp.float32)],
        compiler_params=BIG,
        cost_estimate=cost(
            2 * rows * width * weights.hidden,
            weights.bytes + rows * (2 * weights.hidden + 4 * width),
        ),
        name=name,
    )(held, array, *behind)
    return outs[0] if splits == 1 else outs


def down_part(active, weights, rows, chunk, dtype, behind=()):
    return hidden_to_width(
        down_kernel,
        "down_part",
        active,
        weights,
        weights.down_spec,
        weights.down,
        rows,
        chunk,
        dtype,
        behind,
    )


def up_back(grad, weights, rows, chunk, dtype, behind=(), splits=1):
    return hidden_to_width(
        up_back_kernel,
        "up_back",
        grad,
        weights,
        weights.up_spec,
        weights.up,
        rows,
        chunk,
        dtype,
        behind,
        splits,
    )


def middle_back_kernel(pieces, parts, place, *refs):
    own_ref, base_ref, top_ref, ada_ref, out_w = refs[:5]
    others = refs[5 : 5 + parts]
    outs = refs[-3 - pieces :]
    grad_ref, low_ref, ada_grad_ref = outs[:3]
    grad = own_ref[...] + current(others, 2).astype(jnp.float32)
    normed, inverse = standardise(base_ref[...])
    scaled = grad * (1.0 + ada_ref[0:1, :])
    scale = jnp.sum(grad * normed, axis=0, keepdims=True)
    shift = jnp.sum(grad, axis=0, keepdims=True)
    inner = jnp.mean(scaled * normed, axis=-1, keepdims=True)
    shifted = scaled - jnp.mean(scaled, axis=-1, keepdims=True) - normed * inner
    out = top_ref[...].astype(jnp.float32) + inverse * shifted
    grad_ref[...] = out
    low = out.astype(jnp.bfloat16)
    low_ref[...] = low
    weights = out_w.reshape(out_w.shape[0] * out_w.shape[2], out_w.shape[3])
    spots = head_spots(1 - place[4], 1, pieces)
    for index, mixed_ref in enumerate(outs[3:]):
        size = mixed_ref.shape[1]
        start = pl.multiple_of(spots[index] * size, size)
        mixed_ref[...] = matmul_last(low, weights[pl.ds(start, size), :]).astype(jnp.bfloat16)
    add_rows(ada_grad_ref, scale, shift)


def middle_back(own, other, attended, cotangent, ada, out_w, out_part, spots, sizes, behind):
    rows, width = attended.shape
    count = 2
    block = lambda size: pl.BlockSpec((rows // count, size), lambda j, s: (j, 0))
    items, _, piece, _ = out_w.shape
    _, other_specs = row_specs(other, count)
    return pl.pallas_call(
        partial(middle_back_kernel, len(sizes), len(other)),
        grid_spec=pltpu.PrefetchScalarGridSpec(
            num_scalar_prefetch=1,
            grid=(count,),
            in_specs=[block(width)] * 3
            + [
                pl.BlockSpec((2, width), lambda j, s: (0, 0)),
                pl.BlockSpec((items, 1, piece, width), lambda j, s: (0, out_part, 0, 0)),
            ]
            + other_specs
            + [ANYWHERE] * len(behind),
            out_specs=[block(width), block(width), pl.BlockSpec((2, width), lambda j, s: (0, 0))]
            + [block(size) for size in sizes],
        ),
        out_shape=[
            jax.ShapeDtypeStruct((rows, width), jnp.float32),
            jax.ShapeDtypeStruct((rows, width), jnp.bfloat16),
            jax.ShapeDtypeStruct((2, width), jnp.float32),
        ]
        + [jax.ShapeDtypeStruct((rows, size), jnp.bfloat16) for size in sizes],
        compiler_params=BIG,
        cost_estimate=cost(2 * rows * width * width, 2 * width * width + 20 * rows * width),
        name="middle_back",
    )(spots, own, attended, cotangent, ada, out_w, *other, *behind)


def first_back_kernel(splits, grad_ref, weight_ref, frames, *refs):
    outs, ada_grad_ref = refs[-1 - splits : -1], refs[-1]
    grad = matmul_last(grad_ref[...], weight_ref[...])
    normed, _ = standardise(frames[...].astype(jnp.float32))
    for index, out_ref in enumerate(outs):

        @pl.when((pl.program_id(0) == index) | (splits == 1))
        def _(out_ref=out_ref):
            out_ref[...] = grad.astype(jnp.bfloat16)

    scale = jnp.sum(grad * normed, axis=0, keepdims=True)
    shift = jnp.sum(grad, axis=0, keepdims=True)
    add_rows(ada_grad_ref, scale, shift)


def first_back(grad, weights, frames, part, behind, splits=1):
    width, columns = weights.shape
    count = 2
    rows = frames.shape[0] // count
    block = pl.BlockSpec((rows, width), lambda j: (j, 0))
    out = block if splits == 1 else pl.BlockSpec((rows, width), lambda j: (0, 0))
    return pl.pallas_call(
        partial(first_back_kernel, splits),
        grid=(count,),
        in_specs=[
            pl.BlockSpec((rows, columns), lambda j: (part * count + j, 0)),
            pl.BlockSpec((width, columns), lambda j: (0, 0)),
            block,
        ]
        + [ANYWHERE] * len(behind),
        out_specs=[out] * splits + [pl.BlockSpec((2, width), lambda j: (0, 0))],
        out_shape=[jax.ShapeDtypeStruct((rows * count // splits, width), jnp.bfloat16)] * splits
        + [jax.ShapeDtypeStruct((2, width), jnp.float32)],
        compiler_params=BIG,
        cost_estimate=cost(
            2 * rows * count * width * columns,
            2 * width * columns + 2 * rows * count * (2 * width + columns),
        ),
        name="first_back",
    )(grad, weights, frames, *behind)


def stacked_dot(lefts, rights):
    total = None
    for left, right in zip(lefts, rights):
        part = dot_rows(left, right)
        total = part if total is None else total + part
    return total


def cut_rows(ref, count):
    rows = ref.shape[0] // count
    return [ref[j * rows : (j + 1) * rows, :] for j in range(count)]


def put_sum(out_ref, other_ref, value):
    if other_ref is not None:
        value = value + other_ref[...].astype(jnp.float32)
    out_ref[...] = value.astype(jnp.bfloat16)


def put_first(place, out_ref, firsts):
    for index, ref in enumerate(firsts):
        rows = ref.shape[0]
        start = pl.multiple_of(place[5 + index] * rows, rows)
        ref[...] = out_ref[pl.ds(start, rows), :]


def ring_outputs(width, columns, block, more, chips):
    rows = [width] + [width // chips] * (2 if more else 0)
    specs = [pl.BlockSpec((size, block), lambda j, s: (0, j)) for size in rows]
    return specs, [jax.ShapeDtypeStruct((size, columns), jnp.bfloat16) for size in rows]


def hidden_grads_kernel(count, more, place, *refs):
    active, upward = refs[:2]
    grads, low = refs[2 : 2 + count], refs[2 + count]
    other = refs[3 + count] if more else None
    outs = refs[-3:] if more else refs[-1:]
    out_ref = outs[0]
    step = pl.program_id(0)
    steps = pl.num_programs(0) // 2

    @pl.when(step < steps)
    def _():
        put_sum(
            out_ref, other, stacked_dot(cut_rows(active, count), [ref[...] for ref in grads])
        )

    @pl.when(step >= steps)
    def _():
        put_sum(out_ref, other, dot_rows(low[...], upward[...]))

    put_first(place, out_ref, outs[1:])


def hidden_grads(place, who, chips, active, upward, grads, low, other, behind):
    total, hidden = active.shape
    half = hidden // 2
    rows, width = grads[0].shape
    count = len(grads)
    block = 512
    steps = half // block
    whole = pl.BlockSpec((total, width), lambda j, s: (0, 0))
    grad = pl.BlockSpec((rows, block), lambda j, s: (0, jnp.minimum(j, steps - 1)))
    out = pl.BlockSpec((width, block), lambda j, s: (0, j))
    more = [] if other is None else [other]
    specs, shapes = ring_outputs(width, 2 * half, block, more, chips)
    return pl.pallas_call(
        partial(hidden_grads_kernel, count, bool(more)),
        grid_spec=pltpu.PrefetchScalarGridSpec(
            num_scalar_prefetch=1,
            grid=(2 * steps,),
            in_specs=[
                pl.BlockSpec((total, half), lambda j, s: (0, s[who])),
                pl.BlockSpec(
                    (total, block), lambda j, s: (0, s[who] * steps + jnp.maximum(j - steps, 0))
                ),
            ]
            + [grad] * count
            + [whole]
            + [out] * len(more)
            + [ANYWHERE] * len(behind),
            out_specs=specs,
        ),
        out_shape=shapes,
        compiler_params=BIG,
        cost_estimate=cost(4 * total * half * width, 8 * total * half + 4 * width * half),
        name="hidden_grads",
    )(place, active, upward, *grads, low, *more, *behind)


def tail_grads_kernel(first, more, pieces, calls, place, low, grad, attended, *refs):
    mixed = refs[:pieces]
    other = refs[pieces] if more else None
    outs = refs[-3:] if more else refs[-1:]
    out_ref = outs[0]

    @pl.when(pl.program_id(0) < first)
    def _():
        put_sum(out_ref, other, dot_rows(low[...], grad[...]))

    @pl.when(pl.program_id(0) >= first)
    def _():
        spots = head_spots(place[4], calls, pieces)
        for index, piece in enumerate(mixed):
            size = piece.shape[1]
            rows = pl.ds(pl.multiple_of(spots[index] * size, size), size)
            value = dot_rows(piece[...], attended[...])
            if more:
                value = value + other[rows, :].astype(jnp.float32)
            out_ref[rows, :] = value.astype(jnp.bfloat16)

    put_first(place, out_ref, outs[1:])


def tail_grads(place, who, chips, low_one, grad_qkv, mixed, swapped, attended_low, other, behind):
    total, width = low_one.shape
    rows = attended_low.shape[0]
    block = 256
    first = grad_qkv.shape[1] // 2 // block
    second = width // 2 // block
    out = pl.BlockSpec((width, block), lambda j, s: (0, j))
    more = [] if other is None else [other]
    specs, shapes = ring_outputs(width, (first + second) * block, block, more, chips)
    return pl.pallas_call(
        partial(
            tail_grads_kernel, first, bool(more), len(mixed) + len(swapped), len(mixed)
        ),
        grid_spec=pltpu.PrefetchScalarGridSpec(
            num_scalar_prefetch=1,
            grid=(first + second,),
            in_specs=[
                pl.BlockSpec((total, width), lambda j, s: (0, 0)),
                pl.BlockSpec(
                    (total, block), lambda j, s: (0, s[who] * first + jnp.minimum(j, first - 1))
                ),
                pl.BlockSpec(
                    (rows, block), lambda j, s: (0, s[who] * second + jnp.maximum(j - first, 0))
                ),
            ]
            + [pl.BlockSpec((rows, part.shape[1]), lambda j, s: (0, 0)) for part in mixed]
            + [pl.BlockSpec((rows, part.shape[1]), lambda j, s: (1, 0)) for part in swapped]
            + [out] * len(more)
            + [ANYWHERE] * len(behind),
            out_specs=specs,
        ),
        out_shape=shapes,
        compiler_params=BIG,
        cost_estimate=cost(
            2 * width * block * (total * first + rows * second), 8 * total * width
        ),
        name="tail_grads",
    )(place, low_one, grad_qkv, attended_low, *mixed, *swapped, *more, *behind)


def input_back_kernel(parts, count, own_ref, tokens_ref, ada_ref, base_ref, *refs):
    out_ref = refs[-1]
    grad = own_ref[...].astype(jnp.float32) + current(refs[:parts], count).astype(jnp.float32)
    normed, inverse = standardise(tokens_ref[...].astype(jnp.float32))
    scaled = grad * (1.0 + ada_ref[0:1, :])
    inner = jnp.mean(scaled * normed, axis=-1, keepdims=True)
    shifted = scaled - jnp.mean(scaled, axis=-1, keepdims=True) - normed * inner
    out_ref[...] = base_ref[...] + inverse * shifted


def input_back(own, others, tokens, ada, base):
    rows, width = tokens.shape
    count = 4
    block = pl.BlockSpec((rows // count, width), lambda j: (j, 0))
    _, specs = row_specs(others, count)
    return pl.pallas_call(
        partial(input_back_kernel, len(others), count),
        grid=(count,),
        in_specs=[block, block, pl.BlockSpec((2, width), lambda j: (0, 0)), block] + specs,
        out_specs=block,
        out_shape=jax.ShapeDtypeStruct((rows, width), jnp.float32),
        compiler_params=BIG,
        cost_estimate=cost(20 * rows * width, 14 * rows * width),
        name="input_back",
    )(own, tokens, ada, base, *others)


def join_tail_kernel(held, place, mine, seq_ref, core_ref, both_ref, *outs):
    core, seq = place[2], place[4]
    half = 3 * held // 2
    width = held // 2

    def chosen(side, core_half, spot):
        near = jnp.where(core == core_half, mine[:, spot], core_ref[:, spot])
        far = jnp.where(core == core_half, seq_ref[:, spot], both_ref[:, spot])
        return jnp.where(seq == side, near, far)

    for side in range(2):
        for core_half in range(2):
            for pair in range(width // LANES):
                for which in range(3):
                    start = (3 * pair + which) * LANES
                    to = side * held + core_half * width + pair * LANES
                    value = chosen(side, core_half, slice(start, start + LANES))
                    outs[which][:, to : to + LANES] = value
    for core_half in range(2):
        spot = slice(half, None)
        near = jnp.where(core == core_half, mine[:, spot], core_ref[:, spot])
        far = jnp.where(core == core_half, seq_ref[:, spot], both_ref[:, spot])
        outs[3][:, core_half * held : (core_half + 1) * held] = near + far


def join_tail(place, parts, held):
    rows, columns = parts[0].shape
    whole = lambda size: pl.BlockSpec((rows, size), lambda j, s: (0, 0))
    return pl.pallas_call(
        partial(join_tail_kernel, held),
        grid_spec=pltpu.PrefetchScalarGridSpec(
            num_scalar_prefetch=1,
            grid=(1,),
            in_specs=[whole(columns)] * 4,
            out_specs=[whole(2 * held)] * 4,
        ),
        out_shape=[jax.ShapeDtypeStruct((rows, 2 * held), jnp.float32)] * 4,
        cost_estimate=cost(0, 16 * rows * columns),
        name="join_tail",
    )(place, *parts)


def exact(left, right):
    return jnp.dot(left, right, precision=lax.Precision.HIGHEST)


def rounded(total, other=None):
    if other is not None:
        total = total + other.astype(jnp.float32)
    return total.astype(jnp.bfloat16)


def tie(*values):
    return lax.optimization_barrier(values)


def cut(value, start, size, axis):
    return lax.dynamic_slice_in_dim(value, start, size, axis, allow_negative_indices=False)


def pick(value, index, axis):
    return lax.dynamic_index_in_dim(
        value, index, axis, keepdims=False, allow_negative_indices=False
    )


def ring_of(items_count):
    chips = items_count // 2
    outer = 4 if chips % 4 == 0 else chips
    inner = chips // outer
    order = [a * inner for a in range(outer)]
    for turn, a in enumerate(reversed(range(outer))):
        beside = list(range(1, inner))
        order += [a * inner + b for b in (beside if turn % 2 == 0 else beside[::-1])]
    return order


class Mover:
    def __init__(self, items_count, seq_count):
        self.items_count = items_count
        self.seq_count = seq_count
        self.pair = seq_count == 2
        self.chips = items_count // 2
        order = ring_of(items_count)
        self.forward = []
        self.backward = []
        chips = self.chips
        table = np.zeros((items_count, 2 * chips + 2), np.int32)
        hops = list(range(chips // 2 + 1)) + [-hop for hop in range(1, (chips + 1) // 2)]
        for spot in range(self.chips):
            for core in range(2):
                here = 2 * order[spot] + core
                next_one = 2 * order[(spot + 1) % self.chips] + core
                self.forward.append((here, next_one))
                self.backward.append((next_one, here))
                for ahead in range(self.chips):
                    table[here, ahead] = order[(spot + ahead) % self.chips]
                table[here, chips] = core
                table[here, chips + 1] = 1 - core
                for spot_of, hop in enumerate(hops):
                    ahead = hop if core == 1 else -hop
                    table[here, chips + 2 + spot_of] = order[(spot + ahead) % chips]
        self.both_ways = [p for p in self.forward if p[0] % 2 == 0]
        self.both_ways += [p for p in self.backward if p[0] % 2 == 1]
        self.item = lax.axis_index("items")
        row = pick(jnp.asarray(table), self.item, 0)
        self.ahead = [row[j] for j in range(self.chips)]
        self.core = row[self.chips]
        self.beside = row[self.chips + 1]
        self.spots = row[self.chips + 2 :]
        self.seq = lax.axis_index("seq")
        self.quarter = 2 * self.core + self.seq

    def flip(self, value, bit):
        pairs = [(i, i ^ bit) for i in range(self.items_count)]
        return lax.ppermute(value, "items", pairs)

    def opposite(self, value):
        pairs = [(2 * i + x, 2 * (i ^ 1) + 1 - x) for i in range(self.items_count) for x in (0, 1)]
        return lax.ppermute(value, ("items", "seq"), pairs)

    def across(self, value):
        return lax.ppermute(value, "seq", [(0, 1), (1, 0)])

    def gather_items(self, value, summed, early, late):
        for bit in [1 << k for k in range(self.items_count.bit_length() - 1)]:
            summed = summed + self.flip(summed, bit)
        beside = self.flip(value, 1)
        block = jnp.where(
            self.core == 0,
            jnp.concatenate([value, beside], axis=0),
            jnp.concatenate([beside, value], axis=0),
        )
        direct = [block]
        for hop in range(1, self.chips // 2 + 1):
            moved = lax.ppermute(direct[-1], "items", self.both_ways)
            if hop == min(LATE_HOP, self.chips // 2):
                late, summed, moved, early = tie(late, summed, moved, early)
            direct.append(moved)
        beside = [self.flip(moved, 1) for moved in direct[1 : (self.chips + 1) // 2]]
        return direct + beside, summed, early, late

    def sum_seq(self, value):
        return value + self.across(value) if self.pair else lax.psum(value, "seq")

    def scatter_seq(self, value):
        rows = value.shape[0] // self.seq_count
        if self.pair:
            sent = cut(value, (1 - self.seq) * rows, rows, 0)
            kept = cut(value, self.seq * rows, rows, 0)
            return kept + self.across(sent.astype(jnp.bfloat16)).astype(jnp.float32)
        return lax.psum_scatter(
            value.astype(jnp.bfloat16), "seq", scatter_dimension=0, tiled=True
        ).astype(jnp.float32)

    def join_cores(self, value):
        parts = value.reshape(2, -1, value.shape[1])
        kept = pick(parts, self.core, 0)
        other = self.flip(pick(parts, self.beside, 0), 1)
        return jnp.where(self.core == 0, kept, other), jnp.where(self.core == 0, other, kept)

    def join_columns(self, value):
        rows = value.shape[0] // self.seq_count
        if self.pair:
            kept = cut(value, self.seq * rows, rows, 0)
            other = self.across(cut(value, (1 - self.seq) * rows, rows, 0))
            return jnp.where(self.seq == 0, kept, other), jnp.where(self.seq == 0, other, kept)
        moved = lax.all_to_all(value, "seq", split_axis=0, concat_axis=0, tiled=True)
        return tuple(moved[j * rows : (j + 1) * rows] for j in range(self.seq_count))


class RingSum:
    def __init__(self, mover, make, behind, ready=()):
        self.mover = mover
        self.chips = mover.chips
        self.make = make
        self.flows = None
        sent, self.ready = tie(make(False, None, behind)[0], list(ready))
        self.sent = sent
        self.arriving = [mover.flip(sent, 1)]

    def block(self, ahead):
        return pick(self.both, self.mover.ahead[ahead % self.chips], 0)

    def add_own(self, behind):
        self.whole, *firsts = self.make(True, self.arriving[0], behind)
        self.both = self.whole.reshape(self.chips, -1, self.whole.shape[1])
        self.arrived = []
        flows = [
            (self.mover.forward, 1, self.chips // 2),
            (self.mover.backward, -1, (self.chips - 1) // 2),
        ]
        if not firsts:
            firsts = [self.block(sign * left) for _, sign, left in flows]
        self.send(list(zip(flows, firsts)))

    def send(self, flows):
        self.arriving = [lax.ppermute(value, "items", flow[0]) for flow, value in flows]
        self.flows = [(pairs, sign, left - 1) for (pairs, sign, left), _ in flows]

    def advance(self, anchor=None):
        flows = []
        if anchor is not None:
            self.arriving, anchor = tie(self.arriving, anchor)
        for flow, value in zip(self.flows, self.arriving):
            if flow[2]:
                flows.append((flow, self.block(flow[1] * flow[2]) + value))
            else:
                self.arrived.append(value)
        self.send(flows)
        return anchor

    def finish(self, anchor=None):
        while self.arriving:
            self.advance()
        if anchor is not None:
            self.arrived, anchor = tie(self.arrived, anchor)
        result = self.block(0).astype(jnp.float32)
        for value in self.arrived:
            result = result + value.astype(jnp.float32)
        return result if anchor is None else (result, anchor)


def in_rows(value):
    return with_layout_constraint(value, Layout((0, 1)))


def halves(value, core):
    half = value.shape[1] // 2
    return cut(value, core * half, half, 1)


def parted(value, at):
    return (None, None) if value is None else (value[:, :at], value[:, at:])


def shards(
    tokens,
    cotangent,
    prompt_len,
    section_ids,
    section_table,
    w_query,
    w_key,
    w_value,
    w_out,
    w_up,
    w_down,
    w_ada_one,
    w_ada_two,
):
    items_count = lax.axis_size("items")
    seq_count = lax.axis_size("seq")
    mover = Mover(items_count, seq_count)
    chips = mover.chips
    batch, rows, width = tokens.shape
    total_rows = rows * seq_count
    hidden = w_up.shape[1] // seq_count
    held = width // seq_count
    pairs = held // LANES
    piece = w_query.shape[0]
    units = w_down.shape[0] // seq_count
    tokens = tokens.reshape(rows, width)
    grad_low = cotangent.reshape(rows, width)

    def quarters(one, two):
        return jnp.stack([one[:, :width], one[:, width:], two[:, :width], two[:, width:]])

    up_shard = w_up.reshape(piece, chips, 2, seq_count, units).transpose(3, 0, 2, 1, 4)
    up_shard = pick(up_shard, mover.seq, 0).reshape(piece, hidden)
    down_shard = cut(w_down, mover.seq * units, units, 0)
    merged = hidden % width == 0 and units % piece == 0
    late = down_shard
    if merged:
        folds = hidden // width
        down_parts = units // piece
        up_rows = [up_shard[:, j * width : (j + 1) * width] for j in range(folds)]
        late = jnp.concatenate([down_shard] + up_rows + [w_out], axis=0)

    table_part = cut(section_table, mover.item * piece, piece, 1)
    ada_part = jnp.dot(
        table_part,
        jnp.concatenate([w_ada_one, w_ada_two], axis=1),
        preferred_element_type=jnp.float32,
    )
    ada_part = quarters(ada_part[:, : 2 * width], ada_part[:, 2 * width :])
    prompt_at = mover.seq if mover.pair else jnp.zeros((), jnp.int32)
    place = jnp.stack(
        [prompt_at, prompt_len[0], mover.core, mover.beside, mover.seq]
        + [mover.ahead[chips // 2], mover.ahead[-((chips - 1) // 2) % chips]]
    )
    seq_place = jnp.reshape(mover.seq, (1,)).astype(jnp.int32)
    mine = pack_columns(w_query, w_key, w_value, held, seq_place)
    early = [mover.across(tokens)] if mover.pair else []
    blocks, ada_sum, early, late = mover.gather_items(
        mine, ada_part, early, late
    )

    def gathered(value):
        return lax.all_gather(value, "items", axis=0, tiled=False)

    if merged:
        rest = gathered(late)
        rest = rest.reshape(items_count, down_parts + folds + 1, piece, width)
        by_core = rest.reshape((chips, 2) + rest.shape[1:])
        weights = Weights(rest, down_parts, by_core, down_parts, hidden, width)
        out_w, out_part = rest, down_parts + folds
    else:
        by_core = gathered(late).reshape(chips, 2, 1, units, width)
        weights = Weights(gathered(up_shard)[:, None], 0, by_core, 1, hidden, width)
        out_w, out_part = gathered(w_out)[:, None], 0

    choose = (section_ids[0] == jnp.arange(section_table.shape[0])).astype(jnp.float32)
    ada = jnp.sum(choose[None, :, None] * ada_sum, axis=1)
    ada_one = ada[:2]
    ada_two = ada[2:]

    if mover.pair:
        tokens_other, grad_sent = tie(early[0], grad_low)
        grad_other = mover.across(grad_sent)
        frames = [tokens, tokens_other]
        grads = [grad_low, grad_other]
        calls = 2 if pairs % 2 == 0 else 1
    else:
        frames = [lax.all_gather(tokens, "seq", axis=0, tiled=True)]
        grads = [lax.all_gather(grad_low, "seq", axis=0, tiled=True)]
        calls = 1
    low_one, qkv, qkv_w = first_layer(frames, ada_one, blocks, mover.spots)
    per_call = pairs // calls
    mixed_heads = []
    lse = []
    for call in range(calls):
        behind = grads[1:] + mixed_heads
        out = attend(qkv, place, call * per_call, per_call, behind)
        mixed_heads.append(out[0])
        lse.append(out[1])
    if mover.pair:
        mixed_far = []
        for call in range(calls):
            sent = mixed_heads[call]
            if mixed_far:
                sent, mixed_far[-1] = tie(sent, mixed_far[-1])
            mixed_far.append(mover.across(sent))
        attended, low_two = second_layer(
            mixed_heads, mixed_far, frames[::-1], out_w, out_part, ada_two, place
        )
        lows = low_two
        active, upward = hidden_layer(lows, grads, weights)
        first_half, last_half = up_back(upward, weights, rows, 1, jnp.bfloat16, (), 2)
        start = [first_half]
        ready = [mover.across(first_half), last_half]
    else:
        mixed = lax.all_to_all(mixed_heads[0], "seq", split_axis=0, concat_axis=1, tiled=True)
        attended, low_two = second_layer(
            [mixed], [], [tokens], out_w, out_part, ada_two, place
        )
        lows = lax.all_gather(low_two, "seq", axis=0, tiled=True)
        active, upward = hidden_layer(lows, grads, weights)
        start = []
        ready = []

    down_columns = hidden // 2

    def hidden_parts(own, other, behind):
        who = 2 if own else 3
        if down_columns == width:
            return hidden_grads(place, who, chips, active, upward, grads, lows, other, behind)
        core = mover.core if own else mover.beside
        first, second = parted(other, down_columns)
        down = dot_rows(halves(active, core), grads[0]).reshape(width, down_columns)
        up = dot_rows(lows, halves(upward, core))
        return [in_rows(jnp.concatenate([rounded(down, first), rounded(up, second)], axis=1))]

    ring = RingSum(mover, hidden_parts, start, ready)
    if mover.pair:
        own = up_back(upward, weights, rows, 0, jnp.float32, [ring.sent])
        from_other = [ring.ready[0], mover.across(ring.ready[1])]
        sizes = [held, held]
    else:
        own = lax.psum_scatter(
            up_back(upward, weights, total_rows, 0, jnp.bfloat16),
            "seq",
            scatter_dimension=0,
            tiled=True,
        ).astype(jnp.float32)
        from_other = [jnp.zeros((rows, width), jnp.bfloat16)]
        sizes = [width]
    ring.add_own([own])
    grad_attended, attended_low, ada_two_rows, *grad_mixed = middle_back(
        own,
        from_other,
        attended,
        grad_low,
        ada_two,
        out_w,
        out_part,
        place,
        sizes,
        [ring.whole],
    )
    if mover.pair:
        out_other = down_part(active, weights, rows, 1, jnp.bfloat16, grad_mixed[:1])
        grad_heads = [grad_mixed[1], mover.across(grad_mixed[0])]
        out_other = ring.advance(out_other)
        out_own = down_part(active, weights, rows, 0, jnp.float32, [out_other])
        filler = [out_own]
        out_other = mover.across(out_other)
    else:
        grad_heads = [
            lax.all_to_all(grad_mixed[0], "seq", split_axis=1, concat_axis=0, tiled=True)
        ]
        filler = []

    split = pairs // 2 if pairs % 2 == 0 else 0

    def tail_parts(own, other, behind):
        if mover.pair:
            return tail_grads(
                place,
                2 if own else 3,
                chips,
                low_one,
                grad_qkv,
                mixed_heads,
                mixed_far,
                attended_low,
                other,
                behind,
            )
        core = mover.core if own else mover.beside
        first, second = parted(other, grad_qkv.shape[1] // 2)
        qkv_part = rounded(dot_rows(low_one, halves(grad_qkv, core)), first)
        out_part = rounded(dot_rows(mixed, halves(attended_low, core)), second)
        return [in_rows(jnp.concatenate([qkv_part, out_part], axis=1))]

    tail = None
    grad_qkv = None
    for turn in range(pairs):
        behind = filler
        filler = []
        grad_qkv = attend_back(
            place, turn, pairs, qkv, mixed_heads, grad_heads, lse, grad_qkv, behind
        )
        grad_qkv = ring.advance(grad_qkv)
        if turn + 1 == split:
            tail = RingSum(mover, tail_parts, [])
            filler = [tail.sent]
    if tail is None:
        tail = RingSum(mover, tail_parts, [])
    tail.add_own([])
    if mover.pair:
        near_half, last_half, far_rows = first_back(
            grad_qkv, qkv_w, frames[1], 1, [tail.whole, out_other], 2
        )
        near_half = mover.across(near_half)
        last_half = tail.advance(last_half)
        hidden_total, last_half = ring.finish(last_half)
        own_first, own_rows = first_back(grad_qkv, qkv_w, frames[0], 0, [last_half])
        own_rows, near_half, last_half, out_other = tail.advance(
            [own_rows, near_half, last_half, out_other]
        )
        far_parts = [near_half, mover.across(last_half)]
        ada_rows = jnp.concatenate([own_rows + far_rows, ada_two_rows])
        ada_rows = ada_rows + mover.across(ada_rows)
        layer_sum = out_own + out_other.astype(jnp.float32)
    else:
        grad_first, ada_one_rows = first_back(grad_qkv, qkv_w, frames[0], 0, [tail.whole])
        ada_rows = lax.psum(jnp.concatenate([ada_one_rows, ada_two_rows]), "seq")
        own_first = lax.psum_scatter(grad_first, "seq", scatter_dimension=0, tiled=True)
        far_parts = [jnp.zeros((rows, width), jnp.bfloat16)]
        hidden_total = ring.finish()
        layer_sum = lax.psum_scatter(
            down_part(active, weights, total_rows, 0, jnp.bfloat16),
            "seq",
            scatter_dimension=0,
            tiled=True,
        ).astype(jnp.float32)
    layer_out = (attended + layer_sum).astype(jnp.bfloat16)
    sums = choose[None, :, None] * ada_rows[:, None, :]
    for bit in [1 << k for k in range(items_count.bit_length() - 1)]:
        sums = sums + mover.flip(sums, bit)
        if bit == 1:
            sums = tail.advance(sums)
        if bit == 4:
            sums, far_parts = tie(sums, far_parts)
    input_grad = input_back(own_first, far_parts, tokens, ada_one, grad_attended)
    out_piece = piece // seq_count
    first_row = mover.item * piece + mover.seq * out_piece
    table_rows = cut(section_table, first_row, out_piece, 1).astype(jnp.float32)
    ada_grads = jnp.einsum("sr,ksd->krd", table_rows, sums, precision=lax.Precision.HIGHEST)
    grad_ada_one = jnp.concatenate([ada_grads[0], ada_grads[1]], axis=1)
    grad_ada_two = jnp.concatenate([ada_grads[2], ada_grads[3]], axis=1)
    own_ada = quarters(
        *(cut(w, mover.seq * out_piece, out_piece, 0) for w in (w_ada_one, w_ada_two))
    ).astype(jnp.float32)
    grad_table = jnp.einsum("ksd,krd->sr", sums, own_ada, precision=lax.Precision.HIGHEST)

    grad_down = hidden_total[:, :down_columns].reshape(units, width)
    up_sides = mover.join_columns(
        jnp.concatenate(mover.join_cores(hidden_total[:, down_columns:]), axis=1)
    )
    grad_up = jnp.stack(
        [side.reshape(out_piece, 2, chips, units) for side in up_sides], axis=1
    )
    grad_up = grad_up.transpose(0, 3, 2, 1, 4).reshape(out_piece, hidden * seq_count)
    if mover.pair:
        quarters_of = tail.finish().reshape(4, piece // 2, -1)
        mine, to_seq, to_core, to_both = (
            pick(quarters_of, mover.quarter ^ flipped, 0) for flipped in (0, 1, 2, 3)
        )
        grad_query, grad_key, grad_value, grad_out = join_tail(
            place,
            [mine, mover.across(to_seq), mover.flip(to_core, 1), mover.opposite(to_both)],
            held,
        )
    else:
        tail_total = tail.finish()
        cores = jnp.concatenate(mover.join_cores(tail_total), axis=1)
        half_qkv = 3 * held // 2
        half_all = cores.shape[1] // 2
        qkv_total = jnp.concatenate(
            [cores[:, :half_qkv], cores[:, half_all : half_all + half_qkv]], axis=1
        )
        out_total = jnp.concatenate([cores[:, half_qkv:half_all], cores[:, half_all + half_qkv :]], axis=1)
        sides = mover.join_columns(qkv_total)
        grad_out = mover.scatter_seq(out_total)
        grad_query, grad_key, grad_value = (
            jnp.concatenate(
                [
                    side[:, (3 * p + j) * LANES : (3 * p + j + 1) * LANES]
                    for side in sides
                    for p in range(pairs)
                ],
                axis=1,
            )
            for j in range(3)
        )
    return (
        layer_out.reshape(batch, rows, width),
        input_grad.reshape(batch, rows, width),
        grad_query,
        grad_key,
        grad_value,
        grad_out,
        grad_up,
        grad_down,
        grad_ada_one,
        grad_ada_two,
        grad_table,
    )


def solution(mesh):
    return jax.shard_map(
        shards,
        mesh=mesh,
        in_specs=(
            P("items", "seq", None),
            P("items", "seq", None),
            P("items"),
            P("items"),
            P(),
            P("items", None),
            P("items", None),
            P("items", None),
            P("items", None),
            P("items", None),
            P("items", None),
            P("items", None),
            P("items", None),
        ),
        out_specs=(
            P("items", "seq", None),
            P("items", "seq", None),
            P(("items", "seq"), None),
            P(("items", "seq"), None),
            P(("items", "seq"), None),
            P(("items", "seq"), None),
            P(("items", "seq"), None),
            P(("items", "seq"), None),
            P(("items", "seq"), None),
            P(("items", "seq"), None),
            P(None, ("items", "seq")),
        ),
        check_vma=False,
    )
```

```python
from functools import partial
import math

import jax
import jax.numpy as jnp
import numpy as np
from jax import lax
from jax.experimental.layout import Layout, with_layout_constraint
from jax.experimental import pallas as pl
from jax.experimental.pallas import tpu as pltpu
from jax.sharding import PartitionSpec as P

HEAD_DIM = 64
SCALE = 0.125
MASKED = -1e30
COVER = 0.5
TILE = 128
LANES = 128

def row_ids(shape):
    return lax.broadcasted_iota(jnp.int32, shape, 0)
def lane_ids(shape):
    return lax.broadcasted_iota(jnp.int32, shape, 1)
def matmul(left, right):
    return jnp.dot(left, right, preferred_element_type=jnp.float32)
def twin_lanes(flipped):
    top = row_ids(flipped.shape) < HEAD_DIM
    return jnp.concatenate([jnp.where(top, flipped, 0.0), jnp.where(top, 0.0, flipped)], axis=1)
def twin_rows(block):
    first = lane_ids(block.shape) < HEAD_DIM
    return jnp.concatenate([jnp.where(first, block, 0.0), jnp.where(first, 0.0, block)], axis=0)
def untwin(wide):
    top = row_ids((LANES, LANES)) < HEAD_DIM
    return jnp.where(top, wide[:, :LANES], wide[:, LANES:]).T

def split3(value):
    high = value.astype(jnp.bfloat16).astype(jnp.float32)
    rest = value - high
    mid = rest.astype(jnp.bfloat16).astype(jnp.float32)
    return high, mid, rest - mid

def attend_kernel(place, q_ref, k_ref, v_ref, *refs):
    o_ref, lse_ref, keys_wide, values_t = refs[-4:]
    half = q_ref.shape[0] // 2
    prompt = pl.multiple_of(place[0] * half, TILE)
    target = pl.multiple_of((1 - place[0]) * half, TILE)
    length = place[1]
    shape = (half, LANES)
    keys_wide[:half, :LANES] = k_ref[pl.ds(prompt, half), :]
    keys_wide[half:, :LANES] = k_ref[pl.ds(target, half), :]
    hidden = (lane_ids(shape) == 0) & (row_ids(shape) >= length)
    keys_wide[:half, LANES:] = jnp.where(hidden, MASKED, 0.0).astype(jnp.bfloat16)
    keys_wide[half:, LANES:] = jnp.zeros(shape, jnp.bfloat16)
    for piece in range(half // TILE):
        rows = slice(piece * TILE, (piece + 1) * TILE)
        values_t[:, rows] = v_ref[pl.ds(prompt + piece * TILE, TILE), :].astype(jnp.float32).T.astype(jnp.bfloat16)
        rows = slice(half + piece * TILE, half + (piece + 1) * TILE)
        values_t[:, rows] = v_ref[pl.ds(target + piece * TILE, TILE), :].astype(jnp.float32).T.astype(jnp.bfloat16)
    below = jnp.where(row_ids((LANES, 2 * TILE)) == 0, 1.0, 0.0)

    def score(start, seen):
        q_flip = (q_ref[pl.ds(start, TILE), :].astype(jnp.float32) * SCALE).T
        q_wide = jnp.concatenate([twin_lanes(q_flip), below], axis=0).astype(jnp.bfloat16)
        return matmul(keys_wide[:seen, :], q_wide)

    def tile(scores, start, seen, slot):
        peak = jnp.max(scores, axis=0, keepdims=True)
        expo = jnp.exp(scores - peak)
        total = jnp.sum(expo, axis=0, keepdims=True)
        out = matmul(values_t[:, :seen], expo.astype(jnp.bfloat16)) / total
        o_ref[pl.ds(start, TILE), :] = untwin(out).astype(jnp.bfloat16)
        lse_ref[0, pl.ds(slot, 1), :] = peak + jnp.log(total)

    tiles = half // TILE

    @pl.loop(0, tiles)
    def _(index):
        at_prompt = pl.multiple_of(prompt + index * TILE, TILE)
        at_target = pl.multiple_of(target + index * TILE, TILE)
        first = score(at_prompt, half)
        second = score(at_target, 2 * half)
        tile(first, at_prompt, half, index)
        tile(second, at_target, 2 * half, tiles + index)


def attend(qkv, place, first, pairs, behind):
    rows = qkv.shape[0]
    width = pairs * LANES
    part = lambda shift: pl.BlockSpec((rows, LANES), lambda p, s, shift=shift: (0, 3 * (first + p) + shift))
    seen = rows * rows * 3 // 4
    return pl.pallas_call(
        attend_kernel,
        grid_spec=pltpu.PrefetchScalarGridSpec(
            num_scalar_prefetch=1, grid=(pairs,),
            in_specs=[part(0), part(1), part(2)] + [pl.BlockSpec(memory_space=pl.ANY)] * len(behind),
            out_specs=[pl.BlockSpec((rows, LANES), lambda p, s: (0, p)), pl.BlockSpec((1, rows // TILE, 2 * TILE), lambda p, s: (p, 0, 0))],
            scratch_shapes=[pltpu.VMEM((rows, 2 * LANES), jnp.bfloat16), pltpu.VMEM((LANES, rows), jnp.bfloat16)],
        ),
        out_shape=[jax.ShapeDtypeStruct((rows, width), jnp.bfloat16),
                   jax.ShapeDtypeStruct((pairs, rows // TILE, 2 * TILE), jnp.float32)],
        compiler_params=pltpu.CompilerParams(vmem_limit_bytes=60 << 20),
        cost_estimate=pl.CostEstimate(flops=int(COVER * pairs * 2 * seen * 4 * HEAD_DIM * 4), transcendentals=0, bytes_accessed=rows * width * 8),
        name="attend",
    )(place, qkv, qkv, qkv, *behind)


def attend_back_kernel(parts, calls, per, at, place, q_ref, k_ref, v_ref, *refs):
    o_refs, lse_refs, g_refs = refs[:calls], refs[calls:2 * calls], refs[2 * calls:2 * calls + parts]
    out_ref, keys_wide, values_wide, keys_t, dq, dk, dv = refs[-7:]
    half = q_ref.shape[0] // 2
    step = pl.program_id(0)
    prompt = pl.multiple_of(place[0] * half, TILE)
    target = pl.multiple_of((1 - place[0]) * half, TILE)
    length = place[1]

    @pl.when(step == 0)
    def _():
        shape = (half, LANES)
        lanes = lane_ids(shape)
        ones = jnp.where((lanes >= 1) & (lanes <= 3), 1.0, 0.0)
        hidden = (lanes == 0) & (row_ids(shape) >= length)
        keys_wide[:half, :LANES] = k_ref[pl.ds(prompt, half), :]
        keys_wide[half:, :LANES] = k_ref[pl.ds(target, half), :]
        keys_wide[:half, LANES:] = jnp.where(hidden, MASKED, ones).astype(jnp.bfloat16)
        keys_wide[half:, LANES:] = ones.astype(jnp.bfloat16)
        values_wide[:half, :LANES] = v_ref[pl.ds(prompt, half), :]
        values_wide[half:, :LANES] = v_ref[pl.ds(target, half), :]
        values_wide[:half, LANES:] = ones.astype(jnp.bfloat16)
        values_wide[half:, LANES:] = ones.astype(jnp.bfloat16)
        for piece in range(2 * half // TILE):
            rows = slice(piece * TILE, (piece + 1) * TILE)
            keys_t[:, rows] = keys_wide[rows, :LANES].astype(jnp.float32).T.astype(jnp.bfloat16)
        dk[...] = jnp.zeros_like(dk)
        dv[...] = jnp.zeros_like(dv)
        wide = (LANES, 2 * TILE)
        ids = row_ids(wide)

        def lanes_of(value):
            high, mid, rest = split3(value)
            return jnp.where(ids == 1, -high, jnp.where(ids == 2, -mid, jnp.where(ids == 3, -rest, 0.0)))

        def g_tile(start):
            if parts == 1:
                return g_refs[0][pl.ds(start, TILE), :]
            inside = pl.multiple_of(jnp.where(start < half, start, start - half), TILE)
            first = g_refs[0][pl.ds(inside, TILE), :]
            return jnp.where(start < half, first, g_refs[1][pl.ds(inside, TILE), :])

        def of_call(values):
            value = values[0]
            for call, later in enumerate(values[1:], 1):
                value = jnp.where(at(place) < call * per, value, later)
            return value

        def tile(start, seen, slot):
            spot = pl.ds(start, TILE)
            q_here = q_ref[spot, :].astype(jnp.float32) * SCALE
            g_here = g_tile(start).astype(jnp.float32)
            g_flip = g_here.T
            o_here = of_call([ref[spot, :].astype(jnp.float32) for ref in o_refs])
            product = g_flip * o_here.T
            inner = jnp.concatenate(
                [jnp.sum(product[:HEAD_DIM], axis=0, keepdims=True), jnp.sum(product[HEAD_DIM:], axis=0, keepdims=True)], axis=1)
            lse = of_call([ref[0, pl.ds(slot, 1), :] for ref in lse_refs])
            below = jnp.where(ids == 0, 1.0, lanes_of(lse))
            q_wide = jnp.concatenate([twin_lanes(q_here.T), below], axis=0).astype(jnp.bfloat16)
            g_wide = jnp.concatenate([twin_lanes(g_flip), lanes_of(inner)], axis=0).astype(jnp.bfloat16)
            probs = jnp.exp(matmul(keys_wide[:seen, :], q_wide))
            grads = matmul(values_wide[:seen, :], g_wide)
            scores = (probs * grads).astype(jnp.bfloat16)
            dk[:seen, :] += matmul(scores, twin_rows(q_here).astype(jnp.bfloat16))
            dv[:seen, :] += matmul(probs.astype(jnp.bfloat16), twin_rows(g_here).astype(jnp.bfloat16))
            dq[spot, :] = (untwin(matmul(keys_t[:, :seen], scores)) * SCALE).astype(jnp.bfloat16)

        tiles = half // TILE

        @pl.loop(0, tiles)
        def _(index):
            tile(pl.multiple_of(prompt + index * TILE, TILE), half, index)
            tile(pl.multiple_of(target + index * TILE, TILE), 2 * half, tiles + index)

        out_ref[...] = dq[...]

    for which, held in ((1, dk), (2, dv)):
        @pl.when(step == which)
        def _(held=held):
            out_ref[pl.ds(prompt, half), :] = held[:half, :].astype(jnp.bfloat16)
            out_ref[pl.ds(target, half), :] = held[half:, :].astype(jnp.bfloat16)


def attend_back(place, turn, pairs, qkv, mixed, grads, lse, held, behind):
    rows = qkv.shape[0]
    part = lambda shift: pl.BlockSpec((rows, LANES), lambda j, s, shift=shift: (0, 3 * at(s) + shift))
    calls = len(mixed)
    per = pairs // calls
    split = pairs // 2 if pairs % 2 == 0 else 0
    at = lambda s: (s[3] * split + turn) & (pairs - 1)
    parts = len(grads)
    block = pl.BlockSpec((rows, LANES), lambda j, s: (0, at(s) & (per - 1)))
    lse_block = pl.BlockSpec((1, rows // TILE, 2 * TILE), lambda j, s: (at(s) & (per - 1), 0, 0))
    grad_blocks = [pl.BlockSpec((grad.shape[0], LANES), lambda j, s: (0, at(s))) for grad in grads]
    seen = rows * rows * 3 // 4
    more = [] if held is None else [held]
    return pl.pallas_call(
        partial(attend_back_kernel, parts, calls, per, at),
        grid_spec=pltpu.PrefetchScalarGridSpec(
            num_scalar_prefetch=1, grid=(3,),
            in_specs=[part(0), part(1), part(2)] + [block] * calls + [lse_block] * calls + grad_blocks + [pl.BlockSpec(memory_space=pl.ANY)] * (len(more) + len(behind)),
            out_specs=pl.BlockSpec((rows, LANES), lambda j, s: (0, 3 * at(s) + j)),
            scratch_shapes=[pltpu.VMEM((rows, 2 * LANES), jnp.bfloat16), pltpu.VMEM((rows, 2 * LANES), jnp.bfloat16), pltpu.VMEM((LANES, rows), jnp.bfloat16),
                pltpu.VMEM((rows, LANES), jnp.bfloat16), pltpu.VMEM((rows, LANES), jnp.float32), pltpu.VMEM((rows, LANES), jnp.float32)],
        ),
        out_shape=jax.ShapeDtypeStruct(qkv.shape, jnp.bfloat16),
        input_output_aliases={4 + 2 * calls + parts: 0} if more else {},
        compiler_params=pltpu.CompilerParams(vmem_limit_bytes=60 << 20),
        cost_estimate=pl.CostEstimate(flops=int(COVER * 2 * seen * 10 * HEAD_DIM * 4), transcendentals=0, bytes_accessed=rows * LANES * 20),
        name="attend_back",
    )(place, qkv, qkv, qkv, *mixed, *lse, *grads, *more, *behind)


EPSILON = 1e-05
ROOT_HALF = math.sqrt(0.5)
DENSITY = 1.0 / math.sqrt(2.0 * math.pi)
LATE_HOP = 2
BIG = pltpu.CompilerParams(vmem_limit_bytes=60 << 20)
ANYWHERE = pl.BlockSpec(memory_space=pl.ANY)


def cost(flops, moved, special=0):
    return pl.CostEstimate(
        flops=int(flops * COVER), bytes_accessed=int(moved * COVER), transcendentals=special
    )


def matmul_last(left, right):
    return lax.dot_general(
        left, right, (((1,), (1,)), ((), ())), preferred_element_type=jnp.float32
    )


def dot_rows(left, right):
    return lax.dot_general(
        left, right, (((0,), (0,)), ((), ())), preferred_element_type=jnp.float32
    )


def standardise(values):
    centred = values - jnp.mean(values, axis=-1, keepdims=True)
    spread = jnp.mean(centred * centred, axis=-1, keepdims=True)
    inverse = lax.rsqrt(spread + EPSILON)
    return centred * inverse, inverse


def add_rows(ref, scale, shift):
    step = pl.program_id(0)

    @pl.when(step == 0)
    def _():
        ref[0:1, :] = scale
        ref[1:2, :] = shift

    @pl.when(step > 0)
    def _():
        ref[0:1, :] += scale
        ref[1:2, :] += shift


def row_specs(parts, count):
    rows = sum(part.shape[0] for part in parts) // count
    specs = []
    first = 0
    for part in parts:
        steps = part.shape[0] // rows
        specs.append(
            pl.BlockSpec(
                (rows, part.shape[1]),
                lambda j, *s, first=first, steps=steps: (jnp.clip(j - first, 0, steps - 1), 0),
            )
        )
        first += steps
    return rows, specs


def current(refs, count):
    value = refs[0][...]
    for index, ref in enumerate(refs[1:], 1):
        value = jnp.where(pl.program_id(0) < index * count // len(refs), value, ref[...])
    return value


def pack_kernel(place, query_ref, key_ref, value_ref, out_ref):
    for pair in range(query_ref.shape[1] // LANES):
        for which, ref in enumerate((query_ref, key_ref, value_ref)):
            start = (3 * pair + which) * LANES
            out_ref[:, start : start + LANES] = ref[:, pair * LANES : (pair + 1) * LANES]


def pack_columns(query, key, value, held, place):
    rows = query.shape[0]
    return pl.pallas_call(
        pack_kernel,
        grid_spec=pltpu.PrefetchScalarGridSpec(
            num_scalar_prefetch=1,
            grid=(1,),
            in_specs=[pl.BlockSpec((rows, held), lambda j, s: (0, s[0]))] * 3,
            out_specs=pl.BlockSpec((rows, 3 * held), lambda j, s: (0, 0)),
        ),
        out_shape=jax.ShapeDtypeStruct((rows, 3 * held), query.dtype),
        cost_estimate=cost(0, 12 * rows * held),
        name="pack_columns",
    )(place, query, key, value)


def first_kernel(parts, pieces, count, spots, *refs):
    frames = refs[:parts]
    ada = refs[parts]
    blocks = refs[parts + 1 : parts + 1 + pieces]
    low_ref, qkv_ref, weight_ref, sems = refs[-4:]
    rows = blocks[0].shape[0]

    @pl.when(pl.program_id(0) == 0)
    def _():
        copies = []
        for index, block in enumerate(blocks):
            start = pl.multiple_of(spots[index] * rows, rows)
            copy = pltpu.make_async_copy(
                block, weight_ref.at[pl.ds(start, rows), :], sems.at[index]
            )
            copy.start()
            copies.append(copy)
        for copy in copies:
            copy.wait()

    normed, _ = standardise(current(frames, count).astype(jnp.float32))
    low = ((1.0 + ada[0:1, :]) * normed + ada[1:2, :]).astype(jnp.bfloat16)
    low_ref[...] = low
    qkv_ref[...] = matmul(low, weight_ref[...]).astype(jnp.bfloat16)


def first_layer(frames, ada, blocks, spots):
    count = 4
    rows, specs = row_specs(frames, count)
    width = frames[0].shape[1]
    columns = blocks[0].shape[1]
    out = lambda size: pl.BlockSpec((rows, size), lambda j, s: (j, 0))
    shape = lambda *size: jax.ShapeDtypeStruct(size, jnp.bfloat16)
    return pl.pallas_call(
        partial(first_kernel, len(frames), len(blocks), count),
        grid_spec=pltpu.PrefetchScalarGridSpec(
            num_scalar_prefetch=1,
            grid=(count,),
            in_specs=specs
            + [pl.BlockSpec((2, width), lambda j, s: (0, 0))]
            + [ANYWHERE] * len(blocks),
            out_specs=[
                out(width),
                out(columns),
                pl.BlockSpec((width, columns), lambda j, s: (0, 0)),
            ],
            scratch_shapes=[pltpu.SemaphoreType.DMA((len(blocks),))],
        ),
        out_shape=[
            shape(rows * count, width),
            shape(rows * count, columns),
            shape(width, columns),
        ],
        compiler_params=BIG,
        cost_estimate=cost(
            2 * rows * count * width * columns, 4 * width * columns + 8 * rows * count * width
        ),
        name="first_layer",
    )(spots, *frames, ada, *blocks)


def second_kernel(pieces, calls, parts, count, place, *refs):
    mixed = refs[:pieces]
    tokens = refs[pieces : pieces + parts]
    out_w, ada = refs[pieces + parts : pieces + parts + 2]
    attended_ref, low_ref = refs[-2:]
    weights = out_w.reshape(out_w.shape[0] * out_w.shape[2], out_w.shape[3])
    spots = head_spots(place[4], calls, pieces)
    attended = current(tokens, count).astype(jnp.float32)
    for index, piece in enumerate(mixed):
        size = piece.shape[1]
        start = pl.multiple_of(spots[index] * size, size)
        attended = attended + matmul(piece[...], weights[pl.ds(start, size), :])
    attended_ref[...] = attended
    normed, _ = standardise(attended)
    low_ref[...] = ((1.0 + ada[0:1, :]) * normed + ada[1:2, :]).astype(jnp.bfloat16)


def second_layer(mixed, swapped, tokens, out_w, out_part, ada, spots):
    rows, width = tokens[-1].shape
    parts = len(tokens)
    count = 2 * parts
    size, token_specs = row_specs(tokens, count)
    later = count - 2
    block = lambda columns, order: pl.BlockSpec((size, columns), lambda j, s: (order(j), 0))
    first = lambda j: (j + later) % count
    items, _, piece, _ = out_w.shape
    return pl.pallas_call(
        partial(second_kernel, len(mixed) + len(swapped), len(mixed), parts, count),
        grid_spec=pltpu.PrefetchScalarGridSpec(
            num_scalar_prefetch=1,
            grid=(count,),
            in_specs=[block(part.shape[1], first) for part in mixed]
            + [block(part.shape[1], lambda j: j) for part in swapped]
            + token_specs
            + [
                pl.BlockSpec((items, 1, piece, width), lambda j, s: (0, out_part, 0, 0)),
                pl.BlockSpec((2, width), lambda j, s: (0, 0)),
            ],
            out_specs=[block(width, lambda j: jnp.maximum(j - later, 0)), block(width, first)],
        ),
        out_shape=[
            jax.ShapeDtypeStruct((rows, width), jnp.float32),
            jax.ShapeDtypeStruct((rows * parts, width), jnp.bfloat16),
        ],
        compiler_params=BIG,
        cost_estimate=cost(
            2 * rows * parts * width * width, 2 * width * width + 10 * rows * parts * width
        ),
        name="second_layer",
    )(spots, *mixed, *swapped, *tokens, out_w, ada)


def head_spots(seq, calls, pieces):
    if pieces == 1:
        return [0]
    own = [seq * calls + call for call in range(calls)]
    return own + [(1 - seq) * calls + call for call in range(pieces - calls)]


class Weights:
    def __init__(self, up, up_first, down, down_parts, hidden, width):
        self.up = up
        self.down = down
        self.width = width
        self.hidden = hidden
        fold = up.shape[3]
        self.block = min(512, fold, hidden // 2)
        per_chip = down_parts * down.shape[3]
        per_fold = fold // self.block
        chips, _, _, piece, _ = down.shape
        self.steps = hidden // self.block
        per_core = self.steps // 2
        block = self.block
        self.up_spec = pl.BlockSpec(
            (up.shape[0], 1, up.shape[2], block),
            lambda j: (0, up_first + j // per_fold, 0, j % per_fold),
        )
        self.down_spec = pl.BlockSpec(
            (block // per_chip, 1, down_parts, piece, width),
            lambda j: (j % per_core, j // per_core, 0, 0, 0),
        )
        self.per_chip = per_chip
        self.bytes = 2 * hidden * width


def hidden_kernel(per_chip, parts, x_ref, up_ref, down_ref, *refs):
    g_refs = refs[:parts]
    active_ref, grad_ref = refs[-2:]
    columns = min(256, active_ref.shape[1])
    size = x_ref.shape[0] // parts
    for start in range(0, active_ref.shape[1], columns):
        spot = slice(start, start + columns)
        up = up_ref[:, :, :, spot].reshape(-1, columns)
        chips = slice(start // per_chip, (start + columns) // per_chip)
        down = down_ref[chips].reshape(columns, -1)
        for index, g_ref in enumerate(g_refs):
            rows = slice(index * size, (index + 1) * size)
            upward = matmul(x_ref[rows, :], up)
            grad_active = matmul_last(g_ref[...], down)
            below = 0.5 * (1.0 + lax.erf(upward * ROOT_HALF))
            active_ref[rows, spot] = (upward * below).astype(jnp.bfloat16)
            slope = below + upward * (DENSITY * jnp.exp(-0.5 * upward * upward))
            grad_ref[rows, spot] = (grad_active * slope).astype(jnp.bfloat16)


def hidden_layer(x, grads, weights):
    rows, width = x.shape
    out = pl.BlockSpec((rows, weights.block), lambda j: (0, j))
    shape = jax.ShapeDtypeStruct((rows, weights.hidden), jnp.bfloat16)
    return pl.pallas_call(
        partial(hidden_kernel, weights.per_chip, len(grads)),
        grid=(weights.steps,),
        in_specs=[
            pl.BlockSpec((rows, width), lambda j: (0, 0)),
            weights.up_spec,
            weights.down_spec,
        ]
        + [pl.BlockSpec(grad.shape, lambda j: (0, 0)) for grad in grads],
        out_specs=[out, out],
        out_shape=[shape, shape],
        compiler_params=BIG,
        cost_estimate=cost(
            4 * rows * width * weights.hidden,
            2 * weights.bytes + 4 * rows * (width + weights.hidden),
        ),
        name="hidden_layer",
    )(x, weights.up, weights.down, *grads)


def accumulate(part, outs, total):
    step = pl.program_id(0)

    @pl.when(step == 0)
    def _():
        total[...] = part

    @pl.when(step > 0)
    def _():
        total[...] += part

    @pl.when(step == pl.num_programs(0) - 1)
    def _():
        rows = total.shape[0] // len(outs)
        for index, out_ref in enumerate(outs):
            value = total[index * rows : (index + 1) * rows, :]
            out_ref[...] = value.astype(out_ref.dtype)


def down_kernel(splits, a_ref, down_ref, *refs):
    total = refs[-1]
    part = matmul(a_ref[...], down_ref[...].reshape(-1, total.shape[1]))
    accumulate(part, refs[-1 - splits : -1], total)


def up_back_kernel(splits, g_ref, up_ref, *refs):
    total = refs[-1]
    weights = up_ref[...].reshape(total.shape[1], -1)
    accumulate(matmul_last(g_ref[...], weights), refs[-1 - splits : -1], total)


def hidden_to_width(kernel, name, held, weights, spec, array, rows, chunk, dtype, behind, splits=1):
    width = weights.width
    outs = pl.pallas_call(
        partial(kernel, splits),
        grid=(weights.steps,),
        in_specs=[pl.BlockSpec((rows, weights.block), lambda j: (chunk, j)), spec]
        + [ANYWHERE] * len(behind),
        out_specs=[pl.BlockSpec((rows // splits, width), lambda j: (0, 0))] * splits,
        out_shape=[jax.ShapeDtypeStruct((rows // splits, width), dtype)] * splits,
        scratch_shapes=[pltpu.VMEM((rows, width), jnp.float32)],
        compiler_params=BIG,
        cost_estimate=cost(
            2 * rows * width * weights.hidden,
            weights.bytes + rows * (2 * weights.hidden + 4 * width),
        ),
        name=name,
    )(held, array, *behind)
    return outs[0] if splits == 1 else outs


def down_part(active, weights, rows, chunk, dtype, behind=()):
    return hidden_to_width(
        down_kernel,
        "down_part",
        active,
        weights,
        weights.down_spec,
        weights.down,
        rows,
        chunk,
        dtype,
        behind,
    )


def up_back(grad, weights, rows, chunk, dtype, behind=(), splits=1):
    return hidden_to_width(
        up_back_kernel,
        "up_back",
        grad,
        weights,
        weights.up_spec,
        weights.up,
        rows,
        chunk,
        dtype,
        behind,
        splits,
    )


def middle_back_kernel(pieces, parts, place, *refs):
    own_ref, base_ref, top_ref, ada_ref, out_w = refs[:5]
    others = refs[5 : 5 + parts]
    outs = refs[-3 - pieces :]
    grad_ref, low_ref, ada_grad_ref = outs[:3]
    grad = own_ref[...] + current(others, 2).astype(jnp.float32)
    normed, inverse = standardise(base_ref[...])
    scaled = grad * (1.0 + ada_ref[0:1, :])
    scale = jnp.sum(grad * normed, axis=0, keepdims=True)
    shift = jnp.sum(grad, axis=0, keepdims=True)
    inner = jnp.mean(scaled * normed, axis=-1, keepdims=True)
    shifted = scaled - jnp.mean(scaled, axis=-1, keepdims=True) - normed * inner
    out = top_ref[...].astype(jnp.float32) + inverse * shifted
    grad_ref[...] = out
    low = out.astype(jnp.bfloat16)
    low_ref[...] = low
    weights = out_w.reshape(out_w.shape[0] * out_w.shape[2], out_w.shape[3])
    spots = head_spots(1 - place[4], 1, pieces)
    for index, mixed_ref in enumerate(outs[3:]):
        size = mixed_ref.shape[1]
        start = pl.multiple_of(spots[index] * size, size)
        mixed_ref[...] = matmul_last(low, weights[pl.ds(start, size), :]).astype(jnp.bfloat16)
    add_rows(ada_grad_ref, scale, shift)


def middle_back(own, other, attended, cotangent, ada, out_w, out_part, spots, sizes, behind):
    rows, width = attended.shape
    count = 2
    block = lambda size: pl.BlockSpec((rows // count, size), lambda j, s: (j, 0))
    items, _, piece, _ = out_w.shape
    _, other_specs = row_specs(other, count)
    return pl.pallas_call(
        partial(middle_back_kernel, len(sizes), len(other)),
        grid_spec=pltpu.PrefetchScalarGridSpec(
            num_scalar_prefetch=1,
            grid=(count,),
            in_specs=[block(width)] * 3
            + [
                pl.BlockSpec((2, width), lambda j, s: (0, 0)),
                pl.BlockSpec((items, 1, piece, width), lambda j, s: (0, out_part, 0, 0)),
            ]
            + other_specs
            + [ANYWHERE] * len(behind),
            out_specs=[block(width), block(width), pl.BlockSpec((2, width), lambda j, s: (0, 0))]
            + [block(size) for size in sizes],
        ),
        out_shape=[
            jax.ShapeDtypeStruct((rows, width), jnp.float32),
            jax.ShapeDtypeStruct((rows, width), jnp.bfloat16),
            jax.ShapeDtypeStruct((2, width), jnp.float32),
        ]
        + [jax.ShapeDtypeStruct((rows, size), jnp.bfloat16) for size in sizes],
        compiler_params=BIG,
        cost_estimate=cost(2 * rows * width * width, 2 * width * width + 20 * rows * width),
        name="middle_back",
    )(spots, own, attended, cotangent, ada, out_w, *other, *behind)


def first_back_kernel(splits, grad_ref, weight_ref, frames, *refs):
    outs, ada_grad_ref = refs[-1 - splits : -1], refs[-1]
    grad = matmul_last(grad_ref[...], weight_ref[...])
    normed, _ = standardise(frames[...].astype(jnp.float32))
    for index, out_ref in enumerate(outs):

        @pl.when((pl.program_id(0) == index) | (splits == 1))
        def _(out_ref=out_ref):
            out_ref[...] = grad.astype(jnp.bfloat16)

    scale = jnp.sum(grad * normed, axis=0, keepdims=True)
    shift = jnp.sum(grad, axis=0, keepdims=True)
    add_rows(ada_grad_ref, scale, shift)


def first_back(grad, weights, frames, part, behind, splits=1):
    width, columns = weights.shape
    count = 2
    rows = frames.shape[0] // count
    block = pl.BlockSpec((rows, width), lambda j: (j, 0))
    out = block if splits == 1 else pl.BlockSpec((rows, width), lambda j: (0, 0))
    return pl.pallas_call(
        partial(first_back_kernel, splits),
        grid=(count,),
        in_specs=[
            pl.BlockSpec((rows, columns), lambda j: (part * count + j, 0)),
            pl.BlockSpec((width, columns), lambda j: (0, 0)),
            block,
        ]
        + [ANYWHERE] * len(behind),
        out_specs=[out] * splits + [pl.BlockSpec((2, width), lambda j: (0, 0))],
        out_shape=[jax.ShapeDtypeStruct((rows * count // splits, width), jnp.bfloat16)] * splits
        + [jax.ShapeDtypeStruct((2, width), jnp.float32)],
        compiler_params=BIG,
        cost_estimate=cost(
            2 * rows * count * width * columns,
            2 * width * columns + 2 * rows * count * (2 * width + columns),
        ),
        name="first_back",
    )(grad, weights, frames, *behind)


def stacked_dot(lefts, rights):
    total = None
    for left, right in zip(lefts, rights):
        part = dot_rows(left, right)
        total = part if total is None else total + part
    return total


def cut_rows(ref, count):
    rows = ref.shape[0] // count
    return [ref[j * rows : (j + 1) * rows, :] for j in range(count)]


def put_sum(out_ref, other_ref, value):
    if other_ref is not None:
        value = value + other_ref[...].astype(jnp.float32)
    out_ref[...] = value.astype(jnp.bfloat16)


def put_first(place, out_ref, firsts):
    for index, ref in enumerate(firsts):
        rows = ref.shape[0]
        start = pl.multiple_of(place[5 + index] * rows, rows)
        ref[...] = out_ref[pl.ds(start, rows), :]


def ring_outputs(width, columns, block, more, chips):
    rows = [width] + [width // chips] * (2 if more else 0)
    specs = [pl.BlockSpec((size, block), lambda j, s: (0, j)) for size in rows]
    return specs, [jax.ShapeDtypeStruct((size, columns), jnp.bfloat16) for size in rows]


def hidden_grads_kernel(count, more, place, *refs):
    active, upward = refs[:2]
    grads, low = refs[2 : 2 + count], refs[2 + count]
    other = refs[3 + count] if more else None
    outs = refs[-3:] if more else refs[-1:]
    out_ref = outs[0]
    step = pl.program_id(0)
    steps = pl.num_programs(0) // 2

    @pl.when(step < steps)
    def _():
        put_sum(
            out_ref, other, stacked_dot(cut_rows(active, count), [ref[...] for ref in grads])
        )

    @pl.when(step >= steps)
    def _():
        put_sum(out_ref, other, dot_rows(low[...], upward[...]))

    put_first(place, out_ref, outs[1:])


def hidden_grads(place, who, chips, active, upward, grads, low, other, behind):
    total, hidden = active.shape
    half = hidden // 2
    rows, width = grads[0].shape
    count = len(grads)
    block = 512
    steps = half // block
    whole = pl.BlockSpec((total, width), lambda j, s: (0, 0))
    grad = pl.BlockSpec((rows, block), lambda j, s: (0, jnp.minimum(j, steps - 1)))
    out = pl.BlockSpec((width, block), lambda j, s: (0, j))
    more = [] if other is None else [other]
    specs, shapes = ring_outputs(width, 2 * half, block, more, chips)
    return pl.pallas_call(
        partial(hidden_grads_kernel, count, bool(more)),
        grid_spec=pltpu.PrefetchScalarGridSpec(
            num_scalar_prefetch=1,
            grid=(2 * steps,),
            in_specs=[
                pl.BlockSpec((total, half), lambda j, s: (0, s[who])),
                pl.BlockSpec(
                    (total, block), lambda j, s: (0, s[who] * steps + jnp.maximum(j - steps, 0))
                ),
            ]
            + [grad] * count
            + [whole]
            + [out] * len(more)
            + [ANYWHERE] * len(behind),
            out_specs=specs,
        ),
        out_shape=shapes,
        compiler_params=BIG,
        cost_estimate=cost(4 * total * half * width, 8 * total * half + 4 * width * half),
        name="hidden_grads",
    )(place, active, upward, *grads, low, *more, *behind)


def tail_grads_kernel(first, more, pieces, calls, place, low, grad, attended, *refs):
    mixed = refs[:pieces]
    other = refs[pieces] if more else None
    outs = refs[-3:] if more else refs[-1:]
    out_ref = outs[0]

    @pl.when(pl.program_id(0) < first)
    def _():
        put_sum(out_ref, other, dot_rows(low[...], grad[...]))

    @pl.when(pl.program_id(0) >= first)
    def _():
        spots = head_spots(place[4], calls, pieces)
        for index, piece in enumerate(mixed):
            size = piece.shape[1]
            rows = pl.ds(pl.multiple_of(spots[index] * size, size), size)
            value = dot_rows(piece[...], attended[...])
            if more:
                value = value + other[rows, :].astype(jnp.float32)
            out_ref[rows, :] = value.astype(jnp.bfloat16)

    put_first(place, out_ref, outs[1:])


def tail_grads(place, who, chips, low_one, grad_qkv, mixed, swapped, attended_low, other, behind):
    total, width = low_one.shape
    rows = attended_low.shape[0]
    block = 256
    first = grad_qkv.shape[1] // 2 // block
    second = width // 2 // block
    out = pl.BlockSpec((width, block), lambda j, s: (0, j))
    more = [] if other is None else [other]
    specs, shapes = ring_outputs(width, (first + second) * block, block, more, chips)
    return pl.pallas_call(
        partial(
            tail_grads_kernel, first, bool(more), len(mixed) + len(swapped), len(mixed)
        ),
        grid_spec=pltpu.PrefetchScalarGridSpec(
            num_scalar_prefetch=1,
            grid=(first + second,),
            in_specs=[
                pl.BlockSpec((total, width), lambda j, s: (0, 0)),
                pl.BlockSpec(
                    (total, block), lambda j, s: (0, s[who] * first + jnp.minimum(j, first - 1))
                ),
                pl.BlockSpec(
                    (rows, block), lambda j, s: (0, s[who] * second + jnp.maximum(j - first, 0))
                ),
            ]
            + [pl.BlockSpec((rows, part.shape[1]), lambda j, s: (0, 0)) for part in mixed]
            + [pl.BlockSpec((rows, part.shape[1]), lambda j, s: (1, 0)) for part in swapped]
            + [out] * len(more)
            + [ANYWHERE] * len(behind),
            out_specs=specs,
        ),
        out_shape=shapes,
        compiler_params=BIG,
        cost_estimate=cost(
            2 * width * block * (total * first + rows * second), 8 * total * width
        ),
        name="tail_grads",
    )(place, low_one, grad_qkv, attended_low, *mixed, *swapped, *more, *behind)


def input_back_kernel(parts, count, own_ref, tokens_ref, ada_ref, base_ref, *refs):
    out_ref = refs[-1]
    grad = own_ref[...].astype(jnp.float32) + current(refs[:parts], count).astype(jnp.float32)
    normed, inverse = standardise(tokens_ref[...].astype(jnp.float32))
    scaled = grad * (1.0 + ada_ref[0:1, :])
    inner = jnp.mean(scaled * normed, axis=-1, keepdims=True)
    shifted = scaled - jnp.mean(scaled, axis=-1, keepdims=True) - normed * inner
    out_ref[...] = base_ref[...] + inverse * shifted


def input_back(own, others, tokens, ada, base):
    rows, width = tokens.shape
    count = 4
    block = pl.BlockSpec((rows // count, width), lambda j: (j, 0))
    _, specs = row_specs(others, count)
    return pl.pallas_call(
        partial(input_back_kernel, len(others), count),
        grid=(count,),
        in_specs=[block, block, pl.BlockSpec((2, width), lambda j: (0, 0)), block] + specs,
        out_specs=block,
        out_shape=jax.ShapeDtypeStruct((rows, width), jnp.float32),
        compiler_params=BIG,
        cost_estimate=cost(20 * rows * width, 14 * rows * width),
        name="input_back",
    )(own, tokens, ada, base, *others)


def join_tail_kernel(held, place, mine, seq_ref, core_ref, both_ref, *outs):
    core, seq = place[2], place[4]
    half = 3 * held // 2
    width = held // 2

    def chosen(side, core_half, spot):
        near = jnp.where(core == core_half, mine[:, spot], core_ref[:, spot])
        far = jnp.where(core == core_half, seq_ref[:, spot], both_ref[:, spot])
        return jnp.where(seq == side, near, far)

    for side in range(2):
        for core_half in range(2):
            for pair in range(width // LANES):
                for which in range(3):
                    start = (3 * pair + which) * LANES
                    to = side * held + core_half * width + pair * LANES
                    value = chosen(side, core_half, slice(start, start + LANES))
                    outs[which][:, to : to + LANES] = value
    for core_half in range(2):
        spot = slice(half, None)
        near = jnp.where(core == core_half, mine[:, spot], core_ref[:, spot])
        far = jnp.where(core == core_half, seq_ref[:, spot], both_ref[:, spot])
        outs[3][:, core_half * held : (core_half + 1) * held] = near + far


def join_tail(place, parts, held):
    rows, columns = parts[0].shape
    whole = lambda size: pl.BlockSpec((rows, size), lambda j, s: (0, 0))
    return pl.pallas_call(
        partial(join_tail_kernel, held),
        grid_spec=pltpu.PrefetchScalarGridSpec(
            num_scalar_prefetch=1,
            grid=(1,),
            in_specs=[whole(columns)] * 4,
            out_specs=[whole(2 * held)] * 4,
        ),
        out_shape=[jax.ShapeDtypeStruct((rows, 2 * held), jnp.float32)] * 4,
        cost_estimate=cost(0, 16 * rows * columns),
        name="join_tail",
    )(place, *parts)


def exact(left, right):
    return jnp.dot(left, right, precision=lax.Precision.HIGHEST)


def rounded(total, other=None):
    if other is not None:
        total = total + other.astype(jnp.float32)
    return total.astype(jnp.bfloat16)


def tie(*values):
    return lax.optimization_barrier(values)


def cut(value, start, size, axis):
    return lax.dynamic_slice_in_dim(value, start, size, axis, allow_negative_indices=False)


def pick(value, index, axis):
    return lax.dynamic_index_in_dim(
        value, index, axis, keepdims=False, allow_negative_indices=False
    )


def ring_of(items_count):
    chips = items_count // 2
    outer = 4 if chips % 4 == 0 else chips
    inner = chips // outer
    order = [a * inner for a in range(outer)]
    for turn, a in enumerate(reversed(range(outer))):
        beside = list(range(1, inner))
        order += [a * inner + b for b in (beside if turn % 2 == 0 else beside[::-1])]
    return order


class Mover:
    def __init__(self, items_count, seq_count):
        self.items_count = items_count
        self.seq_count = seq_count
        self.pair = seq_count == 2
        self.chips = items_count // 2
        order = ring_of(items_count)
        self.forward = []
        self.backward = []
        chips = self.chips
        table = np.zeros((items_count, 2 * chips + 2), np.int32)
        hops = list(range(chips // 2 + 1)) + [-hop for hop in range(1, (chips + 1) // 2)]
        for spot in range(self.chips):
            for core in range(2):
                here = 2 * order[spot] + core
                next_one = 2 * order[(spot + 1) % self.chips] + core
                self.forward.append((here, next_one))
                self.backward.append((next_one, here))
                for ahead in range(self.chips):
                    table[here, ahead] = order[(spot + ahead) % self.chips]
                table[here, chips] = core
                table[here, chips + 1] = 1 - core
                for spot_of, hop in enumerate(hops):
                    ahead = hop if core == 1 else -hop
                    table[here, chips + 2 + spot_of] = order[(spot + ahead) % chips]
        self.both_ways = [p for p in self.forward if p[0] % 2 == 0]
        self.both_ways += [p for p in self.backward if p[0] % 2 == 1]
        self.item = lax.axis_index("items")
        row = pick(jnp.asarray(table), self.item, 0)
        self.ahead = [row[j] for j in range(self.chips)]
        self.core = row[self.chips]
        self.beside = row[self.chips + 1]
        self.spots = row[self.chips + 2 :]
        self.seq = lax.axis_index("seq")
        self.quarter = 2 * self.core + self.seq

    def flip(self, value, bit):
        pairs = [(i, i ^ bit) for i in range(self.items_count)]
        return lax.ppermute(value, "items", pairs)

    def opposite(self, value):
        pairs = [(2 * i + x, 2 * (i ^ 1) + 1 - x) for i in range(self.items_count) for x in (0, 1)]
        return lax.ppermute(value, ("items", "seq"), pairs)

    def across(self, value):
        return lax.ppermute(value, "seq", [(0, 1), (1, 0)])

    def gather_items(self, value, summed, early, late):
        for bit in [1 << k for k in range(self.items_count.bit_length() - 1)]:
            summed = summed + self.flip(summed, bit)
        beside = self.flip(value, 1)
        block = jnp.where(
            self.core == 0,
            jnp.concatenate([value, beside], axis=0),
            jnp.concatenate([beside, value], axis=0),
        )
        direct = [block]
        for hop in range(1, self.chips // 2 + 1):
            moved = lax.ppermute(direct[-1], "items", self.both_ways)
            if hop == min(LATE_HOP, self.chips // 2):
                late, summed, moved, early = tie(late, summed, moved, early)
            direct.append(moved)
        beside = [self.flip(moved, 1) for moved in direct[1 : (self.chips + 1) // 2]]
        return direct + beside, summed, early, late

    def sum_seq(self, value):
        return value + self.across(value) if self.pair else lax.psum(value, "seq")

    def scatter_seq(self, value):
        rows = value.shape[0] // self.seq_count
        if self.pair:
            sent = cut(value, (1 - self.seq) * rows, rows, 0)
            kept = cut(value, self.seq * rows, rows, 0)
            return kept + self.across(sent.astype(jnp.bfloat16)).astype(jnp.float32)
        return lax.psum_scatter(
            value.astype(jnp.bfloat16), "seq", scatter_dimension=0, tiled=True
        ).astype(jnp.float32)

    def join_cores(self, value):
        parts = value.reshape(2, -1, value.shape[1])
        kept = pick(parts, self.core, 0)
        other = self.flip(pick(parts, self.beside, 0), 1)
        return jnp.where(self.core == 0, kept, other), jnp.where(self.core == 0, other, kept)

    def join_columns(self, value):
        rows = value.shape[0] // self.seq_count
        if self.pair:
            kept = cut(value, self.seq * rows, rows, 0)
            other = self.across(cut(value, (1 - self.seq) * rows, rows, 0))
            return jnp.where(self.seq == 0, kept, other), jnp.where(self.seq == 0, other, kept)
        moved = lax.all_to_all(value, "seq", split_axis=0, concat_axis=0, tiled=True)
        return tuple(moved[j * rows : (j + 1) * rows] for j in range(self.seq_count))


class RingSum:
    def __init__(self, mover, make, behind, ready=()):
        self.mover = mover
        self.chips = mover.chips
        self.make = make
        self.flows = None
        sent, self.ready = tie(make(False, None, behind)[0], list(ready))
        self.sent = sent
        self.arriving = [mover.flip(sent, 1)]

    def block(self, ahead):
        return pick(self.both, self.mover.ahead[ahead % self.chips], 0)

    def add_own(self, behind):
        self.whole, *firsts = self.make(True, self.arriving[0], behind)
        self.both = self.whole.reshape(self.chips, -1, self.whole.shape[1])
        self.arrived = []
        flows = [
            (self.mover.forward, 1, self.chips // 2),
            (self.mover.backward, -1, (self.chips - 1) // 2),
        ]
        if not firsts:
            firsts = [self.block(sign * left) for _, sign, left in flows]
        self.send(list(zip(flows, firsts)))

    def send(self, flows):
        self.arriving = [lax.ppermute(value, "items", flow[0]) for flow, value in flows]
        self.flows = [(pairs, sign, left - 1) for (pairs, sign, left), _ in flows]

    def advance(self, anchor=None):
        flows = []
        if anchor is not None:
            self.arriving, anchor = tie(self.arriving, anchor)
        for flow, value in zip(self.flows, self.arriving):
            if flow[2]:
                flows.append((flow, self.block(flow[1] * flow[2]) + value))
            else:
                self.arrived.append(value)
        self.send(flows)
        return anchor

    def finish(self, anchor=None):
        while self.arriving:
            self.advance()
        if anchor is not None:
            self.arrived, anchor = tie(self.arrived, anchor)
        result = self.block(0).astype(jnp.float32)
        for value in self.arrived:
            result = result + value.astype(jnp.float32)
        return result if anchor is None else (result, anchor)


def in_rows(value):
    return with_layout_constraint(value, Layout((0, 1)))


def halves(value, core):
    half = value.shape[1] // 2
    return cut(value, core * half, half, 1)


def parted(value, at):
    return (None, None) if value is None else (value[:, :at], value[:, at:])


def shards(
    tokens,
    cotangent,
    prompt_len,
    section_ids,
    section_table,
    w_query,
    w_key,
    w_value,
    w_out,
    w_up,
    w_down,
    w_ada_one,
    w_ada_two,
):
    items_count = lax.axis_size("items")
    seq_count = lax.axis_size("seq")
    mover = Mover(items_count, seq_count)
    chips = mover.chips
    batch, rows, width = tokens.shape
    total_rows = rows * seq_count
    hidden = w_up.shape[1] // seq_count
    held = width // seq_count
    pairs = held // LANES
    piece = w_query.shape[0]
    units = w_down.shape[0] // seq_count
    tokens = tokens.reshape(rows, width)
    grad_low = cotangent.reshape(rows, width)

    def quarters(one, two):
        return jnp.stack([one[:, :width], one[:, width:], two[:, :width], two[:, width:]])

    up_shard = w_up.reshape(piece, chips, 2, seq_count, units).transpose(3, 0, 2, 1, 4)
    up_shard = pick(up_shard, mover.seq, 0).reshape(piece, hidden)
    down_shard = cut(w_down, mover.seq * units, units, 0)
    merged = hidden % width == 0 and units % piece == 0
    late = down_shard
    if merged:
        folds = hidden // width
        down_parts = units // piece
        up_rows = [up_shard[:, j * width : (j + 1) * width] for j in range(folds)]
        late = jnp.concatenate([down_shard] + up_rows + [w_out], axis=0)

    table_part = cut(section_table, mover.item * piece, piece, 1)
    ada_part = jnp.dot(
        table_part,
        jnp.concatenate([w_ada_one, w_ada_two], axis=1),
        preferred_element_type=jnp.float32,
    )
    ada_part = quarters(ada_part[:, : 2 * width], ada_part[:, 2 * width :])
    prompt_at = mover.seq if mover.pair else jnp.zeros((), jnp.int32)
    place = jnp.stack(
        [prompt_at, prompt_len[0], mover.core, mover.beside, mover.seq]
        + [mover.ahead[chips // 2], mover.ahead[-((chips - 1) // 2) % chips]]
    )
    seq_place = jnp.reshape(mover.seq, (1,)).astype(jnp.int32)
    mine = pack_columns(w_query, w_key, w_value, held, seq_place)
    early = [mover.across(tokens)] if mover.pair else []
    blocks, ada_sum, early, late = mover.gather_items(
        mine, ada_part, early, late
    )

    def gathered(value):
        return lax.all_gather(value, "items", axis=0, tiled=False)

    if merged:
        rest = gathered(late)
        rest = rest.reshape(items_count, down_parts + folds + 1, piece, width)
        by_core = rest.reshape((chips, 2) + rest.shape[1:])
        weights = Weights(rest, down_parts, by_core, down_parts, hidden, width)
        out_w, out_part = rest, down_parts + folds
    else:
        by_core = gathered(late).reshape(chips, 2, 1, units, width)
        weights = Weights(gathered(up_shard)[:, None], 0, by_core, 1, hidden, width)
        out_w, out_part = gathered(w_out)[:, None], 0

    choose = (section_ids[0] == jnp.arange(section_table.shape[0])).astype(jnp.float32)
    ada = jnp.sum(choose[None, :, None] * ada_sum, axis=1)
    ada_one = ada[:2]
    ada_two = ada[2:]

    if mover.pair:
        tokens_other, grad_sent = tie(early[0], grad_low)
        grad_other = mover.across(grad_sent)
        frames = [tokens, tokens_other]
        grads = [grad_low, grad_other]
        calls = 2 if pairs % 2 == 0 else 1
    else:
        frames = [lax.all_gather(tokens, "seq", axis=0, tiled=True)]
        grads = [lax.all_gather(grad_low, "seq", axis=0, tiled=True)]
        calls = 1
    low_one, qkv, qkv_w = first_layer(frames, ada_one, blocks, mover.spots)
    per_call = pairs // calls
    mixed_heads = []
    lse = []
    for call in range(calls):
        behind = grads[1:] + mixed_heads
        out = attend(qkv, place, call * per_call, per_call, behind)
        mixed_heads.append(out[0])
        lse.append(out[1])
    if mover.pair:
        mixed_far = []
        for call in range(calls):
            sent = mixed_heads[call]
            if mixed_far:
                sent, mixed_far[-1] = tie(sent, mixed_far[-1])
            mixed_far.append(mover.across(sent))
        attended, low_two = second_layer(
            mixed_heads, mixed_far, frames[::-1], out_w, out_part, ada_two, place
        )
        lows = low_two
        active, upward = hidden_layer(lows, grads, weights)
        first_half, last_half = up_back(upward, weights, rows, 1, jnp.bfloat16, (), 2)
        start = [first_half]
        ready = [mover.across(first_half), last_half]
    else:
        mixed = lax.all_to_all(mixed_heads[0], "seq", split_axis=0, concat_axis=1, tiled=True)
        attended, low_two = second_layer(
            [mixed], [], [tokens], out_w, out_part, ada_two, place
        )
        lows = lax.all_gather(low_two, "seq", axis=0, tiled=True)
        active, upward = hidden_layer(lows, grads, weights)
        start = []
        ready = []

    down_columns = hidden // 2

    def hidden_parts(own, other, behind):
        who = 2 if own else 3
        if down_columns == width:
            return hidden_grads(place, who, chips, active, upward, grads, lows, other, behind)
        core = mover.core if own else mover.beside
        first, second = parted(other, down_columns)
        down = dot_rows(halves(active, core), grads[0]).reshape(width, down_columns)
        up = dot_rows(lows, halves(upward, core))
        return [in_rows(jnp.concatenate([rounded(down, first), rounded(up, second)], axis=1))]

    ring = RingSum(mover, hidden_parts, start, ready)
    if mover.pair:
        own = up_back(upward, weights, rows, 0, jnp.float32, [ring.sent])
        from_other = [ring.ready[0], mover.across(ring.ready[1])]
        sizes = [held, held]
    else:
        own = lax.psum_scatter(
            up_back(upward, weights, total_rows, 0, jnp.bfloat16),
            "seq",
            scatter_dimension=0,
            tiled=True,
        ).astype(jnp.float32)
        from_other = [jnp.zeros((rows, width), jnp.bfloat16)]
        sizes = [width]
    ring.add_own([own])
    grad_attended, attended_low, ada_two_rows, *grad_mixed = middle_back(
        own,
        from_other,
        attended,
        grad_low,
        ada_two,
        out_w,
        out_part,
        place,
        sizes,
        [ring.whole],
    )
    if mover.pair:
        out_other = down_part(active, weights, rows, 1, jnp.bfloat16, grad_mixed[:1])
        grad_heads = [grad_mixed[1], mover.across(grad_mixed[0])]
        out_other = ring.advance(out_other)
        out_own = down_part(active, weights, rows, 0, jnp.bfloat16, [out_other])
        filler = [out_own]
        out_other = mover.across(out_other)
    else:
        grad_heads = [
            lax.all_to_all(grad_mixed[0], "seq", split_axis=1, concat_axis=0, tiled=True)
        ]
        filler = []

    split = pairs // 2 if pairs % 2 == 0 else 0

    def tail_parts(own, other, behind):
        if mover.pair:
            return tail_grads(
                place,
                2 if own else 3,
                chips,
                low_one,
                grad_qkv,
                mixed_heads,
                mixed_far,
                attended_low,
                other,
                behind,
            )
        core = mover.core if own else mover.beside
        first, second = parted(other, grad_qkv.shape[1] // 2)
        qkv_part = rounded(dot_rows(low_one, halves(grad_qkv, core)), first)
        out_part = rounded(dot_rows(mixed, halves(attended_low, core)), second)
        return [in_rows(jnp.concatenate([qkv_part, out_part], axis=1))]

    tail = None
    grad_qkv = None
    for turn in range(pairs):
        behind = filler
        filler = []
        grad_qkv = attend_back(
            place, turn, pairs, qkv, mixed_heads, grad_heads, lse, grad_qkv, behind
        )
        grad_qkv = ring.advance(grad_qkv)
        if turn + 1 == split:
            tail = RingSum(mover, tail_parts, [])
            filler = [tail.sent]
    if tail is None:
        tail = RingSum(mover, tail_parts, [])
    tail.add_own([])
    if mover.pair:
        near_half, last_half, far_rows = first_back(
            grad_qkv, qkv_w, frames[1], 1, [tail.whole, out_other], 2
        )
        near_half = mover.across(near_half)
        last_half = tail.advance(last_half)
        hidden_total, last_half = ring.finish(last_half)
        own_first, own_rows = first_back(grad_qkv, qkv_w, frames[0], 0, [last_half])
        own_rows, near_half, last_half, out_other = tail.advance(
            [own_rows, near_half, last_half, out_other]
        )
        far_parts = [near_half, mover.across(last_half)]
        ada_rows = jnp.concatenate([own_rows + far_rows, ada_two_rows])
        ada_rows = ada_rows + mover.across(ada_rows)
        layer_sum = out_own + out_other.astype(jnp.float32)
    else:
        grad_first, ada_one_rows = first_back(grad_qkv, qkv_w, frames[0], 0, [tail.whole])
        ada_rows = lax.psum(jnp.concatenate([ada_one_rows, ada_two_rows]), "seq")
        own_first = lax.psum_scatter(grad_first, "seq", scatter_dimension=0, tiled=True)
        far_parts = [jnp.zeros((rows, width), jnp.bfloat16)]
        hidden_total = ring.finish()
        layer_sum = lax.psum_scatter(
            down_part(active, weights, total_rows, 0, jnp.bfloat16),
            "seq",
            scatter_dimension=0,
            tiled=True,
        ).astype(jnp.float32)
    layer_out = (attended + layer_sum).astype(jnp.bfloat16)
    sums = choose[None, :, None] * ada_rows[:, None, :]
    for bit in [1 << k for k in range(items_count.bit_length() - 1)]:
        sums = sums + mover.flip(sums, bit)
        if bit == 1:
            sums = tail.advance(sums)
        if bit == 4:
            sums, far_parts = tie(sums, far_parts)
    input_grad = input_back(own_first, far_parts, tokens, ada_one, grad_attended)
    out_piece = piece // seq_count
    first_row = mover.item * piece + mover.seq * out_piece
    table_rows = cut(section_table, first_row, out_piece, 1).astype(jnp.float32)
    ada_grads = jnp.einsum("sr,ksd->krd", table_rows, sums, precision=lax.Precision.HIGHEST)
    grad_ada_one = jnp.concatenate([ada_grads[0], ada_grads[1]], axis=1)
    grad_ada_two = jnp.concatenate([ada_grads[2], ada_grads[3]], axis=1)
    own_ada = quarters(
        *(cut(w, mover.seq * out_piece, out_piece, 0) for w in (w_ada_one, w_ada_two))
    ).astype(jnp.float32)
    grad_table = jnp.einsum("ksd,krd->sr", sums, own_ada, precision=lax.Precision.HIGHEST)

    grad_down = hidden_total[:, :down_columns].reshape(units, width)
    up_sides = mover.join_columns(
        jnp.concatenate(mover.join_cores(hidden_total[:, down_columns:]), axis=1)
    )
    grad_up = jnp.stack(
        [side.reshape(out_piece, 2, chips, units) for side in up_sides], axis=1
    )
    grad_up = grad_up.transpose(0, 3, 2, 1, 4).reshape(out_piece, hidden * seq_count)
    if mover.pair:
        quarters_of = tail.finish().reshape(4, piece // 2, -1)
        mine, to_seq, to_core, to_both = (
            pick(quarters_of, mover.quarter ^ flipped, 0) for flipped in (0, 1, 2, 3)
        )
        grad_query, grad_key, grad_value, grad_out = join_tail(
            place,
            [mine, mover.across(to_seq), mover.flip(to_core, 1), mover.opposite(to_both)],
            held,
        )
    else:
        tail_total = tail.finish()
        cores = jnp.concatenate(mover.join_cores(tail_total), axis=1)
        half_qkv = 3 * held // 2
        half_all = cores.shape[1] // 2
        qkv_total = jnp.concatenate(
            [cores[:, :half_qkv], cores[:, half_all : half_all + half_qkv]], axis=1
        )
        out_total = jnp.concatenate([cores[:, half_qkv:half_all], cores[:, half_all + half_qkv :]], axis=1)
        sides = mover.join_columns(qkv_total)
        grad_out = mover.scatter_seq(out_total)
        grad_query, grad_key, grad_value = (
            jnp.concatenate(
                [
                    side[:, (3 * p + j) * LANES : (3 * p + j + 1) * LANES]
                    for side in sides
                    for p in range(pairs)
                ],
                axis=1,
            )
            for j in range(3)
        )
    return (
        layer_out.reshape(batch, rows, width),
        input_grad.reshape(batch, rows, width),
        grad_query,
        grad_key,
        grad_value,
        grad_out,
        grad_up,
        grad_down,
        grad_ada_one,
        grad_ada_two,
        grad_table,
    )


def solution(mesh):
    return jax.shard_map(
        shards,
        mesh=mesh,
        in_specs=(
            P("items", "seq", None),
            P("items", "seq", None),
            P("items"),
            P("items"),
            P(),
            P("items", None),
            P("items", None),
            P("items", None),
            P("items", None),
            P("items", None),
            P("items", None),
            P("items", None),
            P("items", None),
        ),
        out_specs=(
            P("items", "seq", None),
            P("items", "seq", None),
            P(("items", "seq"), None),
            P(("items", "seq"), None),
            P(("items", "seq"), None),
            P(("items", "seq"), None),
            P(("items", "seq"), None),
            P(("items", "seq"), None),
            P(("items", "seq"), None),
            P(("items", "seq"), None),
            P(None, ("items", "seq")),
        ),
        check_vma=False,
    )
```
